32 devices in a mesh: dp: 16 (over z, y, x), strip: 2 (over core).
Axes of the slice: x: 2, y: 2, z: 4, core: 2. Of those that a mesh axis runs over, the one named last changes fastest.
Arguments:
- weights: float32 [10952704], P(('dp', 'strip'))
- blocks: float32 [512, 128, 128], P('dp'), may hold values from -0.1875 to 0.1875
- stat_left: float32 [512, 128, 128], P('dp')
- stat_right: float32 [512, 128, 128], P('dp')
- root_left: float32 [512, 128, 128], P('dp')
- root_right: float32 [512, 128, 128], P('dp')
- first_moment: float32 [10952704], P(('dp', 'strip')), may hold values from -0.0029296875 to 0.0029296875
- second_moment: float32 [10952704], P(('dp', 'strip')), may hold values from 1.4404297e-07 to 5.7861325e-07
- image: bfloat16 [16, 257, 768], P('dp'), may hold values from -6 to 6
- camera: int32 [16], P('dp'), may hold values from 0 to 31
- samples: int32 [16, 3, 16, 512], P('dp', None, None, 'strip'), may hold values from 0 to 2047
- ray_pixel: int32 [16, 512], P('dp', 'strip'), may hold values from 0 to 4095
- target: float32 [16, 3, 4096], P('dp'), may hold values from 0 to 1
- valid: int32 [16, 4096], P('dp'), may hold values 0 or 1
Outputs:
- loss: float32 [], replicated
- new_weights: float32 [10952704], P(('dp', 'strip'))
- new_first: float32 [10952704], P(('dp', 'strip'))
- new_second: float32 [10952704], P(('dp', 'strip'))
- new_blocks: float32 [512, 128, 128], P('dp')
- block_grads: float32 [512, 128, 128], P('dp')
- new_left: float32 [512, 128, 128], P('dp')
- new_right: float32 [512, 128, 128], P('dp')
- block_rms: float32 [512], P('dp')
The draws below stay inside these ranges and needn't reach their ends.
All inputs are finite; a program needn't handle non-finite values. No bound on the sum of `valid` on one device may be relied on, other than what follows from the above.
Results may differ from the reference program's by a relative error of at most 0.007.
The reference program's roundings to bfloat16 on the way count: a program that leaves them out, or rounds other values in their place, can miss the bound.
Values may be sent and summed in bfloat16 or wider, within the bound.
A program may use at most 320 MiB of HBM per device.

```python
import math
import jax
import jax.numpy as jnp
from jax import lax

D = 1024
HEADS = 16
HEAD_DIM = 64
HID = 4096
DI = 768
CH = 80
DEC_HID = 64
BLOCK = 128
IMG = 257
PR = 8
TC = 32
S = 16
PIX = 4096
NCAM = 32
ADAM_STEP = 10
OBJECTS = 16
PLROWS = 16
CELLS = 2048
RAYS_OBJ = 512
ALL_RAYS = 8192
BLOCKS = 512
NFLAT = 10952704
N_STRIP = 2


def segment_scales():
    return ((D * D, D ** (-0.5)), (DI * 2 * D, DI ** (-0.5)), (D * D, 4.0 * D ** (-0.5)), (D * 3 * D, D ** (-0.5)), (D * D, 4.0 * D ** (-0.5)), (D * 16 * CH, 0.5 * D ** (-0.5)), (CH * DEC_HID, CH ** (-0.5)), (DEC_HID * 4, DEC_HID ** (-0.5)), (NCAM * 6 * D, 0.1), (3 * PLROWS * TC * D, 0.1))


def draw_weights(key, part):
    pieces = [jnp.full((length,), factor, jnp.float32) for length, factor in segment_scales()]
    used_total = 0
    for length, factor in segment_scales():
        used_total = used_total + length
    pieces.append(jnp.full((NFLAT - used_total,), 0.02, jnp.float32))
    return jax.random.normal(key, (NFLAT,), jnp.float32) * jnp.concatenate(pieces)


def stat_level():
    return BLOCK * 0.0225 / ALL_RAYS * (0.1 / 0.9)


def block_factor(key, salt):
    return jnp.exp(jax.random.uniform(jax.random.fold_in(key, salt), (BLOCKS, 1, 1), jnp.float32, 0.0, math.log(4.0)))


def near_identity(key, salt):
    noise = jax.random.normal(jax.random.fold_in(key, salt), (BLOCKS, BLOCK, BLOCK), jnp.float32) * (0.3 / math.sqrt(BLOCK))
    return jnp.eye(BLOCK, dtype=jnp.float32) + 0.5 * (noise + jnp.swapaxes(noise, 1, 2))


def draw_stat_left(key, part):
    return stat_level() * block_factor(key, 11) * near_identity(key, 21)


def draw_stat_right(key, part):
    return stat_level() * block_factor(key, 12) * near_identity(key, 22)


def draw_root_left(key, part):
    return (stat_level() * block_factor(key, 11)) ** (-0.25) * near_identity(key, 23)


def draw_root_right(key, part):
    return (stat_level() * block_factor(key, 12)) ** (-0.25) * near_identity(key, 24)


def set_ends(result, key, least, largest):
    shape = result.shape
    spot = [jax.random.randint(jax.random.fold_in(key, axis), (), 0, shape[axis]) for axis in range(len(shape))]
    result = result.at[tuple(spot)].set(least)
    longest = shape.index(max(shape))
    spot[longest] = (spot[longest] + 1) % shape[longest]
    return result.at[tuple(spot)].set(largest)


def block_scale(rng, dims, shards, low, high):
    factor_of = 1.0
    for position, blocks in shards:
        draws = jax.random.uniform(jax.random.fold_in(jax.random.fold_in(rng, 6), position), (blocks,), jnp.float32, low / len(shards), high / len(shards))
        factor_of = factor_of * jnp.repeat(jnp.exp(draws), dims[position] // blocks).reshape((-1,) + (1,) * (len(dims) - 1 - position))
    return factor_of


def bell_draw(stream_key, shape, scale, limit, shards=(), kind=jnp.bfloat16):
    values = scale * jax.random.normal(stream_key, shape, jnp.float32)
    if shards:
        values = values * block_scale(stream_key, shape, shards, -0.22, 0.18)
    return jnp.clip(values, -limit, limit).astype(kind)


def setup_inputs(seed: int = 0) -> dict:
    arg_keys = jax.random.split(jax.random.key(seed), 15)
    return {
        "weights": draw_weights(jax.random.fold_in(arg_keys[14], 71), 0),
        "blocks": bell_draw(arg_keys[1], (BLOCKS, BLOCK, BLOCK), D ** -0.5, 0.1875, ((0, 16),), jnp.float32),
        "stat_left": draw_stat_left(jax.random.fold_in(arg_keys[14], 71), 0),
        "stat_right": draw_stat_right(jax.random.fold_in(arg_keys[14], 71), 0),
        "root_left": draw_root_left(jax.random.fold_in(arg_keys[14], 71), 0),
        "root_right": draw_root_right(jax.random.fold_in(arg_keys[14], 71), 0),
        "first_moment": bell_draw(arg_keys[6], (NFLAT,), (0.0167 * ALL_RAYS ** -0.5), 0.0029296875, ((0, 32),), jnp.float32),
        "second_moment": jnp.clip(jnp.exp(math.log(5.786132533103228e-07) - 1.3905226 * jax.random.uniform(arg_keys[7], (NFLAT,), jnp.float32) ** block_scale(arg_keys[7], (NFLAT,), ((0, 32),), -0.2, 0.2)), 1.4404297132841748e-07, 5.786132533103228e-07),
        "image": bell_draw(arg_keys[8], (OBJECTS, IMG, DI), 1.0, 6.0, ((0, 16),)),
        "camera": set_ends(jax.random.randint(arg_keys[9], (OBJECTS,), 0, NCAM), jax.random.fold_in(arg_keys[9], 1), 0, NCAM - 1).astype(jnp.int32),
        "samples": set_ends(jax.random.randint(arg_keys[10], (OBJECTS, 3, S, RAYS_OBJ), 0, CELLS), jax.random.fold_in(arg_keys[10], 1), 0, CELLS - 1).astype(jnp.int32),
        "ray_pixel": set_ends(jax.random.randint(arg_keys[11], (OBJECTS, RAYS_OBJ), 0, PIX), jax.random.fold_in(arg_keys[11], 1), 0, PIX - 1).astype(jnp.int32),
        "target": jnp.clip(1.0 * jax.random.uniform(arg_keys[12], (OBJECTS, 3, PIX), jnp.float32) ** block_scale(arg_keys[12], (OBJECTS, 3, PIX), ((0, 16),), -0.2, 0.2), 0.0, 1.0),
        "valid": set_ends((jax.random.randint(arg_keys[13], (OBJECTS, PIX), 0, 4) < 3).astype(jnp.int32), jax.random.fold_in(arg_keys[13], 1), 0, 1),
    }


@jax.custom_vjp
def low(v):
    return lax.optimization_barrier(v.astype(jnp.bfloat16)).astype(jnp.float32)

@jax.custom_vjp
def low_back(v):
    return v

def low_keep(v):
    return (low(v), None)

def low_pass(kept, grad):
    return (grad,)

def back_keep(v):
    return (v, None)

def back_low(kept, grad):
    return (low(grad),)
low.defvjp(low_keep, low_pass)
low_back.defvjp(back_keep, back_low)
NORM_EPS = 1e-05
ADAM_RATE = 0.015
BETA_FIRST = 0.9
BETA_SECOND = 0.95
ADAM_EPS = 1e-08
WEIGHT_DECAY = 0.1
STAT_DECAY = 0.9
SHAMPOO_RATE = 0.01
RMS_EPS = 1e-06
HIGHEST_MODE = lax.Precision.HIGHEST

def segments(plane_rows):
    return (('query_cross', (D, D)), ('keyval_cross', (DI, 2 * D)), ('out_cross', (D, D)), ('qkv_self', (D, 3 * D)), ('out_self', (D, D)), ('deconv', (D, 16 * CH)), ('decode_in', (CH, DEC_HID)), ('decode_out', (DEC_HID, 4)), ('modulate', (NCAM, 6, D)), ('triplane', (3, plane_rows, TC, D)))

def unflatten(flat, plane_rows):
    parts = {}
    offset = 0
    for label, shape in segments(plane_rows):
        length = math.prod(shape)
        parts[label] = flat[offset:offset + length].reshape(shape)
        offset += length
    return parts

def unblock(tiles):
    rows_one, cols_one = (D // BLOCK, HID // BLOCK)
    half = rows_one * cols_one
    leading_value = tiles[:half].reshape(rows_one, cols_one, BLOCK, BLOCK).transpose(0, 2, 1, 3).reshape(D, HID)
    trailing_value = tiles[half:].reshape(cols_one, rows_one, BLOCK, BLOCK).transpose(0, 2, 1, 3).reshape(HID, D)
    return (leading_value, trailing_value)

def matmul_high(left, right):
    return jnp.matmul(left, right, precision=HIGHEST_MODE)

def norm_mod(stream, scale, shift):
    centred = stream - lax.optimization_barrier(jnp.mean(stream, -1, keepdims=True))
    spread = lax.optimization_barrier(jnp.mean(centred * centred, -1, keepdims=True))
    return centred * lax.rsqrt(spread + NORM_EPS) * (1.0 + scale) + shift

def gelu_tanh(value):
    return jax.nn.gelu(value, approximate=True)

def assemble(ydc):
    planes, rows, cols, _ = ydc.shape
    inner = rows - 2
    kernel = ydc.reshape(planes, rows, cols, 4, 4, -1)
    even = kernel[:, 1:inner + 1, :, 1] + kernel[:, 0:inner, :, 3]
    odd = kernel[:, 1:inner + 1, :, 2] + kernel[:, 2:inner + 2, :, 0]
    tall = jnp.stack([even, odd], 2)
    wide = jnp.pad(tall, ((0, 0), (0, 0), (0, 0), (1, 1), (0, 0), (0, 0)))
    left_cols = wide[:, :, :, 1:cols + 1, 1] + wide[:, :, :, 0:cols, 3]
    right_cols = wide[:, :, :, 1:cols + 1, 2] + wide[:, :, :, 2:cols + 2, 0]
    return jnp.stack([left_cols, right_cols], 4).reshape(planes, 2 * inner, 2 * cols, -1)

def render_loss(output, pixel, target, valid):
    sigma = jax.nn.softplus(output[..., 0])
    colour = jax.nn.sigmoid(output[..., 1:])
    absorb = 4.0 / S * sigma
    before = jnp.cumsum(absorb, 0) - absorb
    weight = jnp.exp(-before) * (1.0 - jnp.exp(-absorb))
    colour_sum = lax.optimization_barrier(jnp.sum(weight[..., None] * colour, 0))
    mask = jnp.take(valid, pixel).astype(jnp.float32)
    wanted = jnp.take(target, pixel, axis=1)
    error = colour_sum.T - wanted
    return (jnp.sum(mask * lax.optimization_barrier(jnp.sum(error * error, 0))), jnp.sum(mask))

def attend(query, keys, values):
    rows = query.shape[0]
    size = 512 if rows % 512 == 0 else rows
    query_blocks = query.reshape(rows // size, size, HEADS, HEAD_DIM)
    key_heads = keys.reshape(-1, HEADS, HEAD_DIM)
    value_heads = values.reshape(-1, HEADS, HEAD_DIM)

    def one_block(block):
        scores = low_back(jnp.einsum('qhd,khd->hqk', block, key_heads, precision=HIGHEST_MODE) * HEAD_DIM ** (-0.5))
        shares = low(jax.nn.softmax(scores, axis=-1))
        return jnp.einsum('hqk,khd->qhd', shares, value_heads, precision=HIGHEST_MODE)
    return lax.map(jax.checkpoint(one_block), query_blocks).reshape(rows, D)

def object_loss(params, mlp_one, mlp_two, image, camera, samples, pixel, target, valid):
    mods = jnp.take(params['modulate'], camera, axis=0)
    stream0 = params['triplane'].reshape(-1, D)
    hidden1 = low(norm_mod(stream0, mods[0], mods[1]))
    query1 = low_back(low(matmul_high(hidden1, params['query_cross'])))
    strip_queries = query1.reshape(3, N_STRIP, PR * TC, D)
    pieces = []
    for strip_id in range(N_STRIP):
        image_kv = low_back(low(matmul_high(image, params['keyval_cross'])))
        final_output = attend(strip_queries[:, strip_id].reshape(-1, D), image_kv[:, :D], image_kv[:, D:])
        pieces.append(final_output.reshape(3, PR * TC, D))
    cross_out = low_back(low(jnp.stack(pieces, 1).reshape(-1, D)))
    stream1 = stream0 + low_back(matmul_high(cross_out, params['out_cross']))
    hidden2 = low(norm_mod(stream1, mods[2], mods[3]))
    qkv = low_back(low(matmul_high(hidden2, params['qkv_self'])))
    self_out = low_back(low(attend(qkv[:, :D], qkv[:, D:2 * D], qkv[:, 2 * D:])))
    stream2 = stream1 + low_back(matmul_high(self_out, params['out_self']))
    hidden3 = low(norm_mod(stream2, mods[4], mods[5]))
    up_value = low_back(matmul_high(hidden3, mlp_one))
    act = low(gelu_tanh(up_value))
    stream3 = stream2 + low_back(matmul_high(act, mlp_two))
    grid = low(stream3).reshape(3, PLROWS, TC, D)
    padded = jnp.pad(grid, ((0, 0), (1, 1), (0, 0), (0, 0)))
    feature = low_back(low(assemble(matmul_high(padded, params['deconv'])))).reshape(3, CELLS, CH)
    point = jnp.take(feature[0], samples[0], axis=0) + jnp.take(feature[1], samples[1], axis=0) + jnp.take(feature[2], samples[2], axis=0)
    point = low(point)
    inner = low_back(matmul_high(point, params['decode_in']))
    hidden = low(jax.nn.silu(inner))
    output = low_back(matmul_high(hidden, params['decode_out']))
    return render_loss(output, pixel, target, valid)

def reference(weights, blocks, stat_left, stat_right, root_left, root_right, first_moment, second_moment, image, camera, samples, ray_pixel, target, valid):

    def loss_of(flat, tiles):
        params = unflatten(low(flat), PLROWS)
        mlp_one, mlp_two = unblock(low(tiles))

        def per_object(totals, item):
            img, cam, samp, pix, tgt, val = item
            part_sum, part_count = jax.checkpoint(object_loss)(params, mlp_one, mlp_two, img.astype(jnp.float32), cam, samp, pix, tgt, val)
            return ((totals[0] + part_sum, totals[1] + part_count), None)
        start = (jnp.zeros((), jnp.float32), jnp.zeros((), jnp.float32))
        (loss_sum, count), _ = lax.scan(per_object, start, (image, camera, samples, ray_pixel, target, valid))
        return loss_sum / jnp.maximum(count, 1.0)
    loss, pull = jax.vjp(loss_of, weights, blocks)
    grad_flat, grad_blocks = pull(jnp.ones((), jnp.float32))
    new_first = BETA_FIRST * first_moment + (1.0 - BETA_FIRST) * grad_flat
    new_second = BETA_SECOND * second_moment + (1.0 - BETA_SECOND) * grad_flat * grad_flat
    fix_first = 1.0 - BETA_FIRST ** ADAM_STEP
    fix_second = 1.0 - BETA_SECOND ** ADAM_STEP
    moved = new_first / fix_first / (jnp.sqrt(new_second / fix_second) + ADAM_EPS)
    new_weights = weights - ADAM_RATE * (moved + WEIGHT_DECAY * weights)
    new_left = STAT_DECAY * stat_left + (1.0 - STAT_DECAY) * jnp.einsum('bij,bkj->bik', grad_blocks, grad_blocks, precision=HIGHEST_MODE)
    new_right = STAT_DECAY * stat_right + (1.0 - STAT_DECAY) * jnp.einsum('bji,bjk->bik', grad_blocks, grad_blocks, precision=HIGHEST_MODE)
    half_step = jnp.einsum('bij,bjk->bik', grad_blocks, root_right, precision=HIGHEST_MODE)
    precond = jnp.einsum('bij,bjk->bik', root_left, half_step, precision=HIGHEST_MODE)
    block_rms = jnp.sqrt(lax.optimization_barrier(jnp.mean(precond * precond, axis=(1, 2))) + RMS_EPS)
    new_blocks = blocks - SHAMPOO_RATE * precond / block_rms[:, None, None]
    return (loss, new_weights, new_first, new_second, new_blocks, grad_blocks, new_left, new_right, block_rms)
```

```python
import functools
import math

import jax
import jax.numpy as jnp
from jax import lax
from jax.experimental import pallas as pl
from jax.experimental.pallas import tpu as pltpu
from jax.sharding import PartitionSpec as P

D = 1024
HEAD_DIM = 64
HID = 4096
DI = 768
CH = 80
DEC_HID = 64
BLOCK = 128
PR = 8
TC = 32
S = 16
NCAM = 32
ADAM_STEP = 10


NORM_EPS = 1e-05
ADAM_RATE = 0.015
BETA_FIRST = 0.9
BETA_SECOND = 0.95
ADAM_EPS = 1e-08
WEIGHT_DECAY = 0.1
STAT_DECAY = 0.9
SHAMPOO_RATE = 0.01
RMS_EPS = 1e-06
HIGHEST_MODE = lax.Precision.HIGHEST
group_heads = 4


def with_halo(block, sides, width):
    for axis, dim in sides:
        count = lax.axis_size(axis)
        forward = [(i, i + 1) for i in range(count - 1)]
        backward = [(target, source) for source, target in forward]
        low = lax.ppermute(
            lax.slice_in_dim(block, block.shape[dim] - width, None, axis=dim), axis, forward
        )
        high = lax.ppermute(lax.slice_in_dim(block, 0, width, axis=dim), axis, backward)
        block = jnp.concatenate([low, block, high], axis=dim)
    return block


def product(left, right):
    return jnp.dot(left, right, preferred_element_type=jnp.float32)


def product_back(left, right):
    return lax.dot_general(
        left, right, (((left.ndim - 1,), (1,)), ((), ())), preferred_element_type=jnp.float32
    )


def weight_grad(left, right):
    return lax.dot_general(
        left, right, (((0,), (0,)), ((), ())), preferred_element_type=jnp.float32
    )


def norm_mod(stream, scale, shift):
    centred = stream - jnp.mean(stream, -1, keepdims=True)
    spread = jnp.mean(centred * centred, -1, keepdims=True)
    return centred * lax.rsqrt(spread + NORM_EPS) * (1.0 + scale) + shift


def gelu_tanh(value):
    return jax.nn.gelu(value, approximate=True)


def assemble(ydc):
    planes, rows, cols, _ = ydc.shape
    inner = rows - 2
    kernel = ydc.reshape(planes, rows, cols, 4, 4, -1)
    even = kernel[:, 1 : inner + 1, :, 1] + kernel[:, 0:inner, :, 3]
    odd = kernel[:, 1 : inner + 1, :, 2] + kernel[:, 2 : inner + 2, :, 0]
    tall = jnp.stack([even, odd], 2)
    wide = jnp.pad(tall, ((0, 0), (0, 0), (0, 0), (1, 1), (0, 0), (0, 0)))
    left_cols = wide[:, :, :, 1 : cols + 1, 1] + wide[:, :, :, 0:cols, 3]
    right_cols = wide[:, :, :, 1 : cols + 1, 2] + wide[:, :, :, 2 : cols + 2, 0]
    return jnp.stack([left_cols, right_cols], 4).reshape(planes, 2 * inner, 2 * cols, -1)


def render_loss(output, mask, wanted):
    sigma = jax.nn.softplus(output[..., 0])
    colour = jax.nn.sigmoid(output[..., 1:])
    absorb = 4.0 / S * sigma
    before = jnp.cumsum(absorb, 0) - absorb
    weight = jnp.exp(-before) * (1.0 - jnp.exp(-absorb))
    colour_sum = jnp.sum(weight[..., None] * colour, 0)
    error = colour_sum.T - wanted
    return jnp.sum(mask * jnp.sum(error * error, 0))


def split_heads(matrix):
    return matrix.reshape(matrix.shape[0], -1, group_heads, HEAD_DIM).transpose(1, 0, 2, 3)


def merge_heads(groups):
    return groups.transpose(1, 0, 2, 3).reshape(groups.shape[1], -1)


def attend_fwd(query, keys, values):

    def one_group(operands):
        query_part, key_part, value_part = operands
        scores = jnp.einsum(
            "qhd,khd->hqk", query_part, key_part, preferred_element_type=jnp.float32
        ) * HEAD_DIM ** (-0.5)
        top = jnp.max(scores, -1, keepdims=True)
        log_total = top + jnp.log(jnp.sum(jnp.exp(scores - top), -1, keepdims=True))
        shares = jnp.exp(scores - log_total).astype(jnp.bfloat16)
        final_output = jnp.einsum(
            "hqk,khd->qhd", shares, value_part, preferred_element_type=jnp.float32
        )
        return (final_output, log_total[..., 0])

    final_output, log_total = lax.map(
        one_group, (split_heads(query), split_heads(keys), split_heads(values))
    )
    return (merge_heads(final_output), log_total)


def attend_bwd(query, keys, values, log_total, grad_out):

    def one_group(operands):
        query_part, key_part, value_part, total_part, grad_part = operands
        scores = jnp.einsum(
            "qhd,khd->hqk", query_part, key_part, preferred_element_type=jnp.float32
        ) * HEAD_DIM ** (-0.5)
        shares = jnp.exp(scores - total_part[..., None])
        grad_shares = jnp.einsum(
            "qhd,khd->hqk", grad_part, value_part, preferred_element_type=jnp.float32
        )
        grad_scores = (
            shares * (grad_shares - jnp.sum(grad_shares * shares, -1, keepdims=True))
        ).astype(jnp.bfloat16)
        grad_query = jnp.einsum(
            "hqk,khd->qhd", grad_scores, key_part, preferred_element_type=jnp.float32
        ) * HEAD_DIM ** (-0.5)
        grad_keys = jnp.einsum(
            "hqk,qhd->khd", grad_scores, query_part, preferred_element_type=jnp.float32
        ) * HEAD_DIM ** (-0.5)
        grad_values = jnp.einsum(
            "hqk,qhd->khd",
            shares.astype(jnp.bfloat16),
            grad_part,
            preferred_element_type=jnp.float32,
        )
        return (grad_query, grad_keys, grad_values)

    grads = lax.map(
        one_group,
        (
            split_heads(query),
            split_heads(keys),
            split_heads(values),
            log_total,
            split_heads(grad_out),
        ),
    )
    return (merge_heads(grads[0]), merge_heads(grads[1]), merge_heads(grads[2]))


LANE = 1024
MESH_ID = pl.DeviceIdType.MESH


def places():
    p = lax.axis_index("dp")
    c = lax.axis_index("strip")
    z = p // 4
    flip_x = p + 1 - 2 * (p % 2)
    flip_y = p + 2 - 4 * ((p // 2) % 2)
    both = flip_x + flip_y - p
    near = (1 - c) * flip_x + c * flip_y
    far = (1 - c) * flip_y + c * flip_x
    return p, c, z, near, far, both


def along_z(line, z, k):
    return ((z + k) % 4) * 4 + line % 4


def enter(peers):
    barrier = pltpu.get_barrier_semaphore()
    for peer in peers:
        pl.semaphore_signal(barrier, inc=1, device_id=peer, device_id_type=MESH_ID)
    pl.semaphore_wait(barrier, len(peers))


def flat_chunks(rows, n):
    part = rows // n
    return n, part, lambda p, c, j: (2 * p + c) * rows + j * part


def block_chunk(p, c, k):
    second = p // 8
    return ((1 - second) * ((2 * c + k) * 8 + p) + second * (4 * p + 2 * c + k)) * BLOCK

block_chunks = (2, BLOCK, block_chunk)


ORDER = [("near", 0), ("z", 1), ("z", 3), ("far", 0), ("z", 2), ("near", 1), ("near", 3), ("near", 2)]
ORDER += [("both", 0), ("far", 1), ("far", 3), ("far", 2), ("both", 1), ("both", 3), ("both", 2)]
ORDER += [("core", i) for i in range(16)]

def gather_kernel(layouts, stagger, *refs):
    count = len(layouts)
    sources = refs[:count]
    fulls = refs[count : 2 * count]
    send, recv, local = refs[2 * count :]
    p, c, z, near, far, both = places()
    zs = [along_z(p, z, k) for k in range(4)]
    enter([(q, c) for q in zs[1:]] + [(near, c), (far, c), (p, 1 - c)])
    jobs = [(a, j) for a, layout in enumerate(layouts) for j in range(layout[0])]

    def target(owner, job):
        a, j = jobs[job]
        _, rows, place = layouts[a]
        return fulls[a].at[pl.ds(pl.multiple_of(place(*owner, j), 8), rows)]

    def source(job):
        a, j = jobs[job]
        rows = layouts[a][1]
        return sources[a].at[pl.ds(j * rows, rows)]

    started = []

    def forward(owner, own, event, peer, job):
        t = target(owner, job)
        copy = pltpu.make_async_remote_copy(
            source(job) if own else t, t, send.at[event, job], recv.at[event, job], device_id=peer, device_id_type=MESH_ID
        )
        copy.start()
        started.append(copy)

    def arrive(owner, event, job):
        t = target(owner, job)
        pltpu.make_async_remote_copy(
            t, t, send.at[event, job], recv.at[event, job], device_id=(p, 1 - c), device_id_type=MESH_ID
        ).wait_recv()

    me = (p, c)

    def begin(job):
        forward(me, True, 3, (near, c), job)
        for k in (1, 3, 2):
            forward(me, True, 3 - k, (zs[k], c), job)
        forward(me, True, 7, (far, c), job)
        forward(me, True, 15, (p, 1 - c), job)
        pltpu.make_async_copy(source(job), target(me, job), local.at[job]).start()

    def take(kind, k, job):
        if kind == "z":
            owner = (zs[k], c)
            arrive(owner, k - 1, job)
            forward(owner, False, 3 + k, (near, c), job)
            forward(owner, False, 7 + k, (far, c), job)
            forward(owner, False, 15 + k, (p, 1 - c), job)
        elif kind == "near":
            owner = (along_z(near, z, k), c)
            arrive(owner, 3 + k, job)
            forward(owner, False, 11 + k, (far, c), job)
            forward(owner, False, 19 + k, (p, 1 - c), job)
        elif kind == "far":
            owner = (along_z(far, z, k), c)
            arrive(owner, 7 + k, job)
            forward(owner, False, 23 + k, (p, 1 - c), job)
        elif kind == "both":
            owner = (along_z(both, z, k), c)
            arrive(owner, 11 + k, job)
            forward(owner, False, 27 + k, (p, 1 - c), job)
        elif kind == "core":
            line = (p, far, near, both)[k // 4]
            arrive((along_z(line, z, k % 4), 1 - c), 15 + k, job)

    steps = []
    for job in range(len(jobs)):
        steps.append((stagger * job, -1, job))
        for i in range(len(ORDER)):
            steps.append((stagger * job + i + 1, i, job))
    for _, i, job in sorted(steps):
        if i < 0:
            begin(job)
        else:
            take(*ORDER[i], job)
    for copy in started:
        copy.wait_send()
    for job in range(len(jobs)):
        pltpu.make_async_copy(source(job), target(me, job), local.at[job]).wait()


def gather_all(layouts, stagger, shards_in, name_id):
    copies = sum(l[0] for l in layouts)
    return pl.pallas_call(
        functools.partial(gather_kernel, layouts, stagger),
        out_shape=[jax.ShapeDtypeStruct((32 * s.shape[0],) + s.shape[1:], s.dtype) for s in shards_in],
        in_specs=[pl.BlockSpec(memory_space=pl.ANY)] * len(shards_in),
        out_specs=[pl.BlockSpec(memory_space=pl.ANY)] * len(shards_in),
        scratch_shapes=[
            pltpu.SemaphoreType.DMA((31, copies)),
            pltpu.SemaphoreType.DMA((31, copies)),
            pltpu.SemaphoreType.DMA((copies,)),
        ],
        compiler_params=pltpu.CompilerParams(collective_id=name_id, has_side_effects=True),
        name="gather_all",
    )(*shards_in)


SUM_ORDER = [(3, 0), (3, 1), (3, 3), (3, 2), (2, 0), (2, 1), (2, 3), (2, 2)]
SUM_ORDER += [(1, 1), (1, 3), (1, 2), (1, 0), (0, 1), (0, 3), (0, 2), (0, 0)]
AHEAD = 3


def scatter_kernel(layouts, shared, stagger, *refs):
    count = len(layouts)
    grads = refs[:count]
    outs = refs[count : 2 * count]
    scratch = refs[2 * count :]
    p, c, z, near, far, both = places()
    zs = [along_z(p, z, k) for k in range(4)]
    enter([(q, c) for q in zs[1:]] + [(near, c), (far, c), (p, 1 - c)])
    csend, crecv, bsend, brecv, load_sem, out_sem = scratch[:6]
    buffers = [scratch[6 + 6 * a : 12 + 6 * a] for a in range(count)]
    jobs = [(a, j) for a, layout in enumerate(layouts) for j in range(layout[0])]
    lines = (p, near, far, both)
    partner_lines = (p, far, near, both)

    def view(job, ref, slot):
        a, j = jobs[job]
        rows = layouts[a][1]
        return ref.at[slot, pl.ds(j * rows, rows)]

    def piece(owner, job):
        a, j = jobs[job]
        _, rows, place = layouts[a]
        return grads[a].at[pl.ds(pl.multiple_of(place(*owner, j), 8), rows)]

    def to_core(i, job):
        g, k = SUM_ORDER[i]
        owner = (along_z(partner_lines[g], z, k), 1 - c)
        rc = buffers[jobs[job][0]][0]
        return pltpu.make_async_remote_copy(
            piece(owner, job), view(job, rc, g * 4 + k), csend.at[i, job], crecv.at[i, job],
            device_id=(p, 1 - c), device_id_type=MESH_ID,
        )

    def load(i, job):
        g, k = SUM_ORDER[i]
        own = buffers[jobs[job][0]][4]
        return pltpu.make_async_copy(
            piece((along_z(lines[g], z, k), c), job), view(job, own, i % AHEAD), load_sem.at[i, job]
        )

    def onward(i, job):
        g, k = SUM_ORDER[i]
        rc, rb, ra, rz = buffers[jobs[job][0]][:4]
        if g == 3:
            target, event, peer = view(job, rb, 4 + k), 4 + k, (far, c)
        elif g == 2:
            target, event, peer = view(job, rb, k), k, (far, c)
        elif g == 1:
            target, event, peer = view(job, ra, k), 8 + k, (near, c)
        else:
            target, event, peer = view(job, rz, 3 - k), 12 + 3 - k, (zs[k], c)
        return pltpu.make_async_remote_copy(
            view(job, rc, g * 4 + k), target, bsend.at[event, job], brecv.at[event, job],
            device_id=peer, device_id_type=MESH_ID,
        )

    def landed(event, job):
        rc, rb, ra, rz = buffers[jobs[job][0]][:4]
        if event < 8:
            target = view(job, rb, event)
        elif event < 12:
            target = view(job, ra, event - 8)
        else:
            target = view(job, rz, event - 12)
        pltpu.make_async_remote_copy(
            target, target, bsend.at[event, job], brecv.at[event, job], device_id=(p, 1 - c), device_id_type=MESH_ID
        ).wait_recv()
        return target

    def add_up(parts, target):
        rows = target.shape[0]
        step = math.gcd(rows, 16)

        @pl.loop(0, rows // step)
        def _(n):
            at = pl.ds(pl.multiple_of(n * step, step), step)
            total = parts[0][at].astype(jnp.float32)
            for part in parts[1:]:
                total = total + part[at].astype(jnp.float32)
            target[at] = total.astype(target.dtype)

    def start(i, job):
        to_core(i, job).start()
        load(i, job).start()

    def final_copies(job):
        a, j = jobs[job]
        rows = layouts[a][1]
        done = view(job, buffers[a][5], 0)
        if not shared[a]:
            return [pltpu.make_async_copy(done, outs[a].at[pl.ds(j * rows, rows)], out_sem.at[job, 0])]
        spot = outs[a].at[pl.ds(pl.multiple_of((c * layouts[a][0] + j) * rows, 8), rows)]
        return [
            pltpu.make_async_copy(done, spot, out_sem.at[job, 0]),
            pltpu.make_async_remote_copy(
                done, spot, out_sem.at[job, 1], out_sem.at[job, 2], device_id=(p, 1 - c), device_id_type=MESH_ID
            ),
        ]

    def step(i, job):
        g, k = SUM_ORDER[i]
        rc, rb, ra, rz, own, done = buffers[jobs[job][0]]
        load(i, job).wait()
        to_core(i, job).wait_recv()
        here = view(job, rc, g * 4 + k)
        parts = [here, view(job, own, i % AHEAD)]
        if g == 1:
            parts.append(landed(4 + k, job))
        if g == 0:
            parts.append(landed(k, job))
            parts.append(landed(8 + k, job))
        if (g, k) == (0, 0):
            parts += [landed(12 + n, job) for n in range(3)]
            add_up(parts, view(job, done, 0))
            for copy in final_copies(job):
                copy.start()
        else:
            add_up(parts, here)
            onward(i, job).start()
        if i + AHEAD < 16:
            start(i + AHEAD, job)

    steps = []
    for job in range(len(jobs)):
        for i in range(-1, 16):
            steps.append((stagger * job + i, job, i))
    for _, job, i in sorted(steps):
        if i < 0:
            for n in range(AHEAD):
                start(n, job)
        else:
            step(i, job)
    for job in range(len(jobs)):
        for i in range(16):
            to_core(i, job).wait_send()
            if i < 15:
                onward(i, job).wait_send()
        for copy in final_copies(job):
            copy.wait()


def scatter_sum(layouts, shared, stagger, grads, name_id):
    jobs = sum(l[0] for l in layouts)
    scratch = [
        pltpu.SemaphoreType.DMA((16, jobs)),
        pltpu.SemaphoreType.DMA((16, jobs)),
        pltpu.SemaphoreType.DMA((15, jobs)),
        pltpu.SemaphoreType.DMA((15, jobs)),
        pltpu.SemaphoreType.DMA((16, jobs)),
        pltpu.SemaphoreType.DMA((jobs, 3)),
    ]
    shapes = []
    for layout, both_cores, grad in zip(layouts, shared, grads):
        rows, width = layout[0] * layout[1], grad.shape[1]
        for slots in (16, 8, 4, 3, AHEAD):
            scratch.append(pltpu.VMEM((slots, rows, width), grad.dtype))
        kind = grad.dtype if both_cores else jnp.float32
        scratch.append(pltpu.VMEM((1, rows, width), kind))
        shapes.append(jax.ShapeDtypeStruct(((2 if both_cores else 1) * rows, width), kind))
    return pl.pallas_call(
        functools.partial(scatter_kernel, layouts, shared, stagger),
        out_shape=shapes,
        in_specs=[pl.BlockSpec(memory_space=pl.ANY)] * len(grads),
        out_specs=[pl.BlockSpec(memory_space=pl.ANY)] * len(grads),
        scratch_shapes=scratch,
        compiler_params=pltpu.CompilerParams(
            collective_id=name_id, has_side_effects=True, vmem_limit_bytes=56 * 1024 * 1024
        ),
        name="scatter_sum",
    )(*grads)


WIDE = 1024
TILE = 8 * WIDE
GAP_AT = D * D + DI * 2 * D + D * D + D * 3 * D + D * D + D * 16 * CH + CH * DEC_HID + DEC_HID * 4
GAP = -GAP_AT % TILE
ROWS = {}
_row = 0
for _name, _rows in (
    ("query_cross", D),
    ("keyval_cross", 2 * DI),
    ("out_cross", D),
    ("qkv_self", 3 * D),
    ("out_self", D),
    ("deconv", 16 * CH),
    ("decode", 8),
    ("modulate", 6 * NCAM),
):
    ROWS[_name] = (_row, _row + _rows)
    _row += _rows
PLANE_ROW = _row


def direct_links():
    return lax.axis_size("dp") == 16 and lax.axis_size("strip") == 2


def align(shard):
    length = shard.shape[0]
    rows = -(-length // TILE) * 8
    size = rows * WIDE
    extra = size - length
    reach = -(-32 * extra // WIDE) * WIDE
    place = lax.axis_index("dp") * 2 + lax.axis_index("strip")
    shard = shard.astype(jnp.bfloat16)
    following = lax.ppermute(shard[:reach], ("dp", "strip"), [(n + 1, n) for n in range(31)])
    joined = jnp.concatenate([shard, following])
    shift = place * extra
    early = lax.dynamic_slice_in_dim(joined, shift, size)
    late = lax.dynamic_slice_in_dim(joined, jnp.maximum(shift - GAP, 0), size)
    at = place * size + lax.iota(jnp.int32, size)
    return jnp.where(at < GAP_AT, early, late).reshape(rows, WIDE)


def unalign(summed, length):
    size = summed.size
    extra = size - length
    reach = -(-32 * extra // WIDE) * WIDE
    place = lax.axis_index("dp") * 2 + lax.axis_index("strip")
    summed = summed.reshape(-1)
    before = lax.ppermute(summed[size - reach :], ("dp", "strip"), [(n, n + 1) for n in range(31)])
    joined = jnp.concatenate([before, summed])
    shift = reach - place * extra
    early = lax.dynamic_slice_in_dim(joined, shift, length)
    late = lax.dynamic_slice_in_dim(joined, shift + GAP, length)
    at = place * length + lax.iota(jnp.int32, length)
    return jnp.where(at < GAP_AT, early, late)


def chunks_of(tiles):
    return tiles.reshape(-1, 8, BLOCK, BLOCK).transpose(0, 2, 1, 3).reshape(-1, WIDE)


def tiles_of(chunks):
    return chunks.reshape(-1, BLOCK, 8, BLOCK).transpose(0, 2, 1, 3).reshape(-1, BLOCK, BLOCK)


def panels_of(chunks):
    half = chunks.shape[0] // 2
    first = chunks[:half].reshape(D // BLOCK, HID // WIDE, BLOCK, WIDE).transpose(1, 0, 2, 3)
    return jnp.concatenate([first.reshape(half, WIDE), chunks[half:]])


def chunks_of_panels(panels):
    half = panels.shape[0] // 2
    first = panels[:half].reshape(HID // WIDE, D // BLOCK, BLOCK, WIDE).transpose(1, 0, 2, 3)
    return jnp.concatenate([first.reshape(half, WIDE), panels[half:]])


META = (1, 8, lambda p, c, j: (2 * p + c) * 8)


def gather_weights(weights, blocks, part):
    length = weights.shape[0]
    if direct_links():
        own = align(weights)
        half = blocks.shape[0] // 2
        tiles = lax.dynamic_slice_in_dim(blocks, lax.axis_index("strip") * half, half)
        tiles = chunks_of(tiles.astype(jnp.bfloat16))
        meta = jnp.full((8, 128), part, jnp.float32)
        rows, panels, parts = gather_all(
            [flat_chunks(own.shape[0], 3), block_chunks, META], 6, [own, tiles, meta], 0
        )
        return rows, panels, jnp.sum(parts[::8, 0])
    flat = lax.all_gather(weights.astype(jnp.bfloat16), ("dp", "strip"), axis=0, tiled=True)
    tiles = lax.all_gather(blocks.astype(jnp.bfloat16), "dp", axis=0, tiled=True)
    rows = jnp.concatenate([flat[:GAP_AT], jnp.zeros((GAP,), flat.dtype), flat[GAP_AT:]])
    rows = rows[: rows.shape[0] // TILE * TILE].reshape(-1, WIDE)
    return rows, panels_of(chunks_of(tiles)), lax.psum(part, ("dp", "strip"))


def reduce_grads(pieces, panels, part, length):
    if direct_links():
        rows = -(-length // TILE) * 8
        total = sum(piece.shape[0] for piece in pieces)
        pieces = pieces + [jnp.zeros((32 * rows - total, WIDE), jnp.bfloat16)]
        meta = jnp.full((32 * 8, 128), part, jnp.float32)
        summed, tiles, parts = scatter_sum(
            [flat_chunks(rows, 1), block_chunks, META],
            [False, True, False],
            6,
            [jnp.concatenate(pieces), panels, meta],
            1,
        )
        return unalign(summed, length), tiles_of(tiles).astype(jnp.float32), parts[0, 0]
    flat = jnp.concatenate(pieces).astype(jnp.float32).reshape(-1)
    flat = jnp.concatenate([flat[:GAP_AT], flat[GAP_AT + GAP :]])
    devices = lax.axis_size("dp") * lax.axis_size("strip")
    flat = jnp.pad(flat, (0, devices * length - flat.shape[0]))
    tiles = tiles_of(chunks_of_panels(panels)).astype(jnp.float32)
    flat_sum = lax.psum_scatter(flat, ("dp", "strip"), scatter_dimension=0, tiled=True)
    tile_sum = lax.psum_scatter(tiles, ("dp", "strip"), scatter_dimension=0, tiled=True)
    tile_sum = lax.all_gather(tile_sum.astype(jnp.bfloat16), "strip", axis=0, tiled=True)
    return flat_sum, tile_sum.astype(jnp.float32), lax.psum(part, ("dp", "strip"))


def shards(
    weights,
    blocks,
    stat_left,
    stat_right,
    root_left,
    root_right,
    first_moment,
    second_moment,
    image,
    camera,
    samples,
    ray_pixel,
    target,
    valid,
):
    strips = lax.axis_size("strip")
    place = lax.axis_index("strip")
    plane_rows = PR * strips
    pixel = ray_pixel[0]
    mask = jnp.take(valid[0], pixel).astype(jnp.float32)
    wanted = jnp.take(target[0], pixel, axis=1)
    rows, panels, count = gather_weights(weights, blocks, jnp.sum(mask))
    panels = panels.reshape(-1, WIDE, WIDE)
    first_panels = [panels[n] for n in range(HID // WIDE)]
    second_panels = [panels[n] for n in range(HID // WIDE, 2 * HID // WIDE)]
    params = {name: rows[low:high] for name, (low, high) in ROWS.items()}
    params["keyval_cross"] = params["keyval_cross"].reshape(DI, 2 * D)
    params["qkv_self"] = params["qkv_self"].reshape(D, 3 * D)
    params["deconv"] = params["deconv"].reshape(D, 16 * CH)
    decode = params["decode"].reshape(-1)
    decode_in = decode[: CH * DEC_HID].reshape(CH, DEC_HID)
    decode_out = decode[CH * DEC_HID : CH * DEC_HID + DEC_HID * 4].reshape(DEC_HID, 4)
    picture = image[0]
    cells_read = samples[0].reshape(3, -1)
    mods = lax.dynamic_slice_in_dim(params["modulate"], 6 * camera[0], 6).astype(jnp.float32)
    row_start = place * PR
    triplane = rows[PLANE_ROW : PLANE_ROW + 3 * plane_rows * TC].reshape(3, plane_rows, TC, D)
    own_rows = lax.dynamic_slice_in_dim(triplane, row_start, PR, 1)
    stream0 = own_rows.reshape(-1, D).astype(jnp.float32)
    hidden1, norm_one = jax.vjp(norm_mod, stream0, mods[0], mods[1])
    hidden1 = hidden1.astype(jnp.bfloat16)
    query1 = product(hidden1, params["query_cross"]).astype(jnp.bfloat16)
    image_kv = product(picture, params["keyval_cross"]).astype(jnp.bfloat16)
    cross_out, total_one = attend_fwd(query1, image_kv[:, :D], image_kv[:, D:])
    cross_out = cross_out.astype(jnp.bfloat16)
    stream1 = stream0 + product(cross_out, params["out_cross"])
    hidden2, norm_two = jax.vjp(norm_mod, stream1, mods[2], mods[3])
    hidden2 = hidden2.astype(jnp.bfloat16)
    qkv = product(hidden2, params["qkv_self"]).astype(jnp.bfloat16)
    kv_all = lax.all_gather(qkv[:, D:], "strip", axis=0, tiled=True)
    self_out, total_two = attend_fwd(qkv[:, :D], kv_all[:, :D], kv_all[:, D:])
    self_out = self_out.astype(jnp.bfloat16)
    stream2 = stream1 + product(self_out, params["out_self"])
    hidden3, norm_three = jax.vjp(norm_mod, stream2, mods[4], mods[5])
    hidden3 = hidden3.astype(jnp.bfloat16)
    stream3 = stream2
    acts, gelu_backs = [], []
    for first, second in zip(first_panels, second_panels):
        act, gelu_back = jax.vjp(gelu_tanh, product(hidden3, first))
        acts.append(act.astype(jnp.bfloat16))
        gelu_backs.append(gelu_back)
        stream3 = stream3 + product(acts[-1], second)
    grid = stream3.astype(jnp.bfloat16).reshape(3, PR, -1, D)
    padded = with_halo(grid, (("strip", 1),), 1)
    ydc = jnp.einsum("prcd,dk->prck", padded, params["deconv"], preferred_element_type=jnp.float32)
    feature, assemble_back = jax.vjp(assemble, ydc)
    whole = lax.all_gather(feature.astype(jnp.bfloat16), "strip", axis=1, tiled=True)
    cells = whole.reshape(3, -1, CH)
    point = (
        jnp.take(cells[0], cells_read[0], axis=0).astype(jnp.float32)
        + jnp.take(cells[1], cells_read[1], axis=0).astype(jnp.float32)
        + jnp.take(cells[2], cells_read[2], axis=0).astype(jnp.float32)
    )
    point = point.astype(jnp.bfloat16)
    inner_value = product(point, decode_in)
    hidden, silu_back = jax.vjp(jax.nn.silu, inner_value)
    hidden = hidden.astype(jnp.bfloat16)
    output = product(hidden, decode_out)
    rays = pixel.shape[0]

    def local_loss(values):
        return render_loss(values.reshape(S, rays, 4), mask, wanted)

    loss_part, render_back = jax.vjp(local_loss, output)
    factor = 1.0 / jnp.maximum(count, 1.0)
    (grad_output,) = render_back(factor)
    grad_output = grad_output.astype(jnp.bfloat16)
    grad_decode_out = weight_grad(hidden, grad_output)
    (grad_inner,) = silu_back(product_back(grad_output, decode_out))
    grad_inner = grad_inner.astype(jnp.bfloat16)
    grad_decode_in = weight_grad(point, grad_inner)
    grad_point = product_back(grad_inner, decode_in)
    gradient_cell_grid = jnp.stack(
        [
            jax.ops.segment_sum(grad_point, cells_read[plane], num_segments=cells.shape[1])
            for plane in range(3)
        ]
    )
    grad_feature = lax.psum_scatter(
        gradient_cell_grid.reshape(whole.shape).astype(jnp.bfloat16),
        "strip",
        scatter_dimension=1,
        tiled=True,
    ).astype(jnp.float32)
    grad_feature = lax.optimization_barrier(grad_feature.astype(jnp.bfloat16)).astype(jnp.float32)
    (grad_ydc,) = assemble_back(grad_feature)
    grad_ydc = grad_ydc.astype(jnp.bfloat16)
    grad_deconv = weight_grad(padded.reshape(-1, D), grad_ydc.reshape(-1, 16 * CH))
    grad_padded = product_back(grad_ydc, params["deconv"])
    edges = jnp.concatenate([grad_padded[:, :1], grad_padded[:, -1:]], 1)
    beside = with_halo(edges.astype(jnp.bfloat16), (("strip", 1),), 1).astype(edges.dtype)
    grad_grid = grad_padded[:, 1:-1]
    grad_grid = grad_grid.at[:, 0].add(beside[:, 0]).at[:, -1].add(beside[:, -1])
    grad_stream = grad_grid.reshape(-1, D)
    grad_branch = grad_stream.astype(jnp.bfloat16)
    grad_first, grad_second = [], []
    grad_hidden3 = 0.0
    for first, second, act, gelu_back in zip(first_panels, second_panels, acts, gelu_backs):
        grad_second.append(weight_grad(act, grad_branch).astype(jnp.bfloat16))
        (grad_up,) = gelu_back(product_back(grad_branch, second))
        grad_up = grad_up.astype(jnp.bfloat16)
        grad_first.append(weight_grad(hidden3, grad_up).astype(jnp.bfloat16))
        grad_hidden3 = grad_hidden3 + product_back(grad_up, first)
    grad_norm, grad_mod4, grad_mod5 = norm_three(grad_hidden3)
    grad_stream = grad_stream + grad_norm
    grad_branch = grad_stream.astype(jnp.bfloat16)
    grad_out_self = weight_grad(self_out, grad_branch)
    grad_self = product_back(grad_branch, params["out_self"]).astype(jnp.bfloat16)
    grad_query2, grad_keys2, grad_values2 = attend_bwd(
        qkv[:, :D], kv_all[:, :D], kv_all[:, D:], total_two, grad_self
    )
    grad_kv_own = lax.psum_scatter(
        jnp.concatenate([grad_keys2, grad_values2], 1).astype(jnp.bfloat16),
        "strip",
        scatter_dimension=0,
        tiled=True,
    ).astype(jnp.float32)
    grad_qkv = jnp.concatenate([grad_query2, grad_kv_own], 1).astype(jnp.bfloat16)
    grad_qkv_self = weight_grad(hidden2, grad_qkv)
    grad_norm, grad_mod2, grad_mod3 = norm_two(product_back(grad_qkv, params["qkv_self"]))
    grad_stream = grad_stream + grad_norm
    grad_branch = grad_stream.astype(jnp.bfloat16)
    grad_out_cross = weight_grad(cross_out, grad_branch)
    grad_cross = product_back(grad_branch, params["out_cross"]).astype(jnp.bfloat16)
    grad_query1, grad_keys1, grad_values1 = attend_bwd(
        query1, image_kv[:, :D], image_kv[:, D:], total_one, grad_cross
    )
    grad_query1 = grad_query1.astype(jnp.bfloat16)
    grad_image_kv = jnp.concatenate([grad_keys1, grad_values1], 1).astype(jnp.bfloat16)
    grad_keyval = weight_grad(picture, grad_image_kv)
    grad_query_cross = weight_grad(hidden1, grad_query1)
    grad_norm, grad_mod0, grad_mod1 = norm_one(product_back(grad_query1, params["query_cross"]))
    grad_stream = grad_stream + grad_norm
    grad_mods = jnp.stack([grad_mod0, grad_mod1, grad_mod2, grad_mod3, grad_mod4, grad_mod5])
    grad_modulate = lax.dynamic_update_slice_in_dim(
        jnp.zeros((6 * NCAM, D), jnp.bfloat16), grad_mods.astype(jnp.bfloat16), 6 * camera[0], 0
    )
    grad_triplane = lax.dynamic_update_slice_in_dim(
        jnp.zeros((3, plane_rows, TC, D), jnp.bfloat16),
        grad_stream.astype(jnp.bfloat16).reshape(3, PR, TC, D),
        row_start,
        1,
    )
    grad_decode = jnp.concatenate([grad_decode_in.reshape(-1), grad_decode_out.reshape(-1)])
    grad_decode = jnp.pad(grad_decode, (0, GAP))
    pieces = [
        grad_query_cross,
        grad_keyval,
        grad_out_cross,
        grad_qkv_self,
        grad_out_self,
        grad_deconv,
        grad_decode,
        grad_modulate,
        grad_triplane,
    ]
    pieces = [piece.astype(jnp.bfloat16).reshape(-1, WIDE) for piece in pieces]
    panel_grads = jnp.concatenate(grad_first + grad_second)
    flat_sum, block_sum, loss_sum = reduce_grads(pieces, panel_grads, loss_part, weights.shape[0])
    loss = loss_sum * factor
    new_first = BETA_FIRST * first_moment + (1.0 - BETA_FIRST) * flat_sum
    new_second = BETA_SECOND * second_moment + (1.0 - BETA_SECOND) * flat_sum * flat_sum
    fix_first = 1.0 - BETA_FIRST**ADAM_STEP
    fix_second = 1.0 - BETA_SECOND**ADAM_STEP
    moved = new_first / fix_first / (jnp.sqrt(new_second / fix_second) + ADAM_EPS)
    new_weights = weights - ADAM_RATE * (moved + WEIGHT_DECAY * weights)
    new_left = STAT_DECAY * stat_left + (1.0 - STAT_DECAY) * jnp.einsum(
        "bij,bkj->bik", block_sum, block_sum, precision=HIGHEST_MODE
    )
    new_right = STAT_DECAY * stat_right + (1.0 - STAT_DECAY) * jnp.einsum(
        "bji,bjk->bik", block_sum, block_sum, precision=HIGHEST_MODE
    )
    half_step = jnp.einsum("bij,bjk->bik", block_sum, root_right, precision=HIGHEST_MODE)
    precond = jnp.einsum("bij,bjk->bik", root_left, half_step, precision=HIGHEST_MODE)
    block_rms = jnp.sqrt(jnp.mean(precond * precond, axis=(1, 2)) + RMS_EPS)
    new_blocks = blocks - SHAMPOO_RATE * precond / block_rms[:, None, None]
    return (
        loss,
        new_weights,
        new_first,
        new_second,
        new_blocks,
        block_sum,
        new_left,
        new_right,
        block_rms,
    )


def solution(mesh):
    placed = (
        P(("dp", "strip")),
        P("dp", None, None),
        P("dp", None, None),
        P("dp", None, None),
        P("dp", None, None),
        P("dp", None, None),
        P(("dp", "strip")),
        P(("dp", "strip")),
        P("dp", None, None),
        P("dp"),
        P("dp", None, None, "strip"),
        P("dp", "strip"),
        P("dp", None, None),
        P("dp", None),
    )
    return jax.shard_map(
        shards,
        mesh=mesh,
        in_specs=placed,
        out_specs=(
            P(),
            P(("dp", "strip")),
            P(("dp", "strip")),
            P(("dp", "strip")),
            P("dp", None, None),
            P("dp", None, None),
            P("dp", None, None),
            P("dp", None, None),
            P("dp"),
        ),
        check_vma=False,
    )
```

```python
import functools
import math

import jax
import jax.numpy as jnp
from jax import lax
from jax.experimental import pallas as pl
from jax.experimental.pallas import tpu as pltpu
from jax.sharding import PartitionSpec as P

D = 1024
HEAD_DIM = 64
HID = 4096
DI = 768
CH = 80
DEC_HID = 64
BLOCK = 128
PR = 8
TC = 32
S = 16
NCAM = 32
ADAM_STEP = 10


NORM_EPS = 1e-05
ADAM_RATE = 0.015
BETA_FIRST = 0.9
BETA_SECOND = 0.95
ADAM_EPS = 1e-08
WEIGHT_DECAY = 0.1
STAT_DECAY = 0.9
SHAMPOO_RATE = 0.01
RMS_EPS = 1e-06
HIGHEST_MODE = lax.Precision.HIGHEST
group_heads = 4


def with_halo(block, sides, width):
    for axis, dim in sides:
        count = lax.axis_size(axis)
        forward = [(i, i + 1) for i in range(count - 1)]
        backward = [(target, source) for source, target in forward]
        low = lax.ppermute(
            lax.slice_in_dim(block, block.shape[dim] - width, None, axis=dim), axis, forward
        )
        high = lax.ppermute(lax.slice_in_dim(block, 0, width, axis=dim), axis, backward)
        block = jnp.concatenate([low, block, high], axis=dim)
    return block


def product(left, right):
    return jnp.dot(left, right, preferred_element_type=jnp.float32)


def product_back(left, right):
    return lax.dot_general(
        left, right, (((left.ndim - 1,), (1,)), ((), ())), preferred_element_type=jnp.float32
    )


def weight_grad(left, right):
    return lax.dot_general(
        left, right, (((0,), (0,)), ((), ())), preferred_element_type=jnp.float32
    )


def norm_mod(stream, scale, shift):
    centred = stream - jnp.mean(stream, -1, keepdims=True)
    spread = jnp.mean(centred * centred, -1, keepdims=True)
    return centred * lax.rsqrt(spread + NORM_EPS) * (1.0 + scale) + shift


def gelu_tanh(value):
    return jax.nn.gelu(value, approximate=True)


def assemble(ydc):
    planes, rows, cols, _ = ydc.shape
    inner = rows - 2
    kernel = ydc.reshape(planes, rows, cols, 4, 4, -1)
    even = kernel[:, 1 : inner + 1, :, 1] + kernel[:, 0:inner, :, 3]
    odd = kernel[:, 1 : inner + 1, :, 2] + kernel[:, 2 : inner + 2, :, 0]
    tall = jnp.stack([even, odd], 2)
    wide = jnp.pad(tall, ((0, 0), (0, 0), (0, 0), (1, 1), (0, 0), (0, 0)))
    left_cols = wide[:, :, :, 1 : cols + 1, 1] + wide[:, :, :, 0:cols, 3]
    right_cols = wide[:, :, :, 1 : cols + 1, 2] + wide[:, :, :, 2 : cols + 2, 0]
    return jnp.stack([left_cols, right_cols], 4).reshape(planes, 2 * inner, 2 * cols, -1)


PAIR = 2 * HEAD_DIM
LOG2E = math.log2(math.e)
EXP_SCALE = HEAD_DIM ** (-0.5) * LOG2E


def nt_dot(left, right):
    return lax.dot_general(left, right, (((1,), (1,)), ((), ())), preferred_element_type=jnp.float32)


def head_lanes(shape, head):
    return lax.broadcasted_iota(jnp.int32, shape, len(shape) - 1) // HEAD_DIM == head


def attend_fwd_kernel(real_keys, q_ref, k_ref, v_ref, o_ref, lse_ref):
    query, keys = q_ref[...], k_ref[...]
    values = v_ref[...].T
    outs = []
    for head in range(2):
        own = jnp.where(head_lanes(query.shape, head), query, 0)
        scores = nt_dot(keys, own)
        if real_keys < keys.shape[0]:
            at = lax.broadcasted_iota(jnp.int32, scores.shape, 0)
            scores = jnp.where(at < real_keys, scores, -3e38)
        top = jnp.max(scores, 0, keepdims=True)
        raised = jnp.exp2((scores - top) * EXP_SCALE)
        total = jnp.sum(raised, 0, keepdims=True)
        shares = (raised * (1.0 / total)).astype(jnp.bfloat16)
        outs.append(product(values[head * HEAD_DIM : (head + 1) * HEAD_DIM], shares))
        lse_ref[0, head : head + 1] = top * EXP_SCALE + jnp.log2(total)
    o_ref[...] = jnp.concatenate(outs, 0).T.astype(jnp.bfloat16)


def attend_fwd(query, keys, values, key_col, value_col, real_keys, rows):
    count, total_keys = query.shape[0], keys.shape[0]
    pairs = D // PAIR
    return pl.pallas_call(
        functools.partial(attend_fwd_kernel, real_keys),
        grid=(pairs, count // rows),
        in_specs=[
            pl.BlockSpec((rows, PAIR), lambda j, n: (n, j)),
            pl.BlockSpec((total_keys, PAIR), lambda j, n: (0, key_col + j)),
            pl.BlockSpec((total_keys, PAIR), lambda j, n: (0, value_col + j)),
        ],
        out_specs=[
            pl.BlockSpec((rows, PAIR), lambda j, n: (n, j)),
            pl.BlockSpec((1, 8, rows), lambda j, n: (j, 0, n)),
        ],
        out_shape=[
            jax.ShapeDtypeStruct((count, D), jnp.bfloat16),
            jax.ShapeDtypeStruct((pairs, 8, count), jnp.float32),
        ],
        compiler_params=pltpu.CompilerParams(vmem_limit_bytes=48 * 1024 * 1024),
        cost_estimate=pl.CostEstimate(
            flops=4 * count * total_keys * D, transcendentals=count * total_keys * 16, bytes_accessed=4 * D * (count + total_keys)
        ),
        name="attend_fwd",
    )(query, keys, values)


def attend_bwd_kernel(real_keys, chunk, q_ref, k_ref, v_ref, lse_ref, o_ref, g_ref, dq_ref, dk_ref, dv_ref, kt_ref, dk_sum, dv_sum):
    step = pl.program_id(1)

    @pl.when(step == 0)
    def _():
        kt_ref[...] = k_ref[...].T
        dk_sum[...] = jnp.zeros_like(dk_sum)
        dv_sum[...] = jnp.zeros_like(dv_sum)

    query, grad = q_ref[...], g_ref[...]
    mixed = (grad.astype(jnp.float32) * o_ref[...].astype(jnp.float32)).T
    total_keys = k_ref.shape[0]
    queries = [jnp.where(head_lanes(query.shape, head), query, 0) for head in range(2)]
    grads = [jnp.where(head_lanes(grad.shape, head), grad, 0) for head in range(2)]
    inner = [jnp.sum(mixed[head * HEAD_DIM : (head + 1) * HEAD_DIM], 0, keepdims=True) for head in range(2)]
    grad_query = [jnp.zeros((HEAD_DIM, query.shape[0]), jnp.float32) for head in range(2)]
    for at in range(0, total_keys, chunk):
        part = pl.ds(at, chunk)
        keys, values = k_ref[part], v_ref[part]
        for head in range(2):
            scores = nt_dot(keys, queries[head])
            shares = jnp.exp2(scores * EXP_SCALE - lse_ref[0, head : head + 1])
            if at + chunk > real_keys:
                row = at + lax.broadcasted_iota(jnp.int32, shares.shape, 0)
                shares = jnp.where(row < real_keys, shares, 0.0)
            grad_shares = nt_dot(values, grads[head])
            grad_scores = (shares * (grad_shares - inner[head])).astype(jnp.bfloat16)
            dv_sum[part] += product(shares.astype(jnp.bfloat16), grads[head])
            dk_sum[part] += product(grad_scores, queries[head])
            grad_query[head] += product(
                kt_ref[head * HEAD_DIM : (head + 1) * HEAD_DIM, part], grad_scores
            )
    scale = HEAD_DIM ** (-0.5)
    dq_ref[...] = (jnp.concatenate(grad_query, 0) * scale).T.astype(jnp.bfloat16)

    @pl.when(step == pl.num_programs(1) - 1)
    def _():
        dk_ref[...] = (dk_sum[...] * scale).astype(jnp.bfloat16)
        dv_ref[...] = dv_sum[...].astype(jnp.bfloat16)


def attend_bwd(query, keys, values, key_col, value_col, real_keys, rows, chunk, totals, out, grad):
    count, total_keys = query.shape[0], keys.shape[0]
    pairs = D // PAIR
    by_query = pl.BlockSpec((rows, PAIR), lambda j, n: (n, j))
    by_key = pl.BlockSpec((total_keys, PAIR), lambda j, n: (0, j))
    return pl.pallas_call(
        functools.partial(attend_bwd_kernel, real_keys, chunk),
        grid=(pairs, count // rows),
        in_specs=[
            by_query,
            pl.BlockSpec((total_keys, PAIR), lambda j, n: (0, key_col + j)),
            pl.BlockSpec((total_keys, PAIR), lambda j, n: (0, value_col + j)),
            pl.BlockSpec((1, 8, rows), lambda j, n: (j, 0, n)),
            by_query,
            by_query,
        ],
        out_specs=[by_query, by_key, by_key],
        out_shape=[
            jax.ShapeDtypeStruct((count, D), jnp.bfloat16),
            jax.ShapeDtypeStruct((total_keys, D), jnp.bfloat16),
            jax.ShapeDtypeStruct((total_keys, D), jnp.bfloat16),
        ],
        scratch_shapes=[
            pltpu.VMEM((PAIR, total_keys), jnp.bfloat16),
            pltpu.VMEM((total_keys, PAIR), jnp.float32),
            pltpu.VMEM((total_keys, PAIR), jnp.float32),
        ],
        compiler_params=pltpu.CompilerParams(vmem_limit_bytes=48 * 1024 * 1024),
        cost_estimate=pl.CostEstimate(
            flops=10 * count * total_keys * D, transcendentals=count * total_keys * 16, bytes_accessed=8 * D * (count + total_keys)
        ),
        name="attend_bwd",
    )(query, keys, values, totals, out, grad)


GROUPS = 3


def render_kernel(samples_ref, cells_ref, wanted_ref, mask_ref, factor_ref, win_ref, wout_ref,
                  loss_ref, grad_ref, gin_ref, gout_ref,
                  table, inner_all, hidden_all, point_all, out_all, gout_all, sums):
    block = pl.program_id(0)
    cells = cells_ref.shape[1]
    group = table.shape[2]
    rays = samples_ref.shape[2]
    planes = cells_ref.shape[0]

    @pl.when(block == 0)
    def _():
        loss_ref[...] = jnp.zeros_like(loss_ref)
        gin_ref[...] = jnp.zeros_like(gin_ref)
        gout_ref[...] = jnp.zeros_like(gout_ref)
        sums[...] = jnp.zeros_like(sums)
        table[...] = jnp.zeros_like(table)
        for plane in range(planes):
            turned = cells_ref[plane].T
            for g in range(GROUPS):
                width = min(group, cells - g * group)
                table[plane, g * CH : (g + 1) * CH, :width] = turned[:CH, g * group : g * group + width]

    step = 4
    width = step * rays
    win, wout = win_ref[...], wout_ref[...]

    def places_read(plane, s):
        rows = [samples_ref[plane, s + n : s + n + 1, :] for n in range(step)]
        at = jnp.concatenate(rows, 1)
        owner = at // group
        within = at - owner * group
        hot = lax.broadcasted_iota(jnp.int32, (group, width), 0) == within
        return owner, jnp.where(hot, 1.0, 0.0).astype(jnp.bfloat16)

    def tn_dot(left, right):
        return lax.dot_general(left, right, (((0,), (0,)), ((), ())), preferred_element_type=jnp.float32)

    for s in range(0, S, step):
        here = pl.ds(s * rays, width)
        point = jnp.zeros((CH, width), jnp.float32)
        for plane in range(planes):
            owner, hot = places_read(plane, s)
            found = product(table[plane], hot)
            value = found[:CH]
            for g in range(1, GROUPS):
                value = jnp.where(owner == g, found[g * CH : (g + 1) * CH], value)
            point = point + value
        point = point.astype(jnp.bfloat16)
        inner = tn_dot(win, point)
        hidden = (inner * jax.nn.sigmoid(inner)).astype(jnp.bfloat16)
        out_all[:, here] = tn_dot(wout, hidden)
        inner_all[:, here] = inner
        hidden_all[:, here] = hidden
        point_all[:, here] = point

    factor = factor_ref[0]
    mask = mask_ref[...]
    row = lax.broadcasted_iota(jnp.int32, (8, rays), 0)
    is_colour = (row >= 1) & (row <= 3)
    before = jnp.zeros((1, rays), jnp.float32)
    rgb = jnp.zeros((8, rays), jnp.float32)
    kept = []
    for s in range(S):
        out = out_all[:, s * rays : (s + 1) * rays]
        level = out[0:1]
        absorb = (4.0 / S) * (jnp.maximum(level, 0.0) + jnp.log1p(jnp.exp(-jnp.abs(level))))
        weight = jnp.exp(-before) * (1.0 - jnp.exp(-absorb))
        before = before + absorb
        colour = jax.nn.sigmoid(out)
        rgb = rgb + weight * colour
        kept.append((weight, jnp.exp(-before), colour))
    error = jnp.where(is_colour, rgb - wanted_ref[...], 0.0)
    loss_ref[...] += jnp.sum(mask * jnp.sum(error * error, 0, keepdims=True))
    pull = error * (2.0 * factor * mask)
    tail = jnp.zeros((1, rays), jnp.float32)
    for s in reversed(range(S)):
        weight, left_over, colour = kept[s]
        to_weight = jnp.sum(pull * colour, 0, keepdims=True)
        to_absorb = to_weight * left_over - tail
        tail = tail + to_weight * weight
        to_level = (4.0 / S) * to_absorb * colour[0:1]
        to_colour = weight * pull * colour * (1.0 - colour)
        gout_all[:, s * rays : (s + 1) * rays] = jnp.where(row == 0, to_level, to_colour).astype(jnp.bfloat16)

    for s in range(0, S, step):
        here = pl.ds(s * rays, width)
        pulled = gout_all[:, here]
        inner = inner_all[:, here]
        gate = jax.nn.sigmoid(inner)
        grad_inner = product(wout, pulled) * (gate * (1.0 + inner * (1.0 - gate)))
        grad_inner = grad_inner.astype(jnp.bfloat16)
        gout_ref[...] += nt_dot(hidden_all[:, here], pulled)
        gin_ref[...] += nt_dot(point_all[:, here], grad_inner)
        grad_point = product(win, grad_inner)
        coarse = grad_point.astype(jnp.bfloat16).astype(jnp.float32)
        fine = grad_point - coarse
        for plane in range(planes):
            owner, hot = places_read(plane, s)
            rows = [jnp.where(owner == g, coarse, 0.0) for g in range(GROUPS)]
            rows += [jnp.where(owner == g, fine, 0.0) for g in range(GROUPS)]
            stacked = jnp.concatenate(rows, 0).astype(jnp.bfloat16)
            added = nt_dot(stacked, hot)
            sums[plane] += added[: GROUPS * CH] + added[GROUPS * CH :]

    @pl.when(block == pl.num_programs(0) - 1)
    def _():
        for plane in range(planes):
            for g in range(GROUPS):
                count = min(group, cells - g * group)
                part = sums[plane, g * CH : (g + 1) * CH, :count]
                grad_ref[plane, :, g * group : g * group + count] = part.astype(jnp.bfloat16)


def render(cells, samples, wanted, mask, factor, decode_in, decode_out, rays):
    planes, count, _ = cells.shape
    all_rays = samples.shape[2]
    group = -(-count // (GROUPS * 128)) * 128
    points = S * rays
    whole = lambda *shape: pl.BlockSpec(shape, lambda n: (0,) * len(shape))
    return pl.pallas_call(
        render_kernel,
        grid=(all_rays // rays,),
        in_specs=[
            pl.BlockSpec((planes, S, rays), lambda n: (0, 0, n)),
            whole(*cells.shape),
            pl.BlockSpec((8, rays), lambda n: (0, n)),
            pl.BlockSpec((1, rays), lambda n: (0, n)),
            pl.BlockSpec(memory_space=pltpu.SMEM),
            whole(CH, DEC_HID),
            whole(DEC_HID, 8),
        ],
        out_specs=[whole(8, 128), whole(planes, CH, count), whole(CH, DEC_HID), whole(DEC_HID, 8)],
        out_shape=[
            jax.ShapeDtypeStruct((8, 128), jnp.float32),
            jax.ShapeDtypeStruct((planes, CH, count), jnp.bfloat16),
            jax.ShapeDtypeStruct((CH, DEC_HID), jnp.float32),
            jax.ShapeDtypeStruct((DEC_HID, 8), jnp.float32),
        ],
        scratch_shapes=[
            pltpu.VMEM((planes, GROUPS * CH, group), jnp.bfloat16),
            pltpu.VMEM((DEC_HID, points), jnp.float32),
            pltpu.VMEM((DEC_HID, points), jnp.bfloat16),
            pltpu.VMEM((CH, points), jnp.bfloat16),
            pltpu.VMEM((8, points), jnp.float32),
            pltpu.VMEM((8, points), jnp.bfloat16),
            pltpu.VMEM((planes, GROUPS * CH, group), jnp.float32),
        ],
        compiler_params=pltpu.CompilerParams(vmem_limit_bytes=48 * 1024 * 1024),
        name="render",
    )(samples, cells, wanted, mask, factor, decode_in, decode_out)


LANE = 1024
MESH_ID = pl.DeviceIdType.MESH


def places():
    p = lax.axis_index("dp")
    c = lax.axis_index("strip")
    z = p // 4
    flip_x = p + 1 - 2 * (p % 2)
    flip_y = p + 2 - 4 * ((p // 2) % 2)
    both = flip_x + flip_y - p
    near = (1 - c) * flip_x + c * flip_y
    far = (1 - c) * flip_y + c * flip_x
    return p, c, z, near, far, both


def along_z(line, z, k):
    return ((z + k) % 4) * 4 + line % 4


def enter(peers):
    barrier = pltpu.get_barrier_semaphore()
    for peer in peers:
        pl.semaphore_signal(barrier, inc=1, device_id=peer, device_id_type=MESH_ID)
    pl.semaphore_wait(barrier, len(peers))


def flat_chunks(rows, n):
    part = rows // n
    return n, part, lambda p, c, j: (2 * p + c) * rows + j * part


def block_chunk(p, c, k):
    second = p // 8
    return ((1 - second) * ((2 * c + k) * 8 + p) + second * (4 * p + 2 * c + k)) * BLOCK

block_chunks = (2, BLOCK, block_chunk)


ORDER = [("near", 0), ("z", 1), ("z", 3), ("far", 0), ("z", 2), ("near", 1), ("near", 3), ("near", 2)]
ORDER += [("both", 0), ("far", 1), ("far", 3), ("far", 2), ("both", 1), ("both", 3), ("both", 2)]
ORDER += [("core", i) for i in range(16)]

def gather_kernel(layouts, stagger, *refs):
    count = len(layouts)
    sources = refs[:count]
    fulls = refs[count : 2 * count]
    send, recv, local = refs[2 * count :]
    p, c, z, near, far, both = places()
    zs = [along_z(p, z, k) for k in range(4)]
    enter([(q, c) for q in zs[1:]] + [(near, c), (far, c), (p, 1 - c)])
    jobs = [(a, j) for a, layout in enumerate(layouts) for j in range(layout[0])]

    def target(owner, job):
        a, j = jobs[job]
        _, rows, place = layouts[a]
        return fulls[a].at[pl.ds(pl.multiple_of(place(*owner, j), 8), rows)]

    def source(job):
        a, j = jobs[job]
        rows = layouts[a][1]
        return sources[a].at[pl.ds(j * rows, rows)]

    started = []

    def forward(owner, own, event, peer, job):
        t = target(owner, job)
        copy = pltpu.make_async_remote_copy(
            source(job) if own else t, t, send.at[event, job], recv.at[event, job], device_id=peer, device_id_type=MESH_ID
        )
        copy.start()
        started.append(copy)

    def arrive(owner, event, job):
        t = target(owner, job)
        pltpu.make_async_remote_copy(
            t, t, send.at[event, job], recv.at[event, job], device_id=(p, 1 - c), device_id_type=MESH_ID
        ).wait_recv()

    me = (p, c)

    def begin(job):
        forward(me, True, 3, (near, c), job)
        for k in (1, 3, 2):
            forward(me, True, 3 - k, (zs[k], c), job)
        forward(me, True, 7, (far, c), job)
        forward(me, True, 15, (p, 1 - c), job)
        pltpu.make_async_copy(source(job), target(me, job), local.at[job]).start()

    def take(kind, k, job):
        if kind == "z":
            owner = (zs[k], c)
            arrive(owner, k - 1, job)
            forward(owner, False, 3 + k, (near, c), job)
            forward(owner, False, 7 + k, (far, c), job)
            forward(owner, False, 15 + k, (p, 1 - c), job)
        elif kind == "near":
            owner = (along_z(near, z, k), c)
            arrive(owner, 3 + k, job)
            forward(owner, False, 11 + k, (far, c), job)
            forward(owner, False, 19 + k, (p, 1 - c), job)
        elif kind == "far":
            owner = (along_z(far, z, k), c)
            arrive(owner, 7 + k, job)
            forward(owner, False, 23 + k, (p, 1 - c), job)
        elif kind == "both":
            owner = (along_z(both, z, k), c)
            arrive(owner, 11 + k, job)
            forward(owner, False, 27 + k, (p, 1 - c), job)
        elif kind == "core":
            line = (p, far, near, both)[k // 4]
            arrive((along_z(line, z, k % 4), 1 - c), 15 + k, job)

    steps = []
    for job in range(len(jobs)):
        steps.append((stagger * job, -1, job))
        for i in range(len(ORDER)):
            steps.append((stagger * job + i + 1, i, job))
    for _, i, job in sorted(steps):
        if i < 0:
            begin(job)
        else:
            take(*ORDER[i], job)
    for copy in started:
        copy.wait_send()
    for job in range(len(jobs)):
        pltpu.make_async_copy(source(job), target(me, job), local.at[job]).wait()


def gather_all(layouts, stagger, shards_in, name_id):
    copies = sum(l[0] for l in layouts)
    return pl.pallas_call(
        functools.partial(gather_kernel, layouts, stagger),
        out_shape=[jax.ShapeDtypeStruct((32 * s.shape[0],) + s.shape[1:], s.dtype) for s in shards_in],
        in_specs=[pl.BlockSpec(memory_space=pl.ANY)] * len(shards_in),
        out_specs=[pl.BlockSpec(memory_space=pl.ANY)] * len(shards_in),
        scratch_shapes=[
            pltpu.SemaphoreType.DMA((31, copies)),
            pltpu.SemaphoreType.DMA((31, copies)),
            pltpu.SemaphoreType.DMA((copies,)),
        ],
        compiler_params=pltpu.CompilerParams(collective_id=name_id, has_side_effects=True),
        name="gather_all",
    )(*shards_in)


SUM_ORDER = [(3, 0), (3, 1), (3, 3), (3, 2), (2, 0), (2, 1), (2, 3), (2, 2)]
SUM_ORDER += [(1, 1), (1, 3), (1, 2), (1, 0), (0, 1), (0, 3), (0, 2), (0, 0)]
AHEAD = 3


def scatter_kernel(layouts, shared, stagger, *refs):
    count = len(layouts)
    grads = refs[:count]
    outs = refs[count : 2 * count]
    scratch = refs[2 * count :]
    p, c, z, near, far, both = places()
    zs = [along_z(p, z, k) for k in range(4)]
    enter([(q, c) for q in zs[1:]] + [(near, c), (far, c), (p, 1 - c)])
    csend, crecv, bsend, brecv, load_sem, out_sem = scratch[:6]
    buffers = [scratch[6 + 6 * a : 12 + 6 * a] for a in range(count)]
    jobs = [(a, j) for a, layout in enumerate(layouts) for j in range(layout[0])]
    lines = (p, near, far, both)
    partner_lines = (p, far, near, both)

    def view(job, ref, slot):
        a, j = jobs[job]
        rows = layouts[a][1]
        return ref.at[slot, pl.ds(j * rows, rows)]

    def piece(owner, job):
        a, j = jobs[job]
        _, rows, place = layouts[a]
        return grads[a].at[pl.ds(pl.multiple_of(place(*owner, j), 8), rows)]

    def to_core(i, job):
        g, k = SUM_ORDER[i]
        owner = (along_z(partner_lines[g], z, k), 1 - c)
        rc = buffers[jobs[job][0]][0]
        return pltpu.make_async_remote_copy(
            piece(owner, job), view(job, rc, g * 4 + k), csend.at[i, job], crecv.at[i, job],
            device_id=(p, 1 - c), device_id_type=MESH_ID,
        )

    def load(i, job):
        g, k = SUM_ORDER[i]
        own = buffers[jobs[job][0]][4]
        return pltpu.make_async_copy(
            piece((along_z(lines[g], z, k), c), job), view(job, own, i % AHEAD), load_sem.at[i, job]
        )

    def onward(i, job):
        g, k = SUM_ORDER[i]
        rc, rb, ra, rz = buffers[jobs[job][0]][:4]
        if g == 3:
            target, event, peer = view(job, rb, 4 + k), 4 + k, (far, c)
        elif g == 2:
            target, event, peer = view(job, rb, k), k, (far, c)
        elif g == 1:
            target, event, peer = view(job, ra, k), 8 + k, (near, c)
        else:
            target, event, peer = view(job, rz, 3 - k), 12 + 3 - k, (zs[k], c)
        return pltpu.make_async_remote_copy(
            view(job, rc, g * 4 + k), target, bsend.at[event, job], brecv.at[event, job],
            device_id=peer, device_id_type=MESH_ID,
        )

    def landed(event, job):
        rc, rb, ra, rz = buffers[jobs[job][0]][:4]
        if event < 8:
            target = view(job, rb, event)
        elif event < 12:
            target = view(job, ra, event - 8)
        else:
            target = view(job, rz, event - 12)
        pltpu.make_async_remote_copy(
            target, target, bsend.at[event, job], brecv.at[event, job], device_id=(p, 1 - c), device_id_type=MESH_ID
        ).wait_recv()
        return target

    def add_up(parts, target):
        rows = target.shape[0]
        step = math.gcd(rows, 16)

        @pl.loop(0, rows // step)
        def _(n):
            at = pl.ds(pl.multiple_of(n * step, step), step)
            total = parts[0][at].astype(jnp.float32)
            for part in parts[1:]:
                total = total + part[at].astype(jnp.float32)
            target[at] = total.astype(target.dtype)

    def start(i, job):
        to_core(i, job).start()
        load(i, job).start()

    def final_copies(job):
        a, j = jobs[job]
        rows = layouts[a][1]
        done = view(job, buffers[a][5], 0)
        if not shared[a]:
            return [pltpu.make_async_copy(done, outs[a].at[pl.ds(j * rows, rows)], out_sem.at[job, 0])]
        spot = outs[a].at[pl.ds(pl.multiple_of((c * layouts[a][0] + j) * rows, 8), rows)]
        return [
            pltpu.make_async_copy(done, spot, out_sem.at[job, 0]),
            pltpu.make_async_remote_copy(
                done, spot, out_sem.at[job, 1], out_sem.at[job, 2], device_id=(p, 1 - c), device_id_type=MESH_ID
            ),
        ]

    def step(i, job):
        g, k = SUM_ORDER[i]
        rc, rb, ra, rz, own, done = buffers[jobs[job][0]]
        load(i, job).wait()
        to_core(i, job).wait_recv()
        here = view(job, rc, g * 4 + k)
        parts = [here, view(job, own, i % AHEAD)]
        if g == 1:
            parts.append(landed(4 + k, job))
        if g == 0:
            parts.append(landed(k, job))
            parts.append(landed(8 + k, job))
        if (g, k) == (0, 0):
            parts += [landed(12 + n, job) for n in range(3)]
            add_up(parts, view(job, done, 0))
            for copy in final_copies(job):
                copy.start()
        else:
            add_up(parts, here)
            onward(i, job).start()
        if i + AHEAD < 16:
            start(i + AHEAD, job)

    steps = []
    for job in range(len(jobs)):
        for i in range(-1, 16):
            steps.append((stagger * job + i, job, i))
    for _, job, i in sorted(steps):
        if i < 0:
            for n in range(AHEAD):
                start(n, job)
        else:
            step(i, job)
    for job in range(len(jobs)):
        for i in range(16):
            to_core(i, job).wait_send()
            if i < 15:
                onward(i, job).wait_send()
        for copy in final_copies(job):
            copy.wait()


def scatter_sum(layouts, shared, stagger, grads, name_id):
    jobs = sum(l[0] for l in layouts)
    scratch = [
        pltpu.SemaphoreType.DMA((16, jobs)),
        pltpu.SemaphoreType.DMA((16, jobs)),
        pltpu.SemaphoreType.DMA((15, jobs)),
        pltpu.SemaphoreType.DMA((15, jobs)),
        pltpu.SemaphoreType.DMA((16, jobs)),
        pltpu.SemaphoreType.DMA((jobs, 3)),
    ]
    shapes = []
    for layout, both_cores, grad in zip(layouts, shared, grads):
        rows, width = layout[0] * layout[1], grad.shape[1]
        for slots in (16, 8, 4, 3, AHEAD):
            scratch.append(pltpu.VMEM((slots, rows, width), grad.dtype))
        kind = grad.dtype if both_cores else jnp.float32
        scratch.append(pltpu.VMEM((1, rows, width), kind))
        shapes.append(jax.ShapeDtypeStruct(((2 if both_cores else 1) * rows, width), kind))
    return pl.pallas_call(
        functools.partial(scatter_kernel, layouts, shared, stagger),
        out_shape=shapes,
        in_specs=[pl.BlockSpec(memory_space=pl.ANY)] * len(grads),
        out_specs=[pl.BlockSpec(memory_space=pl.ANY)] * len(grads),
        scratch_shapes=scratch,
        compiler_params=pltpu.CompilerParams(
            collective_id=name_id, has_side_effects=True, vmem_limit_bytes=56 * 1024 * 1024
        ),
        name="scatter_sum",
    )(*grads)


WIDE = 1024
TILE = 8 * WIDE
GAP_AT = D * D + DI * 2 * D + D * D + D * 3 * D + D * D + D * 16 * CH + CH * DEC_HID + DEC_HID * 4
GAP = -GAP_AT % TILE
ROWS = {}
_row = 0
for _name, _rows in (
    ("query_cross", D),
    ("keyval_cross", 2 * DI),
    ("out_cross", D),
    ("qkv_self", 3 * D),
    ("out_self", D),
    ("deconv", 16 * CH),
    ("decode", 8),
    ("modulate", 6 * NCAM),
):
    ROWS[_name] = (_row, _row + _rows)
    _row += _rows
PLANE_ROW = _row


def direct_links():
    return lax.axis_size("dp") == 16 and lax.axis_size("strip") == 2


def align(shard):
    length = shard.shape[0]
    rows = -(-length // TILE) * 8
    size = rows * WIDE
    extra = size - length
    reach = -(-32 * extra // WIDE) * WIDE
    place = lax.axis_index("dp") * 2 + lax.axis_index("strip")
    shard = shard.astype(jnp.bfloat16)
    following = lax.ppermute(shard[:reach], ("dp", "strip"), [(n + 1, n) for n in range(31)])
    joined = jnp.concatenate([shard, following])
    shift = place * extra
    early = lax.dynamic_slice_in_dim(joined, shift, size)
    late = lax.dynamic_slice_in_dim(joined, jnp.maximum(shift - GAP, 0), size)
    at = place * size + lax.iota(jnp.int32, size)
    return jnp.where(at < GAP_AT, early, late).reshape(rows, WIDE)


def unalign(summed, length):
    size = summed.size
    extra = size - length
    reach = -(-32 * extra // WIDE) * WIDE
    place = lax.axis_index("dp") * 2 + lax.axis_index("strip")
    summed = summed.reshape(-1)
    before = lax.ppermute(summed[size - reach :], ("dp", "strip"), [(n, n + 1) for n in range(31)])
    joined = jnp.concatenate([before, summed])
    shift = reach - place * extra
    early = lax.dynamic_slice_in_dim(joined, shift, length)
    late = lax.dynamic_slice_in_dim(joined, shift + GAP, length)
    at = place * length + lax.iota(jnp.int32, length)
    return jnp.where(at < GAP_AT, early, late)


def chunks_of(tiles):
    return tiles.reshape(-1, 8, BLOCK, BLOCK).transpose(0, 2, 1, 3).reshape(-1, WIDE)


def tiles_of(chunks):
    return chunks.reshape(-1, BLOCK, 8, BLOCK).transpose(0, 2, 1, 3).reshape(-1, BLOCK, BLOCK)


def panels_of(chunks):
    half = chunks.shape[0] // 2
    first = chunks[:half].reshape(D // BLOCK, HID // WIDE, BLOCK, WIDE).transpose(1, 0, 2, 3)
    return jnp.concatenate([first.reshape(half, WIDE), chunks[half:]])


def chunks_of_panels(panels):
    half = panels.shape[0] // 2
    first = panels[:half].reshape(HID // WIDE, D // BLOCK, BLOCK, WIDE).transpose(1, 0, 2, 3)
    return jnp.concatenate([first.reshape(half, WIDE), panels[half:]])


META = (1, 8, lambda p, c, j: (2 * p + c) * 8)


def gather_weights(weights, blocks, part):
    length = weights.shape[0]
    if direct_links():
        own = align(weights)
        half = blocks.shape[0] // 2
        tiles = lax.dynamic_slice_in_dim(blocks, lax.axis_index("strip") * half, half)
        tiles = chunks_of(tiles.astype(jnp.bfloat16))
        meta = jnp.full((8, 128), part, jnp.float32)
        rows, panels, parts = gather_all(
            [flat_chunks(own.shape[0], 3), block_chunks, META], 6, [own, tiles, meta], 0
        )
        return rows, panels, jnp.sum(parts[::8, 0])
    flat = lax.all_gather(weights.astype(jnp.bfloat16), ("dp", "strip"), axis=0, tiled=True)
    tiles = lax.all_gather(blocks.astype(jnp.bfloat16), "dp", axis=0, tiled=True)
    rows = jnp.concatenate([flat[:GAP_AT], jnp.zeros((GAP,), flat.dtype), flat[GAP_AT:]])
    rows = rows[: rows.shape[0] // TILE * TILE].reshape(-1, WIDE)
    return rows, panels_of(chunks_of(tiles)), lax.psum(part, ("dp", "strip"))


def reduce_grads(pieces, panels, part, length):
    if direct_links():
        rows = -(-length // TILE) * 8
        total = sum(piece.shape[0] for piece in pieces)
        pieces = pieces + [jnp.zeros((32 * rows - total, WIDE), jnp.bfloat16)]
        meta = jnp.full((32 * 8, 128), part, jnp.float32)
        summed, tiles, parts = scatter_sum(
            [flat_chunks(rows, 1), block_chunks, META],
            [False, True, False],
            6,
            [jnp.concatenate(pieces), panels, meta],
            1,
        )
        return unalign(summed, length), tiles_of(tiles).astype(jnp.float32), parts[0, 0]
    flat = jnp.concatenate(pieces).astype(jnp.float32).reshape(-1)
    flat = jnp.concatenate([flat[:GAP_AT], flat[GAP_AT + GAP :]])
    devices = lax.axis_size("dp") * lax.axis_size("strip")
    flat = jnp.pad(flat, (0, devices * length - flat.shape[0]))
    tiles = tiles_of(chunks_of_panels(panels)).astype(jnp.float32)
    flat_sum = lax.psum_scatter(flat, ("dp", "strip"), scatter_dimension=0, tiled=True)
    tile_sum = lax.psum_scatter(tiles, ("dp", "strip"), scatter_dimension=0, tiled=True)
    tile_sum = lax.all_gather(tile_sum.astype(jnp.bfloat16), "strip", axis=0, tiled=True)
    return flat_sum, tile_sum.astype(jnp.float32), lax.psum(part, ("dp", "strip"))


def shards(
    weights,
    blocks,
    stat_left,
    stat_right,
    root_left,
    root_right,
    first_moment,
    second_moment,
    image,
    camera,
    samples,
    ray_pixel,
    target,
    valid,
):
    strips = lax.axis_size("strip")
    place = lax.axis_index("strip")
    plane_rows = PR * strips
    pixel = ray_pixel[0]
    mask = jnp.take(valid[0], pixel).astype(jnp.float32)
    wanted = jnp.take(target[0], pixel, axis=1)
    rows, panels, count = gather_weights(weights, blocks, jnp.sum(mask))
    panels = panels.reshape(-1, WIDE, WIDE)
    first_panels = [panels[n] for n in range(HID // WIDE)]
    second_panels = [panels[n] for n in range(HID // WIDE, 2 * HID // WIDE)]
    params = {name: rows[low:high] for name, (low, high) in ROWS.items()}
    params["keyval_cross"] = params["keyval_cross"].reshape(DI, 2 * D)
    params["qkv_self"] = params["qkv_self"].reshape(D, 3 * D)
    params["deconv"] = params["deconv"].reshape(D, 16 * CH)
    decode = params["decode"].reshape(-1)
    decode_in = decode[: CH * DEC_HID].reshape(CH, DEC_HID)
    decode_out = decode[CH * DEC_HID : CH * DEC_HID + DEC_HID * 4].reshape(DEC_HID, 4)
    picture = image[0]
    cells_read = samples[0].reshape(3, -1)
    mods = lax.dynamic_slice_in_dim(params["modulate"], 6 * camera[0], 6).astype(jnp.float32)
    row_start = place * PR
    triplane = rows[PLANE_ROW : PLANE_ROW + 3 * plane_rows * TC].reshape(3, plane_rows, TC, D)
    own_rows = lax.dynamic_slice_in_dim(triplane, row_start, PR, 1)
    stream0 = own_rows.reshape(-1, D).astype(jnp.float32)
    hidden1, norm_one = jax.vjp(norm_mod, stream0, mods[0], mods[1])
    hidden1 = hidden1.astype(jnp.bfloat16)
    query1 = product(hidden1, params["query_cross"]).astype(jnp.bfloat16)
    real_keys = picture.shape[0]
    picture = jnp.pad(picture, ((0, -real_keys % 128), (0, 0)))
    image_kv = product(picture, params["keyval_cross"]).astype(jnp.bfloat16)
    tokens = query1.shape[0]
    cross_out, total_one = attend_fwd(query1, image_kv, image_kv, 0, D // PAIR, real_keys, tokens)
    stream1 = stream0 + product(cross_out, params["out_cross"])
    hidden2, norm_two = jax.vjp(norm_mod, stream1, mods[2], mods[3])
    hidden2 = hidden2.astype(jnp.bfloat16)
    qkv = product(hidden2, params["qkv_self"]).astype(jnp.bfloat16)
    kv_all = lax.all_gather(qkv[:, D:], "strip", axis=0, tiled=True)
    all_keys = kv_all.shape[0]
    self_out, total_two = attend_fwd(qkv, kv_all, kv_all, 0, D // PAIR, all_keys, tokens)
    stream2 = stream1 + product(self_out, params["out_self"])
    hidden3, norm_three = jax.vjp(norm_mod, stream2, mods[4], mods[5])
    hidden3 = hidden3.astype(jnp.bfloat16)
    stream3 = stream2
    acts, gelu_backs = [], []
    for first, second in zip(first_panels, second_panels):
        act, gelu_back = jax.vjp(gelu_tanh, product(hidden3, first))
        acts.append(act.astype(jnp.bfloat16))
        gelu_backs.append(gelu_back)
        stream3 = stream3 + product(acts[-1], second)
    grid = stream3.astype(jnp.bfloat16).reshape(3, PR, -1, D)
    padded = with_halo(grid, (("strip", 1),), 1)
    ydc = jnp.einsum("prcd,dk->prck", padded, params["deconv"], preferred_element_type=jnp.float32)
    feature, assemble_back = jax.vjp(assemble, ydc)
    whole = lax.all_gather(feature.astype(jnp.bfloat16), "strip", axis=1, tiled=True)
    cells = whole.reshape(3, -1, CH)
    rays = pixel.shape[0]
    factor = 1.0 / jnp.maximum(count, 1.0)
    loss_part, grad_cells, grad_decode_in, grad_decode_out = render(
        cells,
        samples[0],
        jnp.pad(wanted, ((1, 4), (0, 0))),
        mask[None],
        factor.reshape(1),
        decode_in,
        jnp.pad(decode_out, ((0, 0), (0, 4))),
        rays,
    )
    loss_part = loss_part[0, 0]
    grad_decode_out = grad_decode_out[:, :4]
    grad_feature = lax.psum_scatter(
        grad_cells.transpose(0, 2, 1).reshape(whole.shape),
        "strip",
        scatter_dimension=1,
        tiled=True,
    ).astype(jnp.float32)
    grad_feature = lax.optimization_barrier(grad_feature.astype(jnp.bfloat16)).astype(jnp.float32)
    (grad_ydc,) = assemble_back(grad_feature)
    grad_ydc = grad_ydc.astype(jnp.bfloat16)
    grad_deconv = weight_grad(padded.reshape(-1, D), grad_ydc.reshape(-1, 16 * CH))
    grad_padded = product_back(grad_ydc, params["deconv"])
    edges = jnp.concatenate([grad_padded[:, :1], grad_padded[:, -1:]], 1)
    beside = with_halo(edges.astype(jnp.bfloat16), (("strip", 1),), 1).astype(edges.dtype)
    grad_grid = grad_padded[:, 1:-1]
    grad_grid = grad_grid.at[:, 0].add(beside[:, 0]).at[:, -1].add(beside[:, -1])
    grad_stream = grad_grid.reshape(-1, D)
    grad_branch = grad_stream.astype(jnp.bfloat16)
    grad_first, grad_second = [], []
    grad_hidden3 = 0.0
    for first, second, act, gelu_back in zip(first_panels, second_panels, acts, gelu_backs):
        grad_second.append(weight_grad(act, grad_branch).astype(jnp.bfloat16))
        (grad_up,) = gelu_back(product_back(grad_branch, second))
        grad_up = grad_up.astype(jnp.bfloat16)
        grad_first.append(weight_grad(hidden3, grad_up).astype(jnp.bfloat16))
        grad_hidden3 = grad_hidden3 + product_back(grad_up, first)
    grad_norm, grad_mod4, grad_mod5 = norm_three(grad_hidden3)
    grad_stream = grad_stream + grad_norm
    grad_branch = grad_stream.astype(jnp.bfloat16)
    grad_out_self = weight_grad(self_out, grad_branch)
    grad_self = product_back(grad_branch, params["out_self"]).astype(jnp.bfloat16)
    grad_query2, grad_keys2, grad_values2 = attend_bwd(
        qkv, kv_all, kv_all, 0, D // PAIR, all_keys, tokens, 512, total_two, self_out, grad_self
    )
    grad_kv_own = lax.psum_scatter(
        jnp.concatenate([grad_keys2, grad_values2], 1), "strip", scatter_dimension=0, tiled=True
    )
    grad_qkv = jnp.concatenate([grad_query2, grad_kv_own], 1)
    grad_qkv_self = weight_grad(hidden2, grad_qkv)
    grad_norm, grad_mod2, grad_mod3 = norm_two(product_back(grad_qkv, params["qkv_self"]))
    grad_stream = grad_stream + grad_norm
    grad_branch = grad_stream.astype(jnp.bfloat16)
    grad_out_cross = weight_grad(cross_out, grad_branch)
    grad_cross = product_back(grad_branch, params["out_cross"]).astype(jnp.bfloat16)
    grad_query1, grad_keys1, grad_values1 = attend_bwd(
        query1, image_kv, image_kv, 0, D // PAIR, real_keys, tokens, 128, total_one, cross_out, grad_cross
    )
    grad_image_kv = jnp.concatenate([grad_keys1, grad_values1], 1)
    grad_keyval = weight_grad(picture, grad_image_kv)
    grad_query_cross = weight_grad(hidden1, grad_query1)
    grad_norm, grad_mod0, grad_mod1 = norm_one(product_back(grad_query1, params["query_cross"]))
    grad_stream = grad_stream + grad_norm
    grad_mods = jnp.stack([grad_mod0, grad_mod1, grad_mod2, grad_mod3, grad_mod4, grad_mod5])
    grad_modulate = lax.dynamic_update_slice_in_dim(
        jnp.zeros((6 * NCAM, D), jnp.bfloat16), grad_mods.astype(jnp.bfloat16), 6 * camera[0], 0
    )
    grad_triplane = lax.dynamic_update_slice_in_dim(
        jnp.zeros((3, plane_rows, TC, D), jnp.bfloat16),
        grad_stream.astype(jnp.bfloat16).reshape(3, PR, TC, D),
        row_start,
        1,
    )
    grad_decode = jnp.concatenate([grad_decode_in.reshape(-1), grad_decode_out.reshape(-1)])
    grad_decode = jnp.pad(grad_decode, (0, GAP))
    pieces = [
        grad_query_cross,
        grad_keyval,
        grad_out_cross,
        grad_qkv_self,
        grad_out_self,
        grad_deconv,
        grad_decode,
        grad_modulate,
        grad_triplane,
    ]
    pieces = [piece.astype(jnp.bfloat16).reshape(-1, WIDE) for piece in pieces]
    panel_grads = jnp.concatenate(grad_first + grad_second)
    flat_sum, block_sum, loss_sum = reduce_grads(pieces, panel_grads, loss_part, weights.shape[0])
    loss = loss_sum * factor
    new_first = BETA_FIRST * first_moment + (1.0 - BETA_FIRST) * flat_sum
    new_second = BETA_SECOND * second_moment + (1.0 - BETA_SECOND) * flat_sum * flat_sum
    fix_first = 1.0 - BETA_FIRST**ADAM_STEP
    fix_second = 1.0 - BETA_SECOND**ADAM_STEP
    moved = new_first / fix_first / (jnp.sqrt(new_second / fix_second) + ADAM_EPS)
    new_weights = weights - ADAM_RATE * (moved + WEIGHT_DECAY * weights)
    new_left = STAT_DECAY * stat_left + (1.0 - STAT_DECAY) * jnp.einsum(
        "bij,bkj->bik", block_sum, block_sum, precision=HIGHEST_MODE
    )
    new_right = STAT_DECAY * stat_right + (1.0 - STAT_DECAY) * jnp.einsum(
        "bji,bjk->bik", block_sum, block_sum, precision=HIGHEST_MODE
    )
    half_step = jnp.einsum("bij,bjk->bik", block_sum, root_right, precision=HIGHEST_MODE)
    precond = jnp.einsum("bij,bjk->bik", root_left, half_step, precision=HIGHEST_MODE)
    block_rms = jnp.sqrt(jnp.mean(precond * precond, axis=(1, 2)) + RMS_EPS)
    new_blocks = blocks - SHAMPOO_RATE * precond / block_rms[:, None, None]
    return (
        loss,
        new_weights,
        new_first,
        new_second,
        new_blocks,
        block_sum,
        new_left,
        new_right,
        block_rms,
    )


def solution(mesh):
    placed = (
        P(("dp", "strip")),
        P("dp", None, None),
        P("dp", None, None),
        P("dp", None, None),
        P("dp", None, None),
        P("dp", None, None),
        P(("dp", "strip")),
        P(("dp", "strip")),
        P("dp", None, None),
        P("dp"),
        P("dp", None, None, "strip"),
        P("dp", "strip"),
        P("dp", None, None),
        P("dp", None),
    )
    return jax.shard_map(
        shards,
        mesh=mesh,
        in_specs=placed,
        out_specs=(
            P(),
            P(("dp", "strip")),
            P(("dp", "strip")),
            P(("dp", "strip")),
            P("dp", None, None),
            P("dp", None, None),
            P("dp", None, None),
            P("dp", None, None),
            P("dp"),
        ),
        check_vma=False,
    )
```

```python
import functools
import math

import jax
import jax.numpy as jnp
from jax import lax
from jax.experimental import pallas as pl
from jax.experimental.pallas import tpu as pltpu
from jax.sharding import PartitionSpec as P

D = 1024
HEAD_DIM = 64
HID = 4096
DI = 768
CH = 80
DEC_HID = 64
BLOCK = 128
PR = 8
TC = 32
S = 16
NCAM = 32
ADAM_STEP = 10


NORM_EPS = 1e-05
ADAM_RATE = 0.015
BETA_FIRST = 0.9
BETA_SECOND = 0.95
ADAM_EPS = 1e-08
WEIGHT_DECAY = 0.1
STAT_DECAY = 0.9
SHAMPOO_RATE = 0.01
RMS_EPS = 1e-06
HIGHEST_MODE = lax.Precision.HIGHEST
WIDE = 1024


def product(left, right):
    return jnp.dot(left, right, preferred_element_type=jnp.float32)


def product_back(left, right):
    return lax.dot_general(
        left, right, (((left.ndim - 1,), (1,)), ((), ())), preferred_element_type=jnp.float32
    )


def weight_grad(left, right):
    return lax.dot_general(
        left, right, (((0,), (0,)), ((), ())), preferred_element_type=jnp.float32
    )


def norm_mod(stream, scale, shift):
    centred = stream - jnp.mean(stream, -1, keepdims=True)
    spread = jnp.mean(centred * centred, -1, keepdims=True)
    return centred * lax.rsqrt(spread + NORM_EPS) * (1.0 + scale) + shift


def gelu_tanh(value):
    return jax.nn.gelu(value, approximate=True)


def assemble(ydc):
    planes, rows, cols, _ = ydc.shape
    inner = rows - 2
    kernel = ydc.reshape(planes, rows, cols, 4, 4, -1)
    even = kernel[:, 1 : inner + 1, :, 1] + kernel[:, 0:inner, :, 3]
    odd = kernel[:, 1 : inner + 1, :, 2] + kernel[:, 2 : inner + 2, :, 0]
    tall = jnp.stack([even, odd], 2)
    wide = jnp.pad(tall, ((0, 0), (0, 0), (0, 0), (1, 1), (0, 0), (0, 0)))
    left_cols = wide[:, :, :, 1 : cols + 1, 1] + wide[:, :, :, 0:cols, 3]
    right_cols = wide[:, :, :, 1 : cols + 1, 2] + wide[:, :, :, 2 : cols + 2, 0]
    return jnp.stack([left_cols, right_cols], 4).reshape(planes, 2 * inner, 2 * cols, -1)


PAIR = 2 * HEAD_DIM
BRIEF = pl.CostEstimate(flops=1000000, transcendentals=0, bytes_accessed=100000)
LOG2E = math.log2(math.e)
EXP_SCALE = HEAD_DIM ** (-0.5) * LOG2E


def nt_dot(left, right):
    return lax.dot_general(left, right, (((1,), (1,)), ((), ())), preferred_element_type=jnp.float32)


def head_lanes(shape, head):
    return lax.broadcasted_iota(jnp.int32, shape, len(shape) - 1) // HEAD_DIM == head


def joined(refs, n):
    parts = [ref[n] for ref in refs]
    return parts[0] if len(parts) == 1 else jnp.concatenate(parts, 0)


def attend_fwd_kernel(real_keys, sources, q_ref, *refs):
    o_ref, lse_ref = refs[-2:]
    query, keys = q_ref[...], joined(refs[:sources], 0)
    values = joined(refs[:sources], 1).T
    outs = []
    for head in range(2):
        own = jnp.where(head_lanes(query.shape, head), query, 0)
        scores = nt_dot(keys, own)
        if real_keys < keys.shape[0]:
            at = lax.broadcasted_iota(jnp.int32, scores.shape, 0)
            scores = jnp.where(at < real_keys, scores, -3e38)
        top = jnp.max(scores, 0, keepdims=True)
        raised = jnp.exp2((scores - top) * EXP_SCALE)
        total = jnp.sum(raised, 0, keepdims=True)
        shares = (raised * (1.0 / total)).astype(jnp.bfloat16)
        outs.append(product(values[head * HEAD_DIM : (head + 1) * HEAD_DIM], shares))
        lse_ref[0, head : head + 1] = top * EXP_SCALE + jnp.log2(total)
    o_ref[...] = jnp.concatenate(outs, 0).T.astype(jnp.bfloat16)


def attend_fwd(query, sources, real_keys, span, earlier=()):
    count = query.shape[0]
    total_keys = sum(source.shape[1] for source in sources)
    low, high = span
    by_pair = pl.BlockSpec((count, PAIR), lambda j: (0, low + j))
    work = count * total_keys * (high - low) * PAIR
    return pl.pallas_call(
        functools.partial(attend_fwd_kernel, real_keys, len(sources)),
        grid=(high - low,),
        in_specs=[by_pair]
        + [pl.BlockSpec((2, source.shape[1], PAIR), lambda j: (0, 0, low + j)) for source in sources]
        + [pl.BlockSpec(memory_space=pl.ANY)] * len(earlier),
        out_specs=[by_pair, pl.BlockSpec((1, 8, count), lambda j: (low + j, 0, 0))],
        out_shape=[
            jax.ShapeDtypeStruct((count, D), jnp.bfloat16),
            jax.ShapeDtypeStruct((D // PAIR, 8, count), jnp.float32),
        ],
        input_output_aliases={1 + len(sources) + n: n for n in range(len(earlier))},
        compiler_params=pltpu.CompilerParams(vmem_limit_bytes=48 * 1024 * 1024),
        cost_estimate=BRIEF,
        name="attend_fwd",
    )(query, *sources, *earlier)


def attend_bwd_kernel(real_keys, chunk, sources, extra, q_ref, *refs):
    kv_refs = refs[:sources]
    lse_ref, o_ref, g_ref = refs[sources : sources + 3]
    dq_ref, *grad_refs = refs[sources + 3 + extra : sources + 4 + extra + sources]
    k_all, v_all, kt_ref, dk_sum, dv_sum = refs[sources + 4 + extra + sources :]
    k_all[...] = joined(kv_refs, 0)
    v_all[...] = joined(kv_refs, 1)
    kt_ref[...] = k_all[...].T
    query, grad = q_ref[...], g_ref[...]
    mixed = (grad.astype(jnp.float32) * o_ref[...].astype(jnp.float32)).T
    total_keys = k_all.shape[0]
    queries = [jnp.where(head_lanes(query.shape, head), query, 0) for head in range(2)]
    grads = [jnp.where(head_lanes(grad.shape, head), grad, 0) for head in range(2)]
    inner = [jnp.sum(mixed[head * HEAD_DIM : (head + 1) * HEAD_DIM], 0, keepdims=True) for head in range(2)]
    grad_query = [jnp.zeros((HEAD_DIM, query.shape[0]), jnp.float32) for head in range(2)]
    for at in range(0, total_keys, chunk):
        part = pl.ds(at, chunk)
        keys, values = k_all[part], v_all[part]
        for head in range(2):
            scores = nt_dot(keys, queries[head])
            shares = jnp.exp2(scores * EXP_SCALE - lse_ref[0, head : head + 1])
            if at + chunk > real_keys:
                row = at + lax.broadcasted_iota(jnp.int32, shares.shape, 0)
                shares = jnp.where(row < real_keys, shares, 0.0)
            grad_shares = nt_dot(values, grads[head])
            grad_scores = (shares * (grad_shares - inner[head])).astype(jnp.bfloat16)
            to_values = product(shares.astype(jnp.bfloat16), grads[head])
            to_keys = product(grad_scores, queries[head])
            if head == 0:
                dv_sum[part] = to_values
                dk_sum[part] = to_keys
            else:
                dv_sum[part] += to_values
                dk_sum[part] += to_keys
            grad_query[head] += product(
                kt_ref[head * HEAD_DIM : (head + 1) * HEAD_DIM, part], grad_scores
            )
    scale = HEAD_DIM ** (-0.5)
    dq_ref[...] = (jnp.concatenate(grad_query, 0) * scale).T.astype(jnp.bfloat16)
    start = 0
    for ref in grad_refs:
        part = pl.ds(start, ref.shape[1])
        ref[0] = (dk_sum[part] * scale).astype(jnp.bfloat16)
        ref[1] = dv_sum[part].astype(jnp.bfloat16)
        start += ref.shape[1]


def attend_bwd(query, sources, real_keys, span, chunk, totals, out, grad, earlier=()):
    count = query.shape[0]
    total_keys = sum(source.shape[1] for source in sources)
    low, high = span
    by_pair = pl.BlockSpec((count, PAIR), lambda j: (0, low + j))
    by_source = [pl.BlockSpec((2, source.shape[1], PAIR), lambda j: (0, 0, low + j)) for source in sources]
    first = 1 + len(sources) + 3
    work = count * total_keys * (high - low) * PAIR
    return pl.pallas_call(
        functools.partial(attend_bwd_kernel, real_keys, chunk, len(sources), len(earlier)),
        grid=(high - low,),
        in_specs=[by_pair]
        + by_source
        + [pl.BlockSpec((1, 8, count), lambda j: (low + j, 0, 0)), by_pair, by_pair]
        + [pl.BlockSpec(memory_space=pl.ANY)] * len(earlier),
        out_specs=[by_pair] + by_source,
        out_shape=[jax.ShapeDtypeStruct((count, D), jnp.bfloat16)]
        + [jax.ShapeDtypeStruct(source.shape, jnp.bfloat16) for source in sources],
        input_output_aliases={first + n: n for n in range(len(earlier))},
        scratch_shapes=[
            pltpu.VMEM((total_keys, PAIR), jnp.bfloat16),
            pltpu.VMEM((total_keys, PAIR), jnp.bfloat16),
            pltpu.VMEM((PAIR, total_keys), jnp.bfloat16),
            pltpu.VMEM((total_keys, PAIR), jnp.float32),
            pltpu.VMEM((total_keys, PAIR), jnp.float32),
        ],
        compiler_params=pltpu.CompilerParams(vmem_limit_bytes=48 * 1024 * 1024),
        cost_estimate=BRIEF,
        name="attend_bwd",
    )(query, *sources, totals, out, grad, *earlier)


GROUPS = 3


def render_kernel(samples_ref, near_ref, far_ref, wanted_ref, mask_ref, factor_ref, win_ref, wout_ref,
                  loss_ref, grad_ref, grad_far_ref, gin_ref, gout_ref,
                  table, inner_all, hidden_all, point_all, out_all, gout_all, sums):
    block = pl.program_id(0)
    half = near_ref.shape[1]
    cells = 2 * half
    group = table.shape[2]
    rays = samples_ref.shape[2]
    planes = near_ref.shape[0]

    @pl.when(block == 0)
    def _():
        loss_ref[...] = jnp.zeros_like(loss_ref)
        gin_ref[...] = jnp.zeros_like(gin_ref)
        gout_ref[...] = jnp.zeros_like(gout_ref)
        sums[...] = jnp.zeros_like(sums)
        table[...] = jnp.zeros_like(table)
        for plane in range(planes):
            turned = jnp.concatenate([near_ref[plane], far_ref[plane]], 0).T
            for g in range(GROUPS):
                width = min(group, cells - g * group)
                table[plane, g * CH : (g + 1) * CH, :width] = turned[:CH, g * group : g * group + width]

    step = 4
    width = step * rays
    win, wout = win_ref[...], wout_ref[...]

    def places_read(plane, s):
        rows = [samples_ref[plane, s + n : s + n + 1, :] for n in range(step)]
        at = jnp.concatenate(rows, 1)
        owner = at // group
        within = at - owner * group
        hot = lax.broadcasted_iota(jnp.int32, (group, width), 0) == within
        return owner, jnp.where(hot, 1.0, 0.0).astype(jnp.bfloat16)

    def tn_dot(left, right):
        return lax.dot_general(left, right, (((0,), (0,)), ((), ())), preferred_element_type=jnp.float32)

    for s in range(0, S, step):
        here = pl.ds(s * rays, width)
        point = jnp.zeros((CH, width), jnp.float32)
        for plane in range(planes):
            owner, hot = places_read(plane, s)
            found = product(table[plane], hot)
            value = found[:CH]
            for g in range(1, GROUPS):
                value = jnp.where(owner == g, found[g * CH : (g + 1) * CH], value)
            point = point + value
        point = point.astype(jnp.bfloat16)
        inner = tn_dot(win, point)
        hidden = (inner * jax.nn.sigmoid(inner)).astype(jnp.bfloat16)
        out_all[:, here] = tn_dot(wout, hidden)
        inner_all[:, here] = inner
        hidden_all[:, here] = hidden
        point_all[:, here] = point

    factor = factor_ref[0]
    mask = mask_ref[...]
    row = lax.broadcasted_iota(jnp.int32, (8, rays), 0)
    is_colour = (row >= 1) & (row <= 3)
    before = jnp.zeros((1, rays), jnp.float32)
    rgb = jnp.zeros((8, rays), jnp.float32)
    kept = []
    for s in range(S):
        out = out_all[:, s * rays : (s + 1) * rays]
        level = out[0:1]
        absorb = (4.0 / S) * (jnp.maximum(level, 0.0) + jnp.log1p(jnp.exp(-jnp.abs(level))))
        weight = jnp.exp(-before) * (1.0 - jnp.exp(-absorb))
        before = before + absorb
        colour = jax.nn.sigmoid(out)
        rgb = rgb + weight * colour
        kept.append((weight, jnp.exp(-before), colour))
    error = jnp.where(is_colour, rgb - wanted_ref[...], 0.0)
    loss_ref[...] += jnp.sum(mask * jnp.sum(error * error, 0, keepdims=True))
    pull = error * (2.0 * factor * mask)
    tail = jnp.zeros((1, rays), jnp.float32)
    for s in reversed(range(S)):
        weight, left_over, colour = kept[s]
        to_weight = jnp.sum(pull * colour, 0, keepdims=True)
        to_absorb = to_weight * left_over - tail
        tail = tail + to_weight * weight
        to_level = (4.0 / S) * to_absorb * colour[0:1]
        to_colour = weight * pull * colour * (1.0 - colour)
        gout_all[:, s * rays : (s + 1) * rays] = jnp.where(row == 0, to_level, to_colour).astype(jnp.bfloat16)

    for s in range(0, S, step):
        here = pl.ds(s * rays, width)
        pulled = gout_all[:, here]
        inner = inner_all[:, here]
        gate = jax.nn.sigmoid(inner)
        grad_inner = product(wout, pulled) * (gate * (1.0 + inner * (1.0 - gate)))
        grad_inner = grad_inner.astype(jnp.bfloat16)
        gout_ref[...] += nt_dot(hidden_all[:, here], pulled)
        gin_ref[...] += nt_dot(point_all[:, here], grad_inner)
        grad_point = product(win, grad_inner)
        coarse = grad_point.astype(jnp.bfloat16).astype(jnp.float32)
        fine = grad_point - coarse
        for plane in range(planes):
            owner, hot = places_read(plane, s)
            rows = [jnp.where(owner == g, coarse, 0.0) for g in range(GROUPS)]
            rows += [jnp.where(owner == g, fine, 0.0) for g in range(GROUPS)]
            stacked = jnp.concatenate(rows, 0).astype(jnp.bfloat16)
            added = nt_dot(stacked, hot)
            sums[plane] += added[: GROUPS * CH] + added[GROUPS * CH :]

    @pl.when(block == pl.num_programs(0) - 1)
    def _():
        for plane in range(planes):
            for g in range(GROUPS):
                for low, high, ref in ((0, half, grad_ref), (half, cells, grad_far_ref)):
                    start, stop = max(g * group, low), min((g + 1) * group, high)
                    if start < stop:
                        part = sums[plane, g * CH : (g + 1) * CH, start - g * group : stop - g * group]
                        ref[plane, :, start - low : stop - low] = part.astype(jnp.bfloat16)


def render(near, far, samples, wanted, mask, factor, decode_in, decode_out, rays):
    planes, half, _ = near.shape
    count = 2 * half
    all_rays = samples.shape[2]
    group = -(-count // (GROUPS * 128)) * 128
    points = S * rays
    whole = lambda *shape: pl.BlockSpec(shape, lambda n: (0,) * len(shape))
    return pl.pallas_call(
        render_kernel,
        grid=(all_rays // rays,),
        in_specs=[
            pl.BlockSpec((planes, S, rays), lambda n: (0, 0, n)),
            whole(*near.shape),
            whole(*far.shape),
            pl.BlockSpec((8, rays), lambda n: (0, n)),
            pl.BlockSpec((1, rays), lambda n: (0, n)),
            pl.BlockSpec(memory_space=pltpu.SMEM),
            whole(CH, DEC_HID),
            whole(DEC_HID, 8),
        ],
        out_specs=[whole(8, 128), whole(planes, CH, half), whole(planes, CH, half), whole(CH, DEC_HID), whole(DEC_HID, 8)],
        out_shape=[
            jax.ShapeDtypeStruct((8, 128), jnp.float32),
            jax.ShapeDtypeStruct((planes, CH, half), jnp.bfloat16),
            jax.ShapeDtypeStruct((planes, CH, half), jnp.bfloat16),
            jax.ShapeDtypeStruct((CH, DEC_HID), jnp.float32),
            jax.ShapeDtypeStruct((DEC_HID, 8), jnp.float32),
        ],
        scratch_shapes=[
            pltpu.VMEM((planes, GROUPS * CH, group), jnp.bfloat16),
            pltpu.VMEM((DEC_HID, points), jnp.float32),
            pltpu.VMEM((DEC_HID, points), jnp.bfloat16),
            pltpu.VMEM((CH, points), jnp.bfloat16),
            pltpu.VMEM((8, points), jnp.float32),
            pltpu.VMEM((8, points), jnp.bfloat16),
            pltpu.VMEM((planes, GROUPS * CH, group), jnp.float32),
        ],
        compiler_params=pltpu.CompilerParams(vmem_limit_bytes=48 * 1024 * 1024),
        name="render",
    )(samples, near, far, wanted, mask, factor, decode_in, decode_out)


MESH_ID = pl.DeviceIdType.MESH


def places():
    p = lax.axis_index("dp")
    c = lax.axis_index("strip")
    z = p // 4
    flip_x = p + 1 - 2 * (p % 2)
    flip_y = p + 2 - 4 * ((p // 2) % 2)
    both = flip_x + flip_y - p
    near = (1 - c) * flip_x + c * flip_y
    far = (1 - c) * flip_y + c * flip_x
    return p, c, z, near, far, both


def along_z(line, z, k):
    return ((z + k) % 4) * 4 + line % 4


def enter(peers):
    barrier = pltpu.get_barrier_semaphore()
    for peer in peers:
        pl.semaphore_signal(barrier, inc=1, device_id=peer, device_id_type=MESH_ID)
    pl.semaphore_wait(barrier, len(peers))


def flat_chunks(rows, n):
    part = rows // n
    return n, part, lambda p, c, j: (2 * p + c) * rows + j * part


def block_chunk(p, c, k):
    second = p // 8
    return ((1 - second) * ((2 * c + k) * 8 + p) + second * (4 * p + 2 * c + k)) * BLOCK


ORDER = [("near", 0), ("z", 1), ("z", 3), ("far", 0), ("z", 2), ("near", 1), ("near", 3), ("near", 2)]
ORDER += [("both", 0), ("far", 1), ("far", 3), ("far", 2), ("both", 1), ("both", 3), ("both", 2)]
ORDER += [("core", i) for i in range(16)]

def gather_kernel(layouts, stagger, *refs):
    count = len(layouts)
    fulls = refs[count + 1 : 2 * count + 1]
    line_full = refs[2 * count + 1]
    send, recv, local, line_sems = refs[2 * count + 2 : 2 * count + 6]
    held = refs[2 * count + 6 :]
    brought = [pltpu.make_async_copy(s, h, local.at[n]) for n, (s, h) in enumerate(zip(refs[: count + 1], held))]
    for copy in brought:
        copy.start()
    sources, line_source = held[:count], held[count]
    p, c, z, near, far, both = places()
    zs = [along_z(p, z, k) for k in range(4)]
    enter([(q, c) for q in zs[1:]] + [(near, c), (far, c), (p, 1 - c)])
    for copy in brought:
        copy.wait()
    jobs = [(a, j) for a, layout in enumerate(layouts) for j in range(layout[0])]

    def target(owner, job):
        a, j = jobs[job]
        _, rows, place = layouts[a]
        return fulls[a].at[pl.ds(pl.multiple_of(place(*owner, j), 8), rows)]

    def source(job):
        a, j = jobs[job]
        rows = layouts[a][1]
        return sources[a].at[pl.ds(j * rows, rows)]

    started = []

    def forward(owner, own, event, peer, job):
        t = target(owner, job)
        copy = pltpu.make_async_remote_copy(
            source(job) if own else t, t, send.at[event, job], recv.at[event, job], device_id=peer, device_id_type=MESH_ID
        )
        copy.start()
        started.append(copy)

    def arrive(owner, event, job):
        t = target(owner, job)
        pltpu.make_async_remote_copy(
            t, t, send.at[event, job], recv.at[event, job], device_id=(p, 1 - c), device_id_type=MESH_ID
        ).wait_recv()

    me = (p, c)

    def begin(job):
        forward(me, True, 3, (near, c), job)
        for k in (1, 3, 2):
            forward(me, True, 3 - k, (zs[k], c), job)
        forward(me, True, 7, (far, c), job)
        forward(me, True, 15, (p, 1 - c), job)
        pltpu.make_async_copy(source(job), target(me, job), local.at[job]).start()

    def take(kind, k, job):
        if kind == "z":
            owner = (zs[k], c)
            arrive(owner, k - 1, job)
            forward(owner, False, 3 + k, (near, c), job)
            forward(owner, False, 7 + k, (far, c), job)
            forward(owner, False, 15 + k, (p, 1 - c), job)
        elif kind == "near":
            owner = (along_z(near, z, k), c)
            arrive(owner, 3 + k, job)
            forward(owner, False, 11 + k, (far, c), job)
            forward(owner, False, 19 + k, (p, 1 - c), job)
        elif kind == "far":
            owner = (along_z(far, z, k), c)
            arrive(owner, 7 + k, job)
            forward(owner, False, 23 + k, (p, 1 - c), job)
        elif kind == "both":
            owner = (along_z(both, z, k), c)
            arrive(owner, 11 + k, job)
            forward(owner, False, 27 + k, (p, 1 - c), job)
        elif kind == "core":
            line = (p, far, near, both)[k // 4]
            arrive((along_z(line, z, k % 4), 1 - c), 15 + k, job)

    lines = []
    for k in (1, 3, 2):
        lines.append(
            pltpu.make_async_remote_copy(
                line_source, line_full.at[4 - k], line_sems.at[k], line_sems.at[7 - k],
                device_id=(zs[k], c), device_id_type=MESH_ID,
            )
        )
    lines.append(pltpu.make_async_copy(line_source, line_full.at[0], line_sems.at[0]))

    steps = [(stagger * len(jobs) - 4, -2, 0)]
    for job in range(len(jobs)):
        steps.append((stagger * job, -1, job))
        for i in range(len(ORDER)):
            steps.append((stagger * job + i + 1, i, job))
    for _, i, job in sorted(steps):
        if i == -2:
            for copy in lines:
                copy.start()
        elif i < 0:
            begin(job)
        else:
            take(*ORDER[i], job)
    for k in (1, 2, 3):
        spot = line_full.at[k]
        pltpu.make_async_remote_copy(
            spot, spot, line_sems.at[k], line_sems.at[3 + k], device_id=(p, 1 - c), device_id_type=MESH_ID
        ).wait_recv()
    for copy in lines[:3]:
        copy.wait_send()
    lines[3].wait()
    for copy in started:
        copy.wait_send()
    for job in range(len(jobs)):
        pltpu.make_async_copy(source(job), target(me, job), local.at[job]).wait()


def gather_all(layouts, stagger, shards_in, line, name_id):
    copies = sum(l[0] for l in layouts)
    everywhere = pl.BlockSpec(memory_space=pl.ANY)
    shapes = [jax.ShapeDtypeStruct((32 * s.shape[0],) + s.shape[1:], s.dtype) for s in shards_in]
    shapes.append(jax.ShapeDtypeStruct((4,) + line.shape, line.dtype))
    return pl.pallas_call(
        functools.partial(gather_kernel, layouts, stagger),
        out_shape=shapes,
        in_specs=[everywhere] * len(shapes),
        out_specs=[everywhere] * len(shapes),
        scratch_shapes=[
            pltpu.SemaphoreType.DMA((31, copies)),
            pltpu.SemaphoreType.DMA((31, copies)),
            pltpu.SemaphoreType.DMA((copies,)),
            pltpu.SemaphoreType.DMA((7,)),
        ]
        + [pltpu.VMEM(a.shape, a.dtype) for a in (*shards_in, line)],
        compiler_params=pltpu.CompilerParams(collective_id=name_id, has_side_effects=True),
        name="gather_all",
    )(*shards_in, line)


SUM_ORDER = [(3, 0), (3, 1), (3, 3), (3, 2), (2, 0), (2, 1), (2, 3), (2, 2)]
SUM_ORDER += [(1, 1), (1, 3), (1, 2), (1, 0), (0, 1), (0, 3), (0, 2), (0, 0)]
AHEAD = 3


def scatter_kernel(layouts, stagger, *refs):
    count = len(layouts)
    grads = refs[:count]
    line_grad = refs[count]
    outs = refs[count + 1 : 2 * count + 1]
    line_out = refs[2 * count + 1]
    scratch = refs[2 * count + 2 :]
    line_own, line_got, line_sum, line_sems = scratch[-4:]
    p, c, z, near, far, both = places()
    zs = [along_z(p, z, k) for k in range(4)]
    enter([(q, c) for q in zs[1:]] + [(near, c), (far, c), (p, 1 - c)])
    csend, crecv, bsend, brecv, load_sem, out_sem = scratch[:6]
    buffers = [scratch[6 + 6 * a : 12 + 6 * a] for a in range(count)]
    jobs = [(a, j) for a, layout in enumerate(layouts) for j in range(layout[0])]
    lines = (p, near, far, both)
    partner_lines = (p, far, near, both)

    def view(job, ref, slot):
        a, j = jobs[job]
        rows = layouts[a][1]
        return ref.at[slot, pl.ds(j * rows, rows)]

    def piece(owner, job):
        a, j = jobs[job]
        _, rows, place = layouts[a]
        return grads[a].at[pl.ds(pl.multiple_of(place(*owner, j), 8), rows)]

    def to_core(i, job):
        g, k = SUM_ORDER[i]
        owner = (along_z(partner_lines[g], z, k), 1 - c)
        rc = buffers[jobs[job][0]][0]
        return pltpu.make_async_remote_copy(
            piece(owner, job), view(job, rc, g * 4 + k), csend.at[i, job], crecv.at[i, job],
            device_id=(p, 1 - c), device_id_type=MESH_ID,
        )

    def load(i, job):
        g, k = SUM_ORDER[i]
        own = buffers[jobs[job][0]][4]
        return pltpu.make_async_copy(
            piece((along_z(lines[g], z, k), c), job), view(job, own, i % AHEAD), load_sem.at[i, job]
        )

    def onward(i, job):
        g, k = SUM_ORDER[i]
        rc, rb, ra, rz = buffers[jobs[job][0]][:4]
        if g == 3:
            target, event, peer = view(job, rb, 4 + k), 4 + k, (far, c)
        elif g == 2:
            target, event, peer = view(job, rb, k), k, (far, c)
        elif g == 1:
            target, event, peer = view(job, ra, k), 8 + k, (near, c)
        else:
            target, event, peer = view(job, rz, 3 - k), 12 + 3 - k, (zs[k], c)
        return pltpu.make_async_remote_copy(
            view(job, rc, g * 4 + k), target, bsend.at[event, job], brecv.at[event, job],
            device_id=peer, device_id_type=MESH_ID,
        )

    def landed(event, job):
        rc, rb, ra, rz = buffers[jobs[job][0]][:4]
        if event < 8:
            target = view(job, rb, event)
        elif event < 12:
            target = view(job, ra, event - 8)
        else:
            target = view(job, rz, event - 12)
        pltpu.make_async_remote_copy(
            target, target, bsend.at[event, job], brecv.at[event, job], device_id=(p, 1 - c), device_id_type=MESH_ID
        ).wait_recv()
        return target

    def add_up(parts, target):
        rows = target.shape[0]
        step = math.gcd(rows, 16)

        @pl.loop(0, rows // step)
        def _(n):
            at = pl.ds(pl.multiple_of(n * step, step), step)
            total = parts[0][at].astype(jnp.float32)
            for part in parts[1:]:
                total = total + part[at].astype(jnp.float32)
            target[at] = total.astype(target.dtype)

    def start(i, job):
        to_core(i, job).start()
        load(i, job).start()

    def final_copies(job):
        a, j = jobs[job]
        rows = layouts[a][1]
        return [pltpu.make_async_copy(view(job, buffers[a][5], 0), outs[a].at[pl.ds(j * rows, rows)], out_sem.at[job, 0])]

    line_sends = [
        pltpu.make_async_remote_copy(
            line_grad.at[k], line_got.at[3 - k], line_sems.at[k], line_sems.at[7 - k],
            device_id=(zs[k], c), device_id_type=MESH_ID,
        )
        for k in (1, 3, 2)
    ]
    line_load = pltpu.make_async_copy(line_grad.at[0], line_own, line_sems.at[0])
    half = line_own.shape[0]
    spot = line_out.at[pl.ds(pl.multiple_of(c * half, 8), half)]
    line_stores = [
        pltpu.make_async_copy(line_sum, spot, line_sems.at[7]),
        pltpu.make_async_remote_copy(
            line_sum, spot, line_sems.at[8], line_sems.at[9], device_id=(p, 1 - c), device_id_type=MESH_ID
        ),
    ]

    def line_finish():
        line_load.wait()
        for k in (1, 2, 3):
            target = line_got.at[k - 1]
            pltpu.make_async_remote_copy(
                target, target, line_sems.at[k], line_sems.at[3 + k], device_id=(p, 1 - c), device_id_type=MESH_ID
            ).wait_recv()
        add_up([line_own] + [line_got.at[n] for n in range(3)], line_sum)
        for copy in line_stores:
            copy.start()

    def step(i, job):
        g, k = SUM_ORDER[i]
        rc, rb, ra, rz, own, done = buffers[jobs[job][0]]
        load(i, job).wait()
        to_core(i, job).wait_recv()
        here = view(job, rc, g * 4 + k)
        parts = [here, view(job, own, i % AHEAD)]
        if g == 1:
            parts.append(landed(4 + k, job))
        if g == 0:
            parts.append(landed(k, job))
            parts.append(landed(8 + k, job))
        if (g, k) == (0, 0):
            parts += [landed(12 + n, job) for n in range(3)]
            add_up(parts, view(job, done, 0))
            for copy in final_copies(job):
                copy.start()
        else:
            add_up(parts, here)
            onward(i, job).start()
        if i + AHEAD < 16:
            start(i + AHEAD, job)

    for copy in line_sends:
        copy.start()
    line_load.start()
    steps = [(stagger * (len(jobs) - 1) + 11, -1, -2)]
    for job in range(len(jobs)):
        for i in range(-1, 16):
            steps.append((stagger * job + i, job, i))
    for _, job, i in sorted(steps):
        if i == -2:
            line_finish()
        elif i < 0:
            for n in range(AHEAD):
                start(n, job)
        else:
            step(i, job)
    for job in range(len(jobs)):
        for i in range(16):
            to_core(i, job).wait_send()
            if i < 15:
                onward(i, job).wait_send()
        for copy in final_copies(job):
            copy.wait()
    for copy in line_sends:
        copy.wait_send()
    for copy in line_stores:
        copy.wait()


def scatter_sum(layouts, stagger, grads, line, name_id):
    jobs = sum(l[0] for l in layouts)
    scratch = [
        pltpu.SemaphoreType.DMA((16, jobs)),
        pltpu.SemaphoreType.DMA((16, jobs)),
        pltpu.SemaphoreType.DMA((15, jobs)),
        pltpu.SemaphoreType.DMA((15, jobs)),
        pltpu.SemaphoreType.DMA((16, jobs)),
        pltpu.SemaphoreType.DMA((jobs, 3)),
    ]
    shapes = []
    for layout, grad in zip(layouts, grads):
        rows, width = layout[0] * layout[1], grad.shape[1]
        for slots in (16, 8, 4, 3, AHEAD):
            scratch.append(pltpu.VMEM((slots, rows, width), grad.dtype))
        scratch.append(pltpu.VMEM((1, rows, width), jnp.float32))
        shapes.append(jax.ShapeDtypeStruct((rows, width), jnp.float32))
    piece = line.shape[1:]
    scratch += [pltpu.VMEM(piece, line.dtype), pltpu.VMEM((3,) + piece, line.dtype), pltpu.VMEM(piece, line.dtype)]
    scratch.append(pltpu.SemaphoreType.DMA((10,)))
    shapes.append(jax.ShapeDtypeStruct((2 * piece[0], piece[1]), line.dtype))
    everywhere = pl.BlockSpec(memory_space=pl.ANY)
    return pl.pallas_call(
        functools.partial(scatter_kernel, layouts, stagger),
        out_shape=shapes,
        in_specs=[everywhere] * len(shapes),
        out_specs=[everywhere] * len(shapes),
        scratch_shapes=scratch,
        compiler_params=pltpu.CompilerParams(
            collective_id=name_id, has_side_effects=True, vmem_limit_bytes=48 * 1024 * 1024
        ),
        name="scatter_sum",
    )(*grads, line)


GELU_A = math.sqrt(2.0 / math.pi)
GELU_B = 0.044715


def chunk_sources():
    p, c, z, _, _, _ = places()
    x, y = p % 2, (p // 2) % 2
    out = []
    for other in range(2):
        core = (c + other) % 2
        for g in range(4):
            dx = (1 - core) * (g % 2) + core * (g // 2)
            dy = (1 - core) * (g // 2) + core * (g % 2)
            for k in range(4):
                owner = ((z + k) % 4) * 4 + ((y + dy) % 2) * 2 + (x + dx) % 2
                for half in range(2):
                    out.append((other, g, k, half, block_chunk(owner, core, half) // BLOCK))
    return out


def panel_loads(refs, held, sems):
    if len(refs) == 1:
        for n in range(held.shape[0] // WIDE):
            at = pl.ds(n * WIDE, WIDE)
            pltpu.make_async_copy(refs[0].at[at], held.at[at], sems.at[n]).start()
        return
    for other, g, k, half, chunk in chunk_sources():
        source = refs[other * 4 + g].at[k, pl.ds(half * BLOCK, BLOCK)]
        target = held.at[pl.ds(pl.multiple_of(chunk * BLOCK, BLOCK), BLOCK)]
        pltpu.make_async_copy(source, target, sems.at[chunk // 8]).start()


def panel_ready(held, sems, n):
    at = pl.ds(pl.multiple_of(n * WIDE, WIDE), WIDE)
    pltpu.make_async_copy(held.at[at], held.at[at], sems.at[n]).wait()
    return held.at[at]


def mlp_fwd_kernel(count, *refs):
    sources = refs[:count]
    h_ref, s_ref, up_ref, act_ref, grid_ref, held, total, sems = refs[count:]
    step = pl.program_id(0)
    steps = pl.num_programs(0)

    @pl.when(step == 0)
    def _():
        panel_loads(sources, held, sems)
        total[...] = s_ref[...]

    up = product(h_ref[...], panel_ready(held, sems, step)[...])
    up_ref[0] = up
    act = 0.5 * up * (1.0 + jnp.tanh(GELU_A * (up + GELU_B * up * up * up)))
    act = act.astype(jnp.bfloat16)
    act_ref[0] = act
    total[...] += product(act, panel_ready(held, sems, steps + step)[...])

    @pl.when(step == steps - 1)
    def _():
        grid_ref[...] = total[...].astype(jnp.bfloat16)


def mlp_fwd(panels, hidden, stream):
    rows = hidden.shape[0]
    steps = HID // WIDE
    whole = pl.BlockSpec((rows, WIDE), lambda n: (0, 0))
    part = pl.BlockSpec((1, rows, WIDE), lambda n: (n, 0, 0))
    return pl.pallas_call(
        functools.partial(mlp_fwd_kernel, len(panels)),
        grid=(steps,),
        in_specs=[pl.BlockSpec(memory_space=pl.ANY)] * len(panels) + [whole, whole],
        out_specs=[part, part, whole],
        out_shape=[
            jax.ShapeDtypeStruct((steps, rows, WIDE), jnp.float32),
            jax.ShapeDtypeStruct((steps, rows, WIDE), jnp.bfloat16),
            jax.ShapeDtypeStruct((rows, WIDE), jnp.bfloat16),
        ],
        scratch_shapes=[
            pltpu.VMEM((2 * HID, WIDE), jnp.bfloat16),
            pltpu.VMEM((rows, WIDE), jnp.float32),
            pltpu.SemaphoreType.DMA((2 * steps,)),
        ],
        compiler_params=pltpu.CompilerParams(vmem_limit_bytes=56 * 1024 * 1024),
        cost_estimate=BRIEF,
        name="mlp_fwd",
    )(*panels, hidden, stream)


def mlp_bwd_kernel(count, *refs):
    sources = refs[:count]
    outs = 2 if count > 1 else 1
    h_ref, g_ref, up_ref, act_ref = refs[count : count + 4]
    dh_ref = refs[count + 4]
    grads = refs[count + 5 : count + 5 + outs]
    held, staged, sems, out_sem = refs[count + 5 + outs :]
    step = pl.program_id(0)
    steps = pl.num_programs(0)

    @pl.when(step == 0)
    def _():
        panel_loads(sources, held, sems)
        dh_ref[...] = jnp.zeros_like(dh_ref)

    def tn_dot(left, right):
        return lax.dot_general(left, right, (((0,), (0,)), ((), ())), preferred_element_type=jnp.float32)

    def drain(side):
        pltpu.make_async_copy(staged.at[side], staged.at[side], out_sem.at[side]).wait()

    def store(side):
        panel = side * steps + step
        source = staged.at[side]
        if count == 1:
            at = pl.ds(pl.multiple_of(panel * WIDE, WIDE), WIDE)
            pltpu.make_async_copy(source, grads[0].at[at], out_sem.at[side]).start()
            return
        p, c, z, _, _, _ = places()
        for n in range(8):
            if side == 0:
                owner, core, half = n, step // 2, step % 2
            else:
                row = step * 8 + n
                owner, core, half = 8 + row // 4, (n // 2) % 2, n % 2
            dx = (owner % 2 + p % 2) % 2
            dy = ((owner // 2) % 2 + (p // 2) % 2) % 2
            g = (1 - core) * (dx + 2 * dy) + core * (dy + 2 * dx)
            spot = g * 4 + (owner // 4 - z + 4) % 4
            at = pl.ds(pl.multiple_of(half * BLOCK, BLOCK), BLOCK)
            from_ref = source.at[pl.ds(n * BLOCK, BLOCK)]

            @pl.when((core + c) % 2 == 0)
            def _():
                pltpu.make_async_copy(from_ref, grads[0].at[spot, at], out_sem.at[side]).start()

            @pl.when((core + c) % 2 == 1)
            def _():
                pltpu.make_async_copy(from_ref, grads[1].at[spot, at], out_sem.at[side]).start()

    pulled = g_ref[...]

    @pl.when(step > 0)
    def _():
        drain(1)

    staged[1] = tn_dot(act_ref[0], pulled).astype(jnp.bfloat16)
    store(1)
    grad_act = nt_dot(pulled, panel_ready(held, sems, steps + step)[...])
    up = up_ref[0]
    square = up * up
    bend = jnp.tanh(GELU_A * up * (1.0 + GELU_B * square))
    slope = 0.5 * (1.0 + bend) + 0.5 * GELU_A * up * (1.0 - bend * bend) * (1.0 + 3.0 * GELU_B * square)
    grad_up = (grad_act * slope).astype(jnp.bfloat16)

    @pl.when(step > 0)
    def _():
        drain(0)

    staged[0] = tn_dot(h_ref[...], grad_up).astype(jnp.bfloat16)
    store(0)
    dh_ref[...] += nt_dot(grad_up, panel_ready(held, sems, step)[...])

    @pl.when(step == steps - 1)
    def _():
        drain(0)
        drain(1)


def mlp_bwd(panels, hidden, grad, up, act):
    rows = hidden.shape[0]
    steps = HID // WIDE
    whole = pl.BlockSpec((rows, WIDE), lambda n: (0, 0))
    part = pl.BlockSpec((1, rows, WIDE), lambda n: (n, 0, 0))
    if len(panels) == 1:
        shapes = [jax.ShapeDtypeStruct((2 * HID, WIDE), jnp.bfloat16)]
    else:
        shapes = [jax.ShapeDtypeStruct((16, 2 * BLOCK, WIDE), jnp.bfloat16)] * 2
    return pl.pallas_call(
        functools.partial(mlp_bwd_kernel, len(panels)),
        grid=(steps,),
        in_specs=[pl.BlockSpec(memory_space=pl.ANY)] * len(panels) + [whole, whole, part, part],
        out_specs=[whole] + [pl.BlockSpec(memory_space=pl.ANY)] * len(shapes),
        out_shape=[jax.ShapeDtypeStruct((rows, WIDE), jnp.float32)] + shapes,
        scratch_shapes=[
            pltpu.VMEM((2 * HID, WIDE), jnp.bfloat16),
            pltpu.VMEM((2, WIDE, WIDE), jnp.bfloat16),
            pltpu.SemaphoreType.DMA((2 * steps,)),
            pltpu.SemaphoreType.DMA((2,)),
        ],
        compiler_params=pltpu.CompilerParams(vmem_limit_bytes=58 * 1024 * 1024),
        cost_estimate=BRIEF,
        name="mlp_bwd",
    )(*panels, hidden, grad, up, act)


def panel_view(rows_ref, first, count, depth):
    region = rows_ref.at[pl.ds(first, depth // 8 * count)]
    return region.reshape(depth // 8, count, 8, WIDE)


def project_kernel(first, count, depth, lead, x_ref, rows_ref, *rest):
    outs, held, sems = rest[:-2], rest[-2], rest[-1]
    step = pl.program_id(0)
    panels = panel_view(rows_ref, first, count, depth)

    @pl.when(step == 0)
    def _():
        for n in range(count):
            pltpu.make_async_copy(panels.at[:, n], held.at[n], sems.at[n]).start()

    pltpu.make_async_copy(held.at[step], held.at[step], sems.at[step]).wait()
    result = product(x_ref[...], held[step].reshape(depth, WIDE)).astype(jnp.bfloat16)
    if lead:

        @pl.when(step == 0)
        def _():
            outs[0][...] = result

        @pl.when(step > 0)
        def _():
            outs[1][0] = result

    else:
        outs[0][0] = result


def project(x, rows, first, count, lead):
    tokens, depth = x.shape
    specs = [pl.BlockSpec((1, tokens, WIDE), lambda n: (jnp.maximum(n - lead, 0), 0, 0))]
    shapes = [jax.ShapeDtypeStruct((count - lead, tokens, WIDE), jnp.bfloat16)]
    if lead:
        specs.insert(0, pl.BlockSpec((tokens, WIDE), lambda n: (0, 0)))
        shapes.insert(0, jax.ShapeDtypeStruct((tokens, WIDE), jnp.bfloat16))
    return pl.pallas_call(
        functools.partial(project_kernel, first, count, depth, lead),
        grid=(count,),
        in_specs=[pl.BlockSpec((tokens, depth), lambda n: (0, 0)), pl.BlockSpec(memory_space=pl.ANY)],
        out_specs=specs,
        out_shape=shapes,
        scratch_shapes=[pltpu.VMEM((count, depth // 8, 8, WIDE), jnp.bfloat16), pltpu.SemaphoreType.DMA((count,))],
        compiler_params=pltpu.CompilerParams(vmem_limit_bytes=32 * 1024 * 1024),
        cost_estimate=BRIEF,
        name="project",
    )(x, rows)


def project_back_kernel(first, count, depth, lead_ref, g_ref, rows_ref, o_ref, held, sems):
    step = pl.program_id(0)
    panels = panel_view(rows_ref, first, count, depth)

    @pl.when(step == 0)
    def _():
        for n in range(count):
            pltpu.make_async_copy(panels.at[:, n], held.at[n], sems.at[n]).start()

    pltpu.make_async_copy(held.at[step], held.at[step], sems.at[step]).wait()
    grad = jnp.where(step == 0, lead_ref[...], g_ref[0])
    back = nt_dot(grad, held[step].reshape(depth, WIDE))

    @pl.when(step == 0)
    def _():
        o_ref[...] = back

    @pl.when(step > 0)
    def _():
        o_ref[...] += back


def project_back(lead, grads, rows, first, depth):
    others, tokens, _ = grads.shape
    count = others + 1
    return pl.pallas_call(
        functools.partial(project_back_kernel, first, count, depth),
        grid=(count,),
        in_specs=[
            pl.BlockSpec((tokens, WIDE), lambda n: (0, 0)),
            pl.BlockSpec((1, tokens, WIDE), lambda n: (jnp.maximum(n - 1, 0), 0, 0)),
            pl.BlockSpec(memory_space=pl.ANY),
        ],
        out_specs=pl.BlockSpec((tokens, depth), lambda n: (0, 0)),
        out_shape=jax.ShapeDtypeStruct((tokens, depth), jnp.float32),
        scratch_shapes=[pltpu.VMEM((count, depth // 8, 8, WIDE), jnp.bfloat16), pltpu.SemaphoreType.DMA((count,))],
        compiler_params=pltpu.CompilerParams(vmem_limit_bytes=32 * 1024 * 1024),
        cost_estimate=BRIEF,
        name="project_back",
    )(lead, grads, rows)


def weight_grads_kernel(products, copies, *refs):
    arrays = refs[: len(refs) - 8]
    out, left, right, staged, bounce, load_sem, store_sem, copy_sem = refs[len(refs) - 8 :]
    step = pl.program_id(0)
    steps = len(products)

    def loads(n):
        side, (a, a_pick), (b, b_pick), _, _ = products[n]
        slot = n % 2
        source_a = arrays[a] if a_pick is None else arrays[a].at[a_pick]
        source_b = arrays[b] if b_pick is None else arrays[b].at[b_pick]
        rows, deep = side
        return [
            pltpu.make_async_copy(source_a, left.at[slot, pl.ds(0, rows), pl.ds(0, deep)], load_sem.at[slot, 0]),
            pltpu.make_async_copy(source_b, right.at[slot, pl.ds(0, rows)], load_sem.at[slot, 1]),
        ]

    def stores(n):
        (rows, deep), _, _, first, panels = products[n]
        slot = n % 2
        count, at = panels
        source = staged.at[slot, pl.ds(0, deep // 8)]
        target = panel_view(out, first, count, deep).at[:, at]
        return pltpu.make_async_copy(source, target, store_sem.at[slot])

    def bounced(n):
        a, first, count = copies[n]
        held = bounce.at[pl.ds(sum(c[2] for c in copies[:n]), count)]
        return (
            pltpu.make_async_copy(arrays[a], held, copy_sem.at[n, 0]),
            pltpu.make_async_copy(held, out.at[pl.ds(first, count)], copy_sem.at[n, 1]),
        )

    for n in range(steps):

        @pl.when(step == n)
        def _():
            if n == 0:
                for job in loads(0):
                    job.start()
                for m in range(len(copies)):
                    bounced(m)[0].start()
            if n == 1:
                for m in range(len(copies)):
                    bounced(m)[0].wait()
                    bounced(m)[1].start()
            if n + 1 < steps:
                for job in loads(n + 1):
                    job.start()
            for job in loads(n):
                job.wait()
            if n >= 2:
                stores(n - 2).wait()
            rows, deep = products[n][0]
            slot = n % 2
            total = lax.dot_general(
                left[slot, :rows, :deep], right[slot, :rows], (((0,), (0,)), ((), ())), preferred_element_type=jnp.float32
            )
            staged[slot, : deep // 8] = total.astype(jnp.bfloat16).reshape(deep // 8, 8, WIDE)
            stores(n).start()
            if n == steps - 1:
                if n > 0:
                    stores(n - 1).wait()
                stores(n).wait()
                for m in range(len(copies)):
                    bounced(m)[1].wait()


def weight_grads(arrays, products, copies, tile_rows):
    rows = max(p[0][0] for p in products)
    deep = max(p[0][1] for p in products)
    everywhere = pl.BlockSpec(memory_space=pl.ANY)
    return pl.pallas_call(
        functools.partial(weight_grads_kernel, products, copies),
        grid=(len(products),),
        in_specs=[everywhere] * len(arrays),
        out_specs=everywhere,
        out_shape=jax.ShapeDtypeStruct((tile_rows, 8, WIDE), jnp.bfloat16),
        scratch_shapes=[
            pltpu.VMEM((2, rows, deep), jnp.bfloat16),
            pltpu.VMEM((2, rows, WIDE), jnp.bfloat16),
            pltpu.VMEM((2, deep // 8, 8, WIDE), jnp.bfloat16),
            pltpu.VMEM((sum(c[2] for c in copies), 8, WIDE), jnp.bfloat16),
            pltpu.SemaphoreType.DMA((2, 2)),
            pltpu.SemaphoreType.DMA((2,)),
            pltpu.SemaphoreType.DMA((len(copies), 2)),
        ],
        compiler_params=pltpu.CompilerParams(vmem_limit_bytes=40 * 1024 * 1024),
        cost_estimate=BRIEF,
        name="weight_grads",
    )(*arrays)


TILE = 8 * WIDE
KV_AT = D * D
QKV_AT = KV_AT + DI * 2 * D + D * D
GAP_AT = QKV_AT + D * 3 * D + D * D + D * 16 * CH + CH * DEC_HID + DEC_HID * 4
QKV_GAP = -QKV_AT % (3 * TILE)
END_GAP = -GAP_AT % TILE
TILES = {}
_tile = 0
for _name, _rows in (
    ("query_cross", D),
    ("keyval_cross", 2 * DI),
    ("out_cross", D),
    ("gap", QKV_GAP // WIDE),
    ("qkv_self", 3 * D),
    ("out_self", D),
    ("deconv", 16 * CH),
    ("decode", 8),
    ("modulate", 6 * NCAM),
    ("triplane", 0),
):
    TILES[_name] = _tile
    _tile += _rows // 8


def direct_links():
    return lax.axis_size("dp") == 16 and lax.axis_size("strip") == 2


def regroup(rows, first, back):
    tile = first + lax.broadcasted_iota(jnp.int32, (rows.shape[0], 1), 0) // 8

    def turned(panels):
        shape = (-1, panels, 8, WIDE) if back else (-1, 8, panels, WIDE)
        return rows.reshape(shape).transpose(0, 2, 1, 3).reshape(rows.shape)

    in_kv = (tile >= TILES["keyval_cross"]) & (tile < TILES["out_cross"])
    in_qkv = (tile >= TILES["qkv_self"]) & (tile < TILES["out_self"])
    return jnp.where(in_kv, turned(2), jnp.where(in_qkv, turned(3), rows))


def device_place():
    return lax.axis_index("dp") * lax.axis_size("strip") + lax.axis_index("strip")


def tile_rows(length):
    return -(-length // (6 * TILE)) * 6


def align(shard):
    length = shard.shape[0]
    size = tile_rows(length) * TILE
    extra = size - length
    reach = -(-32 * extra // WIDE) * WIDE
    place = device_place()
    shard = shard.astype(jnp.bfloat16)
    following = lax.ppermute(shard[:reach], AXES, [(n + 1, n) for n in range(31)])
    joined = jnp.concatenate([shard, following])
    shift = place * extra
    at = place * size + lax.iota(jnp.int32, size)
    parts = [
        lax.dynamic_slice_in_dim(joined, jnp.maximum(shift - gap, 0), size)
        for gap in (0, QKV_GAP, QKV_GAP + END_GAP)
    ]
    rows = jnp.where(at < QKV_AT, parts[0], jnp.where(at < GAP_AT + QKV_GAP, parts[1], parts[2]))
    return regroup(rows.reshape(-1, WIDE), place * (size // TILE), False)


def unalign(summed, length):
    size = summed.size
    extra = size - length
    reach = -(-32 * extra // WIDE) * WIDE
    place = device_place()
    summed = regroup(summed, place * (size // TILE), True).reshape(-1)
    before = lax.ppermute(summed[size - reach :], AXES, [(n, n + 1) for n in range(31)])
    joined = jnp.concatenate([before, summed])
    shift = reach - place * extra
    at = place * length + lax.iota(jnp.int32, length)
    parts = [lax.dynamic_slice_in_dim(joined, shift + gap, length) for gap in (0, QKV_GAP, QKV_GAP + END_GAP)]
    return jnp.where(at < QKV_AT, parts[0], jnp.where(at < GAP_AT, parts[1], parts[2]))


def chunks_of(tiles):
    return tiles.reshape(-1, 8, BLOCK, BLOCK).transpose(0, 2, 1, 3).reshape(-1, WIDE)


def tiles_of(chunks):
    return chunks.reshape(-1, BLOCK, 8, BLOCK).transpose(0, 2, 1, 3).reshape(-1, BLOCK, BLOCK)


def panels_of(chunks):
    half = chunks.shape[0] // 2
    first = chunks[:half].reshape(D // BLOCK, HID // WIDE, BLOCK, WIDE).transpose(1, 0, 2, 3)
    return jnp.concatenate([first.reshape(half, WIDE), chunks[half:]])


def chunks_of_panels(panels):
    half = panels.shape[0] // 2
    first = panels[:half].reshape(HID // WIDE, D // BLOCK, BLOCK, WIDE).transpose(1, 0, 2, 3)
    return jnp.concatenate([first.reshape(half, WIDE), panels[half:]])


META = (1, 8, lambda p, c, j: (2 * p + c) * 8)
SWAP = ((0, 1), (1, 0))
AXES = ("dp", "strip")


def pairs_to(target):
    return [(2 * p + c, sum(v * w for v, w in zip(target(p, c), (2, 1)))) for p in range(16) for c in range(2)]


NEAR = pairs_to(lambda p, c: (p ^ (1 + c), c))
FAR = pairs_to(lambda p, c: (p ^ (2 - c), c))
CORE = pairs_to(lambda p, c: (p, 1 - c))


def gather_weights(weights, blocks, part):
    length = weights.shape[0]
    if direct_links():
        own = align(weights)
        half = blocks.shape[0] // 2
        tiles = lax.dynamic_slice_in_dim(blocks, lax.axis_index("strip") * half, half)
        tiles = chunks_of(tiles.astype(jnp.bfloat16))
        meta = jnp.full((8, 128), part, jnp.float32)
        rows, parts, line = gather_all([flat_chunks(own.shape[0], 3), META], 6, [own, meta], tiles, 0)
        near = lax.ppermute(line, AXES, NEAR)
        return rows, [line, near], jnp.sum(parts[::8, 0])
    flat = lax.all_gather(weights.astype(jnp.bfloat16), AXES, axis=0, tiled=True)
    tiles = lax.all_gather(blocks.astype(jnp.bfloat16), "dp", axis=0, tiled=True)
    gaps = [jnp.zeros((QKV_GAP,), flat.dtype), jnp.zeros((END_GAP,), flat.dtype)]
    rows = jnp.concatenate([flat[:QKV_AT], gaps[0], flat[QKV_AT:GAP_AT], gaps[1], flat[GAP_AT:]])
    rows = jnp.pad(rows, (0, -rows.shape[0] % (6 * TILE))).reshape(-1, WIDE)
    return regroup(rows, 0, False), [panels_of(chunks_of(tiles))], lax.psum(part, AXES)


class Panels:
    def __init__(self, parts):
        self.parts = parts
        self.staged = len(parts) > 1

    def first(self, before):
        if not self.staged:
            return before
        line, near = self.parts
        near, before = lax.optimization_barrier((near, before))
        self.parts = [line, near, lax.ppermute(line, AXES, FAR)]
        return before

    def second(self, before):
        if not self.staged:
            return before
        line, near, far = self.parts
        far, before = lax.optimization_barrier((far, before))
        self.parts = [line, near, far, lax.ppermute(near, AXES, FAR)]
        return before

    def third(self, after):
        if not self.staged:
            return self.parts
        line, near, far, both = self.parts
        both, after = lax.optimization_barrier((both, after))
        return [line, near, far, both] + [lax.ppermute(group, AXES, CORE) for group in (line, near, far, both)]


class PanelSums:
    def __init__(self, grads):
        self.parts = grads
        self.staged = len(grads) > 1
        if self.staged:
            self.mine = grads[0]
            self.got = lax.ppermute(grads[1], AXES, CORE)

    def added(self, g, *parts):
        at = slice(4 * g, 4 * g + 4)
        total = self.mine[at].astype(jnp.float32) + self.got[at].astype(jnp.float32)
        for part in parts:
            total = total + part.astype(jnp.float32)
        return total.astype(jnp.bfloat16)

    def first(self, before):
        if not self.staged:
            return before
        both, self.far, before = lax.optimization_barrier((self.added(3), self.added(2), before))
        self.to_near = lax.ppermute(both, AXES, FAR)
        return before

    def second(self, before):
        if not self.staged:
            return before
        self.to_near, self.far, before = lax.optimization_barrier((self.to_near, self.far, before))
        self.to_own = lax.ppermute(self.far, AXES, FAR)
        return before

    def third(self, before):
        if not self.staged:
            return before
        near, self.to_own, before = lax.optimization_barrier((self.added(1, self.to_near), self.to_own, before))
        self.last = lax.ppermute(near, AXES, NEAR)
        return before

    def fourth(self, before):
        if not self.staged:
            return before
        self.last, before = lax.optimization_barrier((self.last, before))
        self.parts = [self.added(0, self.to_own, self.last)]
        return before


def reduce_grads(rows, panels, part, length):
    if direct_links():
        meta = jnp.full((32 * 8, 128), part, jnp.float32)
        summed, parts, tiles = scatter_sum(
            [flat_chunks(rows.shape[0] // 32, 3), META], 6, [rows, meta], panels[0], 1
        )
        return unalign(summed, length), tiles_of(tiles).astype(jnp.float32), parts[0, 0]
    flat = regroup(rows, 0, True).astype(jnp.float32).reshape(-1)
    flat = jnp.concatenate(
        [flat[:QKV_AT], flat[QKV_AT + QKV_GAP : GAP_AT + QKV_GAP], flat[GAP_AT + QKV_GAP + END_GAP :]]
    )
    devices = lax.axis_size("dp") * lax.axis_size("strip")
    flat = jnp.pad(flat, (0, max(0, devices * length - flat.shape[0])))[: devices * length]
    tiles = tiles_of(chunks_of_panels(panels[0])).astype(jnp.float32)
    flat_sum = lax.psum_scatter(flat, AXES, scatter_dimension=0, tiled=True)
    tile_sum = lax.psum_scatter(tiles, AXES, scatter_dimension=0, tiled=True)
    tile_sum = lax.all_gather(tile_sum.astype(jnp.bfloat16), "strip", axis=0, tiled=True)
    return flat_sum, tile_sum.astype(jnp.float32), lax.psum(part, AXES)


def shards(
    weights,
    blocks,
    stat_left,
    stat_right,
    root_left,
    root_right,
    first_moment,
    second_moment,
    image,
    camera,
    samples,
    ray_pixel,
    target,
    valid,
):
    strips = lax.axis_size("strip")
    place = lax.axis_index("strip")
    pixel = ray_pixel[0]
    mask = jnp.take(valid[0], pixel).astype(jnp.float32)
    wanted = jnp.take(target[0], pixel, axis=1)
    rows, panels, count = gather_weights(weights, blocks, jnp.sum(mask))
    tiled = rows.reshape(-1, 8, WIDE)

    def square(name):
        return rows[TILES[name] * 8 : TILES[name] * 8 + D]

    def plain(name, count):
        return rows[TILES[name] * 8 : TILES[name] * 8 + count]

    deconv = plain("deconv", 16 * CH).reshape(D, 16 * CH)
    decode = plain("decode", 8).reshape(-1)
    decode_in = decode[: CH * DEC_HID].reshape(CH, DEC_HID)
    decode_out = decode[CH * DEC_HID : CH * DEC_HID + DEC_HID * 4].reshape(DEC_HID, 4)
    picture = image[0]
    real_keys = picture.shape[0]
    picture = jnp.pad(picture, ((0, -real_keys % 128), (0, 0)))
    mods = lax.dynamic_slice_in_dim(plain("modulate", 6 * NCAM), 6 * camera[0], 6).astype(jnp.float32)
    own_rows = PR * TC
    stream0 = jnp.concatenate(
        [
            lax.dynamic_slice_in_dim(rows, TILES["triplane"] * 8 + (strips * plane + place) * own_rows, own_rows)
            for plane in range(3)
        ]
    ).astype(jnp.float32)
    hidden1, norm_one = jax.vjp(norm_mod, stream0, mods[0], mods[1])
    hidden1 = hidden1.astype(jnp.bfloat16)
    query1 = product(hidden1, square("query_cross")).astype(jnp.bfloat16)
    (image_kv,) = project(picture, tiled, TILES["keyval_cross"], 2, 0)
    pairs = D // PAIR
    tokens = query1.shape[0]
    cross_out, total_one = attend_fwd(query1, [image_kv], real_keys, (0, pairs))
    stream1 = stream0 + product(cross_out, square("out_cross"))
    hidden2, norm_two = jax.vjp(norm_mod, stream1, mods[2], mods[3])
    hidden2 = hidden2.astype(jnp.bfloat16)
    panels = Panels(panels)
    hidden2 = panels.first(hidden2)
    query2, kv_own = project(hidden2, tiled, TILES["qkv_self"], 3, 1)
    kv_both = [kv_own, lax.ppermute(kv_own, "strip", SWAP)]
    all_keys = 2 * kv_own.shape[1]
    early = attend_fwd(query2, kv_both, all_keys, (0, pairs // 2))
    early = (panels.second(early[0]), early[1])
    self_out, total_two = attend_fwd(query2, kv_both, all_keys, (pairs // 2, pairs), early)
    panels = panels.third(self_out)
    stream2 = stream1 + product(self_out, square("out_self"))
    hidden3, norm_three = jax.vjp(norm_mod, stream2, mods[4], mods[5])
    hidden3 = hidden3.astype(jnp.bfloat16)
    up, act, grid = mlp_fwd(panels, hidden3, stream2)
    grid = grid.reshape(3, PR, -1, D)
    edge = lax.ppermute(jnp.where(place == 0, grid[:, -1:], grid[:, :1]), "strip", SWAP)
    nothing = jnp.zeros_like(edge)
    padded = jnp.concatenate(
        [jnp.where(place == 0, nothing, edge), grid, jnp.where(place == 0, edge, nothing)], 1
    )
    ydc = jnp.einsum("prcd,dk->prck", padded, deconv, preferred_element_type=jnp.float32)
    feature, assemble_back = jax.vjp(assemble, ydc)
    cells = feature.astype(jnp.bfloat16).reshape(3, -1, CH)
    cells_far = lax.ppermute(cells, "strip", SWAP)
    rays = pixel.shape[0]
    factor = 1.0 / jnp.maximum(count, 1.0)
    loss_part, grad_cells, grad_far, grad_decode_in, grad_decode_out = render(
        cells,
        cells_far,
        (samples[0] + place * cells.shape[1]) % (2 * cells.shape[1]),
        jnp.pad(wanted, ((1, 4), (0, 0))),
        mask[None],
        factor.reshape(1),
        decode_in,
        jnp.pad(decode_out, ((0, 0), (0, 4))),
        rays,
    )
    loss_part = loss_part[0, 0]
    grad_decode_out = grad_decode_out[:, :4]
    grad_cells = grad_cells.astype(jnp.float32) + lax.ppermute(grad_far, "strip", SWAP).astype(jnp.float32)
    grad_feature = grad_cells.astype(jnp.bfloat16).transpose(0, 2, 1).reshape(feature.shape)
    grad_feature = lax.optimization_barrier(grad_feature).astype(jnp.float32)
    (grad_ydc,) = assemble_back(grad_feature)
    grad_ydc = grad_ydc.astype(jnp.bfloat16)
    grad_deconv = weight_grad(padded.reshape(-1, D), grad_ydc.reshape(-1, 16 * CH))
    grad_padded = product_back(grad_ydc, deconv)
    beside = jnp.where(place == 0, grad_padded[:, -1], grad_padded[:, 0]).astype(jnp.bfloat16)
    beside = lax.ppermute(beside, "strip", SWAP).astype(jnp.float32)
    grad_grid = grad_padded[:, 1:-1]
    grad_grid = grad_grid.at[:, 0].add(jnp.where(place == 0, 0.0, beside))
    grad_grid = grad_grid.at[:, -1].add(jnp.where(place == 0, beside, 0.0))
    grad_stream = grad_grid.reshape(-1, D)
    grad_branch = grad_stream.astype(jnp.bfloat16)
    grad_hidden3, *panel_grads = mlp_bwd(panels, hidden3, grad_branch, up, act)
    grad_norm, grad_mod4, grad_mod5 = norm_three(grad_hidden3)
    grad_stream = grad_stream + grad_norm
    grad_branch2 = grad_stream.astype(jnp.bfloat16)
    grad_self = product_back(grad_branch2, square("out_self")).astype(jnp.bfloat16)
    panel_sums = PanelSums(panel_grads)
    grad_self = panel_sums.first(grad_self)
    early = attend_bwd(query2, kv_both, all_keys, (0, pairs // 2), 512, total_two, self_out, grad_self)
    early = (panel_sums.second(early[0]), *early[1:])
    grad_query2, grad_kv_own, grad_kv_far = attend_bwd(
        query2, kv_both, all_keys, (pairs // 2, pairs), 512, total_two, self_out, grad_self, early
    )
    grad_kv_far = lax.ppermute(grad_kv_far, "strip", SWAP)
    grad_query2 = panel_sums.third(grad_query2)
    grad_kv = (grad_kv_own.astype(jnp.float32) + grad_kv_far.astype(jnp.float32)).astype(jnp.bfloat16)
    grad_hidden2 = project_back(grad_query2, grad_kv, tiled, TILES["qkv_self"], D)
    grad_norm, grad_mod2, grad_mod3 = norm_two(grad_hidden2)
    grad_stream = grad_stream + grad_norm
    grad_branch1 = grad_stream.astype(jnp.bfloat16)
    grad_cross = product_back(grad_branch1, square("out_cross")).astype(jnp.bfloat16)
    grad_query1, grad_image_kv = attend_bwd(
        query1, [image_kv], real_keys, (0, pairs), 128, total_one, cross_out, grad_cross
    )
    grad_query1 = panel_sums.fourth(grad_query1)
    grad_norm, grad_mod0, grad_mod1 = norm_one(product_back(grad_query1, square("query_cross")))
    grad_stream = grad_stream + grad_norm
    grad_mods = jnp.stack([grad_mod0, grad_mod1, grad_mod2, grad_mod3, grad_mod4, grad_mod5])
    grad_modulate = lax.dynamic_update_slice_in_dim(
        jnp.zeros((6 * NCAM, D), jnp.bfloat16), grad_mods.astype(jnp.bfloat16), 6 * camera[0], 0
    )
    grad_triplane = lax.dynamic_update_slice_in_dim(
        jnp.zeros((3, strips, own_rows, D), jnp.bfloat16),
        grad_stream.astype(jnp.bfloat16).reshape(3, 1, own_rows, D),
        place,
        1,
    )
    grad_decode = jnp.concatenate([grad_decode_in.reshape(-1), grad_decode_out.reshape(-1)])
    grad_decode = jnp.pad(grad_decode, (0, END_GAP))
    total_tiles = tiled.shape[0]
    end = TILES["triplane"] + 3 * strips * own_rows // 8
    gap = TILES["qkv_self"] - TILES["gap"]
    arrays = [
        hidden1,
        grad_query1,
        picture,
        grad_image_kv,
        cross_out,
        grad_branch1,
        hidden2,
        grad_query2,
        grad_kv,
        self_out,
        grad_branch2,
    ]
    tall, low = (tokens, D), (picture.shape[0], DI)
    products = [
        (tall, (9, None), (10, None), TILES["out_self"], (1, 0)),
        (tall, (6, None), (7, None), TILES["qkv_self"], (3, 0)),
        (tall, (6, None), (8, 0), TILES["qkv_self"], (3, 1)),
        (tall, (6, None), (8, 1), TILES["qkv_self"], (3, 2)),
        (tall, (4, None), (5, None), TILES["out_cross"], (1, 0)),
        (low, (2, None), (3, 0), TILES["keyval_cross"], (2, 0)),
        (low, (2, None), (3, 1), TILES["keyval_cross"], (2, 1)),
        (tall, (0, None), (1, None), TILES["query_cross"], (1, 0)),
    ]
    copies = []
    for piece, first in (
        (grad_deconv, TILES["deconv"]),
        (grad_decode, TILES["decode"]),
        (grad_modulate, TILES["modulate"]),
        (grad_triplane, TILES["triplane"]),
        (jnp.zeros((gap, 8, WIDE), jnp.bfloat16), TILES["gap"]),
        (jnp.zeros((total_tiles - end, 8, WIDE), jnp.bfloat16), end),
    ):
        piece = piece.astype(jnp.bfloat16).reshape(-1, 8, WIDE)
        if piece.shape[0]:
            copies.append((len(arrays), first, piece.shape[0]))
            arrays.append(piece)
    row_grads = weight_grads(arrays, products, copies, total_tiles).reshape(-1, WIDE)
    flat_sum, block_sum, loss_sum = reduce_grads(row_grads, panel_sums.parts, loss_part, weights.shape[0])
    loss = loss_sum * factor
    new_first = BETA_FIRST * first_moment + (1.0 - BETA_FIRST) * flat_sum
    new_second = BETA_SECOND * second_moment + (1.0 - BETA_SECOND) * flat_sum * flat_sum
    fix_first = 1.0 - BETA_FIRST**ADAM_STEP
    fix_second = 1.0 - BETA_SECOND**ADAM_STEP
    moved = new_first / fix_first / (jnp.sqrt(new_second / fix_second) + ADAM_EPS)
    new_weights = weights - ADAM_RATE * (moved + WEIGHT_DECAY * weights)
    new_left = STAT_DECAY * stat_left + (1.0 - STAT_DECAY) * jnp.einsum(
        "bij,bkj->bik", block_sum, block_sum, precision=HIGHEST_MODE
    )
    new_right = STAT_DECAY * stat_right + (1.0 - STAT_DECAY) * jnp.einsum(
        "bji,bjk->bik", block_sum, block_sum, precision=HIGHEST_MODE
    )
    half_step = jnp.einsum("bij,bjk->bik", block_sum, root_right, precision=HIGHEST_MODE)
    precond = jnp.einsum("bij,bjk->bik", root_left, half_step, precision=HIGHEST_MODE)
    block_rms = jnp.sqrt(jnp.mean(precond * precond, axis=(1, 2)) + RMS_EPS)
    new_blocks = blocks - SHAMPOO_RATE * precond / block_rms[:, None, None]
    return (
        loss,
        new_weights,
        new_first,
        new_second,
        new_blocks,
        block_sum,
        new_left,
        new_right,
        block_rms,
    )


def solution(mesh):
    placed = (
        P(("dp", "strip")),
        P("dp", None, None),
        P("dp", None, None),
        P("dp", None, None),
        P("dp", None, None),
        P("dp", None, None),
        P(("dp", "strip")),
        P(("dp", "strip")),
        P("dp", None, None),
        P("dp"),
        P("dp", None, None, "strip"),
        P("dp", "strip"),
        P("dp", None, None),
        P("dp", None),
    )
    return jax.shard_map(
        shards,
        mesh=mesh,
        in_specs=placed,
        out_specs=(
            P(),
            P(("dp", "strip")),
            P(("dp", "strip")),
            P(("dp", "strip")),
            P("dp", None, None),
            P("dp", None, None),
            P("dp", None, None),
            P("dp", None, None),
            P("dp"),
        ),
        check_vma=False,
    )
```

```python
import functools
import math

import jax
import jax.numpy as jnp
from jax import lax
from jax.experimental import pallas as pl
from jax.experimental.pallas import tpu as pltpu
from jax.sharding import PartitionSpec as P

D = 1024
HEAD_DIM = 64
HID = 4096
DI = 768
CH = 80
DEC_HID = 64
BLOCK = 128
PR = 8
TC = 32
S = 16
NCAM = 32
ADAM_STEP = 10


NORM_EPS = 1e-05
ADAM_RATE = 0.015
BETA_FIRST = 0.9
BETA_SECOND = 0.95
ADAM_EPS = 1e-08
WEIGHT_DECAY = 0.1
STAT_DECAY = 0.9
SHAMPOO_RATE = 0.01
RMS_EPS = 1e-06
HIGHEST_MODE = lax.Precision.HIGHEST
WIDE = 1024


def product(left, right):
    return jnp.dot(left, right, preferred_element_type=jnp.float32)


def product_back(left, right):
    return lax.dot_general(
        left, right, (((left.ndim - 1,), (1,)), ((), ())), preferred_element_type=jnp.float32
    )


def weight_grad(left, right):
    return lax.dot_general(
        left, right, (((0,), (0,)), ((), ())), preferred_element_type=jnp.float32
    )


def norm_mod(stream, scale, shift):
    centred = stream - jnp.mean(stream, -1, keepdims=True)
    spread = jnp.mean(centred * centred, -1, keepdims=True)
    return centred * lax.rsqrt(spread + NORM_EPS) * (1.0 + scale) + shift


def gelu_tanh(value):
    return jax.nn.gelu(value, approximate=True)


PAIR = 2 * HEAD_DIM
BRIEF = pl.CostEstimate(flops=1000000, transcendentals=0, bytes_accessed=100000)
LOG2E = math.log2(math.e)
EXP_SCALE = HEAD_DIM ** (-0.5) * LOG2E


def nt_dot(left, right):
    return lax.dot_general(left, right, (((1,), (1,)), ((), ())), preferred_element_type=jnp.float32)


def head_lanes(shape, head):
    return lax.broadcasted_iota(jnp.int32, shape, len(shape) - 1) // HEAD_DIM == head


def joined(refs, n):
    parts = [ref[n] for ref in refs]
    return parts[0] if len(parts) == 1 else jnp.concatenate(parts, 0)


def attend_fwd_kernel(real_keys, sources, q_ref, *refs):
    o_ref, lse_ref = refs[-2:]
    query, keys = q_ref[...], joined(refs[:sources], 0)
    values = joined(refs[:sources], 1).T
    outs = []
    for head in range(2):
        own = jnp.where(head_lanes(query.shape, head), query, 0)
        scores = nt_dot(keys, own)
        if real_keys < keys.shape[0]:
            at = lax.broadcasted_iota(jnp.int32, scores.shape, 0)
            scores = jnp.where(at < real_keys, scores, -3e38)
        top = jnp.max(scores, 0, keepdims=True)
        raised = jnp.exp2((scores - top) * EXP_SCALE)
        total = jnp.sum(raised, 0, keepdims=True)
        shares = (raised * (1.0 / total)).astype(jnp.bfloat16)
        outs.append(product(values[head * HEAD_DIM : (head + 1) * HEAD_DIM], shares))
        lse_ref[0, head : head + 1] = top * EXP_SCALE + jnp.log2(total)
    o_ref[...] = jnp.concatenate(outs, 0).T.astype(jnp.bfloat16)


def attend_fwd(query, sources, real_keys, span, earlier=()):
    count = query.shape[0]
    total_keys = sum(source.shape[1] for source in sources)
    low, high = span
    by_pair = pl.BlockSpec((count, PAIR), lambda j: (0, low + j))
    work = count * total_keys * (high - low) * PAIR
    return pl.pallas_call(
        functools.partial(attend_fwd_kernel, real_keys, len(sources)),
        grid=(high - low,),
        in_specs=[by_pair]
        + [pl.BlockSpec((2, source.shape[1], PAIR), lambda j: (0, 0, low + j)) for source in sources]
        + [pl.BlockSpec(memory_space=pl.ANY)] * len(earlier),
        out_specs=[by_pair, pl.BlockSpec((1, 8, count), lambda j: (low + j, 0, 0))],
        out_shape=[
            jax.ShapeDtypeStruct((count, D), jnp.bfloat16),
            jax.ShapeDtypeStruct((D // PAIR, 8, count), jnp.float32),
        ],
        input_output_aliases={1 + len(sources) + n: n for n in range(len(earlier))},
        compiler_params=pltpu.CompilerParams(vmem_limit_bytes=48 * 1024 * 1024),
        cost_estimate=BRIEF,
        name="attend_fwd",
    )(query, *sources, *earlier)


def attend_bwd_kernel(real_keys, chunk, sources, extra, q_ref, *refs):
    kv_refs = refs[:sources]
    lse_ref, o_ref, g_ref = refs[sources : sources + 3]
    dq_ref, *grad_refs = refs[sources + 3 + extra : sources + 4 + extra + sources]
    k_all, v_all, kt_ref, dk_sum, dv_sum = refs[sources + 4 + extra + sources :]
    k_all[...] = joined(kv_refs, 0)
    v_all[...] = joined(kv_refs, 1)
    kt_ref[...] = k_all[...].T
    query, grad = q_ref[...], g_ref[...]
    mixed = (grad.astype(jnp.float32) * o_ref[...].astype(jnp.float32)).T
    total_keys = k_all.shape[0]
    queries = [jnp.where(head_lanes(query.shape, head), query, 0) for head in range(2)]
    grads = [jnp.where(head_lanes(grad.shape, head), grad, 0) for head in range(2)]
    inner = [jnp.sum(mixed[head * HEAD_DIM : (head + 1) * HEAD_DIM], 0, keepdims=True) for head in range(2)]
    grad_query = [jnp.zeros((HEAD_DIM, query.shape[0]), jnp.float32) for head in range(2)]
    for at in range(0, total_keys, chunk):
        part = pl.ds(at, chunk)
        keys, values = k_all[part], v_all[part]
        for head in range(2):
            scores = nt_dot(keys, queries[head])
            shares = jnp.exp2(scores * EXP_SCALE - lse_ref[0, head : head + 1])
            if at + chunk > real_keys:
                row = at + lax.broadcasted_iota(jnp.int32, shares.shape, 0)
                shares = jnp.where(row < real_keys, shares, 0.0)
            grad_shares = nt_dot(values, grads[head])
            grad_scores = (shares * (grad_shares - inner[head])).astype(jnp.bfloat16)
            to_values = product(shares.astype(jnp.bfloat16), grads[head])
            to_keys = product(grad_scores, queries[head])
            if head == 0:
                dv_sum[part] = to_values
                dk_sum[part] = to_keys
            else:
                dv_sum[part] += to_values
                dk_sum[part] += to_keys
            grad_query[head] += product(
                kt_ref[head * HEAD_DIM : (head + 1) * HEAD_DIM, part], grad_scores
            )
    scale = HEAD_DIM ** (-0.5)
    dq_ref[...] = (jnp.concatenate(grad_query, 0) * scale).T.astype(jnp.bfloat16)
    start = 0
    for ref in grad_refs:
        part = pl.ds(start, ref.shape[1])
        ref[0] = (dk_sum[part] * scale).astype(jnp.bfloat16)
        ref[1] = dv_sum[part].astype(jnp.bfloat16)
        start += ref.shape[1]


def attend_bwd(query, sources, real_keys, span, chunk, totals, out, grad, earlier=()):
    count = query.shape[0]
    total_keys = sum(source.shape[1] for source in sources)
    low, high = span
    by_pair = pl.BlockSpec((count, PAIR), lambda j: (0, low + j))
    by_source = [pl.BlockSpec((2, source.shape[1], PAIR), lambda j: (0, 0, low + j)) for source in sources]
    first = 1 + len(sources) + 3
    work = count * total_keys * (high - low) * PAIR
    return pl.pallas_call(
        functools.partial(attend_bwd_kernel, real_keys, chunk, len(sources), len(earlier)),
        grid=(high - low,),
        in_specs=[by_pair]
        + by_source
        + [pl.BlockSpec((1, 8, count), lambda j: (low + j, 0, 0)), by_pair, by_pair]
        + [pl.BlockSpec(memory_space=pl.ANY)] * len(earlier),
        out_specs=[by_pair] + by_source,
        out_shape=[jax.ShapeDtypeStruct((count, D), jnp.bfloat16)]
        + [jax.ShapeDtypeStruct(source.shape, jnp.bfloat16) for source in sources],
        input_output_aliases={first + n: n for n in range(len(earlier))},
        scratch_shapes=[
            pltpu.VMEM((total_keys, PAIR), jnp.bfloat16),
            pltpu.VMEM((total_keys, PAIR), jnp.bfloat16),
            pltpu.VMEM((PAIR, total_keys), jnp.bfloat16),
            pltpu.VMEM((total_keys, PAIR), jnp.float32),
            pltpu.VMEM((total_keys, PAIR), jnp.float32),
        ],
        compiler_params=pltpu.CompilerParams(vmem_limit_bytes=48 * 1024 * 1024),
        cost_estimate=BRIEF,
        name="attend_bwd",
    )(query, *sources, totals, out, grad, *earlier)


GROUPS = 3


def render_kernel(samples_ref, near_ref, far_ref, wanted_ref, mask_ref, factor_ref, win_ref, wout_ref,
                  loss_ref, grad_ref, grad_far_ref, gin_ref, gout_ref,
                  table, inner_all, hidden_all, point_all, out_all, gout_all, sums):
    block = pl.program_id(0)
    half = near_ref.shape[1]
    cells = 2 * half
    group = table.shape[2]
    rays = samples_ref.shape[2]
    planes = near_ref.shape[0]

    @pl.when(block == 0)
    def _():
        loss_ref[...] = jnp.zeros_like(loss_ref)
        gin_ref[...] = jnp.zeros_like(gin_ref)
        gout_ref[...] = jnp.zeros_like(gout_ref)
        sums[...] = jnp.zeros_like(sums)
        table[...] = jnp.zeros_like(table)
        for plane in range(planes):
            turned = jnp.concatenate([near_ref[plane], far_ref[plane]], 0).T
            for g in range(GROUPS):
                width = min(group, cells - g * group)
                table[plane, g * CH : (g + 1) * CH, :width] = turned[:CH, g * group : g * group + width]

    step = 4
    width = step * rays
    win, wout = win_ref[...], wout_ref[...]

    def places_read(plane, s):
        rows = [samples_ref[plane, s + n : s + n + 1, :] for n in range(step)]
        at = jnp.concatenate(rows, 1)
        owner = at // group
        within = at - owner * group
        hot = lax.broadcasted_iota(jnp.int32, (group, width), 0) == within
        return owner, jnp.where(hot, 1.0, 0.0).astype(jnp.bfloat16)

    def tn_dot(left, right):
        return lax.dot_general(left, right, (((0,), (0,)), ((), ())), preferred_element_type=jnp.float32)

    for s in range(0, S, step):
        here = pl.ds(s * rays, width)
        point = jnp.zeros((CH, width), jnp.float32)
        for plane in range(planes):
            owner, hot = places_read(plane, s)
            found = product(table[plane], hot)
            value = found[:CH]
            for g in range(1, GROUPS):
                value = jnp.where(owner == g, found[g * CH : (g + 1) * CH], value)
            point = point + value
        point = point.astype(jnp.bfloat16)
        inner = tn_dot(win, point)
        hidden = (inner * jax.nn.sigmoid(inner)).astype(jnp.bfloat16)
        out_all[:, here] = tn_dot(wout, hidden)
        inner_all[:, here] = inner
        hidden_all[:, here] = hidden
        point_all[:, here] = point

    factor = factor_ref[0]
    mask = mask_ref[...]
    row = lax.broadcasted_iota(jnp.int32, (8, rays), 0)
    is_colour = (row >= 1) & (row <= 3)
    before = jnp.zeros((1, rays), jnp.float32)
    rgb = jnp.zeros((8, rays), jnp.float32)
    kept = []
    for s in range(S):
        out = out_all[:, s * rays : (s + 1) * rays]
        level = out[0:1]
        absorb = (4.0 / S) * (jnp.maximum(level, 0.0) + jnp.log1p(jnp.exp(-jnp.abs(level))))
        weight = jnp.exp(-before) * (1.0 - jnp.exp(-absorb))
        before = before + absorb
        colour = jax.nn.sigmoid(out)
        rgb = rgb + weight * colour
        kept.append((weight, jnp.exp(-before), colour))
    error = jnp.where(is_colour, rgb - wanted_ref[...], 0.0)
    loss_ref[...] += jnp.sum(mask * jnp.sum(error * error, 0, keepdims=True))
    pull = error * (2.0 * factor * mask)
    tail = jnp.zeros((1, rays), jnp.float32)
    for s in reversed(range(S)):
        weight, left_over, colour = kept[s]
        to_weight = jnp.sum(pull * colour, 0, keepdims=True)
        to_absorb = to_weight * left_over - tail
        tail = tail + to_weight * weight
        to_level = (4.0 / S) * to_absorb * colour[0:1]
        to_colour = weight * pull * colour * (1.0 - colour)
        gout_all[:, s * rays : (s + 1) * rays] = jnp.where(row == 0, to_level, to_colour).astype(jnp.bfloat16)

    for s in range(0, S, step):
        here = pl.ds(s * rays, width)
        pulled = gout_all[:, here]
        inner = inner_all[:, here]
        gate = jax.nn.sigmoid(inner)
        grad_inner = product(wout, pulled) * (gate * (1.0 + inner * (1.0 - gate)))
        grad_inner = grad_inner.astype(jnp.bfloat16)
        gout_ref[...] += nt_dot(hidden_all[:, here], pulled)
        gin_ref[...] += nt_dot(point_all[:, here], grad_inner)
        grad_point = product(win, grad_inner)
        coarse = grad_point.astype(jnp.bfloat16).astype(jnp.float32)
        fine = grad_point - coarse
        for plane in range(planes):
            owner, hot = places_read(plane, s)
            rows = [jnp.where(owner == g, coarse, 0.0) for g in range(GROUPS)]
            rows += [jnp.where(owner == g, fine, 0.0) for g in range(GROUPS)]
            stacked = jnp.concatenate(rows, 0).astype(jnp.bfloat16)
            added = nt_dot(stacked, hot)
            sums[plane] += added[: GROUPS * CH] + added[GROUPS * CH :]

    @pl.when(block == pl.num_programs(0) - 1)
    def _():
        for plane in range(planes):
            for g in range(GROUPS):
                for low, high, ref in ((0, half, grad_ref), (half, cells, grad_far_ref)):
                    start, stop = max(g * group, low), min((g + 1) * group, high)
                    if start < stop:
                        part = sums[plane, g * CH : (g + 1) * CH, start - g * group : stop - g * group]
                        ref[plane, :, start - low : stop - low] = part.astype(jnp.bfloat16)


def render(near, far, samples, wanted, mask, factor, decode_in, decode_out, rays):
    planes, half, _ = near.shape
    count = 2 * half
    all_rays = samples.shape[2]
    group = -(-count // (GROUPS * 128)) * 128
    points = S * rays
    whole = lambda *shape: pl.BlockSpec(shape, lambda n: (0,) * len(shape))
    return pl.pallas_call(
        render_kernel,
        grid=(all_rays // rays,),
        in_specs=[
            pl.BlockSpec((planes, S, rays), lambda n: (0, 0, n)),
            whole(*near.shape),
            whole(*far.shape),
            pl.BlockSpec((8, rays), lambda n: (0, n)),
            pl.BlockSpec((1, rays), lambda n: (0, n)),
            pl.BlockSpec(memory_space=pltpu.SMEM),
            whole(CH, DEC_HID),
            whole(DEC_HID, 8),
        ],
        out_specs=[whole(8, 128), whole(planes, CH, half), whole(planes, CH, half), whole(CH, DEC_HID), whole(DEC_HID, 8)],
        out_shape=[
            jax.ShapeDtypeStruct((8, 128), jnp.float32),
            jax.ShapeDtypeStruct((planes, CH, half), jnp.bfloat16),
            jax.ShapeDtypeStruct((planes, CH, half), jnp.bfloat16),
            jax.ShapeDtypeStruct((CH, DEC_HID), jnp.float32),
            jax.ShapeDtypeStruct((DEC_HID, 8), jnp.float32),
        ],
        scratch_shapes=[
            pltpu.VMEM((planes, GROUPS * CH, group), jnp.bfloat16),
            pltpu.VMEM((DEC_HID, points), jnp.float32),
            pltpu.VMEM((DEC_HID, points), jnp.bfloat16),
            pltpu.VMEM((CH, points), jnp.bfloat16),
            pltpu.VMEM((8, points), jnp.float32),
            pltpu.VMEM((8, points), jnp.bfloat16),
            pltpu.VMEM((planes, GROUPS * CH, group), jnp.float32),
        ],
        compiler_params=pltpu.CompilerParams(vmem_limit_bytes=48 * 1024 * 1024),
        name="render",
    )(samples, near, far, wanted, mask, factor, decode_in, decode_out)


MESH_ID = pl.DeviceIdType.MESH


def places():
    p = lax.axis_index("dp")
    c = lax.axis_index("strip")
    z = p // 4
    flip_x = p + 1 - 2 * (p % 2)
    flip_y = p + 2 - 4 * ((p // 2) % 2)
    both = flip_x + flip_y - p
    near = (1 - c) * flip_x + c * flip_y
    far = (1 - c) * flip_y + c * flip_x
    return p, c, z, near, far, both


def along_z(line, z, k):
    return ((z + k) % 4) * 4 + line % 4


def enter(peers):
    barrier = pltpu.get_barrier_semaphore()
    for peer in peers:
        pl.semaphore_signal(barrier, inc=1, device_id=peer, device_id_type=MESH_ID)
    pl.semaphore_wait(barrier, len(peers))


def flat_chunks(rows, n):
    part = rows // n
    return n, part, lambda p, c, j: (2 * p + c) * rows + j * part


def block_chunk(p, c, k):
    second = p // 8
    return ((1 - second) * ((2 * c + k) * 8 + p) + second * (4 * p + 2 * c + k)) * BLOCK


ORDER = [("near", 0), ("z", 1), ("z", 3), ("far", 0), ("z", 2), ("near", 1), ("near", 3), ("near", 2)]
ORDER += [("both", 0), ("far", 1), ("far", 3), ("far", 2), ("both", 1), ("both", 3), ("both", 2)]
ORDER += [("core", i) for i in range(16)]

def gather_kernel(layouts, stagger, *refs):
    count = len(layouts)
    fulls = refs[count + 1 : 2 * count + 1]
    line_full = refs[2 * count + 1]
    send, recv, local, line_sems = refs[2 * count + 2 : 2 * count + 6]
    held = refs[2 * count + 6 :]
    brought = [pltpu.make_async_copy(s, h, local.at[n]) for n, (s, h) in enumerate(zip(refs[: count + 1], held))]
    for copy in brought:
        copy.start()
    sources, line_source = held[:count], held[count]
    p, c, z, near, far, both = places()
    zs = [along_z(p, z, k) for k in range(4)]
    enter([(q, c) for q in zs[1:]] + [(near, c), (far, c), (p, 1 - c)])
    for copy in brought:
        copy.wait()
    jobs = [(a, j) for a, layout in enumerate(layouts) for j in range(layout[0])]

    def target(owner, job):
        a, j = jobs[job]
        _, rows, place = layouts[a]
        return fulls[a].at[pl.ds(pl.multiple_of(place(*owner, j), 8), rows)]

    def source(job):
        a, j = jobs[job]
        rows = layouts[a][1]
        return sources[a].at[pl.ds(j * rows, rows)]

    started = []

    def forward(owner, own, event, peer, job):
        t = target(owner, job)
        copy = pltpu.make_async_remote_copy(
            source(job) if own else t, t, send.at[event, job], recv.at[event, job], device_id=peer, device_id_type=MESH_ID
        )
        copy.start()
        started.append(copy)

    def arrive(owner, event, job):
        t = target(owner, job)
        pltpu.make_async_remote_copy(
            t, t, send.at[event, job], recv.at[event, job], device_id=(p, 1 - c), device_id_type=MESH_ID
        ).wait_recv()

    me = (p, c)

    def begin(job):
        forward(me, True, 3, (near, c), job)
        for k in (1, 3, 2):
            forward(me, True, 3 - k, (zs[k], c), job)
        forward(me, True, 7, (far, c), job)
        forward(me, True, 15, (p, 1 - c), job)
        pltpu.make_async_copy(source(job), target(me, job), local.at[job]).start()

    def take(kind, k, job):
        if kind == "z":
            owner = (zs[k], c)
            arrive(owner, k - 1, job)
            forward(owner, False, 3 + k, (near, c), job)
            forward(owner, False, 7 + k, (far, c), job)
            forward(owner, False, 15 + k, (p, 1 - c), job)
        elif kind == "near":
            owner = (along_z(near, z, k), c)
            arrive(owner, 3 + k, job)
            forward(owner, False, 11 + k, (far, c), job)
            forward(owner, False, 19 + k, (p, 1 - c), job)
        elif kind == "far":
            owner = (along_z(far, z, k), c)
            arrive(owner, 7 + k, job)
            forward(owner, False, 23 + k, (p, 1 - c), job)
        elif kind == "both":
            owner = (along_z(both, z, k), c)
            arrive(owner, 11 + k, job)
            forward(owner, False, 27 + k, (p, 1 - c), job)
        elif kind == "core":
            line = (p, far, near, both)[k // 4]
            arrive((along_z(line, z, k % 4), 1 - c), 15 + k, job)

    lines = []
    for k in (1, 3, 2):
        lines.append(
            pltpu.make_async_remote_copy(
                line_source, line_full.at[4 - k], line_sems.at[k], line_sems.at[7 - k],
                device_id=(zs[k], c), device_id_type=MESH_ID,
            )
        )
    lines.append(pltpu.make_async_copy(line_source, line_full.at[0], line_sems.at[0]))

    steps = [(stagger * len(jobs) - 4, -2, 0)]
    for job in range(len(jobs)):
        steps.append((stagger * job, -1, job))
        for i in range(len(ORDER)):
            steps.append((stagger * job + i + 1, i, job))
    for _, i, job in sorted(steps):
        if i == -2:
            for copy in lines:
                copy.start()
        elif i < 0:
            begin(job)
        else:
            take(*ORDER[i], job)
    for k in (1, 2, 3):
        spot = line_full.at[k]
        pltpu.make_async_remote_copy(
            spot, spot, line_sems.at[k], line_sems.at[3 + k], device_id=(p, 1 - c), device_id_type=MESH_ID
        ).wait_recv()
    for copy in lines[:3]:
        copy.wait_send()
    lines[3].wait()
    for copy in started:
        copy.wait_send()
    for job in range(len(jobs)):
        pltpu.make_async_copy(source(job), target(me, job), local.at[job]).wait()


def gather_all(layouts, stagger, shards_in, line, name_id):
    copies = sum(l[0] for l in layouts)
    everywhere = pl.BlockSpec(memory_space=pl.ANY)
    shapes = [jax.ShapeDtypeStruct((32 * s.shape[0],) + s.shape[1:], s.dtype) for s in shards_in]
    shapes.append(jax.ShapeDtypeStruct((4,) + line.shape, line.dtype))
    return pl.pallas_call(
        functools.partial(gather_kernel, layouts, stagger),
        out_shape=shapes,
        in_specs=[everywhere] * len(shapes),
        out_specs=[everywhere] * len(shapes),
        scratch_shapes=[
            pltpu.SemaphoreType.DMA((31, copies)),
            pltpu.SemaphoreType.DMA((31, copies)),
            pltpu.SemaphoreType.DMA((copies,)),
            pltpu.SemaphoreType.DMA((7,)),
        ]
        + [pltpu.VMEM(a.shape, a.dtype) for a in (*shards_in, line)],
        compiler_params=pltpu.CompilerParams(collective_id=name_id, has_side_effects=True),
        name="gather_all",
    )(*shards_in, line)


SUM_ORDER = [(3, 0), (3, 1), (3, 3), (3, 2), (2, 0), (2, 1), (2, 3), (2, 2)]
SUM_ORDER += [(1, 1), (1, 3), (1, 2), (1, 0), (0, 1), (0, 3), (0, 2), (0, 0)]
AHEAD = 3


def scatter_kernel(layouts, stagger, *refs):
    count = len(layouts)
    grads = refs[:count]
    line_grad = refs[count]
    outs = refs[count + 1 : 2 * count + 1]
    line_out = refs[2 * count + 1]
    scratch = refs[2 * count + 2 :]
    line_own, line_got, line_sum, line_sems = scratch[-4:]
    p, c, z, near, far, both = places()
    zs = [along_z(p, z, k) for k in range(4)]
    enter([(q, c) for q in zs[1:]] + [(near, c), (far, c), (p, 1 - c)])
    csend, crecv, bsend, brecv, load_sem, out_sem = scratch[:6]
    buffers = [scratch[6 + 6 * a : 12 + 6 * a] for a in range(count)]
    jobs = [(a, j) for a, layout in enumerate(layouts) for j in range(layout[0])]
    lines = (p, near, far, both)
    partner_lines = (p, far, near, both)

    def view(job, ref, slot):
        a, j = jobs[job]
        rows = layouts[a][1]
        return ref.at[slot, pl.ds(j * rows, rows)]

    def piece(owner, job):
        a, j = jobs[job]
        _, rows, place = layouts[a]
        return grads[a].at[pl.ds(pl.multiple_of(place(*owner, j), 8), rows)]

    def to_core(i, job):
        g, k = SUM_ORDER[i]
        owner = (along_z(partner_lines[g], z, k), 1 - c)
        rc = buffers[jobs[job][0]][0]
        return pltpu.make_async_remote_copy(
            piece(owner, job), view(job, rc, g * 4 + k), csend.at[i, job], crecv.at[i, job],
            device_id=(p, 1 - c), device_id_type=MESH_ID,
        )

    def load(i, job):
        g, k = SUM_ORDER[i]
        own = buffers[jobs[job][0]][4]
        return pltpu.make_async_copy(
            piece((along_z(lines[g], z, k), c), job), view(job, own, i % AHEAD), load_sem.at[i, job]
        )

    def onward(i, job):
        g, k = SUM_ORDER[i]
        rc, rb, ra, rz = buffers[jobs[job][0]][:4]
        if g == 3:
            target, event, peer = view(job, rb, 4 + k), 4 + k, (far, c)
        elif g == 2:
            target, event, peer = view(job, rb, k), k, (far, c)
        elif g == 1:
            target, event, peer = view(job, ra, k), 8 + k, (near, c)
        else:
            target, event, peer = view(job, rz, 3 - k), 12 + 3 - k, (zs[k], c)
        return pltpu.make_async_remote_copy(
            view(job, rc, g * 4 + k), target, bsend.at[event, job], brecv.at[event, job],
            device_id=peer, device_id_type=MESH_ID,
        )

    def landed(event, job):
        rc, rb, ra, rz = buffers[jobs[job][0]][:4]
        if event < 8:
            target = view(job, rb, event)
        elif event < 12:
            target = view(job, ra, event - 8)
        else:
            target = view(job, rz, event - 12)
        pltpu.make_async_remote_copy(
            target, target, bsend.at[event, job], brecv.at[event, job], device_id=(p, 1 - c), device_id_type=MESH_ID
        ).wait_recv()
        return target

    def add_up(parts, target):
        rows = target.shape[0]
        step = math.gcd(rows, 16)

        @pl.loop(0, rows // step)
        def _(n):
            at = pl.ds(pl.multiple_of(n * step, step), step)
            total = parts[0][at].astype(jnp.float32)
            for part in parts[1:]:
                total = total + part[at].astype(jnp.float32)
            target[at] = total.astype(target.dtype)

    def start(i, job):
        to_core(i, job).start()
        load(i, job).start()

    def final_copies(job):
        a, j = jobs[job]
        rows = layouts[a][1]
        return [pltpu.make_async_copy(view(job, buffers[a][5], 0), outs[a].at[pl.ds(j * rows, rows)], out_sem.at[job, 0])]

    line_sends = [
        pltpu.make_async_remote_copy(
            line_grad.at[k], line_got.at[3 - k], line_sems.at[k], line_sems.at[7 - k],
            device_id=(zs[k], c), device_id_type=MESH_ID,
        )
        for k in (1, 3, 2)
    ]
    line_load = pltpu.make_async_copy(line_grad.at[0], line_own, line_sems.at[0])
    half = line_own.shape[0]
    spot = line_out.at[pl.ds(pl.multiple_of(c * half, 8), half)]
    line_stores = [
        pltpu.make_async_copy(line_sum, spot, line_sems.at[7]),
        pltpu.make_async_remote_copy(
            line_sum, spot, line_sems.at[8], line_sems.at[9], device_id=(p, 1 - c), device_id_type=MESH_ID
        ),
    ]

    def line_finish():
        line_load.wait()
        for k in (1, 2, 3):
            target = line_got.at[k - 1]
            pltpu.make_async_remote_copy(
                target, target, line_sems.at[k], line_sems.at[3 + k], device_id=(p, 1 - c), device_id_type=MESH_ID
            ).wait_recv()
        add_up([line_own] + [line_got.at[n] for n in range(3)], line_sum)
        for copy in line_stores:
            copy.start()

    def step(i, job):
        g, k = SUM_ORDER[i]
        rc, rb, ra, rz, own, done = buffers[jobs[job][0]]
        load(i, job).wait()
        to_core(i, job).wait_recv()
        here = view(job, rc, g * 4 + k)
        parts = [here, view(job, own, i % AHEAD)]
        if g == 1:
            parts.append(landed(4 + k, job))
        if g == 0:
            parts.append(landed(k, job))
            parts.append(landed(8 + k, job))
        if (g, k) == (0, 0):
            parts += [landed(12 + n, job) for n in range(3)]
            add_up(parts, view(job, done, 0))
            for copy in final_copies(job):
                copy.start()
        else:
            add_up(parts, here)
            onward(i, job).start()
        if i + AHEAD < 16:
            start(i + AHEAD, job)

    for copy in line_sends:
        copy.start()
    line_load.start()
    for job in range(len(jobs)):
        for n in range(AHEAD):
            start(n, job)
    steps = []
    for job in range(len(jobs)):
        begin = stagger * min(job, layouts[0][0] - 1)
        for i in range(16):
            steps.append((begin + i + 2 * (i // 4 - 1) * (i // 8), job, i))
    steps.append((max(steps)[0] - 6, 0, -1))
    for _, job, i in sorted(steps):
        if i < 0:
            line_finish()
        else:
            step(i, job)
    for job in range(len(jobs)):
        for i in range(16):
            to_core(i, job).wait_send()
            if i < 15:
                onward(i, job).wait_send()
        for copy in final_copies(job):
            copy.wait()
    for copy in line_sends:
        copy.wait_send()
    for copy in line_stores:
        copy.wait()


def scatter_sum(layouts, stagger, grads, line, name_id):
    jobs = sum(l[0] for l in layouts)
    scratch = [
        pltpu.SemaphoreType.DMA((16, jobs)),
        pltpu.SemaphoreType.DMA((16, jobs)),
        pltpu.SemaphoreType.DMA((15, jobs)),
        pltpu.SemaphoreType.DMA((15, jobs)),
        pltpu.SemaphoreType.DMA((16, jobs)),
        pltpu.SemaphoreType.DMA((jobs, 3)),
    ]
    shapes = []
    for layout, grad in zip(layouts, grads):
        rows, width = layout[0] * layout[1], grad.shape[1]
        for slots in (16, 8, 4, 3, AHEAD):
            scratch.append(pltpu.VMEM((slots, rows, width), grad.dtype))
        scratch.append(pltpu.VMEM((1, rows, width), jnp.float32))
        shapes.append(jax.ShapeDtypeStruct((rows, width), jnp.float32))
    piece = line.shape[1:]
    scratch += [pltpu.VMEM(piece, line.dtype), pltpu.VMEM((3,) + piece, line.dtype), pltpu.VMEM(piece, line.dtype)]
    scratch.append(pltpu.SemaphoreType.DMA((10,)))
    shapes.append(jax.ShapeDtypeStruct((2 * piece[0], piece[1]), line.dtype))
    everywhere = pl.BlockSpec(memory_space=pl.ANY)
    return pl.pallas_call(
        functools.partial(scatter_kernel, layouts, stagger),
        out_shape=shapes,
        in_specs=[everywhere] * len(shapes),
        out_specs=[everywhere] * len(shapes),
        scratch_shapes=scratch,
        compiler_params=pltpu.CompilerParams(
            collective_id=name_id, has_side_effects=True, vmem_limit_bytes=48 * 1024 * 1024
        ),
        name="scatter_sum",
    )(*grads, line)


GELU_A = math.sqrt(2.0 / math.pi)
GELU_B = 0.044715


def chunk_sources():
    p, c, z, _, _, _ = places()
    x, y = p % 2, (p // 2) % 2
    out = []
    for other in range(2):
        core = (c + other) % 2
        for g in range(4):
            dx = (1 - core) * (g % 2) + core * (g // 2)
            dy = (1 - core) * (g // 2) + core * (g % 2)
            for k in range(4):
                owner = ((z + k) % 4) * 4 + ((y + dy) % 2) * 2 + (x + dx) % 2
                for half in range(2):
                    out.append((other, g, k, half, block_chunk(owner, core, half) // BLOCK))
    return out


def panel_loads(refs, held, sems):
    if len(refs) == 1:
        for n in range(held.shape[0] // WIDE):
            at = pl.ds(n * WIDE, WIDE)
            pltpu.make_async_copy(refs[0].at[at], held.at[at], sems.at[n]).start()
        return
    for other, g, k, half, chunk in chunk_sources():
        source = refs[other * 4 + g].at[k, pl.ds(half * BLOCK, BLOCK)]
        target = held.at[pl.ds(pl.multiple_of(chunk * BLOCK, BLOCK), BLOCK)]
        pltpu.make_async_copy(source, target, sems.at[chunk // 8]).start()


def panel_ready(held, sems, n):
    at = pl.ds(pl.multiple_of(n * WIDE, WIDE), WIDE)
    pltpu.make_async_copy(held.at[at], held.at[at], sems.at[n]).wait()
    return held.at[at]


def mlp_fwd_kernel(count, *refs):
    sources = refs[:count]
    h_ref, s_ref, up_ref, act_ref, grid_ref, held, total, sems = refs[count:]
    step = pl.program_id(0)
    steps = pl.num_programs(0)

    @pl.when(step == 0)
    def _():
        panel_loads(sources, held, sems)
        total[...] = s_ref[...]

    up = product(h_ref[...], panel_ready(held, sems, step)[...])
    up_ref[0] = up
    act = 0.5 * up * (1.0 + jnp.tanh(GELU_A * (up + GELU_B * up * up * up)))
    act = act.astype(jnp.bfloat16)
    act_ref[0] = act
    total[...] += product(act, panel_ready(held, sems, steps + step)[...])

    @pl.when(step == steps - 1)
    def _():
        grid_ref[...] = total[...].astype(jnp.bfloat16)


def mlp_fwd(panels, hidden, stream):
    rows = hidden.shape[0]
    steps = HID // WIDE
    whole = pl.BlockSpec((rows, WIDE), lambda n: (0, 0))
    part = pl.BlockSpec((1, rows, WIDE), lambda n: (n, 0, 0))
    return pl.pallas_call(
        functools.partial(mlp_fwd_kernel, len(panels)),
        grid=(steps,),
        in_specs=[pl.BlockSpec(memory_space=pl.ANY)] * len(panels) + [whole, whole],
        out_specs=[part, part, whole],
        out_shape=[
            jax.ShapeDtypeStruct((steps, rows, WIDE), jnp.float32),
            jax.ShapeDtypeStruct((steps, rows, WIDE), jnp.bfloat16),
            jax.ShapeDtypeStruct((rows, WIDE), jnp.bfloat16),
        ],
        scratch_shapes=[
            pltpu.VMEM((2 * HID, WIDE), jnp.bfloat16),
            pltpu.VMEM((rows, WIDE), jnp.float32),
            pltpu.SemaphoreType.DMA((2 * steps,)),
        ],
        compiler_params=pltpu.CompilerParams(vmem_limit_bytes=56 * 1024 * 1024),
        cost_estimate=BRIEF,
        name="mlp_fwd",
    )(*panels, hidden, stream)


def mlp_bwd_kernel(count, *refs):
    sources = refs[:count]
    outs = 2 if count > 1 else 1
    h_ref, g_ref, up_ref, act_ref = refs[count : count + 4]
    dh_ref = refs[count + 4]
    grads = refs[count + 5 : count + 5 + outs]
    held, staged, sems, out_sem = refs[count + 5 + outs :]
    step = pl.program_id(0)
    steps = pl.num_programs(0)

    @pl.when(step == 0)
    def _():
        panel_loads(sources, held, sems)
        dh_ref[...] = jnp.zeros_like(dh_ref)

    def tn_dot(left, right):
        return lax.dot_general(left, right, (((0,), (0,)), ((), ())), preferred_element_type=jnp.float32)

    def drain(side):
        pltpu.make_async_copy(staged.at[side], staged.at[side], out_sem.at[side]).wait()

    def store(side):
        panel = side * steps + step
        source = staged.at[side]
        if count == 1:
            at = pl.ds(pl.multiple_of(panel * WIDE, WIDE), WIDE)
            pltpu.make_async_copy(source, grads[0].at[at], out_sem.at[side]).start()
            return
        p, c, z, _, _, _ = places()
        for n in range(8):
            if side == 0:
                owner, core, half = n, step // 2, step % 2
            else:
                row = step * 8 + n
                owner, core, half = 8 + row // 4, (n // 2) % 2, n % 2
            dx = (owner % 2 + p % 2) % 2
            dy = ((owner // 2) % 2 + (p // 2) % 2) % 2
            g = (1 - core) * (dx + 2 * dy) + core * (dy + 2 * dx)
            spot = g * 4 + (owner // 4 - z + 4) % 4
            at = pl.ds(pl.multiple_of(half * BLOCK, BLOCK), BLOCK)
            from_ref = source.at[pl.ds(n * BLOCK, BLOCK)]

            @pl.when((core + c) % 2 == 0)
            def _():
                pltpu.make_async_copy(from_ref, grads[0].at[spot, at], out_sem.at[side]).start()

            @pl.when((core + c) % 2 == 1)
            def _():
                pltpu.make_async_copy(from_ref, grads[1].at[spot, at], out_sem.at[side]).start()

    pulled = g_ref[...]

    @pl.when(step > 0)
    def _():
        drain(1)

    staged[1] = tn_dot(act_ref[0], pulled).astype(jnp.bfloat16)
    store(1)
    grad_act = nt_dot(pulled, panel_ready(held, sems, steps + step)[...])
    up = up_ref[0]
    square = up * up
    bend = jnp.tanh(GELU_A * up * (1.0 + GELU_B * square))
    slope = 0.5 * (1.0 + bend) + 0.5 * GELU_A * up * (1.0 - bend * bend) * (1.0 + 3.0 * GELU_B * square)
    grad_up = (grad_act * slope).astype(jnp.bfloat16)

    @pl.when(step > 0)
    def _():
        drain(0)

    staged[0] = tn_dot(h_ref[...], grad_up).astype(jnp.bfloat16)
    store(0)
    dh_ref[...] += nt_dot(grad_up, panel_ready(held, sems, step)[...])

    @pl.when(step == steps - 1)
    def _():
        drain(0)
        drain(1)


def mlp_bwd(panels, hidden, grad, up, act):
    rows = hidden.shape[0]
    steps = HID // WIDE
    whole = pl.BlockSpec((rows, WIDE), lambda n: (0, 0))
    part = pl.BlockSpec((1, rows, WIDE), lambda n: (n, 0, 0))
    if len(panels) == 1:
        shapes = [jax.ShapeDtypeStruct((2 * HID, WIDE), jnp.bfloat16)]
    else:
        shapes = [jax.ShapeDtypeStruct((16, 2 * BLOCK, WIDE), jnp.bfloat16)] * 2
    return pl.pallas_call(
        functools.partial(mlp_bwd_kernel, len(panels)),
        grid=(steps,),
        in_specs=[pl.BlockSpec(memory_space=pl.ANY)] * len(panels) + [whole, whole, part, part],
        out_specs=[whole] + [pl.BlockSpec(memory_space=pl.ANY)] * len(shapes),
        out_shape=[jax.ShapeDtypeStruct((rows, WIDE), jnp.float32)] + shapes,
        scratch_shapes=[
            pltpu.VMEM((2 * HID, WIDE), jnp.bfloat16),
            pltpu.VMEM((2, WIDE, WIDE), jnp.bfloat16),
            pltpu.SemaphoreType.DMA((2 * steps,)),
            pltpu.SemaphoreType.DMA((2,)),
        ],
        compiler_params=pltpu.CompilerParams(vmem_limit_bytes=58 * 1024 * 1024),
        cost_estimate=BRIEF,
        name="mlp_bwd",
    )(*panels, hidden, grad, up, act)


SLOT = 128
TAPS = 16


def spread_deconv_kernel(first, rows_ref, o_ref, raw, flat, turned, sem):
    load = pltpu.make_async_copy(rows_ref.at[pl.ds(first, raw.shape[0])], raw, sem)
    load.start()
    load.wait()
    whole = raw[...].reshape(TAPS * CH, WIDE).astype(jnp.float32)
    for n in range(WIDE // SLOT):
        flat[n] = whole[:, n * SLOT : (n + 1) * SLOT]
    lane = lax.broadcasted_iota(jnp.int32, (D // 4, SLOT), 1)

    def block(i, j):
        at = 10 * i + j
        return flat[at % 8, pl.ds(at // 8, D // 4, stride=5), :]

    for tap in range(TAPS):
        j, start = divmod(tap * CH, SLOT)
        for i in range(4):
            part = block(i, j)
            if start:
                part = pltpu.roll(part, SLOT - start, 1)
            if start + CH > SLOT:
                part = jnp.where(lane < SLOT - start, part, pltpu.roll(block(i, j + 1), SLOT - start, 1))
            turned[pl.ds(i, D // 4, stride=4), :] = jnp.where(lane < CH, part, 0.0)
        o_ref[:, tap * SLOT : (tap + 1) * SLOT] = turned[...].astype(jnp.bfloat16)


def spread_deconv(rows, first):
    return pl.pallas_call(
        functools.partial(spread_deconv_kernel, first),
        in_specs=[pl.BlockSpec(memory_space=pl.ANY)],
        out_specs=pl.BlockSpec(memory_space=pltpu.VMEM),
        out_shape=jax.ShapeDtypeStruct((D, TAPS * SLOT), jnp.bfloat16),
        scratch_shapes=[
            pltpu.VMEM((TAPS * CH // 8, 8, WIDE), jnp.bfloat16),
            pltpu.VMEM((WIDE // SLOT, TAPS * CH, SLOT), jnp.float32),
            pltpu.VMEM((D, SLOT), jnp.float32),
            pltpu.SemaphoreType.DMA,
        ],
        compiler_params=pltpu.CompilerParams(vmem_limit_bytes=32 * 1024 * 1024),
        name="spread_deconv",
    )(rows)


def with_edges(own, edge):
    place = lax.axis_index("strip")
    above = jnp.where(place == 0, jnp.zeros_like(edge), edge)
    below = jnp.where(place == 0, edge, jnp.zeros_like(edge))
    return jnp.concatenate([above, own, below], 0)


def moved(value, step):
    column = lax.broadcasted_iota(jnp.int32, value.shape, 0) % TC
    inside = (column + step >= 0) & (column + step < TC)
    return jnp.where(inside, pltpu.roll(value, (-step) % value.shape[0], 0), 0.0)


def deconv_fwd_kernel(grid_ref, edge_ref, w_ref, o_ref, taps, fine):
    padded = with_edges(grid_ref[0], edge_ref[0])
    rows = grid_ref.shape[1]
    taps[...] = product(padded, w_ref[...])

    def tap(kr, kc, r):
        slot = kr * 4 + kc
        return taps[pl.ds((r + 1) * TC, rows), slot * SLOT : (slot + 1) * SLOT]

    for i in range(2):
        for j in range(2):
            total = tap(i + 1, j + 1, 0) + tap(3 - 3 * i, j + 1, 2 * i - 1)
            side = tap(i + 1, 3 - 3 * j, 0) + tap(3 - 3 * i, 3 - 3 * j, 2 * i - 1)
            total = total + moved(side, 2 * j - 1)
            for a in range(rows // TC):
                fine[pl.ds((2 * a + i) * 2 * TC + j, TC, stride=2), :] = total[a * TC : (a + 1) * TC]
    o_ref[0] = fine[...].astype(jnp.bfloat16)


def deconv_fwd(grid, edge, weights):
    planes, rows, _ = grid.shape
    return pl.pallas_call(
        deconv_fwd_kernel,
        grid=(planes,),
        in_specs=[
            pl.BlockSpec((1, rows, D), lambda n: (n, 0, 0)),
            pl.BlockSpec((1, TC, D), lambda n: (n, 0, 0)),
            pl.BlockSpec(weights.shape, lambda n: (0, 0)),
        ],
        out_specs=pl.BlockSpec((1, 4 * rows, SLOT), lambda n: (n, 0, 0)),
        out_shape=jax.ShapeDtypeStruct((planes, 4 * rows, SLOT), jnp.bfloat16),
        scratch_shapes=[
            pltpu.VMEM((rows + 2 * TC, TAPS * SLOT), jnp.float32),
            pltpu.VMEM((4 * rows, SLOT), jnp.float32),
        ],
        compiler_params=pltpu.CompilerParams(vmem_limit_bytes=40 * 1024 * 1024),
        name="deconv_fwd",
    )(grid, edge, weights)


def deconv_bwd_kernel(own_ref, got_ref, grid_ref, edge_ref, w_ref, gx_ref, gedge_ref, gw_ref, fine, spread, tokens, sums, flat):
    plane = pl.program_id(0)
    rows = grid_ref.shape[1]
    high = rows + 2 * TC
    place = lax.axis_index("strip")
    total = own_ref[0].astype(jnp.float32) + got_ref[0].astype(jnp.float32)
    total = jnp.concatenate([total, jnp.zeros((SLOT - CH, total.shape[1]), jnp.float32)], 0)
    fine[...] = total.T
    here = pl.ds(plane * high, high)
    tokens[here] = with_edges(grid_ref[0], edge_ref[0])
    for i in range(2):
        for j in range(2):
            parts = [fine[pl.ds((2 * a + i) * 2 * TC + j, TC, stride=2), :] for a in range(rows // TC)]
            part = jnp.concatenate(parts, 0)
            for kr in (i + 1, 3 - 3 * i):
                for kc in (j + 1, 3 - 3 * j):
                    value = part if kc == j + 1 else moved(part, 1 - 2 * j)
                    start = TC if kr == i + 1 else (0 if i == 0 else 2 * TC)
                    pieces = [value]
                    if start:
                        pieces.insert(0, jnp.zeros((start, SLOT), jnp.float32))
                    if high - rows - start:
                        pieces.append(jnp.zeros((high - rows - start, SLOT), jnp.float32))
                    slot = kr * 4 + kc
                    spread[here, slot * SLOT : (slot + 1) * SLOT] = jnp.concatenate(pieces, 0).astype(jnp.bfloat16)
    back = nt_dot(spread[here], w_ref[...])
    gx_ref[0] = back[TC : TC + rows]
    gedge_ref[0] = jnp.where(place == 0, back[TC + rows :], back[:TC]).astype(jnp.bfloat16)

    @pl.when(plane == pl.num_programs(0) - 1)
    def _():
        wide = 512
        for n in range(TAPS * SLOT // wide):
            columns = slice(n * wide, (n + 1) * wide)
            part = lax.dot_general(
                tokens[...], spread[:, columns], (((0,), (0,)), ((), ())), preferred_element_type=jnp.float32
            )
            for m in range(wide // SLOT):
                sums[n * (wide // SLOT) + m] = part[:, m * SLOT : (m + 1) * SLOT]
        lane = lax.broadcasted_iota(jnp.int32, (D // 4, SLOT), 1)
        for i in range(4):
            for j in range(TAPS * CH // SLOT):
                block = None
                for tap in range(j * SLOT // CH, (j * SLOT + SLOT - 1) // CH + 1):
                    part = sums[tap, pl.ds(i, D // 4, stride=4), :]
                    shift = tap * CH - j * SLOT
                    if shift % SLOT:
                        part = pltpu.roll(part, shift % SLOT, 1)
                    block = part if block is None else jnp.where(lane < shift, block, part)
                at = 10 * i + j
                flat[at % 8, pl.ds(at // 8, D // 4, stride=5), :] = block
        whole = jnp.concatenate([flat[n] for n in range(WIDE // SLOT)], 1)
        gw_ref[...] = whole.astype(jnp.bfloat16).reshape(gw_ref.shape)


def deconv_bwd(own, got, grid, edge, weights):
    planes, rows, _ = grid.shape
    high = rows + 2 * TC
    by_plane = lambda *shape: pl.BlockSpec((1,) + shape, lambda n: (n, 0, 0))
    return pl.pallas_call(
        deconv_bwd_kernel,
        grid=(planes,),
        in_specs=[
            by_plane(*own.shape[1:]),
            by_plane(*got.shape[1:]),
            by_plane(rows, D),
            by_plane(TC, D),
            pl.BlockSpec(weights.shape, lambda n: (0, 0)),
        ],
        out_specs=[by_plane(rows, D), by_plane(TC, D), pl.BlockSpec((TAPS * CH // 8, 8, WIDE), lambda n: (0, 0, 0))],
        out_shape=[
            jax.ShapeDtypeStruct((planes, rows, D), jnp.float32),
            jax.ShapeDtypeStruct((planes, TC, D), jnp.bfloat16),
            jax.ShapeDtypeStruct((TAPS * CH // 8, 8, WIDE), jnp.bfloat16),
        ],
        scratch_shapes=[
            pltpu.VMEM((4 * rows, SLOT), jnp.float32),
            pltpu.VMEM((planes * high, TAPS * SLOT), jnp.bfloat16),
            pltpu.VMEM((planes * high, D), jnp.bfloat16),
            pltpu.VMEM((TAPS, D, SLOT), jnp.float32),
            pltpu.VMEM((WIDE // SLOT, TAPS * CH, SLOT), jnp.float32),
        ],
        compiler_params=pltpu.CompilerParams(vmem_limit_bytes=56 * 1024 * 1024),
        name="deconv_bwd",
    )(own, got, grid, edge, weights)


def panel_view(rows_ref, first, count, depth):
    region = rows_ref.at[pl.ds(first, depth // 8 * count)]
    return region.reshape(depth // 8, count, 8, WIDE)


def project_kernel(first, count, depth, lead, x_ref, rows_ref, *rest):
    outs, held, sems = rest[:-2], rest[-2], rest[-1]
    step = pl.program_id(0)
    panels = panel_view(rows_ref, first, count, depth)

    @pl.when(step == 0)
    def _():
        for n in range(count):
            pltpu.make_async_copy(panels.at[:, n], held.at[n], sems.at[n]).start()

    pltpu.make_async_copy(held.at[step], held.at[step], sems.at[step]).wait()
    result = product(x_ref[...], held[step].reshape(depth, WIDE)).astype(jnp.bfloat16)
    if lead:

        @pl.when(step == 0)
        def _():
            outs[0][...] = result

        @pl.when(step > 0)
        def _():
            outs[1][0] = result

    else:
        outs[0][0] = result


def project(x, rows, first, count, lead):
    tokens, depth = x.shape
    specs = [pl.BlockSpec((1, tokens, WIDE), lambda n: (jnp.maximum(n - lead, 0), 0, 0))]
    shapes = [jax.ShapeDtypeStruct((count - lead, tokens, WIDE), jnp.bfloat16)]
    if lead:
        specs.insert(0, pl.BlockSpec((tokens, WIDE), lambda n: (0, 0)))
        shapes.insert(0, jax.ShapeDtypeStruct((tokens, WIDE), jnp.bfloat16))
    return pl.pallas_call(
        functools.partial(project_kernel, first, count, depth, lead),
        grid=(count,),
        in_specs=[pl.BlockSpec((tokens, depth), lambda n: (0, 0)), pl.BlockSpec(memory_space=pl.ANY)],
        out_specs=specs,
        out_shape=shapes,
        scratch_shapes=[pltpu.VMEM((count, depth // 8, 8, WIDE), jnp.bfloat16), pltpu.SemaphoreType.DMA((count,))],
        compiler_params=pltpu.CompilerParams(vmem_limit_bytes=32 * 1024 * 1024),
        cost_estimate=BRIEF,
        name="project",
    )(x, rows)


def project_back_kernel(first, count, depth, lead_ref, g_ref, rows_ref, o_ref, held, sems):
    step = pl.program_id(0)
    panels = panel_view(rows_ref, first, count, depth)

    @pl.when(step == 0)
    def _():
        for n in range(count):
            pltpu.make_async_copy(panels.at[:, n], held.at[n], sems.at[n]).start()

    pltpu.make_async_copy(held.at[step], held.at[step], sems.at[step]).wait()
    grad = jnp.where(step == 0, lead_ref[...], g_ref[0])
    back = nt_dot(grad, held[step].reshape(depth, WIDE))

    @pl.when(step == 0)
    def _():
        o_ref[...] = back

    @pl.when(step > 0)
    def _():
        o_ref[...] += back


def project_back(lead, grads, rows, first, depth):
    others, tokens, _ = grads.shape
    count = others + 1
    return pl.pallas_call(
        functools.partial(project_back_kernel, first, count, depth),
        grid=(count,),
        in_specs=[
            pl.BlockSpec((tokens, WIDE), lambda n: (0, 0)),
            pl.BlockSpec((1, tokens, WIDE), lambda n: (jnp.maximum(n - 1, 0), 0, 0)),
            pl.BlockSpec(memory_space=pl.ANY),
        ],
        out_specs=pl.BlockSpec((tokens, depth), lambda n: (0, 0)),
        out_shape=jax.ShapeDtypeStruct((tokens, depth), jnp.float32),
        scratch_shapes=[pltpu.VMEM((count, depth // 8, 8, WIDE), jnp.bfloat16), pltpu.SemaphoreType.DMA((count,))],
        compiler_params=pltpu.CompilerParams(vmem_limit_bytes=32 * 1024 * 1024),
        cost_estimate=BRIEF,
        name="project_back",
    )(lead, grads, rows)


def weight_grads_kernel(products, copies, *refs):
    arrays = refs[: len(refs) - 8]
    out, left, right, staged, bounce, load_sem, store_sem, copy_sem = refs[len(refs) - 8 :]
    step = pl.program_id(0)
    steps = len(products)

    def loads(n):
        side, (a, a_pick), (b, b_pick), _, _ = products[n]
        slot = n % 2
        source_a = arrays[a] if a_pick is None else arrays[a].at[a_pick]
        source_b = arrays[b] if b_pick is None else arrays[b].at[b_pick]
        rows, deep = side
        return [
            pltpu.make_async_copy(source_a, left.at[slot, pl.ds(0, rows), pl.ds(0, deep)], load_sem.at[slot, 0]),
            pltpu.make_async_copy(source_b, right.at[slot, pl.ds(0, rows)], load_sem.at[slot, 1]),
        ]

    def stores(n):
        (rows, deep), _, _, first, panels = products[n]
        slot = n % 2
        count, at = panels
        source = staged.at[slot, pl.ds(0, deep // 8)]
        target = panel_view(out, first, count, deep).at[:, at]
        return pltpu.make_async_copy(source, target, store_sem.at[slot])

    def bounced(n):
        a, first, count = copies[n]
        held = bounce.at[pl.ds(sum(c[2] for c in copies[:n]), count)]
        return (
            pltpu.make_async_copy(arrays[a], held, copy_sem.at[n, 0]),
            pltpu.make_async_copy(held, out.at[pl.ds(first, count)], copy_sem.at[n, 1]),
        )

    for n in range(steps):

        @pl.when(step == n)
        def _():
            if n == 0:
                for job in loads(0):
                    job.start()
                for m in range(len(copies)):
                    bounced(m)[0].start()
            if n == 1:
                for m in range(len(copies)):
                    bounced(m)[0].wait()
                    bounced(m)[1].start()
            if n + 1 < steps:
                for job in loads(n + 1):
                    job.start()
            for job in loads(n):
                job.wait()
            if n >= 2:
                stores(n - 2).wait()
            rows, deep = products[n][0]
            slot = n % 2
            total = lax.dot_general(
                left[slot, :rows, :deep], right[slot, :rows], (((0,), (0,)), ((), ())), preferred_element_type=jnp.float32
            )
            staged[slot, : deep // 8] = total.astype(jnp.bfloat16).reshape(deep // 8, 8, WIDE)
            stores(n).start()
            if n == steps - 1:
                if n > 0:
                    stores(n - 1).wait()
                stores(n).wait()
                for m in range(len(copies)):
                    bounced(m)[1].wait()


def weight_grads(arrays, products, copies, tile_rows):
    rows = max(p[0][0] for p in products)
    deep = max(p[0][1] for p in products)
    everywhere = pl.BlockSpec(memory_space=pl.ANY)
    return pl.pallas_call(
        functools.partial(weight_grads_kernel, products, copies),
        grid=(len(products),),
        in_specs=[everywhere] * len(arrays),
        out_specs=everywhere,
        out_shape=jax.ShapeDtypeStruct((tile_rows, 8, WIDE), jnp.bfloat16),
        scratch_shapes=[
            pltpu.VMEM((2, rows, deep), jnp.bfloat16),
            pltpu.VMEM((2, rows, WIDE), jnp.bfloat16),
            pltpu.VMEM((2, deep // 8, 8, WIDE), jnp.bfloat16),
            pltpu.VMEM((sum(c[2] for c in copies), 8, WIDE), jnp.bfloat16),
            pltpu.SemaphoreType.DMA((2, 2)),
            pltpu.SemaphoreType.DMA((2,)),
            pltpu.SemaphoreType.DMA((len(copies), 2)),
        ],
        compiler_params=pltpu.CompilerParams(vmem_limit_bytes=60 * 1024 * 1024),
        cost_estimate=BRIEF,
        name="weight_grads",
    )(*arrays)


TILE = 8 * WIDE
KV_AT = D * D
QKV_AT = KV_AT + DI * 2 * D + D * D
GAP_AT = QKV_AT + D * 3 * D + D * D + D * 16 * CH + CH * DEC_HID + DEC_HID * 4
QKV_GAP = -QKV_AT % (3 * TILE)
END_GAP = -GAP_AT % TILE
TILES = {}
_tile = 0
for _name, _rows in (
    ("query_cross", D),
    ("keyval_cross", 2 * DI),
    ("out_cross", D),
    ("gap", QKV_GAP // WIDE),
    ("qkv_self", 3 * D),
    ("out_self", D),
    ("deconv", 16 * CH),
    ("decode", 8),
    ("modulate", 6 * NCAM),
    ("triplane", 0),
):
    TILES[_name] = _tile
    _tile += _rows // 8


def direct_links():
    return lax.axis_size("dp") == 16 and lax.axis_size("strip") == 2


def regroup(rows, first, back):
    tile = first + lax.broadcasted_iota(jnp.int32, (rows.shape[0], 1), 0) // 8

    def turned(panels):
        shape = (-1, panels, 8, WIDE) if back else (-1, 8, panels, WIDE)
        return rows.reshape(shape).transpose(0, 2, 1, 3).reshape(rows.shape)

    in_kv = (tile >= TILES["keyval_cross"]) & (tile < TILES["out_cross"])
    in_qkv = (tile >= TILES["qkv_self"]) & (tile < TILES["out_self"])
    return jnp.where(in_kv, turned(2), jnp.where(in_qkv, turned(3), rows))


def tile_rows(length):
    return -(-length // (6 * TILE)) * 6


LANES = 128
TILE_LINES = TILE // LANES


def tile_place(tile):
    gap = QKV_GAP // LANES * jnp.where(tile >= TILES["gap"], 1, 0)
    return gap + END_GAP // LANES * jnp.where(tile >= TILES["modulate"], 1, 0)


def by_region(tile, work):
    in_kv = (tile >= TILES["keyval_cross"]) & (tile < TILES["out_cross"])
    in_qkv = (tile >= TILES["qkv_self"]) & (tile < TILES["out_self"])

    @pl.when(in_kv)
    def _():
        work(2)

    @pl.when(in_qkv)
    def _():
        work(3)

    @pl.when(jnp.logical_not(in_kv | in_qkv))
    def _():
        work(1)


def tile_lines(tile, first, panels):
    panel = lax.rem(tile, panels)
    return (tile - panel - first) * TILE_LINES + panel * 8


def prepare_kernel(own_ref, next_ref, blocks_ref, o_ref, chunks_ref, lines, tiles, sem):
    half = tiles.shape[0]
    core = lax.axis_index("strip")
    load = pltpu.make_async_copy(blocks_ref.at[pl.ds(core * half, half)], tiles, sem)
    load.start()
    place = lax.axis_index("dp") * 2 + core
    count = own_ref.shape[0]
    lines[:count] = own_ref[...]
    lines[count : count + next_ref.shape[0]] = next_ref[...]
    held = o_ref.shape[0] // 8
    first = place * held
    shift = place * (held * TILE_LINES - count)

    @pl.loop(0, held // 2)
    def _(n):
        def work(panels):
            rows = []
            for m in range(2):
                tile = first + 2 * n + m
                start = tile_lines(tile, first, panels) + shift - tile_place(tile)
                rows.append(jnp.concatenate([lines[pl.ds(start + j, 8, stride=8 * panels), :] for j in range(8)], 1))
            o_ref[pl.ds(pl.multiple_of(16 * n, 16), 16)] = jnp.concatenate(rows, 0).astype(jnp.bfloat16)

        by_region(first + 2 * n, work)

    load.wait()
    for n in range(half):
        at, column = n // 8 * BLOCK, n % 8 * BLOCK
        chunks_ref[at : at + BLOCK, column : column + BLOCK] = tiles[n].astype(jnp.bfloat16)


def prepare(weights, blocks):
    lines = weights.reshape(-1, LANES)
    count = lines.shape[0]
    held = tile_rows(weights.shape[0])
    reach = -(-32 * (held * TILE_LINES - count) // 8) * 8
    following = lax.ppermute(lines[:reach], AXES, [(n + 1, n) for n in range(31)])
    half = blocks.shape[0] // 2
    vmem = pl.BlockSpec(memory_space=pltpu.VMEM)
    return pl.pallas_call(
        prepare_kernel,
        in_specs=[vmem, vmem, pl.BlockSpec(memory_space=pl.ANY)],
        out_specs=[vmem, vmem],
        out_shape=[
            jax.ShapeDtypeStruct((held * 8, WIDE), jnp.bfloat16),
            jax.ShapeDtypeStruct((half // 8 * BLOCK, WIDE), jnp.bfloat16),
        ],
        scratch_shapes=[
            pltpu.VMEM((-(-(count + reach) // 8) * 8, LANES), jnp.float32),
            pltpu.VMEM((half, BLOCK, BLOCK), jnp.float32),
            pltpu.SemaphoreType.DMA,
        ],
        compiler_params=pltpu.CompilerParams(vmem_limit_bytes=16 * 1024 * 1024),
        name="prepare",
    )(lines, following, blocks)


def ungroup_kernel(rows_ref, o_ref):
    place = lax.axis_index("dp") * 2 + lax.axis_index("strip")
    held = rows_ref.shape[0] // 8
    first = place * held

    @pl.loop(0, held)
    def _(n):
        def work(panels):
            start = tile_lines(first + n, first, panels)
            at = pl.ds(pl.multiple_of(8 * n, 8), 8)
            for j in range(8):
                o_ref[pl.ds(start + j, 8, stride=8 * panels), :] = rows_ref[at, j * LANES : (j + 1) * LANES]

        by_region(first + n, work)


def ungroup(rows):
    vmem = pl.BlockSpec(memory_space=pltpu.VMEM)
    return pl.pallas_call(
        ungroup_kernel,
        in_specs=[vmem],
        out_specs=vmem,
        out_shape=jax.ShapeDtypeStruct((rows.size // LANES, LANES), jnp.float32),
        compiler_params=pltpu.CompilerParams(vmem_limit_bytes=16 * 1024 * 1024),
        name="ungroup",
    )(rows)


def adam_kernel(before_ref, sum_ref, w_ref, first_ref, second_ref, nw_ref, nfirst_ref, nsecond_ref, lines):
    place = lax.axis_index("dp") * 2 + lax.axis_index("strip")
    reach, summed, count = before_ref.shape[0], sum_ref.shape[0], w_ref.shape[0]
    lines[:reach] = before_ref[...]
    lines[reach : reach + summed] = sum_ref[...]
    shift = reach - place * (summed - count)
    gaps = (0, QKV_GAP // LANES, (QKV_GAP + END_GAP) // LANES)

    def update(at, rows):
        parts = [lines[pl.ds(shift + at + gap, rows), :] for gap in gaps]
        line = place * count + at + lax.broadcasted_iota(jnp.int32, (rows, LANES), 0)
        grad = jnp.where(line < QKV_AT // LANES, parts[0], jnp.where(line < GAP_AT // LANES, parts[1], parts[2]))
        here = pl.ds(at, rows)
        weights = w_ref[here]
        first = BETA_FIRST * first_ref[here] + (1.0 - BETA_FIRST) * grad
        second = BETA_SECOND * second_ref[here] + (1.0 - BETA_SECOND) * grad * grad
        nfirst_ref[here] = first
        nsecond_ref[here] = second
        fix_first = 1.0 - BETA_FIRST**ADAM_STEP
        fix_second = 1.0 - BETA_SECOND**ADAM_STEP
        step = first / fix_first / (jnp.sqrt(second / fix_second) + ADAM_EPS)
        nw_ref[here] = weights - ADAM_RATE * (step + WEIGHT_DECAY * weights)

    block = 32

    @pl.loop(0, count // block)
    def _(n):
        update(pl.multiple_of(block * n, block), block)

    if count % block:
        update(count - count % block, count % block)


def adam(rows, weights, first_moment, second_moment):
    length = weights.shape[0]
    count = length // LANES
    summed = ungroup(rows)
    reach = -(-32 * (summed.shape[0] - count) // 8) * 8
    before = lax.ppermute(summed[summed.shape[0] - reach :], AXES, [(n, n + 1) for n in range(31)])
    vmem = pl.BlockSpec(memory_space=pltpu.VMEM)
    gap = (QKV_GAP + END_GAP) // LANES
    results = pl.pallas_call(
        adam_kernel,
        in_specs=[vmem] * 5,
        out_specs=[vmem] * 3,
        out_shape=[jax.ShapeDtypeStruct((count, LANES), jnp.float32)] * 3,
        scratch_shapes=[pltpu.VMEM((-(-(reach + summed.shape[0] + gap) // 8) * 8, LANES), jnp.float32)],
        compiler_params=pltpu.CompilerParams(vmem_limit_bytes=32 * 1024 * 1024),
        name="adam",
    )(before, summed, *(a.reshape(count, LANES) for a in (weights, first_moment, second_moment)))
    return [result.reshape(length) for result in results]


def shampoo_kernel(tiles_ref, blocks_ref, sl_ref, sr_ref, rl_ref, rr_ref, nb_ref, g_ref, nl_ref, nr_ref, rms_ref):
    for n in range(8):
        grad = tiles_ref[:, n * BLOCK : (n + 1) * BLOCK]
        wide = grad.astype(jnp.float32)
        g_ref[n] = wide
        nl_ref[n] = STAT_DECAY * sl_ref[n] + (1.0 - STAT_DECAY) * nt_dot(grad, grad)
        square = lax.dot_general(grad, grad, (((0,), (0,)), ((), ())), preferred_element_type=jnp.float32)
        nr_ref[n] = STAT_DECAY * sr_ref[n] + (1.0 - STAT_DECAY) * square
        half = jnp.dot(wide, rr_ref[n], precision=HIGHEST_MODE, preferred_element_type=jnp.float32)
        cond = jnp.dot(rl_ref[n], half, precision=HIGHEST_MODE, preferred_element_type=jnp.float32)
        rms = jnp.sqrt(jnp.mean(cond * cond, axis=(0, 1), keepdims=True) + RMS_EPS)
        nb_ref[n] = blocks_ref[n] - SHAMPOO_RATE * cond / rms
        rms_ref[n : n + 1] = jnp.broadcast_to(rms, (1, LANES))


def shampoo(chunks, blocks, stat_left, stat_right, root_left, root_right):
    count = blocks.shape[0]
    eight = pl.BlockSpec((8, BLOCK, BLOCK), lambda n: (n, 0, 0))
    whole = jax.ShapeDtypeStruct(blocks.shape, jnp.float32)
    *results, rms = pl.pallas_call(
        shampoo_kernel,
        grid=(count // 8,),
        in_specs=[pl.BlockSpec((BLOCK, WIDE), lambda n: (n, 0))] + [eight] * 5,
        out_specs=[eight] * 4 + [pl.BlockSpec((8, LANES), lambda n: (n, 0))],
        out_shape=[whole] * 4 + [jax.ShapeDtypeStruct((count, LANES), jnp.float32)],
        compiler_params=pltpu.CompilerParams(vmem_limit_bytes=60 * 1024 * 1024),
        name="shampoo",
    )(chunks, blocks, stat_left, stat_right, root_left, root_right)
    return *results, rms[:, 0]


def chunks_of(tiles):
    return tiles.reshape(-1, 8, BLOCK, BLOCK).transpose(0, 2, 1, 3).reshape(-1, WIDE)


def tiles_of(chunks):
    return chunks.reshape(-1, BLOCK, 8, BLOCK).transpose(0, 2, 1, 3).reshape(-1, BLOCK, BLOCK)


def panels_of(chunks):
    half = chunks.shape[0] // 2
    first = chunks[:half].reshape(D // BLOCK, HID // WIDE, BLOCK, WIDE).transpose(1, 0, 2, 3)
    return jnp.concatenate([first.reshape(half, WIDE), chunks[half:]])


def chunks_of_panels(panels):
    half = panels.shape[0] // 2
    first = panels[:half].reshape(HID // WIDE, D // BLOCK, BLOCK, WIDE).transpose(1, 0, 2, 3)
    return jnp.concatenate([first.reshape(half, WIDE), panels[half:]])


META = (1, 8, lambda p, c, j: (2 * p + c) * 8)
SWAP = ((0, 1), (1, 0))
AXES = ("dp", "strip")


def pairs_to(target):
    return [(2 * p + c, sum(v * w for v, w in zip(target(p, c), (2, 1)))) for p in range(16) for c in range(2)]


NEAR = pairs_to(lambda p, c: (p ^ (1 + c), c))
FAR = pairs_to(lambda p, c: (p ^ (2 - c), c))
CORE = pairs_to(lambda p, c: (p, 1 - c))


def gather_weights(weights, blocks, part):
    if direct_links():
        own, tiles = prepare(weights, blocks)
        meta = jnp.full((8, 128), part, jnp.float32)
        rows, parts, line = gather_all([flat_chunks(own.shape[0], 3), META], 6, [own, meta], tiles, 0)
        near = lax.ppermute(line, AXES, NEAR)
        return rows, [line, near], jnp.sum(parts[::8, 0])
    flat = lax.all_gather(weights.astype(jnp.bfloat16), AXES, axis=0, tiled=True)
    tiles = lax.all_gather(blocks.astype(jnp.bfloat16), "dp", axis=0, tiled=True)
    gaps = [jnp.zeros((QKV_GAP,), flat.dtype), jnp.zeros((END_GAP,), flat.dtype)]
    rows = jnp.concatenate([flat[:QKV_AT], gaps[0], flat[QKV_AT:GAP_AT], gaps[1], flat[GAP_AT:]])
    rows = jnp.pad(rows, (0, -rows.shape[0] % (6 * TILE))).reshape(-1, WIDE)
    return regroup(rows, 0, False), [panels_of(chunks_of(tiles))], lax.psum(part, AXES)


class Panels:
    def __init__(self, parts):
        self.parts = parts
        self.staged = len(parts) > 1

    def first(self, before):
        if not self.staged:
            return before
        line, near = self.parts
        near, before = lax.optimization_barrier((near, before))
        self.parts = [line, near, lax.ppermute(line, AXES, FAR)]
        return before

    def second(self, before):
        if not self.staged:
            return before
        line, near, far = self.parts
        far, before = lax.optimization_barrier((far, before))
        self.parts = [line, near, far, lax.ppermute(near, AXES, FAR)]
        return before

    def third(self, after):
        if not self.staged:
            return self.parts
        line, near, far, both = self.parts
        both, after = lax.optimization_barrier((both, after))
        return [line, near, far, both] + [lax.ppermute(group, AXES, CORE) for group in (line, near, far, both)]


class PanelSums:
    def __init__(self, grads):
        self.parts = grads
        self.staged = len(grads) > 1
        if self.staged:
            self.mine = grads[0]
            self.got = lax.ppermute(grads[1], AXES, CORE)

    def added(self, at, *parts):
        total = self.mine[at].astype(jnp.float32) + self.got[at].astype(jnp.float32)
        for part in parts:
            total = total + part.astype(jnp.float32)
        return total.astype(jnp.bfloat16)

    def first(self, before):
        if not self.staged:
            return before
        away, before = lax.optimization_barrier((self.added(slice(8, 16)), before))
        self.away = lax.ppermute(away, AXES, FAR)
        return before

    def second(self, before):
        if not self.staged:
            return before
        self.away, before = lax.optimization_barrier((self.away, before))
        near, before = lax.optimization_barrier((self.added(slice(4, 8), self.away[4:]), before))
        self.last = lax.ppermute(near, AXES, NEAR)
        return before

    def third(self, before):
        if not self.staged:
            return before
        self.last, before = lax.optimization_barrier((self.last, before))
        self.parts = [self.added(slice(0, 4), self.away[:4], self.last)]
        return before


def reduce_grads(rows, panels, part):
    meta = jnp.full((32 * 8, 128), part, jnp.float32)
    summed, parts, tiles = scatter_sum([flat_chunks(rows.shape[0] // 32, 3), META], 6, [rows, meta], panels[0], 1)
    return summed, tiles, parts[0, 0]


def reduce_grads_plainly(rows, panels, part, length):
    flat = regroup(rows, 0, True).astype(jnp.float32).reshape(-1)
    flat = jnp.concatenate(
        [flat[:QKV_AT], flat[QKV_AT + QKV_GAP : GAP_AT + QKV_GAP], flat[GAP_AT + QKV_GAP + END_GAP :]]
    )
    devices = lax.axis_size("dp") * lax.axis_size("strip")
    flat = jnp.pad(flat, (0, max(0, devices * length - flat.shape[0])))[: devices * length]
    tiles = tiles_of(chunks_of_panels(panels[0])).astype(jnp.float32)
    flat_sum = lax.psum_scatter(flat, AXES, scatter_dimension=0, tiled=True)
    tile_sum = lax.psum_scatter(tiles, AXES, scatter_dimension=0, tiled=True)
    tile_sum = lax.all_gather(tile_sum.astype(jnp.bfloat16), "strip", axis=0, tiled=True)
    return flat_sum, chunks_of(tile_sum), lax.psum(part, AXES)


def adam_plainly(grad, weights, first_moment, second_moment):
    new_first = BETA_FIRST * first_moment + (1.0 - BETA_FIRST) * grad
    new_second = BETA_SECOND * second_moment + (1.0 - BETA_SECOND) * grad * grad
    fix_first = 1.0 - BETA_FIRST**ADAM_STEP
    fix_second = 1.0 - BETA_SECOND**ADAM_STEP
    moved = new_first / fix_first / (jnp.sqrt(new_second / fix_second) + ADAM_EPS)
    return weights - ADAM_RATE * (moved + WEIGHT_DECAY * weights), new_first, new_second


def shards(
    weights,
    blocks,
    stat_left,
    stat_right,
    root_left,
    root_right,
    first_moment,
    second_moment,
    image,
    camera,
    samples,
    ray_pixel,
    target,
    valid,
):
    strips = lax.axis_size("strip")
    place = lax.axis_index("strip")
    pixel = ray_pixel[0]
    mask = jnp.take(valid[0], pixel).astype(jnp.float32)
    wanted = jnp.take(target[0], pixel, axis=1)
    rows, panels, count = gather_weights(weights, blocks, jnp.sum(mask))
    tiled = rows.reshape(-1, 8, WIDE)

    def square(name):
        return rows[TILES[name] * 8 : TILES[name] * 8 + D]

    def plain(name, count):
        return rows[TILES[name] * 8 : TILES[name] * 8 + count]

    deconv = spread_deconv(tiled, TILES["deconv"])
    decode = plain("decode", 8).reshape(-1)
    decode_in = decode[: CH * DEC_HID].reshape(CH, DEC_HID)
    decode_out = decode[CH * DEC_HID : CH * DEC_HID + DEC_HID * 4].reshape(DEC_HID, 4)
    picture = image[0]
    real_keys = picture.shape[0]
    picture = jnp.pad(picture, ((0, -real_keys % 128), (0, 0)))
    mods = lax.dynamic_slice_in_dim(plain("modulate", 6 * NCAM), 6 * camera[0], 6).astype(jnp.float32)
    own_rows = PR * TC
    stream0 = jnp.concatenate(
        [
            lax.dynamic_slice_in_dim(rows, TILES["triplane"] * 8 + (strips * plane + place) * own_rows, own_rows)
            for plane in range(3)
        ]
    ).astype(jnp.float32)
    hidden1, norm_one = jax.vjp(norm_mod, stream0, mods[0], mods[1])
    hidden1 = hidden1.astype(jnp.bfloat16)
    query1 = product(hidden1, square("query_cross")).astype(jnp.bfloat16)
    (image_kv,) = project(picture, tiled, TILES["keyval_cross"], 2, 0)
    pairs = D // PAIR
    tokens = query1.shape[0]
    cross_out, total_one = attend_fwd(query1, [image_kv], real_keys, (0, pairs))
    stream1 = stream0 + product(cross_out, square("out_cross"))
    hidden2, norm_two = jax.vjp(norm_mod, stream1, mods[2], mods[3])
    hidden2 = hidden2.astype(jnp.bfloat16)
    panels = Panels(panels)
    hidden2 = panels.first(hidden2)
    query2, kv_own = project(hidden2, tiled, TILES["qkv_self"], 3, 1)
    kv_both = [kv_own, lax.ppermute(kv_own, "strip", SWAP)]
    all_keys = 2 * kv_own.shape[1]
    early = attend_fwd(query2, kv_both, all_keys, (0, pairs // 2))
    early = (panels.second(early[0]), early[1])
    self_out, total_two = attend_fwd(query2, kv_both, all_keys, (pairs // 2, pairs), early)
    panels = panels.third(self_out)
    stream2 = stream1 + product(self_out, square("out_self"))
    hidden3, norm_three = jax.vjp(norm_mod, stream2, mods[4], mods[5])
    hidden3 = hidden3.astype(jnp.bfloat16)
    up, act, grid = mlp_fwd(panels, hidden3, stream2)
    grid = grid.reshape(3, own_rows, D)
    edge = lax.ppermute(jnp.where(place == 0, grid[:, -TC:], grid[:, :TC]), "strip", SWAP)
    cells = deconv_fwd(grid, edge, deconv)
    cells_far = lax.ppermute(cells, "strip", SWAP)
    rays = pixel.shape[0]
    factor = 1.0 / jnp.maximum(count, 1.0)
    loss_part, grad_cells, grad_far, grad_decode_in, grad_decode_out = render(
        cells,
        cells_far,
        (samples[0] + place * cells.shape[1]) % (2 * cells.shape[1]),
        jnp.pad(wanted, ((1, 4), (0, 0))),
        mask[None],
        factor.reshape(1),
        decode_in,
        jnp.pad(decode_out, ((0, 0), (0, 4))),
        rays,
    )
    loss_part = loss_part[0, 0]
    grad_decode_out = grad_decode_out[:, :4]
    grad_far = lax.ppermute(grad_far, "strip", SWAP)
    grad_grid, beside, grad_deconv = deconv_bwd(grad_cells, grad_far, grid, edge, deconv)
    beside = lax.ppermute(beside, "strip", SWAP).astype(jnp.float32)
    grad_grid = grad_grid.at[:, :TC].add(jnp.where(place == 0, 0.0, beside))
    grad_grid = grad_grid.at[:, -TC:].add(jnp.where(place == 0, beside, 0.0))
    grad_stream = grad_grid.reshape(-1, D)
    grad_branch = grad_stream.astype(jnp.bfloat16)
    grad_hidden3, *panel_grads = mlp_bwd(panels, hidden3, grad_branch, up, act)
    grad_norm, grad_mod4, grad_mod5 = norm_three(grad_hidden3)
    grad_stream = grad_stream + grad_norm
    grad_branch2 = grad_stream.astype(jnp.bfloat16)
    grad_self = product_back(grad_branch2, square("out_self")).astype(jnp.bfloat16)
    panel_sums = PanelSums(panel_grads)
    grad_self = panel_sums.first(grad_self)
    early = attend_bwd(query2, kv_both, all_keys, (0, pairs - 1), 512, total_two, self_out, grad_self)
    early = (panel_sums.second(early[0]), *early[1:])
    grad_query2, grad_kv_own, grad_kv_far = attend_bwd(
        query2, kv_both, all_keys, (pairs - 1, pairs), 512, total_two, self_out, grad_self, early
    )
    grad_kv_far = lax.ppermute(grad_kv_far, "strip", SWAP)
    grad_kv = (grad_kv_own.astype(jnp.float32) + grad_kv_far.astype(jnp.float32)).astype(jnp.bfloat16)
    grad_hidden2 = project_back(grad_query2, grad_kv, tiled, TILES["qkv_self"], D)
    grad_norm, grad_mod2, grad_mod3 = norm_two(grad_hidden2)
    grad_stream = grad_stream + grad_norm
    grad_branch1 = grad_stream.astype(jnp.bfloat16)
    grad_cross = product_back(grad_branch1, square("out_cross")).astype(jnp.bfloat16)
    grad_query1, grad_image_kv = attend_bwd(
        query1, [image_kv], real_keys, (0, pairs), 128, total_one, cross_out, grad_cross
    )
    grad_query1 = panel_sums.third(grad_query1)
    grad_norm, grad_mod0, grad_mod1 = norm_one(product_back(grad_query1, square("query_cross")))
    grad_stream = grad_stream + grad_norm
    grad_mods = jnp.stack([grad_mod0, grad_mod1, grad_mod2, grad_mod3, grad_mod4, grad_mod5])
    grad_modulate = lax.dynamic_update_slice_in_dim(
        jnp.zeros((6 * NCAM, D), jnp.bfloat16), grad_mods.astype(jnp.bfloat16), 6 * camera[0], 0
    )
    grad_triplane = lax.dynamic_update_slice_in_dim(
        jnp.zeros((3, strips, own_rows, D), jnp.bfloat16),
        grad_stream.astype(jnp.bfloat16).reshape(3, 1, own_rows, D),
        place,
        1,
    )
    grad_decode = jnp.concatenate([grad_decode_in.reshape(-1), grad_decode_out.reshape(-1)])
    grad_decode = jnp.pad(grad_decode, (0, END_GAP))
    total_tiles = tiled.shape[0]
    end = TILES["triplane"] + 3 * strips * own_rows // 8
    gap = TILES["qkv_self"] - TILES["gap"]
    arrays = [
        hidden1,
        grad_query1,
        picture,
        grad_image_kv,
        cross_out,
        grad_branch1,
        hidden2,
        grad_query2,
        grad_kv,
        self_out,
        grad_branch2,
    ]
    tall, low = (tokens, D), (picture.shape[0], DI)
    products = [
        (tall, (9, None), (10, None), TILES["out_self"], (1, 0)),
        (tall, (6, None), (7, None), TILES["qkv_self"], (3, 0)),
        (tall, (6, None), (8, 0), TILES["qkv_self"], (3, 1)),
        (tall, (6, None), (8, 1), TILES["qkv_self"], (3, 2)),
        (tall, (4, None), (5, None), TILES["out_cross"], (1, 0)),
        (low, (2, None), (3, 0), TILES["keyval_cross"], (2, 0)),
        (low, (2, None), (3, 1), TILES["keyval_cross"], (2, 1)),
        (tall, (0, None), (1, None), TILES["query_cross"], (1, 0)),
    ]
    copies = []
    for piece, first in (
        (grad_deconv, TILES["deconv"]),
        (grad_decode, TILES["decode"]),
        (grad_modulate, TILES["modulate"]),
        (grad_triplane, TILES["triplane"]),
        (jnp.zeros((gap, 8, WIDE), jnp.bfloat16), TILES["gap"]),
        (jnp.zeros((total_tiles - end, 8, WIDE), jnp.bfloat16), end),
    ):
        piece = piece.astype(jnp.bfloat16).reshape(-1, 8, WIDE)
        if piece.shape[0]:
            copies.append((len(arrays), first, piece.shape[0]))
            arrays.append(piece)
    row_grads = weight_grads(arrays, products, copies, total_tiles).reshape(-1, WIDE)
    if direct_links():
        summed, chunks, loss_sum = reduce_grads(row_grads, panel_sums.parts, loss_part)
        new_weights, new_first, new_second = adam(summed, weights, first_moment, second_moment)
    else:
        summed, chunks, loss_sum = reduce_grads_plainly(row_grads, panel_sums.parts, loss_part, weights.shape[0])
        new_weights, new_first, new_second = adam_plainly(summed, weights, first_moment, second_moment)
    new_blocks, block_grads, new_left, new_right, block_rms = shampoo(
        chunks, blocks, stat_left, stat_right, root_left, root_right
    )
    loss = loss_sum * factor
    return (
        loss,
        new_weights,
        new_first,
        new_second,
        new_blocks,
        block_grads,
        new_left,
        new_right,
        block_rms,
    )


def solution(mesh):
    placed = (
        P(("dp", "strip")),
        P("dp", None, None),
        P("dp", None, None),
        P("dp", None, None),
        P("dp", None, None),
        P("dp", None, None),
        P(("dp", "strip")),
        P(("dp", "strip")),
        P("dp", None, None),
        P("dp"),
        P("dp", None, None, "strip"),
        P("dp", "strip"),
        P("dp", None, None),
        P("dp", None),
    )
    return jax.shard_map(
        shards,
        mesh=mesh,
        in_specs=placed,
        out_specs=(
            P(),
            P(("dp", "strip")),
            P(("dp", "strip")),
            P(("dp", "strip")),
            P("dp", None, None),
            P("dp", None, None),
            P("dp", None, None),
            P("dp", None, None),
            P("dp"),
        ),
        check_vma=False,
    )
```

```python
import functools
import math

import jax
import jax.numpy as jnp
from jax import lax
from jax.experimental import pallas as pl
from jax.experimental.pallas import tpu as pltpu
from jax.sharding import PartitionSpec as P

D = 1024
HEAD_DIM = 64
HID = 4096
DI = 768
CH = 80
DEC_HID = 64
BLOCK = 128
PR = 8
TC = 32
S = 16
NCAM = 32
ADAM_STEP = 10


NORM_EPS = 1e-05
ADAM_RATE = 0.015
BETA_FIRST = 0.9
BETA_SECOND = 0.95
ADAM_EPS = 1e-08
WEIGHT_DECAY = 0.1
STAT_DECAY = 0.9
SHAMPOO_RATE = 0.01
RMS_EPS = 1e-06
HIGHEST_MODE = lax.Precision.HIGHEST
WIDE = 1024


def product(left, right):
    return jnp.dot(left, right, preferred_element_type=jnp.float32)


def product_back(left, right):
    return lax.dot_general(
        left, right, (((left.ndim - 1,), (1,)), ((), ())), preferred_element_type=jnp.float32
    )


def weight_grad(left, right):
    return lax.dot_general(
        left, right, (((0,), (0,)), ((), ())), preferred_element_type=jnp.float32
    )


def norm_mod(stream, scale, shift):
    centred = stream - jnp.mean(stream, -1, keepdims=True)
    spread = jnp.mean(centred * centred, -1, keepdims=True)
    return centred * lax.rsqrt(spread + NORM_EPS) * (1.0 + scale) + shift


def gelu_tanh(value):
    return jax.nn.gelu(value, approximate=True)


PAIR = 2 * HEAD_DIM
BRIEF = pl.CostEstimate(flops=1000000, transcendentals=0, bytes_accessed=100000)
LOG2E = math.log2(math.e)
EXP_SCALE = HEAD_DIM ** (-0.5) * LOG2E


def nt_dot(left, right):
    return lax.dot_general(left, right, (((1,), (1,)), ((), ())), preferred_element_type=jnp.float32)


def head_lanes(shape, head):
    return lax.broadcasted_iota(jnp.int32, shape, len(shape) - 1) // HEAD_DIM == head


def joined(refs, n):
    parts = [ref[n] for ref in refs]
    return parts[0] if len(parts) == 1 else jnp.concatenate(parts, 0)


def attend_fwd_kernel(real_keys, sources, q_ref, *refs):
    o_ref, lse_ref = refs[-2:]
    query, keys = q_ref[...], joined(refs[:sources], 0)
    values = joined(refs[:sources], 1).T
    outs = []
    for head in range(2):
        own = jnp.where(head_lanes(query.shape, head), query, 0)
        scores = nt_dot(keys, own)
        if real_keys < keys.shape[0]:
            at = lax.broadcasted_iota(jnp.int32, scores.shape, 0)
            scores = jnp.where(at < real_keys, scores, -3e38)
        top = jnp.max(scores, 0, keepdims=True)
        raised = jnp.exp2((scores - top) * EXP_SCALE)
        total = jnp.sum(raised, 0, keepdims=True)
        shares = (raised * (1.0 / total)).astype(jnp.bfloat16)
        outs.append(product(values[head * HEAD_DIM : (head + 1) * HEAD_DIM], shares))
        lse_ref[0, head : head + 1] = top * EXP_SCALE + jnp.log2(total)
    o_ref[...] = jnp.concatenate(outs, 0).T.astype(jnp.bfloat16)


def attend_fwd(query, sources, real_keys, span, earlier=()):
    count = query.shape[0]
    total_keys = sum(source.shape[1] for source in sources)
    low, high = span
    by_pair = pl.BlockSpec((count, PAIR), lambda j: (0, low + j))
    work = count * total_keys * (high - low) * PAIR
    return pl.pallas_call(
        functools.partial(attend_fwd_kernel, real_keys, len(sources)),
        grid=(high - low,),
        in_specs=[by_pair]
        + [pl.BlockSpec((2, source.shape[1], PAIR), lambda j: (0, 0, low + j)) for source in sources]
        + [pl.BlockSpec(memory_space=pl.ANY)] * len(earlier),
        out_specs=[by_pair, pl.BlockSpec((1, 8, count), lambda j: (low + j, 0, 0))],
        out_shape=[
            jax.ShapeDtypeStruct((count, D), jnp.bfloat16),
            jax.ShapeDtypeStruct((D // PAIR, 8, count), jnp.float32),
        ],
        input_output_aliases={1 + len(sources) + n: n for n in range(len(earlier))},
        compiler_params=pltpu.CompilerParams(vmem_limit_bytes=48 * 1024 * 1024),
        cost_estimate=BRIEF,
        name="attend_fwd",
    )(query, *sources, *earlier)


def attend_bwd_kernel(real_keys, chunk, sources, extra, q_ref, *refs):
    kv_refs = refs[:sources]
    lse_ref, o_ref, g_ref = refs[sources : sources + 3]
    dq_ref, *grad_refs = refs[sources + 3 + extra : sources + 4 + extra + sources]
    k_all, v_all, kt_ref, dk_sum, dv_sum = refs[sources + 4 + extra + sources :]
    k_all[...] = joined(kv_refs, 0)
    v_all[...] = joined(kv_refs, 1)
    kt_ref[...] = k_all[...].T
    query, grad = q_ref[...], g_ref[...]
    mixed = (grad.astype(jnp.float32) * o_ref[...].astype(jnp.float32)).T
    total_keys = k_all.shape[0]
    queries = [jnp.where(head_lanes(query.shape, head), query, 0) for head in range(2)]
    grads = [jnp.where(head_lanes(grad.shape, head), grad, 0) for head in range(2)]
    inner = [jnp.sum(mixed[head * HEAD_DIM : (head + 1) * HEAD_DIM], 0, keepdims=True) for head in range(2)]
    grad_query = [jnp.zeros((HEAD_DIM, query.shape[0]), jnp.float32) for head in range(2)]
    for at in range(0, total_keys, chunk):
        part = pl.ds(at, chunk)
        keys, values = k_all[part], v_all[part]
        for head in range(2):
            scores = nt_dot(keys, queries[head])
            shares = jnp.exp2(scores * EXP_SCALE - lse_ref[0, head : head + 1])
            if at + chunk > real_keys:
                row = at + lax.broadcasted_iota(jnp.int32, shares.shape, 0)
                shares = jnp.where(row < real_keys, shares, 0.0)
            grad_shares = nt_dot(values, grads[head])
            grad_scores = (shares * (grad_shares - inner[head])).astype(jnp.bfloat16)
            to_values = product(shares.astype(jnp.bfloat16), grads[head])
            to_keys = product(grad_scores, queries[head])
            if head == 0:
                dv_sum[part] = to_values
                dk_sum[part] = to_keys
            else:
                dv_sum[part] += to_values
                dk_sum[part] += to_keys
            grad_query[head] += product(
                kt_ref[head * HEAD_DIM : (head + 1) * HEAD_DIM, part], grad_scores
            )
    scale = HEAD_DIM ** (-0.5)
    dq_ref[...] = (jnp.concatenate(grad_query, 0) * scale).T.astype(jnp.bfloat16)
    start = 0
    for ref in grad_refs:
        part = pl.ds(start, ref.shape[1])
        ref[0] = (dk_sum[part] * scale).astype(jnp.bfloat16)
        ref[1] = dv_sum[part].astype(jnp.bfloat16)
        start += ref.shape[1]


def attend_bwd(query, sources, real_keys, span, chunk, totals, out, grad, earlier=()):
    count = query.shape[0]
    total_keys = sum(source.shape[1] for source in sources)
    low, high = span
    by_pair = pl.BlockSpec((count, PAIR), lambda j: (0, low + j))
    by_source = [pl.BlockSpec((2, source.shape[1], PAIR), lambda j: (0, 0, low + j)) for source in sources]
    first = 1 + len(sources) + 3
    work = count * total_keys * (high - low) * PAIR
    return pl.pallas_call(
        functools.partial(attend_bwd_kernel, real_keys, chunk, len(sources), len(earlier)),
        grid=(high - low,),
        in_specs=[by_pair]
        + by_source
        + [pl.BlockSpec((1, 8, count), lambda j: (low + j, 0, 0)), by_pair, by_pair]
        + [pl.BlockSpec(memory_space=pl.ANY)] * len(earlier),
        out_specs=[by_pair] + by_source,
        out_shape=[jax.ShapeDtypeStruct((count, D), jnp.bfloat16)]
        + [jax.ShapeDtypeStruct(source.shape, jnp.bfloat16) for source in sources],
        input_output_aliases={first + n: n for n in range(len(earlier))},
        scratch_shapes=[
            pltpu.VMEM((total_keys, PAIR), jnp.bfloat16),
            pltpu.VMEM((total_keys, PAIR), jnp.bfloat16),
            pltpu.VMEM((PAIR, total_keys), jnp.bfloat16),
            pltpu.VMEM((total_keys, PAIR), jnp.float32),
            pltpu.VMEM((total_keys, PAIR), jnp.float32),
        ],
        compiler_params=pltpu.CompilerParams(vmem_limit_bytes=48 * 1024 * 1024),
        cost_estimate=BRIEF,
        name="attend_bwd",
    )(query, *sources, totals, out, grad, *earlier)


GROUPS = 3


def render_kernel(samples_ref, near_ref, far_ref, wanted_ref, mask_ref, factor_ref, win_ref, wout_ref,
                  loss_ref, grad_ref, grad_far_ref, gin_ref, gout_ref,
                  table, inner_all, hidden_all, point_all, out_all, gout_all, sums):
    block = pl.program_id(0)
    half = near_ref.shape[1]
    cells = 2 * half
    group = table.shape[2]
    rays = samples_ref.shape[2]
    planes = near_ref.shape[0]

    @pl.when(block == 0)
    def _():
        loss_ref[...] = jnp.zeros_like(loss_ref)
        gin_ref[...] = jnp.zeros_like(gin_ref)
        gout_ref[...] = jnp.zeros_like(gout_ref)
        sums[...] = jnp.zeros_like(sums)
        table[...] = jnp.zeros_like(table)
        for plane in range(planes):
            turned = jnp.concatenate([near_ref[plane], far_ref[plane]], 0).T
            for g in range(GROUPS):
                width = min(group, cells - g * group)
                table[plane, g * CH : (g + 1) * CH, :width] = turned[:CH, g * group : g * group + width]

    step = 4
    width = step * rays
    win, wout = win_ref[...], wout_ref[...]

    def places_read(plane, s):
        rows = [samples_ref[plane, s + n : s + n + 1, :] for n in range(step)]
        at = jnp.concatenate(rows, 1)
        owner = at // group
        within = at - owner * group
        hot = lax.broadcasted_iota(jnp.int32, (group, width), 0) == within
        return owner, jnp.where(hot, 1.0, 0.0).astype(jnp.bfloat16)

    def tn_dot(left, right):
        return lax.dot_general(left, right, (((0,), (0,)), ((), ())), preferred_element_type=jnp.float32)

    for s in range(0, S, step):
        here = pl.ds(s * rays, width)
        point = jnp.zeros((CH, width), jnp.float32)
        for plane in range(planes):
            owner, hot = places_read(plane, s)
            found = product(table[plane], hot)
            value = found[:CH]
            for g in range(1, GROUPS):
                value = jnp.where(owner == g, found[g * CH : (g + 1) * CH], value)
            point = point + value
        point = point.astype(jnp.bfloat16)
        inner = tn_dot(win, point)
        hidden = (inner * jax.nn.sigmoid(inner)).astype(jnp.bfloat16)
        out_all[:, here] = tn_dot(wout, hidden)
        inner_all[:, here] = inner
        hidden_all[:, here] = hidden
        point_all[:, here] = point

    factor = factor_ref[0]
    mask = mask_ref[...]
    row = lax.broadcasted_iota(jnp.int32, (8, rays), 0)
    is_colour = (row >= 1) & (row <= 3)
    before = jnp.zeros((1, rays), jnp.float32)
    rgb = jnp.zeros((8, rays), jnp.float32)
    kept = []
    for s in range(S):
        out = out_all[:, s * rays : (s + 1) * rays]
        level = out[0:1]
        absorb = (4.0 / S) * (jnp.maximum(level, 0.0) + jnp.log1p(jnp.exp(-jnp.abs(level))))
        weight = jnp.exp(-before) * (1.0 - jnp.exp(-absorb))
        before = before + absorb
        colour = jax.nn.sigmoid(out)
        rgb = rgb + weight * colour
        kept.append((weight, jnp.exp(-before), colour))
    error = jnp.where(is_colour, rgb - wanted_ref[...], 0.0)
    loss_ref[...] += jnp.sum(mask * jnp.sum(error * error, 0, keepdims=True))
    pull = error * (2.0 * factor * mask)
    tail = jnp.zeros((1, rays), jnp.float32)
    for s in reversed(range(S)):
        weight, left_over, colour = kept[s]
        to_weight = jnp.sum(pull * colour, 0, keepdims=True)
        to_absorb = to_weight * left_over - tail
        tail = tail + to_weight * weight
        to_level = (4.0 / S) * to_absorb * colour[0:1]
        to_colour = weight * pull * colour * (1.0 - colour)
        gout_all[:, s * rays : (s + 1) * rays] = jnp.where(row == 0, to_level, to_colour).astype(jnp.bfloat16)

    for s in range(0, S, step):
        here = pl.ds(s * rays, width)
        pulled = gout_all[:, here]
        inner = inner_all[:, here]
        gate = jax.nn.sigmoid(inner)
        grad_inner = product(wout, pulled) * (gate * (1.0 + inner * (1.0 - gate)))
        grad_inner = grad_inner.astype(jnp.bfloat16)
        gout_ref[...] += nt_dot(hidden_all[:, here], pulled)
        gin_ref[...] += nt_dot(point_all[:, here], grad_inner)
        grad_point = product(win, grad_inner)
        coarse = grad_point.astype(jnp.bfloat16).astype(jnp.float32)
        fine = grad_point - coarse
        for plane in range(planes):
            owner, hot = places_read(plane, s)
            rows = [jnp.where(owner == g, coarse, 0.0) for g in range(GROUPS)]
            rows += [jnp.where(owner == g, fine, 0.0) for g in range(GROUPS)]
            stacked = jnp.concatenate(rows, 0).astype(jnp.bfloat16)
            added = nt_dot(stacked, hot)
            sums[plane] += added[: GROUPS * CH] + added[GROUPS * CH :]

    @pl.when(block == pl.num_programs(0) - 1)
    def _():
        for plane in range(planes):
            for g in range(GROUPS):
                for low, high, ref in ((0, half, grad_ref), (half, cells, grad_far_ref)):
                    start, stop = max(g * group, low), min((g + 1) * group, high)
                    if start < stop:
                        part = sums[plane, g * CH : (g + 1) * CH, start - g * group : stop - g * group]
                        ref[plane, :, start - low : stop - low] = part.astype(jnp.bfloat16)


def render(near, far, samples, wanted, mask, factor, decode_in, decode_out, rays):
    planes, half, _ = near.shape
    count = 2 * half
    all_rays = samples.shape[2]
    group = -(-count // (GROUPS * 128)) * 128
    points = S * rays
    whole = lambda *shape: pl.BlockSpec(shape, lambda n: (0,) * len(shape))
    return pl.pallas_call(
        render_kernel,
        grid=(all_rays // rays,),
        in_specs=[
            pl.BlockSpec((planes, S, rays), lambda n: (0, 0, n)),
            whole(*near.shape),
            whole(*far.shape),
            pl.BlockSpec((8, rays), lambda n: (0, n)),
            pl.BlockSpec((1, rays), lambda n: (0, n)),
            pl.BlockSpec(memory_space=pltpu.SMEM),
            whole(CH, DEC_HID),
            whole(DEC_HID, 8),
        ],
        out_specs=[whole(8, 128), whole(planes, CH, half), whole(planes, CH, half), whole(CH, DEC_HID), whole(DEC_HID, 8)],
        out_shape=[
            jax.ShapeDtypeStruct((8, 128), jnp.float32),
            jax.ShapeDtypeStruct((planes, CH, half), jnp.bfloat16),
            jax.ShapeDtypeStruct((planes, CH, half), jnp.bfloat16),
            jax.ShapeDtypeStruct((CH, DEC_HID), jnp.float32),
            jax.ShapeDtypeStruct((DEC_HID, 8), jnp.float32),
        ],
        scratch_shapes=[
            pltpu.VMEM((planes, GROUPS * CH, group), jnp.bfloat16),
            pltpu.VMEM((DEC_HID, points), jnp.float32),
            pltpu.VMEM((DEC_HID, points), jnp.bfloat16),
            pltpu.VMEM((CH, points), jnp.bfloat16),
            pltpu.VMEM((8, points), jnp.float32),
            pltpu.VMEM((8, points), jnp.bfloat16),
            pltpu.VMEM((planes, GROUPS * CH, group), jnp.float32),
        ],
        compiler_params=pltpu.CompilerParams(vmem_limit_bytes=48 * 1024 * 1024),
        name="render",
    )(samples, near, far, wanted, mask, factor, decode_in, decode_out)


def pick_kernel(pixel_ref, valid_ref, target_ref, mask_ref, wanted_ref, count_ref):
    pixels = valid_ref.shape[1]
    rays = pixel_ref.shape[1]
    hot = lax.broadcasted_iota(jnp.int32, (pixels, rays), 0) == pixel_ref[...]
    hot = jnp.where(hot, 1.0, 0.0).astype(jnp.bfloat16)
    rest = target_ref[...]
    rows = [valid_ref[...].astype(jnp.float32)]
    for _ in range(3):
        part = rest.astype(jnp.bfloat16).astype(jnp.float32)
        rows.append(part)
        rest = rest - part
    rows.append(jnp.zeros((6, pixels), jnp.float32))
    found = product(jnp.concatenate(rows, 0).astype(jnp.bfloat16), hot)
    mask = found[:1]
    mask_ref[...] = mask
    wanted_ref[...] = jnp.zeros_like(wanted_ref)
    wanted_ref[1:4] = found[1:4] + found[4:7] + found[7:10]
    count_ref[...] = jnp.broadcast_to(jnp.sum(mask, 1, keepdims=True), count_ref.shape)


def pick(pixel, valid, target):
    rays = pixel.shape[1]
    vmem = pl.BlockSpec(memory_space=pltpu.VMEM)
    return pl.pallas_call(
        pick_kernel,
        in_specs=[vmem] * 3,
        out_specs=[vmem] * 3,
        out_shape=[
            jax.ShapeDtypeStruct((1, rays), jnp.float32),
            jax.ShapeDtypeStruct((8, rays), jnp.float32),
            jax.ShapeDtypeStruct((8, 128), jnp.float32),
        ],
        compiler_params=pltpu.CompilerParams(vmem_limit_bytes=24 * 1024 * 1024),
        name="pick",
    )(pixel, valid, target)


MESH_ID = pl.DeviceIdType.MESH


def places():
    p = lax.axis_index("dp")
    c = lax.axis_index("strip")
    z = p // 4
    flip_x = p + 1 - 2 * (p % 2)
    flip_y = p + 2 - 4 * ((p // 2) % 2)
    both = flip_x + flip_y - p
    near = (1 - c) * flip_x + c * flip_y
    far = (1 - c) * flip_y + c * flip_x
    return p, c, z, near, far, both


def along_z(line, z, k):
    return ((z + k) % 4) * 4 + line % 4


def enter(peers):
    barrier = pltpu.get_barrier_semaphore()
    for peer in peers:
        pl.semaphore_signal(barrier, inc=1, device_id=peer, device_id_type=MESH_ID)
    pl.semaphore_wait(barrier, len(peers))


def flat_chunks(rows, n):
    part = rows // n
    return n, part, lambda p, c, j: (2 * p + c) * rows + j * part


def block_chunk(p, c, k):
    second = p // 8
    return ((1 - second) * ((2 * c + k) * 8 + p) + second * (4 * p + 2 * c + k)) * BLOCK


ORDER = [("near", 0), ("z", 1), ("z", 3), ("far", 0), ("z", 2), ("near", 1), ("near", 3), ("near", 2)]
ORDER += [("both", 0), ("far", 1), ("far", 3), ("far", 2), ("both", 1), ("both", 3), ("both", 2)]
ORDER += [("core", i) for i in range(16)]

def gather_kernel(layouts, stagger, *refs):
    count = len(layouts)
    fulls = refs[count + 1 : 2 * count + 1]
    line_full = refs[2 * count + 1]
    send, recv, local, line_sems = refs[2 * count + 2 : 2 * count + 6]
    held = refs[2 * count + 6 :]
    brought = [pltpu.make_async_copy(s, h, local.at[n]) for n, (s, h) in enumerate(zip(refs[: count + 1], held))]
    for copy in brought:
        copy.start()
    sources, line_source = held[:count], held[count]
    p, c, z, near, far, both = places()
    zs = [along_z(p, z, k) for k in range(4)]
    enter([(q, c) for q in zs[1:]] + [(near, c), (far, c), (p, 1 - c)])
    for copy in brought:
        copy.wait()
    jobs = [(a, j) for a, layout in enumerate(layouts) for j in range(layout[0])]

    def target(owner, job):
        a, j = jobs[job]
        _, rows, place = layouts[a]
        return fulls[a].at[pl.ds(pl.multiple_of(place(*owner, j), 8), rows)]

    def source(job):
        a, j = jobs[job]
        rows = layouts[a][1]
        return sources[a].at[pl.ds(j * rows, rows)]

    started = []

    def forward(owner, own, event, peer, job):
        t = target(owner, job)
        copy = pltpu.make_async_remote_copy(
            source(job) if own else t, t, send.at[event, job], recv.at[event, job], device_id=peer, device_id_type=MESH_ID
        )
        copy.start()
        started.append(copy)

    def arrive(owner, event, job):
        t = target(owner, job)
        pltpu.make_async_remote_copy(
            t, t, send.at[event, job], recv.at[event, job], device_id=(p, 1 - c), device_id_type=MESH_ID
        ).wait_recv()

    me = (p, c)

    def begin(job):
        forward(me, True, 3, (near, c), job)
        for k in (1, 3, 2):
            forward(me, True, 3 - k, (zs[k], c), job)
        forward(me, True, 7, (far, c), job)
        forward(me, True, 15, (p, 1 - c), job)
        pltpu.make_async_copy(source(job), target(me, job), local.at[job]).start()

    def take(kind, k, job):
        if kind == "z":
            owner = (zs[k], c)
            arrive(owner, k - 1, job)
            forward(owner, False, 3 + k, (near, c), job)
            forward(owner, False, 7 + k, (far, c), job)
            forward(owner, False, 15 + k, (p, 1 - c), job)
        elif kind == "near":
            owner = (along_z(near, z, k), c)
            arrive(owner, 3 + k, job)
            forward(owner, False, 11 + k, (far, c), job)
            forward(owner, False, 19 + k, (p, 1 - c), job)
        elif kind == "far":
            owner = (along_z(far, z, k), c)
            arrive(owner, 7 + k, job)
            forward(owner, False, 23 + k, (p, 1 - c), job)
        elif kind == "both":
            owner = (along_z(both, z, k), c)
            arrive(owner, 11 + k, job)
            forward(owner, False, 27 + k, (p, 1 - c), job)
        elif kind == "core":
            line = (p, far, near, both)[k // 4]
            arrive((along_z(line, z, k % 4), 1 - c), 15 + k, job)

    lines = []
    for k in (1, 3, 2):
        lines.append(
            pltpu.make_async_remote_copy(
                line_source, line_full.at[4 - k], line_sems.at[k], line_sems.at[7 - k],
                device_id=(zs[k], c), device_id_type=MESH_ID,
            )
        )
    lines.append(pltpu.make_async_copy(line_source, line_full.at[0], line_sems.at[0]))

    steps = [(2 * stagger + 2, -2, 0)]
    for job in range(len(jobs)):
        begin_at = stagger * min(job, layouts[0][0] - 1)
        for i in range(-1, len(ORDER)):
            steps.append((begin_at + i + 1, i, job))
    for _, i, job in sorted(steps):
        if i == -2:
            for copy in lines:
                copy.start()
        elif i < 0:
            begin(job)
        else:
            take(*ORDER[i], job)
    for k in (1, 2, 3):
        spot = line_full.at[k]
        pltpu.make_async_remote_copy(
            spot, spot, line_sems.at[k], line_sems.at[3 + k], device_id=(p, 1 - c), device_id_type=MESH_ID
        ).wait_recv()
    for copy in lines[:3]:
        copy.wait_send()
    lines[3].wait()
    for copy in started:
        copy.wait_send()
    for job in range(len(jobs)):
        pltpu.make_async_copy(source(job), target(me, job), local.at[job]).wait()


def gather_all(layouts, stagger, shards_in, line, name_id):
    copies = sum(l[0] for l in layouts)
    everywhere = pl.BlockSpec(memory_space=pl.ANY)
    shapes = [jax.ShapeDtypeStruct((32 * s.shape[0],) + s.shape[1:], s.dtype) for s in shards_in]
    shapes.append(jax.ShapeDtypeStruct((4,) + line.shape, line.dtype))
    return pl.pallas_call(
        functools.partial(gather_kernel, layouts, stagger),
        out_shape=shapes,
        in_specs=[everywhere] * len(shapes),
        out_specs=[everywhere] * len(shapes),
        scratch_shapes=[
            pltpu.SemaphoreType.DMA((31, copies)),
            pltpu.SemaphoreType.DMA((31, copies)),
            pltpu.SemaphoreType.DMA((copies,)),
            pltpu.SemaphoreType.DMA((7,)),
        ]
        + [pltpu.VMEM(a.shape, a.dtype) for a in (*shards_in, line)],
        compiler_params=pltpu.CompilerParams(collective_id=name_id, has_side_effects=True),
        name="gather_all",
    )(*shards_in, line)


SUM_ORDER = [(3, 0), (3, 1), (3, 3), (3, 2), (2, 0), (2, 1), (2, 3), (2, 2)]
SUM_ORDER += [(1, 1), (1, 3), (1, 2), (1, 0), (0, 1), (0, 3), (0, 2), (0, 0)]
AHEAD = 3


def scatter_kernel(layouts, stagger, *refs):
    count = len(layouts)
    grads = refs[:count]
    line_grads = refs[count : count + 4]
    outs = refs[count + 4 : 2 * count + 4]
    line_out = refs[2 * count + 4]
    scratch = refs[2 * count + 5 :]
    line_parts, line_sums, line_got, line_sum, line_sems, line_load_sems = scratch[-6:]
    p, c, z, near, far, both = places()
    zs = [along_z(p, z, k) for k in range(4)]
    enter([(q, c) for q in zs[1:]] + [(near, c), (far, c), (p, 1 - c)])
    csend, crecv, bsend, brecv, load_sem, out_sem = scratch[:6]
    buffers = [scratch[6 + 6 * a : 12 + 6 * a] for a in range(count)]
    jobs = [(a, j) for a, layout in enumerate(layouts) for j in range(layout[0])]
    lines = (p, near, far, both)
    partner_lines = (p, far, near, both)

    def view(job, ref, slot):
        a, j = jobs[job]
        rows = layouts[a][1]
        return ref.at[slot, pl.ds(j * rows, rows)]

    def piece(owner, job):
        a, j = jobs[job]
        _, rows, place = layouts[a]
        return grads[a].at[pl.ds(pl.multiple_of(place(*owner, j), 8), rows)]

    def to_core(i, job):
        g, k = SUM_ORDER[i]
        owner = (along_z(partner_lines[g], z, k), 1 - c)
        rc = buffers[jobs[job][0]][0]
        return pltpu.make_async_remote_copy(
            piece(owner, job), view(job, rc, g * 4 + k), csend.at[i, job], crecv.at[i, job],
            device_id=(p, 1 - c), device_id_type=MESH_ID,
        )

    def load(i, job):
        g, k = SUM_ORDER[i]
        own = buffers[jobs[job][0]][4]
        return pltpu.make_async_copy(
            piece((along_z(lines[g], z, k), c), job), view(job, own, i % AHEAD), load_sem.at[i, job]
        )

    def onward(i, job):
        g, k = SUM_ORDER[i]
        rc, rb, ra, rz = buffers[jobs[job][0]][:4]
        if g == 3:
            target, event, peer = view(job, rb, 4 + k), 4 + k, (far, c)
        elif g == 2:
            target, event, peer = view(job, rb, k), k, (far, c)
        elif g == 1:
            target, event, peer = view(job, ra, k), 8 + k, (near, c)
        else:
            target, event, peer = view(job, rz, 3 - k), 12 + 3 - k, (zs[k], c)
        return pltpu.make_async_remote_copy(
            view(job, rc, g * 4 + k), target, bsend.at[event, job], brecv.at[event, job],
            device_id=peer, device_id_type=MESH_ID,
        )

    def landed(event, job):
        rc, rb, ra, rz = buffers[jobs[job][0]][:4]
        if event < 8:
            target = view(job, rb, event)
        elif event < 12:
            target = view(job, ra, event - 8)
        else:
            target = view(job, rz, event - 12)
        pltpu.make_async_remote_copy(
            target, target, bsend.at[event, job], brecv.at[event, job], device_id=(p, 1 - c), device_id_type=MESH_ID
        ).wait_recv()
        return target

    def add_up(parts, target):
        rows = target.shape[0]
        step = math.gcd(rows, 16)

        @pl.loop(0, rows // step)
        def _(n):
            at = pl.ds(pl.multiple_of(n * step, step), step)
            total = parts[0][at].astype(jnp.float32)
            for part in parts[1:]:
                total = total + part[at].astype(jnp.float32)
            target[at] = total.astype(target.dtype)

    def start(i, job):
        to_core(i, job).start()
        load(i, job).start()

    def final_copies(job):
        a, j = jobs[job]
        rows = layouts[a][1]
        return [pltpu.make_async_copy(view(job, buffers[a][5], 0), outs[a].at[pl.ds(j * rows, rows)], out_sem.at[job, 0])]

    line_loads = [
        [pltpu.make_async_copy(ref.at[k], line_parts.at[k, n], line_load_sems.at[k, n]) for n, ref in enumerate(line_grads)]
        for k in range(4)
    ]
    line_sends = {
        k: pltpu.make_async_remote_copy(
            line_sums.at[k], line_got.at[3 - k], line_sems.at[k], line_sems.at[7 - k],
            device_id=(zs[k], c), device_id_type=MESH_ID,
        )
        for k in (1, 3, 2)
    }

    def line_step(k):
        for load_part in line_loads[k]:
            load_part.wait()
        add_up([line_parts.at[k, n] for n in range(4)], line_sums.at[k])
        if k:
            line_sends[k].start()

    half = line_sum.shape[0]
    spot = line_out.at[pl.ds(pl.multiple_of(c * half, 8), half)]
    line_stores = [
        pltpu.make_async_copy(line_sum, spot, line_sems.at[7]),
        pltpu.make_async_remote_copy(
            line_sum, spot, line_sems.at[8], line_sems.at[9], device_id=(p, 1 - c), device_id_type=MESH_ID
        ),
    ]

    def line_finish():
        for k in (1, 2, 3):
            target = line_got.at[k - 1]
            pltpu.make_async_remote_copy(
                target, target, line_sems.at[k], line_sems.at[3 + k], device_id=(p, 1 - c), device_id_type=MESH_ID
            ).wait_recv()
        add_up([line_sums.at[0]] + [line_got.at[n] for n in range(3)], line_sum)
        for copy in line_stores:
            copy.start()

    def step(i, job):
        g, k = SUM_ORDER[i]
        rc, rb, ra, rz, own, done = buffers[jobs[job][0]]
        load(i, job).wait()
        to_core(i, job).wait_recv()
        here = view(job, rc, g * 4 + k)
        parts = [here, view(job, own, i % AHEAD)]
        if g == 1:
            parts.append(landed(4 + k, job))
        if g == 0:
            parts.append(landed(k, job))
            parts.append(landed(8 + k, job))
        if (g, k) == (0, 0):
            parts += [landed(12 + n, job) for n in range(3)]
            add_up(parts, view(job, done, 0))
            for copy in final_copies(job):
                copy.start()
        else:
            add_up(parts, here)
            onward(i, job).start()
        if i + AHEAD < 16:
            start(i + AHEAD, job)

    for k in (1, 3, 2, 0):
        for load_part in line_loads[k]:
            load_part.start()
    for job in range(len(jobs)):
        for n in range(AHEAD):
            start(n, job)
    steps = []
    for job in range(len(jobs)):
        begin = stagger * min(job, layouts[0][0] - 1)
        for i in range(16):
            steps.append((begin + i + 2 * (i // 4 - 1) * (i // 8), job, i))
    steps.append((max(steps)[0] - 6, 0, -1))
    for n, k in enumerate((1, 3, 2, 0)):
        steps.append((n, len(jobs), -2 - k))
    for _, job, i in sorted(steps):
        if i == -1:
            line_finish()
        elif i < 0:
            line_step(-2 - i)
        else:
            step(i, job)
    for job in range(len(jobs)):
        for i in range(16):
            to_core(i, job).wait_send()
            if i < 15:
                onward(i, job).wait_send()
        for copy in final_copies(job):
            copy.wait()
    for copy in line_sends.values():
        copy.wait_send()
    for copy in line_stores:
        copy.wait()


def scatter_sum(layouts, stagger, grads, lines, name_id):
    jobs = sum(l[0] for l in layouts)
    scratch = [
        pltpu.SemaphoreType.DMA((16, jobs)),
        pltpu.SemaphoreType.DMA((16, jobs)),
        pltpu.SemaphoreType.DMA((15, jobs)),
        pltpu.SemaphoreType.DMA((15, jobs)),
        pltpu.SemaphoreType.DMA((16, jobs)),
        pltpu.SemaphoreType.DMA((jobs, 3)),
    ]
    shapes = []
    for layout, grad in zip(layouts, grads):
        rows, width = layout[0] * layout[1], grad.shape[1]
        for slots in (16, 8, 4, 3, AHEAD):
            scratch.append(pltpu.VMEM((slots, rows, width), grad.dtype))
        scratch.append(pltpu.VMEM((1, rows, width), jnp.float32))
        shapes.append(jax.ShapeDtypeStruct((rows, width), jnp.float32))
    piece, kind = lines[-1].shape[1:], lines[-1].dtype
    scratch += [
        pltpu.VMEM((4, 4) + piece, kind),
        pltpu.VMEM((4,) + piece, kind),
        pltpu.VMEM((3,) + piece, kind),
        pltpu.VMEM(piece, kind),
        pltpu.SemaphoreType.DMA((10,)),
        pltpu.SemaphoreType.DMA((4, 4)),
    ]
    shapes.append(jax.ShapeDtypeStruct((2 * piece[0], piece[1]), kind))
    everywhere = pl.BlockSpec(memory_space=pl.ANY)
    return pl.pallas_call(
        functools.partial(scatter_kernel, layouts, stagger),
        out_shape=shapes,
        in_specs=[everywhere] * (len(grads) + len(lines)),
        out_specs=[everywhere] * len(shapes),
        scratch_shapes=scratch,
        compiler_params=pltpu.CompilerParams(
            collective_id=name_id, has_side_effects=True, vmem_limit_bytes=48 * 1024 * 1024
        ),
        name="scatter_sum",
    )(*grads, *lines)


GELU_A = math.sqrt(2.0 / math.pi)
GELU_B = 0.044715


def chunk_sources():
    p, c, z, _, _, _ = places()
    x, y = p % 2, (p // 2) % 2
    out = []
    for other in range(2):
        core = (c + other) % 2
        for g in range(4):
            dx = (1 - core) * (g % 2) + core * (g // 2)
            dy = (1 - core) * (g // 2) + core * (g % 2)
            for k in range(4):
                owner = ((z + k) % 4) * 4 + ((y + dy) % 2) * 2 + (x + dx) % 2
                for half in range(2):
                    out.append((other, g, k, half, block_chunk(owner, core, half) // BLOCK))
    return out


def panel_loads(refs, held, sems):
    if len(refs) == 1:
        for n in range(held.shape[0] // WIDE):
            at = pl.ds(n * WIDE, WIDE)
            pltpu.make_async_copy(refs[0].at[at], held.at[at], sems.at[n]).start()
        return
    for other, g, k, half, chunk in chunk_sources():
        source = refs[other * 4 + g].at[k, pl.ds(half * BLOCK, BLOCK)]
        target = held.at[pl.ds(pl.multiple_of(chunk * BLOCK, BLOCK), BLOCK)]
        pltpu.make_async_copy(source, target, sems.at[chunk // 8]).start()


def panel_ready(held, sems, n):
    at = pl.ds(pl.multiple_of(n * WIDE, WIDE), WIDE)
    pltpu.make_async_copy(held.at[at], held.at[at], sems.at[n]).wait()
    return held.at[at]


def mlp_fwd_kernel(count, *refs):
    sources = refs[:count]
    h_ref, s_ref, up_ref, act_ref, grid_ref, held, total, sems = refs[count:]
    step = pl.program_id(0)
    steps = pl.num_programs(0)

    @pl.when(step == 0)
    def _():
        panel_loads(sources, held, sems)
        total[...] = s_ref[...]

    up = product(h_ref[...], panel_ready(held, sems, step)[...])
    up_ref[0] = up
    act = 0.5 * up * (1.0 + jnp.tanh(GELU_A * (up + GELU_B * up * up * up)))
    act = act.astype(jnp.bfloat16)
    act_ref[0] = act
    total[...] += product(act, panel_ready(held, sems, steps + step)[...])

    @pl.when(step == steps - 1)
    def _():
        grid_ref[...] = total[...].astype(jnp.bfloat16)


def mlp_fwd(panels, hidden, stream):
    rows = hidden.shape[0]
    steps = HID // WIDE
    whole = pl.BlockSpec((rows, WIDE), lambda n: (0, 0))
    part = pl.BlockSpec((1, rows, WIDE), lambda n: (n, 0, 0))
    return pl.pallas_call(
        functools.partial(mlp_fwd_kernel, len(panels)),
        grid=(steps,),
        in_specs=[pl.BlockSpec(memory_space=pl.ANY)] * len(panels) + [whole, whole],
        out_specs=[part, part, whole],
        out_shape=[
            jax.ShapeDtypeStruct((steps, rows, WIDE), jnp.float32),
            jax.ShapeDtypeStruct((steps, rows, WIDE), jnp.bfloat16),
            jax.ShapeDtypeStruct((rows, WIDE), jnp.bfloat16),
        ],
        scratch_shapes=[
            pltpu.VMEM((2 * HID, WIDE), jnp.bfloat16),
            pltpu.VMEM((rows, WIDE), jnp.float32),
            pltpu.SemaphoreType.DMA((2 * steps,)),
        ],
        compiler_params=pltpu.CompilerParams(vmem_limit_bytes=56 * 1024 * 1024),
        cost_estimate=BRIEF,
        name="mlp_fwd",
    )(*panels, hidden, stream)


def mlp_bwd_kernel(count, *refs):
    sources = refs[:count]
    outs = 2 if count > 1 else 1
    h_ref, g_ref, up_ref, act_ref = refs[count : count + 4]
    dh_ref = refs[count + 4]
    grads = refs[count + 5 : count + 5 + outs]
    held, staged, sems, out_sem = refs[count + 5 + outs :]
    step = pl.program_id(0)
    steps = pl.num_programs(0)

    @pl.when(step == 0)
    def _():
        panel_loads(sources, held, sems)
        dh_ref[...] = jnp.zeros_like(dh_ref)

    def tn_dot(left, right):
        return lax.dot_general(left, right, (((0,), (0,)), ((), ())), preferred_element_type=jnp.float32)

    def drain(side):
        pltpu.make_async_copy(staged.at[side], staged.at[side], out_sem.at[side]).wait()

    def store(side):
        panel = side * steps + step
        source = staged.at[side]
        if count == 1:
            at = pl.ds(pl.multiple_of(panel * WIDE, WIDE), WIDE)
            pltpu.make_async_copy(source, grads[0].at[at], out_sem.at[side]).start()
            return
        p, c, z, _, _, _ = places()
        for n in range(8):
            if side == 0:
                owner, core, half = n, step // 2, step % 2
            else:
                row = step * 8 + n
                owner, core, half = 8 + row // 4, (n // 2) % 2, n % 2
            dx = (owner % 2 + p % 2) % 2
            dy = ((owner // 2) % 2 + (p // 2) % 2) % 2
            g = (1 - core) * (dx + 2 * dy) + core * (dy + 2 * dx)
            spot = g * 4 + (owner // 4 - z + 4) % 4
            at = pl.ds(pl.multiple_of(half * BLOCK, BLOCK), BLOCK)
            from_ref = source.at[pl.ds(n * BLOCK, BLOCK)]

            @pl.when((core + c) % 2 == 0)
            def _():
                pltpu.make_async_copy(from_ref, grads[0].at[spot, at], out_sem.at[side]).start()

            @pl.when((core + c) % 2 == 1)
            def _():
                pltpu.make_async_copy(from_ref, grads[1].at[spot, at], out_sem.at[side]).start()

    pulled = g_ref[...]

    @pl.when(step > 0)
    def _():
        drain(1)

    staged[1] = tn_dot(act_ref[0], pulled).astype(jnp.bfloat16)
    store(1)
    grad_act = nt_dot(pulled, panel_ready(held, sems, steps + step)[...])
    up = up_ref[0]
    square = up * up
    bend = jnp.tanh(GELU_A * up * (1.0 + GELU_B * square))
    slope = 0.5 * (1.0 + bend) + 0.5 * GELU_A * up * (1.0 - bend * bend) * (1.0 + 3.0 * GELU_B * square)
    grad_up = (grad_act * slope).astype(jnp.bfloat16)

    @pl.when(step > 0)
    def _():
        drain(0)

    staged[0] = tn_dot(h_ref[...], grad_up).astype(jnp.bfloat16)
    store(0)
    dh_ref[...] += nt_dot(grad_up, panel_ready(held, sems, step)[...])

    @pl.when(step == steps - 1)
    def _():
        drain(0)
        drain(1)


def mlp_bwd(panels, hidden, grad, up, act):
    rows = hidden.shape[0]
    steps = HID // WIDE
    whole = pl.BlockSpec((rows, WIDE), lambda n: (0, 0))
    part = pl.BlockSpec((1, rows, WIDE), lambda n: (n, 0, 0))
    if len(panels) == 1:
        shapes = [jax.ShapeDtypeStruct((2 * HID, WIDE), jnp.bfloat16)]
    else:
        shapes = [jax.ShapeDtypeStruct((16, 2 * BLOCK, WIDE), jnp.bfloat16)] * 2
    return pl.pallas_call(
        functools.partial(mlp_bwd_kernel, len(panels)),
        grid=(steps,),
        in_specs=[pl.BlockSpec(memory_space=pl.ANY)] * len(panels) + [whole, whole, part, part],
        out_specs=[whole] + [pl.BlockSpec(memory_space=pl.ANY)] * len(shapes),
        out_shape=[jax.ShapeDtypeStruct((rows, WIDE), jnp.float32)] + shapes,
        scratch_shapes=[
            pltpu.VMEM((2 * HID, WIDE), jnp.bfloat16),
            pltpu.VMEM((2, WIDE, WIDE), jnp.bfloat16),
            pltpu.SemaphoreType.DMA((2 * steps,)),
            pltpu.SemaphoreType.DMA((2,)),
        ],
        compiler_params=pltpu.CompilerParams(vmem_limit_bytes=58 * 1024 * 1024),
        cost_estimate=BRIEF,
        name="mlp_bwd",
    )(*panels, hidden, grad, up, act)


SLOT = 128
TAPS = 16


def spread_deconv_kernel(first, rows_ref, o_ref, raw, flat, turned, sem):
    load = pltpu.make_async_copy(rows_ref.at[pl.ds(first, raw.shape[0])], raw, sem)
    load.start()
    load.wait()
    whole = raw[...].reshape(TAPS * CH, WIDE).astype(jnp.float32)
    for n in range(WIDE // SLOT):
        flat[n] = whole[:, n * SLOT : (n + 1) * SLOT]
    lane = lax.broadcasted_iota(jnp.int32, (D // 4, SLOT), 1)

    def block(i, j):
        at = 10 * i + j
        return flat[at % 8, pl.ds(at // 8, D // 4, stride=5), :]

    for tap in range(TAPS):
        j, start = divmod(tap * CH, SLOT)
        for i in range(4):
            part = block(i, j)
            if start:
                part = pltpu.roll(part, SLOT - start, 1)
            if start + CH > SLOT:
                part = jnp.where(lane < SLOT - start, part, pltpu.roll(block(i, j + 1), SLOT - start, 1))
            turned[pl.ds(i, D // 4, stride=4), :] = jnp.where(lane < CH, part, 0.0)
        o_ref[:, tap * SLOT : (tap + 1) * SLOT] = turned[...].astype(jnp.bfloat16)


def spread_deconv(rows, first):
    return pl.pallas_call(
        functools.partial(spread_deconv_kernel, first),
        in_specs=[pl.BlockSpec(memory_space=pl.ANY)],
        out_specs=pl.BlockSpec(memory_space=pltpu.VMEM),
        out_shape=jax.ShapeDtypeStruct((D, TAPS * SLOT), jnp.bfloat16),
        scratch_shapes=[
            pltpu.VMEM((TAPS * CH // 8, 8, WIDE), jnp.bfloat16),
            pltpu.VMEM((WIDE // SLOT, TAPS * CH, SLOT), jnp.float32),
            pltpu.VMEM((D, SLOT), jnp.float32),
            pltpu.SemaphoreType.DMA,
        ],
        compiler_params=pltpu.CompilerParams(vmem_limit_bytes=32 * 1024 * 1024),
        name="spread_deconv",
    )(rows)


def with_edges(own, edge):
    place = lax.axis_index("strip")
    above = jnp.where(place == 0, jnp.zeros_like(edge), edge)
    below = jnp.where(place == 0, edge, jnp.zeros_like(edge))
    return jnp.concatenate([above, own, below], 0)


def moved(value, step):
    column = lax.broadcasted_iota(jnp.int32, value.shape, 0) % TC
    inside = (column + step >= 0) & (column + step < TC)
    return jnp.where(inside, pltpu.roll(value, (-step) % value.shape[0], 0), 0.0)


def deconv_fwd_kernel(grid_ref, edge_ref, w_ref, o_ref, taps, fine):
    padded = with_edges(grid_ref[0], edge_ref[0])
    rows = grid_ref.shape[1]
    taps[...] = product(padded, w_ref[...])

    def tap(kr, kc, r):
        slot = kr * 4 + kc
        return taps[pl.ds((r + 1) * TC, rows), slot * SLOT : (slot + 1) * SLOT]

    for i in range(2):
        for j in range(2):
            total = tap(i + 1, j + 1, 0) + tap(3 - 3 * i, j + 1, 2 * i - 1)
            side = tap(i + 1, 3 - 3 * j, 0) + tap(3 - 3 * i, 3 - 3 * j, 2 * i - 1)
            total = total + moved(side, 2 * j - 1)
            for a in range(rows // TC):
                fine[pl.ds((2 * a + i) * 2 * TC + j, TC, stride=2), :] = total[a * TC : (a + 1) * TC]
    o_ref[0] = fine[...].astype(jnp.bfloat16)


def deconv_fwd(grid, edge, weights):
    planes, rows, _ = grid.shape
    return pl.pallas_call(
        deconv_fwd_kernel,
        grid=(planes,),
        in_specs=[
            pl.BlockSpec((1, rows, D), lambda n: (n, 0, 0)),
            pl.BlockSpec((1, TC, D), lambda n: (n, 0, 0)),
            pl.BlockSpec(weights.shape, lambda n: (0, 0)),
        ],
        out_specs=pl.BlockSpec((1, 4 * rows, SLOT), lambda n: (n, 0, 0)),
        out_shape=jax.ShapeDtypeStruct((planes, 4 * rows, SLOT), jnp.bfloat16),
        scratch_shapes=[
            pltpu.VMEM((rows + 2 * TC, TAPS * SLOT), jnp.float32),
            pltpu.VMEM((4 * rows, SLOT), jnp.float32),
        ],
        compiler_params=pltpu.CompilerParams(vmem_limit_bytes=40 * 1024 * 1024),
        name="deconv_fwd",
    )(grid, edge, weights)


def deconv_bwd_kernel(own_ref, got_ref, grid_ref, edge_ref, w_ref, gx_ref, gedge_ref, gw_ref, fine, spread, tokens, sums, flat):
    plane = pl.program_id(0)
    rows = grid_ref.shape[1]
    high = rows + 2 * TC
    place = lax.axis_index("strip")
    total = own_ref[0].astype(jnp.float32) + got_ref[0].astype(jnp.float32)
    total = jnp.concatenate([total, jnp.zeros((SLOT - CH, total.shape[1]), jnp.float32)], 0)
    fine[...] = total.T
    here = pl.ds(plane * high, high)
    tokens[here] = with_edges(grid_ref[0], edge_ref[0])
    for i in range(2):
        for j in range(2):
            parts = [fine[pl.ds((2 * a + i) * 2 * TC + j, TC, stride=2), :] for a in range(rows // TC)]
            part = jnp.concatenate(parts, 0)
            for kr in (i + 1, 3 - 3 * i):
                for kc in (j + 1, 3 - 3 * j):
                    value = part if kc == j + 1 else moved(part, 1 - 2 * j)
                    start = TC if kr == i + 1 else (0 if i == 0 else 2 * TC)
                    pieces = [value]
                    if start:
                        pieces.insert(0, jnp.zeros((start, SLOT), jnp.float32))
                    if high - rows - start:
                        pieces.append(jnp.zeros((high - rows - start, SLOT), jnp.float32))
                    slot = kr * 4 + kc
                    spread[here, slot * SLOT : (slot + 1) * SLOT] = jnp.concatenate(pieces, 0).astype(jnp.bfloat16)
    back = nt_dot(spread[here], w_ref[...])
    gx_ref[0] = back[TC : TC + rows]
    gedge_ref[0] = jnp.where(place == 0, back[TC + rows :], back[:TC]).astype(jnp.bfloat16)

    @pl.when(plane == pl.num_programs(0) - 1)
    def _():
        wide = 512
        for n in range(TAPS * SLOT // wide):
            columns = slice(n * wide, (n + 1) * wide)
            part = lax.dot_general(
                tokens[...], spread[:, columns], (((0,), (0,)), ((), ())), preferred_element_type=jnp.float32
            )
            for m in range(wide // SLOT):
                sums[n * (wide // SLOT) + m] = part[:, m * SLOT : (m + 1) * SLOT]
        lane = lax.broadcasted_iota(jnp.int32, (D // 4, SLOT), 1)
        for i in range(4):
            for j in range(TAPS * CH // SLOT):
                block = None
                for tap in range(j * SLOT // CH, (j * SLOT + SLOT - 1) // CH + 1):
                    part = sums[tap, pl.ds(i, D // 4, stride=4), :]
                    shift = tap * CH - j * SLOT
                    if shift % SLOT:
                        part = pltpu.roll(part, shift % SLOT, 1)
                    block = part if block is None else jnp.where(lane < shift, block, part)
                at = 10 * i + j
                flat[at % 8, pl.ds(at // 8, D // 4, stride=5), :] = block
        whole = jnp.concatenate([flat[n] for n in range(WIDE // SLOT)], 1)
        gw_ref[...] = whole.astype(jnp.bfloat16).reshape(gw_ref.shape)


def deconv_bwd(own, got, grid, edge, weights):
    planes, rows, _ = grid.shape
    high = rows + 2 * TC
    by_plane = lambda *shape: pl.BlockSpec((1,) + shape, lambda n: (n, 0, 0))
    return pl.pallas_call(
        deconv_bwd_kernel,
        grid=(planes,),
        in_specs=[
            by_plane(*own.shape[1:]),
            by_plane(*got.shape[1:]),
            by_plane(rows, D),
            by_plane(TC, D),
            pl.BlockSpec(weights.shape, lambda n: (0, 0)),
        ],
        out_specs=[by_plane(rows, D), by_plane(TC, D), pl.BlockSpec((TAPS * CH // 8, 8, WIDE), lambda n: (0, 0, 0))],
        out_shape=[
            jax.ShapeDtypeStruct((planes, rows, D), jnp.float32),
            jax.ShapeDtypeStruct((planes, TC, D), jnp.bfloat16),
            jax.ShapeDtypeStruct((TAPS * CH // 8, 8, WIDE), jnp.bfloat16),
        ],
        scratch_shapes=[
            pltpu.VMEM((4 * rows, SLOT), jnp.float32),
            pltpu.VMEM((planes * high, TAPS * SLOT), jnp.bfloat16),
            pltpu.VMEM((planes * high, D), jnp.bfloat16),
            pltpu.VMEM((TAPS, D, SLOT), jnp.float32),
            pltpu.VMEM((WIDE // SLOT, TAPS * CH, SLOT), jnp.float32),
        ],
        compiler_params=pltpu.CompilerParams(vmem_limit_bytes=56 * 1024 * 1024),
        name="deconv_bwd",
    )(own, got, grid, edge, weights)


def panel_view(rows_ref, first, count, depth):
    region = rows_ref.at[pl.ds(first, depth // 8 * count)]
    return region.reshape(depth // 8, count, 8, WIDE)


def project_kernel(first, count, depth, lead, x_ref, rows_ref, *rest):
    outs, held, sems = rest[:-2], rest[-2], rest[-1]
    step = pl.program_id(0)
    panels = panel_view(rows_ref, first, count, depth)

    @pl.when(step == 0)
    def _():
        for n in range(count):
            pltpu.make_async_copy(panels.at[:, n], held.at[n], sems.at[n]).start()

    pltpu.make_async_copy(held.at[step], held.at[step], sems.at[step]).wait()
    result = product(x_ref[...], held[step].reshape(depth, WIDE)).astype(jnp.bfloat16)
    if lead:

        @pl.when(step == 0)
        def _():
            outs[0][...] = result

        @pl.when(step > 0)
        def _():
            outs[1][0] = result

    else:
        outs[0][0] = result


def project(x, rows, first, count, lead):
    tokens, depth = x.shape
    specs = [pl.BlockSpec((1, tokens, WIDE), lambda n: (jnp.maximum(n - lead, 0), 0, 0))]
    shapes = [jax.ShapeDtypeStruct((count - lead, tokens, WIDE), jnp.bfloat16)]
    if lead:
        specs.insert(0, pl.BlockSpec((tokens, WIDE), lambda n: (0, 0)))
        shapes.insert(0, jax.ShapeDtypeStruct((tokens, WIDE), jnp.bfloat16))
    return pl.pallas_call(
        functools.partial(project_kernel, first, count, depth, lead),
        grid=(count,),
        in_specs=[pl.BlockSpec((tokens, depth), lambda n: (0, 0)), pl.BlockSpec(memory_space=pl.ANY)],
        out_specs=specs,
        out_shape=shapes,
        scratch_shapes=[pltpu.VMEM((count, depth // 8, 8, WIDE), jnp.bfloat16), pltpu.SemaphoreType.DMA((count,))],
        compiler_params=pltpu.CompilerParams(vmem_limit_bytes=32 * 1024 * 1024),
        cost_estimate=BRIEF,
        name="project",
    )(x, rows)


def project_back_kernel(first, count, depth, lead_ref, g_ref, rows_ref, o_ref, held, sems):
    step = pl.program_id(0)
    panels = panel_view(rows_ref, first, count, depth)

    @pl.when(step == 0)
    def _():
        for n in range(count):
            pltpu.make_async_copy(panels.at[:, n], held.at[n], sems.at[n]).start()

    pltpu.make_async_copy(held.at[step], held.at[step], sems.at[step]).wait()
    grad = jnp.where(step == 0, lead_ref[...], g_ref[0])
    back = nt_dot(grad, held[step].reshape(depth, WIDE))

    @pl.when(step == 0)
    def _():
        o_ref[...] = back

    @pl.when(step > 0)
    def _():
        o_ref[...] += back


def project_back(lead, grads, rows, first, depth):
    others, tokens, _ = grads.shape
    count = others + 1
    return pl.pallas_call(
        functools.partial(project_back_kernel, first, count, depth),
        grid=(count,),
        in_specs=[
            pl.BlockSpec((tokens, WIDE), lambda n: (0, 0)),
            pl.BlockSpec((1, tokens, WIDE), lambda n: (jnp.maximum(n - 1, 0), 0, 0)),
            pl.BlockSpec(memory_space=pl.ANY),
        ],
        out_specs=pl.BlockSpec((tokens, depth), lambda n: (0, 0)),
        out_shape=jax.ShapeDtypeStruct((tokens, depth), jnp.float32),
        scratch_shapes=[pltpu.VMEM((count, depth // 8, 8, WIDE), jnp.bfloat16), pltpu.SemaphoreType.DMA((count,))],
        compiler_params=pltpu.CompilerParams(vmem_limit_bytes=32 * 1024 * 1024),
        cost_estimate=BRIEF,
        name="project_back",
    )(lead, grads, rows)


def weight_grads_kernel(products, copies, *refs):
    arrays = refs[: len(refs) - 8]
    out, left, right, staged, bounce, load_sem, store_sem, copy_sem = refs[len(refs) - 8 :]
    step = pl.program_id(0)
    steps = len(products)

    def loads(n):
        side, (a, a_pick), (b, b_pick), _, _ = products[n]
        slot = n % 2
        source_a = arrays[a] if a_pick is None else arrays[a].at[a_pick]
        source_b = arrays[b] if b_pick is None else arrays[b].at[b_pick]
        rows, deep = side
        return [
            pltpu.make_async_copy(source_a, left.at[slot, pl.ds(0, rows), pl.ds(0, deep)], load_sem.at[slot, 0]),
            pltpu.make_async_copy(source_b, right.at[slot, pl.ds(0, rows)], load_sem.at[slot, 1]),
        ]

    def stores(n):
        (rows, deep), _, _, first, panels = products[n]
        slot = n % 2
        count, at = panels
        source = staged.at[slot, pl.ds(0, deep // 8)]
        target = panel_view(out, first, count, deep).at[:, at]
        return pltpu.make_async_copy(source, target, store_sem.at[slot])

    def bounced(n):
        a, first, count = copies[n]
        held = bounce.at[pl.ds(sum(c[2] for c in copies[:n]), count)]
        return (
            pltpu.make_async_copy(arrays[a], held, copy_sem.at[n, 0]),
            pltpu.make_async_copy(held, out.at[pl.ds(first, count)], copy_sem.at[n, 1]),
        )

    for n in range(steps):

        @pl.when(step == n)
        def _():
            if n == 0:
                for job in loads(0):
                    job.start()
                for m in range(len(copies)):
                    bounced(m)[0].start()
            if n == 1:
                for m in range(len(copies)):
                    bounced(m)[0].wait()
                    bounced(m)[1].start()
            if n + 1 < steps:
                for job in loads(n + 1):
                    job.start()
            for job in loads(n):
                job.wait()
            if n >= 2:
                stores(n - 2).wait()
            rows, deep = products[n][0]
            slot = n % 2
            total = lax.dot_general(
                left[slot, :rows, :deep], right[slot, :rows], (((0,), (0,)), ((), ())), preferred_element_type=jnp.float32
            )
            staged[slot, : deep // 8] = total.astype(jnp.bfloat16).reshape(deep // 8, 8, WIDE)
            stores(n).start()
            if n == steps - 1:
                if n > 0:
                    stores(n - 1).wait()
                stores(n).wait()
                for m in range(len(copies)):
                    bounced(m)[1].wait()


def weight_grads(arrays, products, copies, tile_rows):
    rows = max(p[0][0] for p in products)
    deep = max(p[0][1] for p in products)
    everywhere = pl.BlockSpec(memory_space=pl.ANY)
    return pl.pallas_call(
        functools.partial(weight_grads_kernel, products, copies),
        grid=(len(products),),
        in_specs=[everywhere] * len(arrays),
        out_specs=everywhere,
        out_shape=jax.ShapeDtypeStruct((tile_rows, 8, WIDE), jnp.bfloat16),
        scratch_shapes=[
            pltpu.VMEM((2, rows, deep), jnp.bfloat16),
            pltpu.VMEM((2, rows, WIDE), jnp.bfloat16),
            pltpu.VMEM((2, deep // 8, 8, WIDE), jnp.bfloat16),
            pltpu.VMEM((sum(c[2] for c in copies), 8, WIDE), jnp.bfloat16),
            pltpu.SemaphoreType.DMA((2, 2)),
            pltpu.SemaphoreType.DMA((2,)),
            pltpu.SemaphoreType.DMA((len(copies), 2)),
        ],
        compiler_params=pltpu.CompilerParams(vmem_limit_bytes=60 * 1024 * 1024),
        cost_estimate=BRIEF,
        name="weight_grads",
    )(*arrays)


TILE = 8 * WIDE
KV_AT = D * D
QKV_AT = KV_AT + DI * 2 * D + D * D
GAP_AT = QKV_AT + D * 3 * D + D * D + D * 16 * CH + CH * DEC_HID + DEC_HID * 4
QKV_GAP = -QKV_AT % (3 * TILE)
END_GAP = -GAP_AT % TILE
TILES = {}
_tile = 0
for _name, _rows in (
    ("query_cross", D),
    ("keyval_cross", 2 * DI),
    ("out_cross", D),
    ("gap", QKV_GAP // WIDE),
    ("qkv_self", 3 * D),
    ("out_self", D),
    ("deconv", 16 * CH),
    ("decode", 8),
    ("modulate", 6 * NCAM),
    ("triplane", 0),
):
    TILES[_name] = _tile
    _tile += _rows // 8


def direct_links():
    return lax.axis_size("dp") == 16 and lax.axis_size("strip") == 2


def regroup(rows, first, back):
    tile = first + lax.broadcasted_iota(jnp.int32, (rows.shape[0], 1), 0) // 8

    def turned(panels):
        shape = (-1, panels, 8, WIDE) if back else (-1, 8, panels, WIDE)
        return rows.reshape(shape).transpose(0, 2, 1, 3).reshape(rows.shape)

    in_kv = (tile >= TILES["keyval_cross"]) & (tile < TILES["out_cross"])
    in_qkv = (tile >= TILES["qkv_self"]) & (tile < TILES["out_self"])
    return jnp.where(in_kv, turned(2), jnp.where(in_qkv, turned(3), rows))


def tile_rows(length):
    return -(-length // (6 * TILE)) * 6


LANES = 128
TILE_LINES = TILE // LANES


def tile_place(tile):
    gap = QKV_GAP // LANES * jnp.where(tile >= TILES["gap"], 1, 0)
    return gap + END_GAP // LANES * jnp.where(tile >= TILES["modulate"], 1, 0)


def by_region(tile, work):
    in_kv = (tile >= TILES["keyval_cross"]) & (tile < TILES["out_cross"])
    in_qkv = (tile >= TILES["qkv_self"]) & (tile < TILES["out_self"])

    @pl.when(in_kv)
    def _():
        work(2)

    @pl.when(in_qkv)
    def _():
        work(3)

    @pl.when(jnp.logical_not(in_kv | in_qkv))
    def _():
        work(1)


def tile_lines(tile, first, panels):
    panel = lax.rem(tile, panels)
    return (tile - panel - first) * TILE_LINES + panel * 8


def prepare_kernel(own_ref, next_ref, blocks_ref, o_ref, chunks_ref, lines, tiles, sem):
    half = tiles.shape[0]
    core = lax.axis_index("strip")
    load = pltpu.make_async_copy(blocks_ref.at[pl.ds(core * half, half)], tiles, sem)
    load.start()
    place = lax.axis_index("dp") * 2 + core
    count = own_ref.shape[0]
    lines[:count] = own_ref[...]
    lines[count : count + next_ref.shape[0]] = next_ref[...]
    held = o_ref.shape[0] // 8
    first = place * held
    shift = place * (held * TILE_LINES - count)

    @pl.loop(0, held // 2)
    def _(n):
        def work(panels):
            rows = []
            for m in range(2):
                tile = first + 2 * n + m
                start = tile_lines(tile, first, panels) + shift - tile_place(tile)
                rows.append(jnp.concatenate([lines[pl.ds(start + j, 8, stride=8 * panels), :] for j in range(8)], 1))
            o_ref[pl.ds(pl.multiple_of(16 * n, 16), 16)] = jnp.concatenate(rows, 0).astype(jnp.bfloat16)

        by_region(first + 2 * n, work)

    load.wait()
    for n in range(half):
        at, column = n // 8 * BLOCK, n % 8 * BLOCK
        chunks_ref[at : at + BLOCK, column : column + BLOCK] = tiles[n].astype(jnp.bfloat16)


def prepare(weights, blocks):
    lines = weights.reshape(-1, LANES)
    count = lines.shape[0]
    held = tile_rows(weights.shape[0])
    reach = -(-32 * (held * TILE_LINES - count) // 8) * 8
    following = lax.ppermute(lines[:reach], AXES, [(n + 1, n) for n in range(31)])
    half = blocks.shape[0] // 2
    vmem = pl.BlockSpec(memory_space=pltpu.VMEM)
    return pl.pallas_call(
        prepare_kernel,
        in_specs=[vmem, vmem, pl.BlockSpec(memory_space=pl.ANY)],
        out_specs=[vmem, vmem],
        out_shape=[
            jax.ShapeDtypeStruct((held * 8, WIDE), jnp.bfloat16),
            jax.ShapeDtypeStruct((half // 8 * BLOCK, WIDE), jnp.bfloat16),
        ],
        scratch_shapes=[
            pltpu.VMEM((-(-(count + reach) // 8) * 8, LANES), jnp.float32),
            pltpu.VMEM((half, BLOCK, BLOCK), jnp.float32),
            pltpu.SemaphoreType.DMA,
        ],
        compiler_params=pltpu.CompilerParams(vmem_limit_bytes=16 * 1024 * 1024),
        name="prepare",
    )(lines, following, blocks)


def ungroup_kernel(rows_ref, o_ref):
    place = lax.axis_index("dp") * 2 + lax.axis_index("strip")
    held = rows_ref.shape[0] // 8
    first = place * held

    @pl.loop(0, held)
    def _(n):
        def work(panels):
            start = tile_lines(first + n, first, panels)
            at = pl.ds(pl.multiple_of(8 * n, 8), 8)
            for j in range(8):
                o_ref[pl.ds(start + j, 8, stride=8 * panels), :] = rows_ref[at, j * LANES : (j + 1) * LANES]

        by_region(first + n, work)


def ungroup(rows):
    vmem = pl.BlockSpec(memory_space=pltpu.VMEM)
    return pl.pallas_call(
        ungroup_kernel,
        in_specs=[vmem],
        out_specs=vmem,
        out_shape=jax.ShapeDtypeStruct((rows.size // LANES, LANES), jnp.float32),
        compiler_params=pltpu.CompilerParams(vmem_limit_bytes=16 * 1024 * 1024),
        name="ungroup",
    )(rows)


def adam_kernel(before_ref, sum_ref, w_ref, first_ref, second_ref, nw_ref, nfirst_ref, nsecond_ref, lines):
    place = lax.axis_index("dp") * 2 + lax.axis_index("strip")
    reach, summed, count = before_ref.shape[0], sum_ref.shape[0], w_ref.shape[0]
    lines[:reach] = before_ref[...]
    lines[reach : reach + summed] = sum_ref[...]
    shift = reach - place * (summed - count)
    gaps = (0, QKV_GAP // LANES, (QKV_GAP + END_GAP) // LANES)

    def update(at, rows):
        parts = [lines[pl.ds(shift + at + gap, rows), :] for gap in gaps]
        line = place * count + at + lax.broadcasted_iota(jnp.int32, (rows, LANES), 0)
        grad = jnp.where(line < QKV_AT // LANES, parts[0], jnp.where(line < GAP_AT // LANES, parts[1], parts[2]))
        here = pl.ds(at, rows)
        weights = w_ref[here]
        first = BETA_FIRST * first_ref[here] + (1.0 - BETA_FIRST) * grad
        second = BETA_SECOND * second_ref[here] + (1.0 - BETA_SECOND) * grad * grad
        nfirst_ref[here] = first
        nsecond_ref[here] = second
        fix_first = 1.0 - BETA_FIRST**ADAM_STEP
        fix_second = 1.0 - BETA_SECOND**ADAM_STEP
        step = first / fix_first / (jnp.sqrt(second / fix_second) + ADAM_EPS)
        nw_ref[here] = weights - ADAM_RATE * (step + WEIGHT_DECAY * weights)

    block = 32

    @pl.loop(0, count // block)
    def _(n):
        update(pl.multiple_of(block * n, block), block)

    if count % block:
        update(count - count % block, count % block)


def adam(rows, weights, first_moment, second_moment):
    length = weights.shape[0]
    count = length // LANES
    summed = ungroup(rows)
    reach = -(-32 * (summed.shape[0] - count) // 8) * 8
    before = lax.ppermute(summed[summed.shape[0] - reach :], AXES, [(n, n + 1) for n in range(31)])
    vmem = pl.BlockSpec(memory_space=pltpu.VMEM)
    gap = (QKV_GAP + END_GAP) // LANES
    results = pl.pallas_call(
        adam_kernel,
        in_specs=[vmem] * 5,
        out_specs=[vmem] * 3,
        out_shape=[jax.ShapeDtypeStruct((count, LANES), jnp.float32)] * 3,
        scratch_shapes=[pltpu.VMEM((-(-(reach + summed.shape[0] + gap) // 8) * 8, LANES), jnp.float32)],
        compiler_params=pltpu.CompilerParams(vmem_limit_bytes=32 * 1024 * 1024),
        name="adam",
    )(before, summed, *(a.reshape(count, LANES) for a in (weights, first_moment, second_moment)))
    return [result.reshape(length) for result in results]


def two_parts(value):
    coarse = value.astype(jnp.bfloat16)
    return coarse, (value - coarse.astype(jnp.float32)).astype(jnp.bfloat16)


def shampoo_kernel(tiles_ref, blocks_ref, sl_ref, sr_ref, rl_ref, rr_ref, nb_ref, g_ref, nl_ref, nr_ref, rms_ref):
    for n in range(8):
        grad = tiles_ref[:, n * BLOCK : (n + 1) * BLOCK]
        wide = grad.astype(jnp.float32)
        g_ref[n] = wide
        nl_ref[n] = STAT_DECAY * sl_ref[n] + (1.0 - STAT_DECAY) * nt_dot(grad, grad)
        square = lax.dot_general(grad, grad, (((0,), (0,)), ((), ())), preferred_element_type=jnp.float32)
        nr_ref[n] = STAT_DECAY * sr_ref[n] + (1.0 - STAT_DECAY) * square
        coarse, fine = two_parts(rr_ref[n])
        half = product(grad, jnp.concatenate([coarse, fine], 1))
        half_coarse, half_fine = two_parts(half[:, :BLOCK] + half[:, BLOCK:])
        coarse, fine = two_parts(rl_ref[n])
        cond = product(jnp.concatenate([coarse, fine], 1), jnp.concatenate([half_coarse, half_coarse], 0))
        cond = cond + product(coarse, half_fine)
        rms = jnp.sqrt(jnp.mean(cond * cond, axis=(0, 1), keepdims=True) + RMS_EPS)
        nb_ref[n] = blocks_ref[n] - SHAMPOO_RATE * cond / rms
        rms_ref[n : n + 1] = jnp.broadcast_to(rms, (1, LANES))


def shampoo(chunks, blocks, stat_left, stat_right, root_left, root_right):
    count = blocks.shape[0]
    eight = pl.BlockSpec((8, BLOCK, BLOCK), lambda n: (n, 0, 0))
    whole = jax.ShapeDtypeStruct(blocks.shape, jnp.float32)
    *results, rms = pl.pallas_call(
        shampoo_kernel,
        grid=(count // 8,),
        in_specs=[pl.BlockSpec((BLOCK, WIDE), lambda n: (n, 0))] + [eight] * 5,
        out_specs=[eight] * 4 + [pl.BlockSpec((8, LANES), lambda n: (n, 0))],
        out_shape=[whole] * 4 + [jax.ShapeDtypeStruct((count, LANES), jnp.float32)],
        compiler_params=pltpu.CompilerParams(vmem_limit_bytes=60 * 1024 * 1024),
        name="shampoo",
    )(chunks, blocks, stat_left, stat_right, root_left, root_right)
    return *results, rms[:, 0]


def chunks_of(tiles):
    return tiles.reshape(-1, 8, BLOCK, BLOCK).transpose(0, 2, 1, 3).reshape(-1, WIDE)


def tiles_of(chunks):
    return chunks.reshape(-1, BLOCK, 8, BLOCK).transpose(0, 2, 1, 3).reshape(-1, BLOCK, BLOCK)


def panels_of(chunks):
    half = chunks.shape[0] // 2
    first = chunks[:half].reshape(D // BLOCK, HID // WIDE, BLOCK, WIDE).transpose(1, 0, 2, 3)
    return jnp.concatenate([first.reshape(half, WIDE), chunks[half:]])


def chunks_of_panels(panels):
    half = panels.shape[0] // 2
    first = panels[:half].reshape(HID // WIDE, D // BLOCK, BLOCK, WIDE).transpose(1, 0, 2, 3)
    return jnp.concatenate([first.reshape(half, WIDE), panels[half:]])


META = (1, 8, lambda p, c, j: (2 * p + c) * 8)
SWAP = ((0, 1), (1, 0))
AXES = ("dp", "strip")


def pairs_to(target):
    return [(2 * p + c, sum(v * w for v, w in zip(target(p, c), (2, 1)))) for p in range(16) for c in range(2)]


NEAR = pairs_to(lambda p, c: (p ^ (1 + c), c))
FAR = pairs_to(lambda p, c: (p ^ (2 - c), c))
CORE = pairs_to(lambda p, c: (p, 1 - c))


def gather_weights(weights, blocks, part):
    if direct_links():
        own, tiles = prepare(weights, blocks)
        rows, parts, line = gather_all([flat_chunks(own.shape[0], 3), META], 6, [own, part], tiles, 0)
        near = lax.ppermute(line, AXES, NEAR)
        return rows, [line, near], jnp.sum(parts[::8, 0])
    flat = lax.all_gather(weights.astype(jnp.bfloat16), AXES, axis=0, tiled=True)
    tiles = lax.all_gather(blocks.astype(jnp.bfloat16), "dp", axis=0, tiled=True)
    gaps = [jnp.zeros((QKV_GAP,), flat.dtype), jnp.zeros((END_GAP,), flat.dtype)]
    rows = jnp.concatenate([flat[:QKV_AT], gaps[0], flat[QKV_AT:GAP_AT], gaps[1], flat[GAP_AT:]])
    rows = jnp.pad(rows, (0, -rows.shape[0] % (6 * TILE))).reshape(-1, WIDE)
    return regroup(rows, 0, False), [panels_of(chunks_of(tiles))], lax.psum(part[0, 0], AXES)


class Panels:
    def __init__(self, parts):
        self.parts = parts
        self.staged = len(parts) > 1

    def first(self, before):
        if not self.staged:
            return before
        line, near = self.parts
        near, before = lax.optimization_barrier((near, before))
        self.parts = [line, near, lax.ppermute(line, AXES, FAR)]
        return before

    def second(self, before):
        if not self.staged:
            return before
        line, near, far = self.parts
        far, before = lax.optimization_barrier((far, before))
        self.parts = [line, near, far, lax.ppermute(near, AXES, FAR)]
        return before

    def third(self, after):
        if not self.staged:
            return self.parts
        line, near, far, both = self.parts
        both, after = lax.optimization_barrier((both, after))
        return [line, near, far, both] + [lax.ppermute(group, AXES, CORE) for group in (line, near, far, both)]


class PanelSums:
    def __init__(self, grads):
        self.parts = grads
        self.staged = len(grads) > 1
        if self.staged:
            self.mine = grads[0]
            self.got = lax.ppermute(grads[1], AXES, CORE)

    def added(self, at, *parts):
        total = self.mine[at].astype(jnp.float32) + self.got[at].astype(jnp.float32)
        for part in parts:
            total = total + part.astype(jnp.float32)
        return total.astype(jnp.bfloat16)

    def first(self, before):
        if not self.staged:
            return before
        away, before = lax.optimization_barrier((self.added(slice(8, 16)), before))
        self.away = lax.ppermute(away, AXES, FAR)
        return before

    def second(self, before):
        if not self.staged:
            return before
        self.away, before = lax.optimization_barrier((self.away, before))
        near, before = lax.optimization_barrier((self.added(slice(4, 8), self.away[4:]), before))
        self.last = lax.ppermute(near, AXES, NEAR)
        return before

    def third(self, before):
        if not self.staged:
            return before
        self.last, before = lax.optimization_barrier((self.last, before))
        self.parts = [self.mine, self.got, self.away, self.last]
        return before


def reduce_grads(rows, panels, part):
    meta = jnp.full((32 * 8, 128), part, jnp.float32)
    summed, parts, tiles = scatter_sum([flat_chunks(rows.shape[0] // 32, 3), META], 6, [rows, meta], panels, 1)
    return summed, tiles, parts[0, 0]


def reduce_grads_plainly(rows, panels, part, length):
    flat = regroup(rows, 0, True).astype(jnp.float32).reshape(-1)
    flat = jnp.concatenate(
        [flat[:QKV_AT], flat[QKV_AT + QKV_GAP : GAP_AT + QKV_GAP], flat[GAP_AT + QKV_GAP + END_GAP :]]
    )
    devices = lax.axis_size("dp") * lax.axis_size("strip")
    flat = jnp.pad(flat, (0, max(0, devices * length - flat.shape[0])))[: devices * length]
    tiles = tiles_of(chunks_of_panels(panels[0])).astype(jnp.float32)
    flat_sum = lax.psum_scatter(flat, AXES, scatter_dimension=0, tiled=True)
    tile_sum = lax.psum_scatter(tiles, AXES, scatter_dimension=0, tiled=True)
    tile_sum = lax.all_gather(tile_sum.astype(jnp.bfloat16), "strip", axis=0, tiled=True)
    return flat_sum, chunks_of(tile_sum), lax.psum(part, AXES)


def adam_plainly(grad, weights, first_moment, second_moment):
    new_first = BETA_FIRST * first_moment + (1.0 - BETA_FIRST) * grad
    new_second = BETA_SECOND * second_moment + (1.0 - BETA_SECOND) * grad * grad
    fix_first = 1.0 - BETA_FIRST**ADAM_STEP
    fix_second = 1.0 - BETA_SECOND**ADAM_STEP
    moved = new_first / fix_first / (jnp.sqrt(new_second / fix_second) + ADAM_EPS)
    return weights - ADAM_RATE * (moved + WEIGHT_DECAY * weights), new_first, new_second


def shards(
    weights,
    blocks,
    stat_left,
    stat_right,
    root_left,
    root_right,
    first_moment,
    second_moment,
    image,
    camera,
    samples,
    ray_pixel,
    target,
    valid,
):
    strips = lax.axis_size("strip")
    place = lax.axis_index("strip")
    mask, wanted, own_count = pick(ray_pixel, valid, target[0])
    rows, panels, count = gather_weights(weights, blocks, own_count)
    tiled = rows.reshape(-1, 8, WIDE)

    def square(name):
        return rows[TILES[name] * 8 : TILES[name] * 8 + D]

    def plain(name, count):
        return rows[TILES[name] * 8 : TILES[name] * 8 + count]

    deconv = spread_deconv(tiled, TILES["deconv"])
    decode = plain("decode", 8).reshape(-1)
    decode_in = decode[: CH * DEC_HID].reshape(CH, DEC_HID)
    decode_out = decode[CH * DEC_HID : CH * DEC_HID + DEC_HID * 4].reshape(DEC_HID, 4)
    picture = image[0]
    real_keys = picture.shape[0]
    picture = jnp.pad(picture, ((0, -real_keys % 16), (0, 0)))
    mods = lax.dynamic_slice_in_dim(plain("modulate", 6 * NCAM), 6 * camera[0], 6).astype(jnp.float32)
    own_rows = PR * TC
    stream0 = jnp.concatenate(
        [
            lax.dynamic_slice_in_dim(rows, TILES["triplane"] * 8 + (strips * plane + place) * own_rows, own_rows)
            for plane in range(3)
        ]
    ).astype(jnp.float32)
    hidden1, norm_one = jax.vjp(norm_mod, stream0, mods[0], mods[1])
    hidden1 = hidden1.astype(jnp.bfloat16)
    query1 = product(hidden1, square("query_cross")).astype(jnp.bfloat16)
    (image_kv,) = project(picture, tiled, TILES["keyval_cross"], 2, 0)
    pairs = D // PAIR
    tokens = query1.shape[0]
    cross_out, total_one = attend_fwd(query1, [image_kv], real_keys, (0, pairs))
    stream1 = stream0 + product(cross_out, square("out_cross"))
    hidden2, norm_two = jax.vjp(norm_mod, stream1, mods[2], mods[3])
    hidden2 = hidden2.astype(jnp.bfloat16)
    panels = Panels(panels)
    hidden2 = panels.first(hidden2)
    query2, kv_own = project(hidden2, tiled, TILES["qkv_self"], 3, 1)
    kv_both = [kv_own, lax.ppermute(kv_own, "strip", SWAP)]
    all_keys = 2 * kv_own.shape[1]
    early = attend_fwd(query2, kv_both, all_keys, (0, pairs // 2))
    early = (panels.second(early[0]), early[1])
    self_out, total_two = attend_fwd(query2, kv_both, all_keys, (pairs // 2, pairs), early)
    panels = panels.third(self_out)
    stream2 = stream1 + product(self_out, square("out_self"))
    hidden3, norm_three = jax.vjp(norm_mod, stream2, mods[4], mods[5])
    hidden3 = hidden3.astype(jnp.bfloat16)
    up, act, grid = mlp_fwd(panels, hidden3, stream2)
    grid = grid.reshape(3, own_rows, D)
    edge = lax.ppermute(jnp.where(place == 0, grid[:, -TC:], grid[:, :TC]), "strip", SWAP)
    cells = deconv_fwd(grid, edge, deconv)
    cells_far = lax.ppermute(cells, "strip", SWAP)
    rays = ray_pixel.shape[1]
    factor = 1.0 / jnp.maximum(count, 1.0)
    loss_part, grad_cells, grad_far, grad_decode_in, grad_decode_out = render(
        cells,
        cells_far,
        (samples[0] + place * cells.shape[1]) % (2 * cells.shape[1]),
        wanted,
        mask,
        factor.reshape(1),
        decode_in,
        jnp.pad(decode_out, ((0, 0), (0, 4))),
        rays,
    )
    loss_part = loss_part[0, 0]
    grad_decode_out = grad_decode_out[:, :4]
    grad_far = lax.ppermute(grad_far, "strip", SWAP)
    grad_grid, beside, grad_deconv = deconv_bwd(grad_cells, grad_far, grid, edge, deconv)
    beside = lax.ppermute(beside, "strip", SWAP).astype(jnp.float32)
    grad_grid = grad_grid.at[:, :TC].add(jnp.where(place == 0, 0.0, beside))
    grad_grid = grad_grid.at[:, -TC:].add(jnp.where(place == 0, beside, 0.0))
    grad_stream = grad_grid.reshape(-1, D)
    grad_branch = grad_stream.astype(jnp.bfloat16)
    grad_hidden3, *panel_grads = mlp_bwd(panels, hidden3, grad_branch, up, act)
    grad_norm, grad_mod4, grad_mod5 = norm_three(grad_hidden3)
    grad_stream = grad_stream + grad_norm
    grad_branch2 = grad_stream.astype(jnp.bfloat16)
    grad_self = product_back(grad_branch2, square("out_self")).astype(jnp.bfloat16)
    panel_sums = PanelSums(panel_grads)
    grad_self = panel_sums.first(grad_self)
    early = attend_bwd(query2, kv_both, all_keys, (0, pairs - 1), 512, total_two, self_out, grad_self)
    early = (panel_sums.second(early[0]), *early[1:])
    grad_query2, grad_kv_own, grad_kv_far = attend_bwd(
        query2, kv_both, all_keys, (pairs - 1, pairs), 512, total_two, self_out, grad_self, early
    )
    grad_kv_far = lax.ppermute(grad_kv_far, "strip", SWAP)
    grad_kv = (grad_kv_own.astype(jnp.float32) + grad_kv_far.astype(jnp.float32)).astype(jnp.bfloat16)
    grad_hidden2 = project_back(grad_query2, grad_kv, tiled, TILES["qkv_self"], D)
    grad_norm, grad_mod2, grad_mod3 = norm_two(grad_hidden2)
    grad_stream = grad_stream + grad_norm
    grad_branch1 = grad_stream.astype(jnp.bfloat16)
    grad_cross = product_back(grad_branch1, square("out_cross")).astype(jnp.bfloat16)
    grad_query1, grad_image_kv = attend_bwd(
        query1, [image_kv], real_keys, (0, pairs), picture.shape[0], total_one, cross_out, grad_cross
    )
    grad_query1 = panel_sums.third(grad_query1)
    grad_norm, grad_mod0, grad_mod1 = norm_one(product_back(grad_query1, square("query_cross")))
    grad_stream = grad_stream + grad_norm
    grad_mods = jnp.stack([grad_mod0, grad_mod1, grad_mod2, grad_mod3, grad_mod4, grad_mod5])
    grad_modulate = lax.dynamic_update_slice_in_dim(
        jnp.zeros((6 * NCAM, D), jnp.bfloat16), grad_mods.astype(jnp.bfloat16), 6 * camera[0], 0
    )
    grad_triplane = lax.dynamic_update_slice_in_dim(
        jnp.zeros((3, strips, own_rows, D), jnp.bfloat16),
        grad_stream.astype(jnp.bfloat16).reshape(3, 1, own_rows, D),
        place,
        1,
    )
    grad_decode = jnp.concatenate([grad_decode_in.reshape(-1), grad_decode_out.reshape(-1)])
    grad_decode = jnp.pad(grad_decode, (0, END_GAP))
    total_tiles = tiled.shape[0]
    end = TILES["triplane"] + 3 * strips * own_rows // 8
    gap = TILES["qkv_self"] - TILES["gap"]
    arrays = [
        hidden1,
        grad_query1,
        picture,
        grad_image_kv,
        cross_out,
        grad_branch1,
        hidden2,
        grad_query2,
        grad_kv,
        self_out,
        grad_branch2,
    ]
    tall, low = (tokens, D), (picture.shape[0], DI)
    products = [
        (tall, (9, None), (10, None), TILES["out_self"], (1, 0)),
        (tall, (6, None), (7, None), TILES["qkv_self"], (3, 0)),
        (tall, (6, None), (8, 0), TILES["qkv_self"], (3, 1)),
        (tall, (6, None), (8, 1), TILES["qkv_self"], (3, 2)),
        (tall, (4, None), (5, None), TILES["out_cross"], (1, 0)),
        (low, (2, None), (3, 0), TILES["keyval_cross"], (2, 0)),
        (low, (2, None), (3, 1), TILES["keyval_cross"], (2, 1)),
        (tall, (0, None), (1, None), TILES["query_cross"], (1, 0)),
    ]
    copies = []
    for piece, first in (
        (grad_deconv, TILES["deconv"]),
        (grad_decode, TILES["decode"]),
        (grad_modulate, TILES["modulate"]),
        (grad_triplane, TILES["triplane"]),
        (jnp.zeros((gap, 8, WIDE), jnp.bfloat16), TILES["gap"]),
        (jnp.zeros((total_tiles - end, 8, WIDE), jnp.bfloat16), end),
    ):
        piece = piece.astype(jnp.bfloat16).reshape(-1, 8, WIDE)
        if piece.shape[0]:
            copies.append((len(arrays), first, piece.shape[0]))
            arrays.append(piece)
    row_grads = weight_grads(arrays, products, copies, total_tiles).reshape(-1, WIDE)
    if direct_links():
        summed, chunks, loss_sum = reduce_grads(row_grads, panel_sums.parts, loss_part)
        new_weights, new_first, new_second = adam(summed, weights, first_moment, second_moment)
    else:
        summed, chunks, loss_sum = reduce_grads_plainly(row_grads, panel_sums.parts, loss_part, weights.shape[0])
        new_weights, new_first, new_second = adam_plainly(summed, weights, first_moment, second_moment)
    new_blocks, block_grads, new_left, new_right, block_rms = shampoo(
        chunks, blocks, stat_left, stat_right, root_left, root_right
    )
    loss = loss_sum * factor
    return (
        loss,
        new_weights,
        new_first,
        new_second,
        new_blocks,
        block_grads,
        new_left,
        new_right,
        block_rms,
    )


def solution(mesh):
    placed = (
        P(("dp", "strip")),
        P("dp", None, None),
        P("dp", None, None),
        P("dp", None, None),
        P("dp", None, None),
        P("dp", None, None),
        P(("dp", "strip")),
        P(("dp", "strip")),
        P("dp", None, None),
        P("dp"),
        P("dp", None, None, "strip"),
        P("dp", "strip"),
        P("dp", None, None),
        P("dp", None),
    )
    return jax.shard_map(
        shards,
        mesh=mesh,
        in_specs=placed,
        out_specs=(
            P(),
            P(("dp", "strip")),
            P(("dp", "strip")),
            P(("dp", "strip")),
            P("dp", None, None),
            P("dp", None, None),
            P("dp", None, None),
            P("dp", None, None),
            P("dp"),
        ),
        check_vma=False,
    )
```

```python
import functools
import math

import jax
import jax.numpy as jnp
from jax import lax
from jax.experimental import pallas as pl
from jax.experimental.pallas import tpu as pltpu
from jax.sharding import PartitionSpec as P

D = 1024
HEAD_DIM = 64
HID = 4096
DI = 768
CH = 80
DEC_HID = 64
BLOCK = 128
PR = 8
TC = 32
S = 16
NCAM = 32
ADAM_STEP = 10


NORM_EPS = 1e-05
ADAM_RATE = 0.015
BETA_FIRST = 0.9
BETA_SECOND = 0.95
ADAM_EPS = 1e-08
WEIGHT_DECAY = 0.1
STAT_DECAY = 0.9
SHAMPOO_RATE = 0.01
RMS_EPS = 1e-06
HIGHEST_MODE = lax.Precision.HIGHEST
WIDE = 1024


def product(left, right):
    return jnp.dot(left, right, preferred_element_type=jnp.float32)


def product_back(left, right):
    return lax.dot_general(
        left, right, (((left.ndim - 1,), (1,)), ((), ())), preferred_element_type=jnp.float32
    )


def weight_grad(left, right):
    return lax.dot_general(
        left, right, (((0,), (0,)), ((), ())), preferred_element_type=jnp.float32
    )


def norm_mod(stream, scale, shift):
    centred = stream - jnp.mean(stream, -1, keepdims=True)
    spread = jnp.mean(centred * centred, -1, keepdims=True)
    return centred * lax.rsqrt(spread + NORM_EPS) * (1.0 + scale) + shift


def gelu_tanh(value):
    return jax.nn.gelu(value, approximate=True)


PAIR = 2 * HEAD_DIM
BRIEF = pl.CostEstimate(flops=1000000, transcendentals=0, bytes_accessed=100000)
LOG2E = math.log2(math.e)
EXP_SCALE = HEAD_DIM ** (-0.5) * LOG2E


def nt_dot(left, right):
    return lax.dot_general(left, right, (((1,), (1,)), ((), ())), preferred_element_type=jnp.float32)


def head_lanes(shape, head):
    return lax.broadcasted_iota(jnp.int32, shape, len(shape) - 1) // HEAD_DIM == head


def joined(refs, n):
    parts = [ref[n] for ref in refs]
    return parts[0] if len(parts) == 1 else jnp.concatenate(parts, 0)


def attend_fwd_kernel(real_keys, sources, q_ref, *refs):
    o_ref, lse_ref = refs[-2:]
    query, keys = q_ref[...], joined(refs[:sources], 0)
    values = joined(refs[:sources], 1).T
    outs = []
    for head in range(2):
        own = jnp.where(head_lanes(query.shape, head), query, 0)
        scores = nt_dot(keys, own)
        if real_keys < keys.shape[0]:
            at = lax.broadcasted_iota(jnp.int32, scores.shape, 0)
            scores = jnp.where(at < real_keys, scores, -3e38)
        top = jnp.max(scores, 0, keepdims=True)
        raised = jnp.exp2((scores - top) * EXP_SCALE)
        total = jnp.sum(raised, 0, keepdims=True)
        shares = (raised * (1.0 / total)).astype(jnp.bfloat16)
        outs.append(product(values[head * HEAD_DIM : (head + 1) * HEAD_DIM], shares))
        lse_ref[0, head : head + 1] = top * EXP_SCALE + jnp.log2(total)
    o_ref[...] = jnp.concatenate(outs, 0).T.astype(jnp.bfloat16)


def attend_fwd(query, sources, real_keys, span, earlier=()):
    count = query.shape[0]
    total_keys = sum(source.shape[1] for source in sources)
    low, high = span
    by_pair = pl.BlockSpec((count, PAIR), lambda j: (0, low + j))
    work = count * total_keys * (high - low) * PAIR
    return pl.pallas_call(
        functools.partial(attend_fwd_kernel, real_keys, len(sources)),
        grid=(high - low,),
        in_specs=[by_pair]
        + [pl.BlockSpec((2, source.shape[1], PAIR), lambda j: (0, 0, low + j)) for source in sources]
        + [pl.BlockSpec(memory_space=pl.ANY)] * len(earlier),
        out_specs=[by_pair, pl.BlockSpec((1, 8, count), lambda j: (low + j, 0, 0))],
        out_shape=[
            jax.ShapeDtypeStruct((count, D), jnp.bfloat16),
            jax.ShapeDtypeStruct((D // PAIR, 8, count), jnp.float32),
        ],
        input_output_aliases={1 + len(sources) + n: n for n in range(len(earlier))},
        compiler_params=pltpu.CompilerParams(vmem_limit_bytes=48 * 1024 * 1024),
        cost_estimate=BRIEF,
        name="attend_fwd",
    )(query, *sources, *earlier)


def attend_bwd_kernel(real_keys, chunk, sources, extra, q_ref, *refs):
    kv_refs = refs[:sources]
    lse_ref, o_ref, g_ref = refs[sources : sources + 3]
    dq_ref, *grad_refs = refs[sources + 3 + extra : sources + 4 + extra + sources]
    k_all, v_all, kt_ref, dk_sum, dv_sum = refs[sources + 4 + extra + sources :]
    k_all[...] = joined(kv_refs, 0)
    v_all[...] = joined(kv_refs, 1)
    kt_ref[...] = k_all[...].T
    query, grad = q_ref[...], g_ref[...]
    mixed = (grad.astype(jnp.float32) * o_ref[...].astype(jnp.float32)).T
    total_keys = k_all.shape[0]
    queries = [jnp.where(head_lanes(query.shape, head), query, 0) for head in range(2)]
    grads = [jnp.where(head_lanes(grad.shape, head), grad, 0) for head in range(2)]
    inner = [jnp.sum(mixed[head * HEAD_DIM : (head + 1) * HEAD_DIM], 0, keepdims=True) for head in range(2)]
    grad_query = [jnp.zeros((HEAD_DIM, query.shape[0]), jnp.float32) for head in range(2)]
    for at in range(0, total_keys, chunk):
        part = pl.ds(at, chunk)
        keys, values = k_all[part], v_all[part]
        for head in range(2):
            scores = nt_dot(keys, queries[head])
            shares = jnp.exp2(scores * EXP_SCALE - lse_ref[0, head : head + 1])
            if at + chunk > real_keys:
                row = at + lax.broadcasted_iota(jnp.int32, shares.shape, 0)
                shares = jnp.where(row < real_keys, shares, 0.0)
            grad_shares = nt_dot(values, grads[head])
            grad_scores = (shares * (grad_shares - inner[head])).astype(jnp.bfloat16)
            to_values = product(shares.astype(jnp.bfloat16), grads[head])
            to_keys = product(grad_scores, queries[head])
            if head == 0:
                dv_sum[part] = to_values
                dk_sum[part] = to_keys
            else:
                dv_sum[part] += to_values
                dk_sum[part] += to_keys
            grad_query[head] += product(
                kt_ref[head * HEAD_DIM : (head + 1) * HEAD_DIM, part], grad_scores
            )
    scale = HEAD_DIM ** (-0.5)
    dq_ref[...] = (jnp.concatenate(grad_query, 0) * scale).T.astype(jnp.bfloat16)
    start = 0
    for ref in grad_refs:
        part = pl.ds(start, ref.shape[1])
        ref[0] = (dk_sum[part] * scale).astype(jnp.bfloat16)
        ref[1] = dv_sum[part].astype(jnp.bfloat16)
        start += ref.shape[1]


def attend_bwd(query, sources, real_keys, span, chunk, totals, out, grad, earlier=()):
    count = query.shape[0]
    total_keys = sum(source.shape[1] for source in sources)
    low, high = span
    by_pair = pl.BlockSpec((count, PAIR), lambda j: (0, low + j))
    by_source = [pl.BlockSpec((2, source.shape[1], PAIR), lambda j: (0, 0, low + j)) for source in sources]
    first = 1 + len(sources) + 3
    work = count * total_keys * (high - low) * PAIR
    return pl.pallas_call(
        functools.partial(attend_bwd_kernel, real_keys, chunk, len(sources), len(earlier)),
        grid=(high - low,),
        in_specs=[by_pair]
        + by_source
        + [pl.BlockSpec((1, 8, count), lambda j: (low + j, 0, 0)), by_pair, by_pair]
        + [pl.BlockSpec(memory_space=pl.ANY)] * len(earlier),
        out_specs=[by_pair] + by_source,
        out_shape=[jax.ShapeDtypeStruct((count, D), jnp.bfloat16)]
        + [jax.ShapeDtypeStruct(source.shape, jnp.bfloat16) for source in sources],
        input_output_aliases={first + n: n for n in range(len(earlier))},
        scratch_shapes=[
            pltpu.VMEM((total_keys, PAIR), jnp.bfloat16),
            pltpu.VMEM((total_keys, PAIR), jnp.bfloat16),
            pltpu.VMEM((PAIR, total_keys), jnp.bfloat16),
            pltpu.VMEM((total_keys, PAIR), jnp.float32),
            pltpu.VMEM((total_keys, PAIR), jnp.float32),
        ],
        compiler_params=pltpu.CompilerParams(vmem_limit_bytes=48 * 1024 * 1024),
        cost_estimate=BRIEF,
        name="attend_bwd",
    )(query, *sources, totals, out, grad, *earlier)


GROUPS = 3


def render_kernel(samples_ref, near_ref, far_ref, wanted_ref, mask_ref, factor_ref, win_ref, wout_ref,
                  loss_ref, grad_ref, grad_far_ref, gin_ref, gout_ref,
                  table, inner_all, hidden_all, point_all, out_all, gout_all, sums):
    block = pl.program_id(0)
    half = near_ref.shape[1]
    cells = 2 * half
    group = table.shape[2]
    rays = samples_ref.shape[2]
    planes = near_ref.shape[0]

    @pl.when(block == 0)
    def _():
        loss_ref[...] = jnp.zeros_like(loss_ref)
        gin_ref[...] = jnp.zeros_like(gin_ref)
        gout_ref[...] = jnp.zeros_like(gout_ref)
        sums[...] = jnp.zeros_like(sums)
        table[...] = jnp.zeros_like(table)
        for plane in range(planes):
            turned = jnp.concatenate([near_ref[plane], far_ref[plane]], 0).T
            for g in range(GROUPS):
                width = min(group, cells - g * group)
                table[plane, g * CH : (g + 1) * CH, :width] = turned[:CH, g * group : g * group + width]

    step = 4
    width = step * rays
    win, wout = win_ref[...], wout_ref[...]

    def places_read(plane, s):
        rows = [samples_ref[plane, s + n : s + n + 1, :] for n in range(step)]
        at = jnp.concatenate(rows, 1)
        owner = at // group
        within = at - owner * group
        hot = lax.broadcasted_iota(jnp.int32, (group, width), 0) == within
        return owner, jnp.where(hot, 1.0, 0.0).astype(jnp.bfloat16)

    def tn_dot(left, right):
        return lax.dot_general(left, right, (((0,), (0,)), ((), ())), preferred_element_type=jnp.float32)

    for s in range(0, S, step):
        here = pl.ds(s * rays, width)
        point = jnp.zeros((CH, width), jnp.float32)
        for plane in range(planes):
            owner, hot = places_read(plane, s)
            found = product(table[plane], hot)
            value = found[:CH]
            for g in range(1, GROUPS):
                value = jnp.where(owner == g, found[g * CH : (g + 1) * CH], value)
            point = point + value
        point = point.astype(jnp.bfloat16)
        inner = tn_dot(win, point)
        hidden = (inner * jax.nn.sigmoid(inner)).astype(jnp.bfloat16)
        out_all[:, here] = tn_dot(wout, hidden)
        inner_all[:, here] = inner
        hidden_all[:, here] = hidden
        point_all[:, here] = point

    factor = factor_ref[0]
    mask = mask_ref[...]
    row = lax.broadcasted_iota(jnp.int32, (8, rays), 0)
    is_colour = (row >= 1) & (row <= 3)
    before = jnp.zeros((1, rays), jnp.float32)
    rgb = jnp.zeros((8, rays), jnp.float32)
    kept = []
    for s in range(S):
        out = out_all[:, s * rays : (s + 1) * rays]
        level = out[0:1]
        absorb = (4.0 / S) * (jnp.maximum(level, 0.0) + jnp.log1p(jnp.exp(-jnp.abs(level))))
        weight = jnp.exp(-before) * (1.0 - jnp.exp(-absorb))
        before = before + absorb
        colour = jax.nn.sigmoid(out)
        rgb = rgb + weight * colour
        kept.append((weight, jnp.exp(-before), colour))
    error = jnp.where(is_colour, rgb - wanted_ref[...], 0.0)
    loss_ref[...] += jnp.sum(mask * jnp.sum(error * error, 0, keepdims=True))
    pull = error * (2.0 * factor * mask)
    tail = jnp.zeros((1, rays), jnp.float32)
    for s in reversed(range(S)):
        weight, left_over, colour = kept[s]
        to_weight = jnp.sum(pull * colour, 0, keepdims=True)
        to_absorb = to_weight * left_over - tail
        tail = tail + to_weight * weight
        to_level = (4.0 / S) * to_absorb * colour[0:1]
        to_colour = weight * pull * colour * (1.0 - colour)
        gout_all[:, s * rays : (s + 1) * rays] = jnp.where(row == 0, to_level, to_colour).astype(jnp.bfloat16)

    for s in range(0, S, step):
        here = pl.ds(s * rays, width)
        pulled = gout_all[:, here]
        inner = inner_all[:, here]
        gate = jax.nn.sigmoid(inner)
        grad_inner = product(wout, pulled) * (gate * (1.0 + inner * (1.0 - gate)))
        grad_inner = grad_inner.astype(jnp.bfloat16)
        gout_ref[...] += nt_dot(hidden_all[:, here], pulled)
        gin_ref[...] += nt_dot(point_all[:, here], grad_inner)
        grad_point = product(win, grad_inner)
        coarse = grad_point.astype(jnp.bfloat16).astype(jnp.float32)
        fine = grad_point - coarse
        for plane in range(planes):
            owner, hot = places_read(plane, s)
            rows = [jnp.where(owner == g, coarse, 0.0) for g in range(GROUPS)]
            rows += [jnp.where(owner == g, fine, 0.0) for g in range(GROUPS)]
            stacked = jnp.concatenate(rows, 0).astype(jnp.bfloat16)
            added = nt_dot(stacked, hot)
            sums[plane] += added[: GROUPS * CH] + added[GROUPS * CH :]

    @pl.when(block == pl.num_programs(0) - 1)
    def _():
        for plane in range(planes):
            for g in range(GROUPS):
                for low, high, ref in ((0, half, grad_ref), (half, cells, grad_far_ref)):
                    start, stop = max(g * group, low), min((g + 1) * group, high)
                    if start < stop:
                        part = sums[plane, g * CH : (g + 1) * CH, start - g * group : stop - g * group]
                        ref[plane, :, start - low : stop - low] = part.astype(jnp.bfloat16)


def render(near, far, samples, wanted, mask, factor, decode_in, decode_out, rays):
    planes, half, _ = near.shape
    count = 2 * half
    all_rays = samples.shape[2]
    group = -(-count // (GROUPS * 128)) * 128
    points = S * rays
    whole = lambda *shape: pl.BlockSpec(shape, lambda n: (0,) * len(shape))
    return pl.pallas_call(
        render_kernel,
        grid=(all_rays // rays,),
        in_specs=[
            pl.BlockSpec((planes, S, rays), lambda n: (0, 0, n)),
            whole(*near.shape),
            whole(*far.shape),
            pl.BlockSpec((8, rays), lambda n: (0, n)),
            pl.BlockSpec((1, rays), lambda n: (0, n)),
            pl.BlockSpec(memory_space=pltpu.SMEM),
            whole(CH, DEC_HID),
            whole(DEC_HID, 8),
        ],
        out_specs=[whole(8, 128), whole(planes, CH, half), whole(planes, CH, half), whole(CH, DEC_HID), whole(DEC_HID, 8)],
        out_shape=[
            jax.ShapeDtypeStruct((8, 128), jnp.float32),
            jax.ShapeDtypeStruct((planes, CH, half), jnp.bfloat16),
            jax.ShapeDtypeStruct((planes, CH, half), jnp.bfloat16),
            jax.ShapeDtypeStruct((CH, DEC_HID), jnp.float32),
            jax.ShapeDtypeStruct((DEC_HID, 8), jnp.float32),
        ],
        scratch_shapes=[
            pltpu.VMEM((planes, GROUPS * CH, group), jnp.bfloat16),
            pltpu.VMEM((DEC_HID, points), jnp.float32),
            pltpu.VMEM((DEC_HID, points), jnp.bfloat16),
            pltpu.VMEM((CH, points), jnp.bfloat16),
            pltpu.VMEM((8, points), jnp.float32),
            pltpu.VMEM((8, points), jnp.bfloat16),
            pltpu.VMEM((planes, GROUPS * CH, group), jnp.float32),
        ],
        compiler_params=pltpu.CompilerParams(vmem_limit_bytes=48 * 1024 * 1024),
        name="render",
    )(samples, near, far, wanted, mask, factor, decode_in, decode_out)


def pick_kernel(pixel_ref, valid_ref, target_ref, mask_ref, wanted_ref, count_ref):
    pixels = valid_ref.shape[1]
    rays = pixel_ref.shape[1]
    hot = lax.broadcasted_iota(jnp.int32, (pixels, rays), 0) == pixel_ref[...]
    hot = jnp.where(hot, 1.0, 0.0).astype(jnp.bfloat16)
    rest = target_ref[...]
    rows = [valid_ref[...].astype(jnp.float32)]
    for _ in range(3):
        part = rest.astype(jnp.bfloat16).astype(jnp.float32)
        rows.append(part)
        rest = rest - part
    rows.append(jnp.zeros((6, pixels), jnp.float32))
    found = product(jnp.concatenate(rows, 0).astype(jnp.bfloat16), hot)
    mask = found[:1]
    mask_ref[...] = mask
    wanted_ref[...] = jnp.zeros_like(wanted_ref)
    wanted_ref[1:4] = found[1:4] + found[4:7] + found[7:10]
    count_ref[...] = jnp.broadcast_to(jnp.sum(mask, 1, keepdims=True), count_ref.shape)


def pick(pixel, valid, target):
    rays = pixel.shape[1]
    vmem = pl.BlockSpec(memory_space=pltpu.VMEM)
    return pl.pallas_call(
        pick_kernel,
        in_specs=[vmem] * 3,
        out_specs=[vmem] * 3,
        out_shape=[
            jax.ShapeDtypeStruct((1, rays), jnp.float32),
            jax.ShapeDtypeStruct((8, rays), jnp.float32),
            jax.ShapeDtypeStruct((8, 128), jnp.float32),
        ],
        compiler_params=pltpu.CompilerParams(vmem_limit_bytes=24 * 1024 * 1024),
        name="pick",
    )(pixel, valid, target)


MESH_ID = pl.DeviceIdType.MESH


def places():
    p = lax.axis_index("dp")
    c = lax.axis_index("strip")
    z = p // 4
    flip_x = p + 1 - 2 * (p % 2)
    flip_y = p + 2 - 4 * ((p // 2) % 2)
    both = flip_x + flip_y - p
    near = (1 - c) * flip_x + c * flip_y
    far = (1 - c) * flip_y + c * flip_x
    return p, c, z, near, far, both


def along_z(line, z, k):
    return ((z + k) % 4) * 4 + line % 4


def enter(peers):
    barrier = pltpu.get_barrier_semaphore()
    for peer in peers:
        pl.semaphore_signal(barrier, inc=1, device_id=peer, device_id_type=MESH_ID)
    pl.semaphore_wait(barrier, len(peers))


def flat_chunks(rows, n):
    part = rows // n
    return n, part, lambda p, c, j: (2 * p + c) * rows + j * part


def block_chunk(p, c, k):
    second = p // 8
    return ((1 - second) * ((2 * c + k) * 8 + p) + second * (4 * p + 2 * c + k)) * BLOCK


ORDER = [("near", 0), ("z", 1), ("far", 0), ("z", 2), ("z", 3), ("near", 1), ("near", 2), ("near", 3)]
ORDER += [("both", 0), ("far", 1), ("far", 2), ("far", 3), ("both", 1), ("both", 2), ("both", 3)]
ORDER += [("core", i) for i in range(16)]


def gather_kernel(layouts, stagger, *refs):
    count = len(layouts)
    fulls = refs[count + 1 : 2 * count + 1]
    line_full = refs[2 * count + 1]
    send, recv, local, z_send, line_recv, line_send = refs[2 * count + 2 : 2 * count + 8]
    held = refs[2 * count + 8 :]
    brought = [pltpu.make_async_copy(s, h, local.at[n]) for n, (s, h) in enumerate(zip(refs[: count + 1], held))]
    for copy in brought:
        copy.start()
    sources, line_source = held[:count], held[count]
    p, c, z, near, far, both = places()
    zs = [along_z(p, z, k) for k in range(4)]
    enter([(q, c) for q in zs[1:]] + [(near, c), (far, c), (p, 1 - c)])
    for copy in brought:
        copy.wait()
    jobs = [(a, j) for a, layout in enumerate(layouts) for j in range(layout[0])]
    me = (p, c)
    up, down = (p + 4, c), (p - 4, c)

    def target(owner, job):
        a, j = jobs[job]
        _, rows, place = layouts[a]
        return fulls[a].at[pl.ds(pl.multiple_of(place(*owner, j), 8), rows)]

    def source(owner, job):
        if owner is not me:
            return target(owner, job)
        a, j = jobs[job]
        rows = layouts[a][1]
        return sources[a].at[pl.ds(j * rows, rows)]

    def sending(owner, event, peer, job, sem=None):
        return pltpu.make_async_remote_copy(
            source(owner, job), target(owner, job), send.at[event, job] if sem is None else sem, recv.at[event, job],
            device_id=peer, device_id_type=MESH_ID,
        )

    def arrive(owner, event, job):
        t = target(owner, job)
        pltpu.make_async_remote_copy(
            t, t, send.at[event, job], recv.at[event, job], device_id=(p, 1 - c), device_id_type=MESH_ID
        ).wait_recv()

    def sending_up(distance, job):
        owner = me if distance == 1 else (zs[5 - distance], c)
        return sending(owner, 3 - distance, up, job, z_send.at[0, distance - 1, job])

    def sending_down(distance, job):
        owner = me if distance == 1 else (zs[distance - 1], c)
        return sending(owner, distance - 1, down, job, z_send.at[1, distance - 1, job])

    def line_up(distance):
        held_at = line_source if distance == 1 else line_full.at[5 - distance]
        return pltpu.make_async_remote_copy(
            held_at, line_full.at[4 - distance], line_send.at[0, distance - 1], line_recv.at[4 - distance],
            device_id=up, device_id_type=MESH_ID,
        )

    def line_down(distance):
        held_at = line_source if distance == 1 else line_full.at[distance - 1]
        return pltpu.make_async_remote_copy(
            held_at, line_full.at[distance], line_send.at[1, distance - 1], line_recv.at[distance],
            device_id=down, device_id_type=MESH_ID,
        )

    def each_way(distance, work):
        @pl.when(z + distance <= 3)
        def _():
            work(distance, True)

        @pl.when(z >= distance)
        def _():
            work(4 - distance, False)

    def pass_on(ups, downs, distance, *job):
        if distance > 3:
            return

        @pl.when((z < 3) & (z >= distance - 1))
        def _():
            ups(distance, *job)

        @pl.when((z > 0) & (z + distance - 1 <= 3))
        def _():
            downs(distance, *job)

    def begin(job):
        sending(me, 3, (near, c), job).start()

        @pl.when(z < 3)
        def _():
            sending_up(1, job).start()

        @pl.when(z > 0)
        def _():
            sending_down(1, job).start()

        sending(me, 7, (far, c), job).start()
        sending(me, 15, (p, 1 - c), job).start()
        pltpu.make_async_copy(source(me, job), target(me, job), local.at[job]).start()

    def take_z(k, above, job):
        owner = (zs[k], c)
        arrive(owner, k - 1, job)
        distance = k if above else 4 - k
        if distance < 3:

            @pl.when(z > 0 if above else z < 3)
            def _():
                (sending_down if above else sending_up)(distance + 1, job).start()

        sending(owner, 3 + k, (near, c), job).start()
        sending(owner, 7 + k, (far, c), job).start()
        sending(owner, 15 + k, (p, 1 - c), job).start()

    def take(kind, k, job):
        if kind == "near":
            owner = (along_z(near, z, k), c)
            arrive(owner, 3 + k, job)
            sending(owner, 11 + k, (far, c), job).start()
            sending(owner, 19 + k, (p, 1 - c), job).start()
        elif kind == "far":
            owner = (along_z(far, z, k), c)
            arrive(owner, 7 + k, job)
            sending(owner, 23 + k, (p, 1 - c), job).start()
        elif kind == "both":
            owner = (along_z(both, z, k), c)
            arrive(owner, 11 + k, job)
            sending(owner, 27 + k, (p, 1 - c), job).start()
        elif kind == "core":
            line = (p, far, near, both)[k // 4]
            arrive((along_z(line, z, k % 4), 1 - c), 15 + k, job)

    def line_arrive(k):
        spot = line_full.at[k]
        pltpu.make_async_remote_copy(
            spot, spot, line_send.at[0, 0], line_recv.at[k], device_id=(p, 1 - c), device_id_type=MESH_ID
        ).wait_recv()

    def line_take(k, above):
        line_arrive(k)
        distance = k if above else 4 - k
        if distance < 3:

            @pl.when(z > 0 if above else z < 3)
            def _():
                (line_down if above else line_up)(distance + 1).start()

    steps = [(2 * stagger + 2 + 3 * n, -2, n) for n in range(4)]
    for job in range(len(jobs)):
        begin_at = stagger * min(job, layouts[0][0] - 1)
        for i in range(-1, len(ORDER)):
            steps.append((begin_at + i + 1, i, job))
    own_line = pltpu.make_async_copy(line_source, line_full.at[0], line_recv.at[0])
    for _, i, job in sorted(steps):
        if i == -2:
            if job == 0:

                @pl.when(z < 3)
                def _():
                    line_up(1).start()

                @pl.when(z > 0)
                def _():
                    line_down(1).start()

                own_line.start()
            else:
                each_way(job, line_take)
        elif i < 0:
            begin(job)
        else:
            kind, k = ORDER[i]
            if kind == "z":
                each_way(k, lambda n, above: take_z(n, above, job))
            elif kind == "core" or k == 0:
                take(kind, k, job)
            else:
                each_way(k, lambda n, above: take(kind, n, job))
    own_line.wait()
    for distance in (1, 2, 3):
        pass_on(lambda d: line_up(d).wait_send(), lambda d: line_down(d).wait_send(), distance)
    for job in range(len(jobs)):
        for distance in (1, 2, 3):
            pass_on(lambda d, n: sending_up(d, n).wait_send(), lambda d, n: sending_down(d, n).wait_send(), distance, job)
        for k in range(4):
            owner = (zs[k], c) if k else me
            sending(owner, 3 + k, (near, c), job).wait_send()
            sending(owner, 7 + k, (far, c), job).wait_send()
            sending((along_z(near, z, k), c), 11 + k, (far, c), job).wait_send()
            sending(owner, 15 + k, (p, 1 - c), job).wait_send()
            for line, first in ((near, 19), (far, 23), (both, 27)):
                sending((along_z(line, z, k), c), first + k, (p, 1 - c), job).wait_send()
        pltpu.make_async_copy(source(me, job), target(me, job), local.at[job]).wait()


def gather_all(layouts, stagger, shards_in, line, name_id):
    copies = sum(l[0] for l in layouts)
    everywhere = pl.BlockSpec(memory_space=pl.ANY)
    shapes = [jax.ShapeDtypeStruct((32 * s.shape[0],) + s.shape[1:], s.dtype) for s in shards_in]
    shapes.append(jax.ShapeDtypeStruct((4,) + line.shape, line.dtype))
    return pl.pallas_call(
        functools.partial(gather_kernel, layouts, stagger),
        out_shape=shapes,
        in_specs=[everywhere] * len(shapes),
        out_specs=[everywhere] * len(shapes),
        scratch_shapes=[
            pltpu.SemaphoreType.DMA((31, copies)),
            pltpu.SemaphoreType.DMA((31, copies)),
            pltpu.SemaphoreType.DMA((copies,)),
            pltpu.SemaphoreType.DMA((2, 3, copies)),
            pltpu.SemaphoreType.DMA((4,)),
            pltpu.SemaphoreType.DMA((2, 3)),
        ]
        + [pltpu.VMEM(a.shape, a.dtype) for a in (*shards_in, line)],
        compiler_params=pltpu.CompilerParams(collective_id=name_id, has_side_effects=True),
        name="gather_all",
    )(*shards_in, line)


SUM_ORDER = [(3, 0), (3, 1), (3, 3), (3, 2), (2, 0), (2, 1), (2, 3), (2, 2)]
SUM_ORDER += [(1, 1), (1, 3), (1, 2), (1, 0), (0, 1), (0, 3), (0, 2), (0, 0)]
AHEAD = 3


def scatter_kernel(layouts, stagger, *refs):
    count = len(layouts)
    grads = refs[:count]
    line_grads = refs[count : count + 4]
    outs = refs[count + 4 : 2 * count + 4]
    line_out = refs[2 * count + 4]
    scratch = refs[2 * count + 5 :]
    line_parts, line_sums, line_got, line_sum, line_sems, line_load_sems = scratch[-6:]
    p, c, z, near, far, both = places()
    zs = [along_z(p, z, k) for k in range(4)]
    enter([(q, c) for q in zs[1:]] + [(near, c), (far, c), (p, 1 - c)])
    csend, crecv, bsend, brecv, load_sem, out_sem = scratch[:6]
    buffers = [scratch[6 + 6 * a : 12 + 6 * a] for a in range(count)]
    jobs = [(a, j) for a, layout in enumerate(layouts) for j in range(layout[0])]
    lines = (p, near, far, both)
    partner_lines = (p, far, near, both)

    def view(job, ref, slot):
        a, j = jobs[job]
        rows = layouts[a][1]
        return ref.at[slot, pl.ds(j * rows, rows)]

    def piece(owner, job):
        a, j = jobs[job]
        _, rows, place = layouts[a]
        return grads[a].at[pl.ds(pl.multiple_of(place(*owner, j), 8), rows)]

    def to_core(i, job):
        g, k = SUM_ORDER[i]
        owner = (along_z(partner_lines[g], z, k), 1 - c)
        rc = buffers[jobs[job][0]][0]
        return pltpu.make_async_remote_copy(
            piece(owner, job), view(job, rc, g * 4 + k), csend.at[i, job], crecv.at[i, job],
            device_id=(p, 1 - c), device_id_type=MESH_ID,
        )

    def load(i, job):
        g, k = SUM_ORDER[i]
        own = buffers[jobs[job][0]][4]
        return pltpu.make_async_copy(
            piece((along_z(lines[g], z, k), c), job), view(job, own, i % AHEAD), load_sem.at[i, job]
        )

    def onward(i, job):
        g, k = SUM_ORDER[i]
        rc, rb, ra, rz = buffers[jobs[job][0]][:4]
        if g == 3:
            target, event, peer = view(job, rb, 4 + k), 4 + k, (far, c)
        elif g == 2:
            target, event, peer = view(job, rb, k), k, (far, c)
        elif g == 1:
            target, event, peer = view(job, ra, k), 8 + k, (near, c)
        else:
            target, event, peer = view(job, rz, 3 - k), 12 + 3 - k, (zs[k], c)
        return pltpu.make_async_remote_copy(
            view(job, rc, g * 4 + k), target, bsend.at[event, job], brecv.at[event, job],
            device_id=peer, device_id_type=MESH_ID,
        )

    def landed(event, job):
        rc, rb, ra, rz = buffers[jobs[job][0]][:4]
        if event < 8:
            target = view(job, rb, event)
        elif event < 12:
            target = view(job, ra, event - 8)
        else:
            target = view(job, rz, event - 12)
        pltpu.make_async_remote_copy(
            target, target, bsend.at[event, job], brecv.at[event, job], device_id=(p, 1 - c), device_id_type=MESH_ID
        ).wait_recv()
        return target

    def add_up(parts, target):
        rows = target.shape[0]
        step = math.gcd(rows, 16)

        @pl.loop(0, rows // step)
        def _(n):
            at = pl.ds(pl.multiple_of(n * step, step), step)
            total = parts[0][at].astype(jnp.float32)
            for part in parts[1:]:
                total = total + part[at].astype(jnp.float32)
            target[at] = total.astype(target.dtype)

    def start(i, job):
        to_core(i, job).start()
        load(i, job).start()

    def final_copies(job):
        a, j = jobs[job]
        rows = layouts[a][1]
        return [pltpu.make_async_copy(view(job, buffers[a][5], 0), outs[a].at[pl.ds(j * rows, rows)], out_sem.at[job, 0])]

    line_loads = [
        [pltpu.make_async_copy(ref.at[k], line_parts.at[k, n], line_load_sems.at[k, n]) for n, ref in enumerate(line_grads)]
        for k in range(4)
    ]
    line_sends = {
        k: pltpu.make_async_remote_copy(
            line_sums.at[k], line_got.at[3 - k], line_sems.at[k], line_sems.at[7 - k],
            device_id=(zs[k], c), device_id_type=MESH_ID,
        )
        for k in (1, 3, 2)
    }

    def line_step(k):
        for load_part in line_loads[k]:
            load_part.wait()
        add_up([line_parts.at[k, n] for n in range(4)], line_sums.at[k])
        if k:
            line_sends[k].start()

    half = line_sum.shape[0]
    spot = line_out.at[pl.ds(pl.multiple_of(c * half, 8), half)]
    line_stores = [
        pltpu.make_async_copy(line_sum, spot, line_sems.at[7]),
        pltpu.make_async_remote_copy(
            line_sum, spot, line_sems.at[8], line_sems.at[9], device_id=(p, 1 - c), device_id_type=MESH_ID
        ),
    ]

    def line_finish():
        for k in (1, 2, 3):
            target = line_got.at[k - 1]
            pltpu.make_async_remote_copy(
                target, target, line_sems.at[k], line_sems.at[3 + k], device_id=(p, 1 - c), device_id_type=MESH_ID
            ).wait_recv()
        add_up([line_sums.at[0]] + [line_got.at[n] for n in range(3)], line_sum)
        for copy in line_stores:
            copy.start()

    def step(i, job):
        g, k = SUM_ORDER[i]
        rc, rb, ra, rz, own, done = buffers[jobs[job][0]]
        load(i, job).wait()
        to_core(i, job).wait_recv()
        here = view(job, rc, g * 4 + k)
        parts = [here, view(job, own, i % AHEAD)]
        if g == 1:
            parts.append(landed(4 + k, job))
        if g == 0:
            parts.append(landed(k, job))
            parts.append(landed(8 + k, job))
        if (g, k) == (0, 0):
            parts += [landed(12 + n, job) for n in range(3)]
            add_up(parts, view(job, done, 0))
            for copy in final_copies(job):
                copy.start()
        else:
            add_up(parts, here)
            onward(i, job).start()
        if i + AHEAD < 16:
            start(i + AHEAD, job)

    for k in (1, 3, 2, 0):
        for load_part in line_loads[k]:
            load_part.start()
    for job in range(len(jobs)):
        for n in range(AHEAD):
            start(n, job)
    steps = []
    for job in range(len(jobs)):
        begin = stagger * min(job, layouts[0][0] - 1)
        for i in range(16):
            steps.append((begin + i + 2 * (i // 4 - 1) * (i // 8), job, i))
    steps.append((max(steps)[0] - 6, 0, -1))
    for n, k in enumerate((1, 3, 2, 0)):
        steps.append((n, len(jobs), -2 - k))
    for _, job, i in sorted(steps):
        if i == -1:
            line_finish()
        elif i < 0:
            line_step(-2 - i)
        else:
            step(i, job)
    for job in range(len(jobs)):
        for i in range(16):
            to_core(i, job).wait_send()
            if i < 15:
                onward(i, job).wait_send()
        for copy in final_copies(job):
            copy.wait()
    for copy in line_sends.values():
        copy.wait_send()
    for copy in line_stores:
        copy.wait()


def scatter_sum(layouts, stagger, grads, lines, name_id):
    jobs = sum(l[0] for l in layouts)
    scratch = [
        pltpu.SemaphoreType.DMA((16, jobs)),
        pltpu.SemaphoreType.DMA((16, jobs)),
        pltpu.SemaphoreType.DMA((15, jobs)),
        pltpu.SemaphoreType.DMA((15, jobs)),
        pltpu.SemaphoreType.DMA((16, jobs)),
        pltpu.SemaphoreType.DMA((jobs, 3)),
    ]
    shapes = []
    for layout, grad in zip(layouts, grads):
        rows, width = layout[0] * layout[1], grad.shape[1]
        for slots in (16, 8, 4, 3, AHEAD):
            scratch.append(pltpu.VMEM((slots, rows, width), grad.dtype))
        scratch.append(pltpu.VMEM((1, rows, width), jnp.float32))
        shapes.append(jax.ShapeDtypeStruct((rows, width), jnp.float32))
    piece, kind = lines[-1].shape[1:], lines[-1].dtype
    scratch += [
        pltpu.VMEM((4, 4) + piece, kind),
        pltpu.VMEM((4,) + piece, kind),
        pltpu.VMEM((3,) + piece, kind),
        pltpu.VMEM(piece, kind),
        pltpu.SemaphoreType.DMA((10,)),
        pltpu.SemaphoreType.DMA((4, 4)),
    ]
    shapes.append(jax.ShapeDtypeStruct((2 * piece[0], piece[1]), kind))
    everywhere = pl.BlockSpec(memory_space=pl.ANY)
    return pl.pallas_call(
        functools.partial(scatter_kernel, layouts, stagger),
        out_shape=shapes,
        in_specs=[everywhere] * (len(grads) + len(lines)),
        out_specs=[everywhere] * len(shapes),
        scratch_shapes=scratch,
        compiler_params=pltpu.CompilerParams(
            collective_id=name_id, has_side_effects=True, vmem_limit_bytes=48 * 1024 * 1024
        ),
        name="scatter_sum",
    )(*grads, *lines)


GELU_A = math.sqrt(2.0 / math.pi)
GELU_B = 0.044715


def chunk_sources(first):
    p, c, z, _, _, _ = places()
    x, y = p % 2, (p // 2) % 2
    out = []
    for n in range(4):
        owner_z = (first + n) % 4
        k = (owner_z - z + 4) % 4
        for half in range(2):
            for other in range(2):
                core = (c + other) % 2
                for g in range(4):
                    dx = (1 - core) * (g % 2) + core * (g // 2)
                    dy = (1 - core) * (g // 2) + core * (g % 2)
                    owner = owner_z * 4 + ((y + dy) % 2) * 2 + (x + dx) % 2
                    out.append((other, g, k, half, block_chunk(owner, core, half) // BLOCK))
    return out


def panel_loads(refs, held, sems, first):
    if len(refs) == 1:
        for n in range(held.shape[0] // WIDE):
            at = pl.ds(n * WIDE, WIDE)
            pltpu.make_async_copy(refs[0].at[at], held.at[at], sems.at[n]).start()
        return
    for other, g, k, half, chunk in chunk_sources(first):
        source = refs[other * 4 + g].at[k, pl.ds(half * BLOCK, BLOCK)]
        target = held.at[pl.ds(pl.multiple_of(chunk * BLOCK, BLOCK), BLOCK)]
        pltpu.make_async_copy(source, target, sems.at[chunk // 8]).start()


def panel_ready(held, sems, n):
    at = pl.ds(pl.multiple_of(n * WIDE, WIDE), WIDE)
    pltpu.make_async_copy(held.at[at], held.at[at], sems.at[n]).wait()
    return held.at[at]


def mlp_fwd_kernel(count, *refs):
    sources = refs[:count]
    h_ref, s_ref, up_ref, act_ref, grid_ref, held, total, sems = refs[count:]
    step = pl.program_id(0)
    steps = pl.num_programs(0)

    @pl.when(step == 0)
    def _():
        panel_loads(sources, held, sems, 0)
        total[...] = s_ref[...]

    up = product(h_ref[...], panel_ready(held, sems, step)[...])
    up_ref[0] = up
    act = 0.5 * up * (1.0 + jnp.tanh(GELU_A * (up + GELU_B * up * up * up)))
    act = act.astype(jnp.bfloat16)
    act_ref[0] = act
    total[...] += product(act, panel_ready(held, sems, steps + step)[...])

    @pl.when(step == steps - 1)
    def _():
        grid_ref[...] = total[...].astype(jnp.bfloat16)


def mlp_fwd(panels, hidden, stream):
    rows = hidden.shape[0]
    steps = HID // WIDE
    whole = pl.BlockSpec((rows, WIDE), lambda n: (0, 0))
    part = pl.BlockSpec((1, rows, WIDE), lambda n: (n, 0, 0))
    return pl.pallas_call(
        functools.partial(mlp_fwd_kernel, len(panels)),
        grid=(steps,),
        in_specs=[pl.BlockSpec(memory_space=pl.ANY)] * len(panels) + [whole, whole],
        out_specs=[part, part, whole],
        out_shape=[
            jax.ShapeDtypeStruct((steps, rows, WIDE), jnp.float32),
            jax.ShapeDtypeStruct((steps, rows, WIDE), jnp.bfloat16),
            jax.ShapeDtypeStruct((rows, WIDE), jnp.bfloat16),
        ],
        scratch_shapes=[
            pltpu.VMEM((2 * HID, WIDE), jnp.bfloat16),
            pltpu.VMEM((rows, WIDE), jnp.float32),
            pltpu.SemaphoreType.DMA((2 * steps,)),
        ],
        compiler_params=pltpu.CompilerParams(vmem_limit_bytes=56 * 1024 * 1024),
        cost_estimate=BRIEF,
        name="mlp_fwd",
    )(*panels, hidden, stream)


def mlp_bwd_kernel(count, *refs):
    sources = refs[:count]
    outs = 2 if count > 1 else 1
    h_ref, g_ref, up_ref, act_ref = refs[count : count + 4]
    dh_ref = refs[count + 4]
    grads = refs[count + 5 : count + 5 + outs]
    held, staged, sems, out_sem = refs[count + 5 + outs :]
    step = pl.program_id(0)
    steps = pl.num_programs(0)

    @pl.when(step == 0)
    def _():
        panel_loads(sources, held, sems, 2)
        dh_ref[...] = jnp.zeros_like(dh_ref)

    def tn_dot(left, right):
        return lax.dot_general(left, right, (((0,), (0,)), ((), ())), preferred_element_type=jnp.float32)

    def drain(side):
        pltpu.make_async_copy(staged.at[side], staged.at[side], out_sem.at[side]).wait()

    def store(side):
        panel = side * steps + step
        source = staged.at[side]
        if count == 1:
            at = pl.ds(pl.multiple_of(panel * WIDE, WIDE), WIDE)
            pltpu.make_async_copy(source, grads[0].at[at], out_sem.at[side]).start()
            return
        p, c, z, _, _, _ = places()
        for n in range(8):
            if side == 0:
                owner, core, half = n, step // 2, step % 2
            else:
                row = step * 8 + n
                owner, core, half = 8 + row // 4, (n // 2) % 2, n % 2
            dx = (owner % 2 + p % 2) % 2
            dy = ((owner // 2) % 2 + (p // 2) % 2) % 2
            g = (1 - core) * (dx + 2 * dy) + core * (dy + 2 * dx)
            spot = g * 4 + (owner // 4 - z + 4) % 4
            at = pl.ds(pl.multiple_of(half * BLOCK, BLOCK), BLOCK)
            from_ref = source.at[pl.ds(n * BLOCK, BLOCK)]

            @pl.when((core + c) % 2 == 0)
            def _():
                pltpu.make_async_copy(from_ref, grads[0].at[spot, at], out_sem.at[side]).start()

            @pl.when((core + c) % 2 == 1)
            def _():
                pltpu.make_async_copy(from_ref, grads[1].at[spot, at], out_sem.at[side]).start()

    pulled = g_ref[...]

    @pl.when(step > 0)
    def _():
        drain(1)

    staged[1] = tn_dot(act_ref[0], pulled).astype(jnp.bfloat16)
    store(1)
    grad_act = nt_dot(pulled, panel_ready(held, sems, steps + step)[...])
    up = up_ref[0]
    square = up * up
    bend = jnp.tanh(GELU_A * up * (1.0 + GELU_B * square))
    slope = 0.5 * (1.0 + bend) + 0.5 * GELU_A * up * (1.0 - bend * bend) * (1.0 + 3.0 * GELU_B * square)
    grad_up = (grad_act * slope).astype(jnp.bfloat16)

    @pl.when(step > 0)
    def _():
        drain(0)

    staged[0] = tn_dot(h_ref[...], grad_up).astype(jnp.bfloat16)
    store(0)
    dh_ref[...] += nt_dot(grad_up, panel_ready(held, sems, step)[...])

    @pl.when(step == steps - 1)
    def _():
        drain(0)
        drain(1)


def mlp_bwd(panels, hidden, grad, up, act):
    rows = hidden.shape[0]
    steps = HID // WIDE
    whole = pl.BlockSpec((rows, WIDE), lambda n: (0, 0))
    part = pl.BlockSpec((1, rows, WIDE), lambda n: (n, 0, 0))
    if len(panels) == 1:
        shapes = [jax.ShapeDtypeStruct((2 * HID, WIDE), jnp.bfloat16)]
    else:
        shapes = [jax.ShapeDtypeStruct((16, 2 * BLOCK, WIDE), jnp.bfloat16)] * 2
    return pl.pallas_call(
        functools.partial(mlp_bwd_kernel, len(panels)),
        grid=(steps,),
        in_specs=[pl.BlockSpec(memory_space=pl.ANY)] * len(panels) + [whole, whole, part, part],
        out_specs=[whole] + [pl.BlockSpec(memory_space=pl.ANY)] * len(shapes),
        out_shape=[jax.ShapeDtypeStruct((rows, WIDE), jnp.float32)] + shapes,
        scratch_shapes=[
            pltpu.VMEM((2 * HID, WIDE), jnp.bfloat16),
            pltpu.VMEM((2, WIDE, WIDE), jnp.bfloat16),
            pltpu.SemaphoreType.DMA((2 * steps,)),
            pltpu.SemaphoreType.DMA((2,)),
        ],
        compiler_params=pltpu.CompilerParams(vmem_limit_bytes=58 * 1024 * 1024),
        cost_estimate=BRIEF,
        name="mlp_bwd",
    )(*panels, hidden, grad, up, act)


SLOT = 128
TAPS = 16


def spread_deconv_kernel(first, rows_ref, o_ref, raw, flat, turned, sem):
    load = pltpu.make_async_copy(rows_ref.at[pl.ds(first, raw.shape[0])], raw, sem)
    load.start()
    load.wait()
    whole = raw[...].reshape(TAPS * CH, WIDE).astype(jnp.float32)
    for n in range(WIDE // SLOT):
        flat[n] = whole[:, n * SLOT : (n + 1) * SLOT]
    lane = lax.broadcasted_iota(jnp.int32, (D // 4, SLOT), 1)

    def block(i, j):
        at = 10 * i + j
        return flat[at % 8, pl.ds(at // 8, D // 4, stride=5), :]

    for tap in range(TAPS):
        j, start = divmod(tap * CH, SLOT)
        for i in range(4):
            part = block(i, j)
            if start:
                part = pltpu.roll(part, SLOT - start, 1)
            if start + CH > SLOT:
                part = jnp.where(lane < SLOT - start, part, pltpu.roll(block(i, j + 1), SLOT - start, 1))
            turned[pl.ds(i, D // 4, stride=4), :] = jnp.where(lane < CH, part, 0.0)
        o_ref[:, tap * SLOT : (tap + 1) * SLOT] = turned[...].astype(jnp.bfloat16)


def spread_deconv(rows, first):
    return pl.pallas_call(
        functools.partial(spread_deconv_kernel, first),
        in_specs=[pl.BlockSpec(memory_space=pl.ANY)],
        out_specs=pl.BlockSpec(memory_space=pltpu.VMEM),
        out_shape=jax.ShapeDtypeStruct((D, TAPS * SLOT), jnp.bfloat16),
        scratch_shapes=[
            pltpu.VMEM((TAPS * CH // 8, 8, WIDE), jnp.bfloat16),
            pltpu.VMEM((WIDE // SLOT, TAPS * CH, SLOT), jnp.float32),
            pltpu.VMEM((D, SLOT), jnp.float32),
            pltpu.SemaphoreType.DMA,
        ],
        compiler_params=pltpu.CompilerParams(vmem_limit_bytes=32 * 1024 * 1024),
        name="spread_deconv",
    )(rows)


def with_edges(own, edge):
    place = lax.axis_index("strip")
    above = jnp.where(place == 0, jnp.zeros_like(edge), edge)
    below = jnp.where(place == 0, edge, jnp.zeros_like(edge))
    return jnp.concatenate([above, own, below], 0)


def moved(value, step):
    column = lax.broadcasted_iota(jnp.int32, value.shape, 0) % TC
    inside = (column + step >= 0) & (column + step < TC)
    return jnp.where(inside, pltpu.roll(value, (-step) % value.shape[0], 0), 0.0)


def deconv_fwd_kernel(grid_ref, edge_ref, w_ref, o_ref, taps, fine):
    padded = with_edges(grid_ref[0], edge_ref[0])
    rows = grid_ref.shape[1]
    taps[...] = product(padded, w_ref[...])

    def tap(kr, kc, r):
        slot = kr * 4 + kc
        return taps[pl.ds((r + 1) * TC, rows), slot * SLOT : (slot + 1) * SLOT]

    for i in range(2):
        for j in range(2):
            total = tap(i + 1, j + 1, 0) + tap(3 - 3 * i, j + 1, 2 * i - 1)
            side = tap(i + 1, 3 - 3 * j, 0) + tap(3 - 3 * i, 3 - 3 * j, 2 * i - 1)
            total = total + moved(side, 2 * j - 1)
            for a in range(rows // TC):
                fine[pl.ds((2 * a + i) * 2 * TC + j, TC, stride=2), :] = total[a * TC : (a + 1) * TC]
    o_ref[0] = fine[...].astype(jnp.bfloat16)


def deconv_fwd(grid, edge, weights):
    planes, rows, _ = grid.shape
    return pl.pallas_call(
        deconv_fwd_kernel,
        grid=(planes,),
        in_specs=[
            pl.BlockSpec((1, rows, D), lambda n: (n, 0, 0)),
            pl.BlockSpec((1, TC, D), lambda n: (n, 0, 0)),
            pl.BlockSpec(weights.shape, lambda n: (0, 0)),
        ],
        out_specs=pl.BlockSpec((1, 4 * rows, SLOT), lambda n: (n, 0, 0)),
        out_shape=jax.ShapeDtypeStruct((planes, 4 * rows, SLOT), jnp.bfloat16),
        scratch_shapes=[
            pltpu.VMEM((rows + 2 * TC, TAPS * SLOT), jnp.float32),
            pltpu.VMEM((4 * rows, SLOT), jnp.float32),
        ],
        compiler_params=pltpu.CompilerParams(vmem_limit_bytes=40 * 1024 * 1024),
        name="deconv_fwd",
    )(grid, edge, weights)


def deconv_bwd_kernel(own_ref, got_ref, grid_ref, edge_ref, w_ref, gx_ref, gedge_ref, gw_ref, fine, spread, tokens, sums, flat):
    plane = pl.program_id(0)
    rows = grid_ref.shape[1]
    high = rows + 2 * TC
    place = lax.axis_index("strip")
    total = own_ref[0].astype(jnp.float32) + got_ref[0].astype(jnp.float32)
    total = jnp.concatenate([total, jnp.zeros((SLOT - CH, total.shape[1]), jnp.float32)], 0)
    fine[...] = total.T
    here = pl.ds(plane * high, high)
    tokens[here] = with_edges(grid_ref[0], edge_ref[0])
    for i in range(2):
        for j in range(2):
            parts = [fine[pl.ds((2 * a + i) * 2 * TC + j, TC, stride=2), :] for a in range(rows // TC)]
            part = jnp.concatenate(parts, 0)
            for kr in (i + 1, 3 - 3 * i):
                for kc in (j + 1, 3 - 3 * j):
                    value = part if kc == j + 1 else moved(part, 1 - 2 * j)
                    start = TC if kr == i + 1 else (0 if i == 0 else 2 * TC)
                    pieces = [value]
                    if start:
                        pieces.insert(0, jnp.zeros((start, SLOT), jnp.float32))
                    if high - rows - start:
                        pieces.append(jnp.zeros((high - rows - start, SLOT), jnp.float32))
                    slot = kr * 4 + kc
                    spread[here, slot * SLOT : (slot + 1) * SLOT] = jnp.concatenate(pieces, 0).astype(jnp.bfloat16)
    back = nt_dot(spread[here], w_ref[...])
    gx_ref[0] = back[TC : TC + rows]
    gedge_ref[0] = jnp.where(place == 0, back[TC + rows :], back[:TC]).astype(jnp.bfloat16)

    @pl.when(plane == pl.num_programs(0) - 1)
    def _():
        wide = 512
        for n in range(TAPS * SLOT // wide):
            columns = slice(n * wide, (n + 1) * wide)
            part = lax.dot_general(
                tokens[...], spread[:, columns], (((0,), (0,)), ((), ())), preferred_element_type=jnp.float32
            )
            for m in range(wide // SLOT):
                sums[n * (wide // SLOT) + m] = part[:, m * SLOT : (m + 1) * SLOT]
        lane = lax.broadcasted_iota(jnp.int32, (D // 4, SLOT), 1)
        for i in range(4):
            for j in range(TAPS * CH // SLOT):
                block = None
                for tap in range(j * SLOT // CH, (j * SLOT + SLOT - 1) // CH + 1):
                    part = sums[tap, pl.ds(i, D // 4, stride=4), :]
                    shift = tap * CH - j * SLOT
                    if shift % SLOT:
                        part = pltpu.roll(part, shift % SLOT, 1)
                    block = part if block is None else jnp.where(lane < shift, block, part)
                at = 10 * i + j
                flat[at % 8, pl.ds(at // 8, D // 4, stride=5), :] = block
        whole = jnp.concatenate([flat[n] for n in range(WIDE // SLOT)], 1)
        gw_ref[...] = whole.astype(jnp.bfloat16).reshape(gw_ref.shape)


def deconv_bwd(own, got, grid, edge, weights):
    planes, rows, _ = grid.shape
    high = rows + 2 * TC
    by_plane = lambda *shape: pl.BlockSpec((1,) + shape, lambda n: (n, 0, 0))
    return pl.pallas_call(
        deconv_bwd_kernel,
        grid=(planes,),
        in_specs=[
            by_plane(*own.shape[1:]),
            by_plane(*got.shape[1:]),
            by_plane(rows, D),
            by_plane(TC, D),
            pl.BlockSpec(weights.shape, lambda n: (0, 0)),
        ],
        out_specs=[by_plane(rows, D), by_plane(TC, D), pl.BlockSpec((TAPS * CH // 8, 8, WIDE), lambda n: (0, 0, 0))],
        out_shape=[
            jax.ShapeDtypeStruct((planes, rows, D), jnp.float32),
            jax.ShapeDtypeStruct((planes, TC, D), jnp.bfloat16),
            jax.ShapeDtypeStruct((TAPS * CH // 8, 8, WIDE), jnp.bfloat16),
        ],
        scratch_shapes=[
            pltpu.VMEM((4 * rows, SLOT), jnp.float32),
            pltpu.VMEM((planes * high, TAPS * SLOT), jnp.bfloat16),
            pltpu.VMEM((planes * high, D), jnp.bfloat16),
            pltpu.VMEM((TAPS, D, SLOT), jnp.float32),
            pltpu.VMEM((WIDE // SLOT, TAPS * CH, SLOT), jnp.float32),
        ],
        compiler_params=pltpu.CompilerParams(vmem_limit_bytes=56 * 1024 * 1024),
        name="deconv_bwd",
    )(own, got, grid, edge, weights)


def panel_view(rows_ref, first, count, depth):
    region = rows_ref.at[pl.ds(first, depth // 8 * count)]
    return region.reshape(depth // 8, count, 8, WIDE)


def project_kernel(first, count, depth, lead, x_ref, rows_ref, *rest):
    outs, held, sems = rest[:-2], rest[-2], rest[-1]
    step = pl.program_id(0)
    panels = panel_view(rows_ref, first, count, depth)

    @pl.when(step == 0)
    def _():
        for n in range(count):
            pltpu.make_async_copy(panels.at[:, n], held.at[n], sems.at[n]).start()

    pltpu.make_async_copy(held.at[step], held.at[step], sems.at[step]).wait()
    result = product(x_ref[...], held[step].reshape(depth, WIDE)).astype(jnp.bfloat16)
    if lead:

        @pl.when(step == 0)
        def _():
            outs[0][...] = result

        @pl.when(step > 0)
        def _():
            outs[1][0] = result

    else:
        outs[0][0] = result


def project(x, rows, first, count, lead):
    tokens, depth = x.shape
    specs = [pl.BlockSpec((1, tokens, WIDE), lambda n: (jnp.maximum(n - lead, 0), 0, 0))]
    shapes = [jax.ShapeDtypeStruct((count - lead, tokens, WIDE), jnp.bfloat16)]
    if lead:
        specs.insert(0, pl.BlockSpec((tokens, WIDE), lambda n: (0, 0)))
        shapes.insert(0, jax.ShapeDtypeStruct((tokens, WIDE), jnp.bfloat16))
    return pl.pallas_call(
        functools.partial(project_kernel, first, count, depth, lead),
        grid=(count,),
        in_specs=[pl.BlockSpec((tokens, depth), lambda n: (0, 0)), pl.BlockSpec(memory_space=pl.ANY)],
        out_specs=specs,
        out_shape=shapes,
        scratch_shapes=[pltpu.VMEM((count, depth // 8, 8, WIDE), jnp.bfloat16), pltpu.SemaphoreType.DMA((count,))],
        compiler_params=pltpu.CompilerParams(vmem_limit_bytes=32 * 1024 * 1024),
        cost_estimate=BRIEF,
        name="project",
    )(x, rows)


def project_back_kernel(first, count, depth, lead_ref, g_ref, rows_ref, o_ref, held, sems):
    step = pl.program_id(0)
    panels = panel_view(rows_ref, first, count, depth)

    @pl.when(step == 0)
    def _():
        for n in range(count):
            pltpu.make_async_copy(panels.at[:, n], held.at[n], sems.at[n]).start()

    pltpu.make_async_copy(held.at[step], held.at[step], sems.at[step]).wait()
    grad = jnp.where(step == 0, lead_ref[...], g_ref[0])
    back = nt_dot(grad, held[step].reshape(depth, WIDE))

    @pl.when(step == 0)
    def _():
        o_ref[...] = back

    @pl.when(step > 0)
    def _():
        o_ref[...] += back


def project_back(lead, grads, rows, first, depth):
    others, tokens, _ = grads.shape
    count = others + 1
    return pl.pallas_call(
        functools.partial(project_back_kernel, first, count, depth),
        grid=(count,),
        in_specs=[
            pl.BlockSpec((tokens, WIDE), lambda n: (0, 0)),
            pl.BlockSpec((1, tokens, WIDE), lambda n: (jnp.maximum(n - 1, 0), 0, 0)),
            pl.BlockSpec(memory_space=pl.ANY),
        ],
        out_specs=pl.BlockSpec((tokens, depth), lambda n: (0, 0)),
        out_shape=jax.ShapeDtypeStruct((tokens, depth), jnp.float32),
        scratch_shapes=[pltpu.VMEM((count, depth // 8, 8, WIDE), jnp.bfloat16), pltpu.SemaphoreType.DMA((count,))],
        compiler_params=pltpu.CompilerParams(vmem_limit_bytes=32 * 1024 * 1024),
        cost_estimate=BRIEF,
        name="project_back",
    )(lead, grads, rows)


def weight_grads_kernel(products, copies, *refs):
    arrays = refs[: len(refs) - 8]
    out, left, right, staged, bounce, load_sem, store_sem, copy_sem = refs[len(refs) - 8 :]
    step = pl.program_id(0)
    steps = len(products)

    def loads(n):
        side, (a, a_pick), (b, b_pick), _, _ = products[n]
        slot = n % 2
        source_a = arrays[a] if a_pick is None else arrays[a].at[a_pick]
        source_b = arrays[b] if b_pick is None else arrays[b].at[b_pick]
        rows, deep = side
        return [
            pltpu.make_async_copy(source_a, left.at[slot, pl.ds(0, rows), pl.ds(0, deep)], load_sem.at[slot, 0]),
            pltpu.make_async_copy(source_b, right.at[slot, pl.ds(0, rows)], load_sem.at[slot, 1]),
        ]

    def stores(n):
        (rows, deep), _, _, first, panels = products[n]
        slot = n % 2
        count, at = panels
        source = staged.at[slot, pl.ds(0, deep // 8)]
        target = panel_view(out, first, count, deep).at[:, at]
        return pltpu.make_async_copy(source, target, store_sem.at[slot])

    def bounced(n):
        a, first, count = copies[n]
        held = bounce.at[pl.ds(sum(c[2] for c in copies[:n]), count)]
        return (
            pltpu.make_async_copy(arrays[a], held, copy_sem.at[n, 0]),
            pltpu.make_async_copy(held, out.at[pl.ds(first, count)], copy_sem.at[n, 1]),
        )

    for n in range(steps):

        @pl.when(step == n)
        def _():
            if n == 0:
                for job in loads(0):
                    job.start()
                for m in range(len(copies)):
                    bounced(m)[0].start()
            if n == 1:
                for m in range(len(copies)):
                    bounced(m)[0].wait()
                    bounced(m)[1].start()
            if n + 1 < steps:
                for job in loads(n + 1):
                    job.start()
            for job in loads(n):
                job.wait()
            if n >= 2:
                stores(n - 2).wait()
            rows, deep = products[n][0]
            slot = n % 2
            total = lax.dot_general(
                left[slot, :rows, :deep], right[slot, :rows], (((0,), (0,)), ((), ())), preferred_element_type=jnp.float32
            )
            staged[slot, : deep // 8] = total.astype(jnp.bfloat16).reshape(deep // 8, 8, WIDE)
            stores(n).start()
            if n == steps - 1:
                if n > 0:
                    stores(n - 1).wait()
                stores(n).wait()
                for m in range(len(copies)):
                    bounced(m)[1].wait()


def weight_grads(arrays, products, copies, tile_rows):
    rows = max(p[0][0] for p in products)
    deep = max(p[0][1] for p in products)
    everywhere = pl.BlockSpec(memory_space=pl.ANY)
    return pl.pallas_call(
        functools.partial(weight_grads_kernel, products, copies),
        grid=(len(products),),
        in_specs=[everywhere] * len(arrays),
        out_specs=everywhere,
        out_shape=jax.ShapeDtypeStruct((tile_rows, 8, WIDE), jnp.bfloat16),
        scratch_shapes=[
            pltpu.VMEM((2, rows, deep), jnp.bfloat16),
            pltpu.VMEM((2, rows, WIDE), jnp.bfloat16),
            pltpu.VMEM((2, deep // 8, 8, WIDE), jnp.bfloat16),
            pltpu.VMEM((sum(c[2] for c in copies), 8, WIDE), jnp.bfloat16),
            pltpu.SemaphoreType.DMA((2, 2)),
            pltpu.SemaphoreType.DMA((2,)),
            pltpu.SemaphoreType.DMA((len(copies), 2)),
        ],
        compiler_params=pltpu.CompilerParams(vmem_limit_bytes=60 * 1024 * 1024),
        cost_estimate=BRIEF,
        name="weight_grads",
    )(*arrays)


TILE = 8 * WIDE
KV_AT = D * D
QKV_AT = KV_AT + DI * 2 * D + D * D
GAP_AT = QKV_AT + D * 3 * D + D * D + D * 16 * CH + CH * DEC_HID + DEC_HID * 4
QKV_GAP = -QKV_AT % (3 * TILE)
END_GAP = -GAP_AT % TILE
TILES = {}
_tile = 0
for _name, _rows in (
    ("query_cross", D),
    ("keyval_cross", 2 * DI),
    ("out_cross", D),
    ("gap", QKV_GAP // WIDE),
    ("qkv_self", 3 * D),
    ("out_self", D),
    ("deconv", 16 * CH),
    ("decode", 8),
    ("modulate", 6 * NCAM),
    ("triplane", 0),
):
    TILES[_name] = _tile
    _tile += _rows // 8


def direct_links():
    return lax.axis_size("dp") == 16 and lax.axis_size("strip") == 2


def regroup(rows, first, back):
    tile = first + lax.broadcasted_iota(jnp.int32, (rows.shape[0], 1), 0) // 8

    def turned(panels):
        shape = (-1, panels, 8, WIDE) if back else (-1, 8, panels, WIDE)
        return rows.reshape(shape).transpose(0, 2, 1, 3).reshape(rows.shape)

    in_kv = (tile >= TILES["keyval_cross"]) & (tile < TILES["out_cross"])
    in_qkv = (tile >= TILES["qkv_self"]) & (tile < TILES["out_self"])
    return jnp.where(in_kv, turned(2), jnp.where(in_qkv, turned(3), rows))


def tile_rows(length):
    return -(-length // (6 * TILE)) * 6


LANES = 128
TILE_LINES = TILE // LANES


def tile_place(tile):
    gap = QKV_GAP // LANES * jnp.where(tile >= TILES["gap"], 1, 0)
    return gap + END_GAP // LANES * jnp.where(tile >= TILES["modulate"], 1, 0)


def by_region(tile, work):
    in_kv = (tile >= TILES["keyval_cross"]) & (tile < TILES["out_cross"])
    in_qkv = (tile >= TILES["qkv_self"]) & (tile < TILES["out_self"])

    @pl.when(in_kv)
    def _():
        work(2)

    @pl.when(in_qkv)
    def _():
        work(3)

    @pl.when(jnp.logical_not(in_kv | in_qkv))
    def _():
        work(1)


def tile_lines(tile, first, panels):
    panel = lax.rem(tile, panels)
    return (tile - panel - first) * TILE_LINES + panel * 8


def prepare_kernel(own_ref, next_ref, blocks_ref, o_ref, chunks_ref, lines, tiles, sem):
    half = tiles.shape[0]
    core = lax.axis_index("strip")
    load = pltpu.make_async_copy(blocks_ref.at[pl.ds(core * half, half)], tiles, sem)
    load.start()
    place = lax.axis_index("dp") * 2 + core
    count = own_ref.shape[0]
    lines[:count] = own_ref[...]
    lines[count : count + next_ref.shape[0]] = next_ref[...]
    held = o_ref.shape[0] // 8
    first = place * held
    shift = place * (held * TILE_LINES - count)

    @pl.loop(0, held // 2)
    def _(n):
        def work(panels):
            rows = []
            for m in range(2):
                tile = first + 2 * n + m
                start = tile_lines(tile, first, panels) + shift - tile_place(tile)
                rows.append(jnp.concatenate([lines[pl.ds(start + j, 8, stride=8 * panels), :] for j in range(8)], 1))
            o_ref[pl.ds(pl.multiple_of(16 * n, 16), 16)] = jnp.concatenate(rows, 0).astype(jnp.bfloat16)

        by_region(first + 2 * n, work)

    load.wait()
    for n in range(half):
        at, column = n // 8 * BLOCK, n % 8 * BLOCK
        chunks_ref[at : at + BLOCK, column : column + BLOCK] = tiles[n].astype(jnp.bfloat16)


def prepare(weights, blocks):
    lines = weights.reshape(-1, LANES)
    count = lines.shape[0]
    held = tile_rows(weights.shape[0])
    reach = -(-32 * (held * TILE_LINES - count) // 8) * 8
    following = lax.ppermute(lines[:reach], AXES, [(n + 1, n) for n in range(31)])
    half = blocks.shape[0] // 2
    vmem = pl.BlockSpec(memory_space=pltpu.VMEM)
    return pl.pallas_call(
        prepare_kernel,
        in_specs=[vmem, vmem, pl.BlockSpec(memory_space=pl.ANY)],
        out_specs=[vmem, vmem],
        out_shape=[
            jax.ShapeDtypeStruct((held * 8, WIDE), jnp.bfloat16),
            jax.ShapeDtypeStruct((half // 8 * BLOCK, WIDE), jnp.bfloat16),
        ],
        scratch_shapes=[
            pltpu.VMEM((-(-(count + reach) // 8) * 8, LANES), jnp.float32),
            pltpu.VMEM((half, BLOCK, BLOCK), jnp.float32),
            pltpu.SemaphoreType.DMA,
        ],
        compiler_params=pltpu.CompilerParams(vmem_limit_bytes=16 * 1024 * 1024),
        name="prepare",
    )(lines, following, blocks)


def ungroup_kernel(rows_ref, o_ref):
    place = lax.axis_index("dp") * 2 + lax.axis_index("strip")
    held = rows_ref.shape[0] // 8
    first = place * held

    @pl.loop(0, held)
    def _(n):
        def work(panels):
            start = tile_lines(first + n, first, panels)
            at = pl.ds(pl.multiple_of(8 * n, 8), 8)
            for j in range(8):
                o_ref[pl.ds(start + j, 8, stride=8 * panels), :] = rows_ref[at, j * LANES : (j + 1) * LANES]

        by_region(first + n, work)


def ungroup(rows):
    vmem = pl.BlockSpec(memory_space=pltpu.VMEM)
    return pl.pallas_call(
        ungroup_kernel,
        in_specs=[vmem],
        out_specs=vmem,
        out_shape=jax.ShapeDtypeStruct((rows.size // LANES, LANES), jnp.float32),
        compiler_params=pltpu.CompilerParams(vmem_limit_bytes=16 * 1024 * 1024),
        name="ungroup",
    )(rows)


def adam_kernel(before_ref, sum_ref, w_ref, first_ref, second_ref, nw_ref, nfirst_ref, nsecond_ref, lines):
    place = lax.axis_index("dp") * 2 + lax.axis_index("strip")
    reach, summed, count = before_ref.shape[0], sum_ref.shape[0], w_ref.shape[0]
    lines[:reach] = before_ref[...]
    lines[reach : reach + summed] = sum_ref[...]
    shift = reach - place * (summed - count)
    gaps = (0, QKV_GAP // LANES, (QKV_GAP + END_GAP) // LANES)

    def update(at, rows):
        parts = [lines[pl.ds(shift + at + gap, rows), :] for gap in gaps]
        line = place * count + at + lax.broadcasted_iota(jnp.int32, (rows, LANES), 0)
        grad = jnp.where(line < QKV_AT // LANES, parts[0], jnp.where(line < GAP_AT // LANES, parts[1], parts[2]))
        here = pl.ds(at, rows)
        weights = w_ref[here]
        first = BETA_FIRST * first_ref[here] + (1.0 - BETA_FIRST) * grad
        second = BETA_SECOND * second_ref[here] + (1.0 - BETA_SECOND) * grad * grad
        nfirst_ref[here] = first
        nsecond_ref[here] = second
        fix_first = 1.0 - BETA_FIRST**ADAM_STEP
        fix_second = 1.0 - BETA_SECOND**ADAM_STEP
        step = first / fix_first / (jnp.sqrt(second / fix_second) + ADAM_EPS)
        nw_ref[here] = weights - ADAM_RATE * (step + WEIGHT_DECAY * weights)

    block = 32

    @pl.loop(0, count // block)
    def _(n):
        update(pl.multiple_of(block * n, block), block)

    if count % block:
        update(count - count % block, count % block)


def adam(rows, weights, first_moment, second_moment):
    length = weights.shape[0]
    count = length // LANES
    summed = ungroup(rows)
    reach = -(-32 * (summed.shape[0] - count) // 8) * 8
    before = lax.ppermute(summed[summed.shape[0] - reach :], AXES, [(n, n + 1) for n in range(31)])
    vmem = pl.BlockSpec(memory_space=pltpu.VMEM)
    gap = (QKV_GAP + END_GAP) // LANES
    results = pl.pallas_call(
        adam_kernel,
        in_specs=[vmem] * 5,
        out_specs=[vmem] * 3,
        out_shape=[jax.ShapeDtypeStruct((count, LANES), jnp.float32)] * 3,
        scratch_shapes=[pltpu.VMEM((-(-(reach + summed.shape[0] + gap) // 8) * 8, LANES), jnp.float32)],
        compiler_params=pltpu.CompilerParams(vmem_limit_bytes=32 * 1024 * 1024),
        name="adam",
    )(before, summed, *(a.reshape(count, LANES) for a in (weights, first_moment, second_moment)))
    return [result.reshape(length) for result in results]


def two_parts(value):
    coarse = value.astype(jnp.bfloat16)
    return coarse, (value - coarse.astype(jnp.float32)).astype(jnp.bfloat16)


def shampoo_kernel(tiles_ref, blocks_ref, sl_ref, sr_ref, rl_ref, rr_ref, nb_ref, g_ref, nl_ref, nr_ref, rms_ref):
    for n in range(8):
        grad = tiles_ref[:, n * BLOCK : (n + 1) * BLOCK]
        wide = grad.astype(jnp.float32)
        g_ref[n] = wide
        nl_ref[n] = STAT_DECAY * sl_ref[n] + (1.0 - STAT_DECAY) * nt_dot(grad, grad)
        square = lax.dot_general(grad, grad, (((0,), (0,)), ((), ())), preferred_element_type=jnp.float32)
        nr_ref[n] = STAT_DECAY * sr_ref[n] + (1.0 - STAT_DECAY) * square
        coarse, fine = two_parts(rr_ref[n])
        half = product(grad, jnp.concatenate([coarse, fine], 1))
        half_coarse, half_fine = two_parts(half[:, :BLOCK] + half[:, BLOCK:])
        coarse, fine = two_parts(rl_ref[n])
        cond = product(jnp.concatenate([coarse, fine], 1), jnp.concatenate([half_coarse, half_coarse], 0))
        cond = cond + product(coarse, half_fine)
        rms = jnp.sqrt(jnp.mean(cond * cond, axis=(0, 1), keepdims=True) + RMS_EPS)
        nb_ref[n] = blocks_ref[n] - SHAMPOO_RATE * cond / rms
        rms_ref[n : n + 1] = jnp.broadcast_to(rms, (1, LANES))


def shampoo(chunks, blocks, stat_left, stat_right, root_left, root_right):
    count = blocks.shape[0]
    eight = pl.BlockSpec((8, BLOCK, BLOCK), lambda n: (n, 0, 0))
    whole = jax.ShapeDtypeStruct(blocks.shape, jnp.float32)
    *results, rms = pl.pallas_call(
        shampoo_kernel,
        grid=(count // 8,),
        in_specs=[pl.BlockSpec((BLOCK, WIDE), lambda n: (n, 0))] + [eight] * 5,
        out_specs=[eight] * 4 + [pl.BlockSpec((8, LANES), lambda n: (n, 0))],
        out_shape=[whole] * 4 + [jax.ShapeDtypeStruct((count, LANES), jnp.float32)],
        compiler_params=pltpu.CompilerParams(vmem_limit_bytes=60 * 1024 * 1024),
        name="shampoo",
    )(chunks, blocks, stat_left, stat_right, root_left, root_right)
    return *results, rms[:, 0]


def chunks_of(tiles):
    return tiles.reshape(-1, 8, BLOCK, BLOCK).transpose(0, 2, 1, 3).reshape(-1, WIDE)


def tiles_of(chunks):
    return chunks.reshape(-1, BLOCK, 8, BLOCK).transpose(0, 2, 1, 3).reshape(-1, BLOCK, BLOCK)


def panels_of(chunks):
    half = chunks.shape[0] // 2
    first = chunks[:half].reshape(D // BLOCK, HID // WIDE, BLOCK, WIDE).transpose(1, 0, 2, 3)
    return jnp.concatenate([first.reshape(half, WIDE), chunks[half:]])


def chunks_of_panels(panels):
    half = panels.shape[0] // 2
    first = panels[:half].reshape(HID // WIDE, D // BLOCK, BLOCK, WIDE).transpose(1, 0, 2, 3)
    return jnp.concatenate([first.reshape(half, WIDE), panels[half:]])


META = (1, 8, lambda p, c, j: (2 * p + c) * 8)
SWAP = ((0, 1), (1, 0))
AXES = ("dp", "strip")


def pairs_to(target):
    return [(2 * p + c, sum(v * w for v, w in zip(target(p, c), (2, 1)))) for p in range(16) for c in range(2)]


NEAR = pairs_to(lambda p, c: (p ^ (1 + c), c))
FAR = pairs_to(lambda p, c: (p ^ (2 - c), c))
CORE = pairs_to(lambda p, c: (p, 1 - c))


def gather_weights(weights, blocks, part):
    if direct_links():
        own, tiles = prepare(weights, blocks)
        rows, parts, line = gather_all([flat_chunks(own.shape[0], 3), META], 6, [own, part], tiles, 0)
        near = lax.ppermute(line, AXES, NEAR)
        return rows, [line, near], jnp.sum(parts[::8, 0])
    flat = lax.all_gather(weights.astype(jnp.bfloat16), AXES, axis=0, tiled=True)
    tiles = lax.all_gather(blocks.astype(jnp.bfloat16), "dp", axis=0, tiled=True)
    gaps = [jnp.zeros((QKV_GAP,), flat.dtype), jnp.zeros((END_GAP,), flat.dtype)]
    rows = jnp.concatenate([flat[:QKV_AT], gaps[0], flat[QKV_AT:GAP_AT], gaps[1], flat[GAP_AT:]])
    rows = jnp.pad(rows, (0, -rows.shape[0] % (6 * TILE))).reshape(-1, WIDE)
    return regroup(rows, 0, False), [panels_of(chunks_of(tiles))], lax.psum(part[0, 0], AXES)


class Panels:
    def __init__(self, parts):
        self.parts = parts
        self.staged = len(parts) > 1

    def first(self, before):
        if not self.staged:
            return before
        line, near = self.parts
        near, before = lax.optimization_barrier((near, before))
        self.parts = [line, near, lax.ppermute(line, AXES, FAR)]
        return before

    def second(self, before):
        if not self.staged:
            return before
        line, near, far = self.parts
        far, before = lax.optimization_barrier((far, before))
        self.parts = [line, near, far, lax.ppermute(near, AXES, FAR)]
        return before

    def third(self, after):
        if not self.staged:
            return self.parts
        line, near, far, both = self.parts
        both, after = lax.optimization_barrier((both, after))
        return [line, near, far, both] + [lax.ppermute(group, AXES, CORE) for group in (line, near, far, both)]


class PanelSums:
    def __init__(self, grads):
        self.parts = grads
        self.staged = len(grads) > 1
        if self.staged:
            self.mine = grads[0]
            self.got = lax.ppermute(grads[1], AXES, CORE)

    def added(self, at, *parts):
        total = self.mine[at].astype(jnp.float32) + self.got[at].astype(jnp.float32)
        for part in parts:
            total = total + part.astype(jnp.float32)
        return total.astype(jnp.bfloat16)

    def first(self, before):
        if not self.staged:
            return before
        away, before = lax.optimization_barrier((self.added(slice(8, 16)), before))
        self.away = lax.ppermute(away, AXES, FAR)
        return before

    def second(self, before):
        if not self.staged:
            return before
        self.away, before = lax.optimization_barrier((self.away, before))
        near, before = lax.optimization_barrier((self.added(slice(4, 8), self.away[4:]), before))
        self.last = lax.ppermute(near, AXES, NEAR)
        return before

    def third(self, before):
        if not self.staged:
            return before
        self.last, before = lax.optimization_barrier((self.last, before))
        self.parts = [self.mine, self.got, self.away, self.last]
        return before


def reduce_grads(rows, panels, part):
    meta = jnp.full((32 * 8, 128), part, jnp.float32)
    summed, parts, tiles = scatter_sum([flat_chunks(rows.shape[0] // 32, 3), META], 6, [rows, meta], panels, 1)
    return summed, tiles, parts[0, 0]


def reduce_grads_plainly(rows, panels, part, length):
    flat = regroup(rows, 0, True).astype(jnp.float32).reshape(-1)
    flat = jnp.concatenate(
        [flat[:QKV_AT], flat[QKV_AT + QKV_GAP : GAP_AT + QKV_GAP], flat[GAP_AT + QKV_GAP + END_GAP :]]
    )
    devices = lax.axis_size("dp") * lax.axis_size("strip")
    flat = jnp.pad(flat, (0, max(0, devices * length - flat.shape[0])))[: devices * length]
    tiles = tiles_of(chunks_of_panels(panels[0])).astype(jnp.float32)
    flat_sum = lax.psum_scatter(flat, AXES, scatter_dimension=0, tiled=True)
    tile_sum = lax.psum_scatter(tiles, AXES, scatter_dimension=0, tiled=True)
    tile_sum = lax.all_gather(tile_sum.astype(jnp.bfloat16), "strip", axis=0, tiled=True)
    return flat_sum, chunks_of(tile_sum), lax.psum(part, AXES)


def adam_plainly(grad, weights, first_moment, second_moment):
    new_first = BETA_FIRST * first_moment + (1.0 - BETA_FIRST) * grad
    new_second = BETA_SECOND * second_moment + (1.0 - BETA_SECOND) * grad * grad
    fix_first = 1.0 - BETA_FIRST**ADAM_STEP
    fix_second = 1.0 - BETA_SECOND**ADAM_STEP
    moved = new_first / fix_first / (jnp.sqrt(new_second / fix_second) + ADAM_EPS)
    return weights - ADAM_RATE * (moved + WEIGHT_DECAY * weights), new_first, new_second


def shards(
    weights,
    blocks,
    stat_left,
    stat_right,
    root_left,
    root_right,
    first_moment,
    second_moment,
    image,
    camera,
    samples,
    ray_pixel,
    target,
    valid,
):
    strips = lax.axis_size("strip")
    place = lax.axis_index("strip")
    mask, wanted, own_count = pick(ray_pixel, valid, target[0])
    rows, panels, count = gather_weights(weights, blocks, own_count)
    tiled = rows.reshape(-1, 8, WIDE)

    def square(name):
        return rows[TILES[name] * 8 : TILES[name] * 8 + D]

    def plain(name, count):
        return rows[TILES[name] * 8 : TILES[name] * 8 + count]

    deconv = spread_deconv(tiled, TILES["deconv"])
    decode = plain("decode", 8).reshape(-1)
    decode_in = decode[: CH * DEC_HID].reshape(CH, DEC_HID)
    decode_out = decode[CH * DEC_HID : CH * DEC_HID + DEC_HID * 4].reshape(DEC_HID, 4)
    picture = image[0]
    real_keys = picture.shape[0]
    picture = jnp.pad(picture, ((0, -real_keys % 16), (0, 0)))
    mods = lax.dynamic_slice_in_dim(plain("modulate", 6 * NCAM), 6 * camera[0], 6).astype(jnp.float32)
    own_rows = PR * TC
    stream0 = jnp.concatenate(
        [
            lax.dynamic_slice_in_dim(rows, TILES["triplane"] * 8 + (strips * plane + place) * own_rows, own_rows)
            for plane in range(3)
        ]
    ).astype(jnp.float32)
    hidden1, norm_one = jax.vjp(norm_mod, stream0, mods[0], mods[1])
    hidden1 = hidden1.astype(jnp.bfloat16)
    query1 = product(hidden1, square("query_cross")).astype(jnp.bfloat16)
    (image_kv,) = project(picture, tiled, TILES["keyval_cross"], 2, 0)
    pairs = D // PAIR
    tokens = query1.shape[0]
    cross_out, total_one = attend_fwd(query1, [image_kv], real_keys, (0, pairs))
    stream1 = stream0 + product(cross_out, square("out_cross"))
    hidden2, norm_two = jax.vjp(norm_mod, stream1, mods[2], mods[3])
    hidden2 = hidden2.astype(jnp.bfloat16)
    panels = Panels(panels)
    hidden2 = panels.first(hidden2)
    query2, kv_own = project(hidden2, tiled, TILES["qkv_self"], 3, 1)
    kv_both = [kv_own, lax.ppermute(kv_own, "strip", SWAP)]
    all_keys = 2 * kv_own.shape[1]
    early = attend_fwd(query2, kv_both, all_keys, (0, pairs // 2))
    early = (panels.second(early[0]), early[1])
    self_out, total_two = attend_fwd(query2, kv_both, all_keys, (pairs // 2, pairs), early)
    panels = panels.third(self_out)
    stream2 = stream1 + product(self_out, square("out_self"))
    hidden3, norm_three = jax.vjp(norm_mod, stream2, mods[4], mods[5])
    hidden3 = hidden3.astype(jnp.bfloat16)
    up, act, grid = mlp_fwd(panels, hidden3, stream2)
    grid = grid.reshape(3, own_rows, D)
    edge = lax.ppermute(jnp.where(place == 0, grid[:, -TC:], grid[:, :TC]), "strip", SWAP)
    cells = deconv_fwd(grid, edge, deconv)
    cells_far = lax.ppermute(cells, "strip", SWAP)
    rays = ray_pixel.shape[1]
    factor = 1.0 / jnp.maximum(count, 1.0)
    loss_part, grad_cells, grad_far, grad_decode_in, grad_decode_out = render(
        cells,
        cells_far,
        (samples[0] + place * cells.shape[1]) % (2 * cells.shape[1]),
        wanted,
        mask,
        factor.reshape(1),
        decode_in,
        jnp.pad(decode_out, ((0, 0), (0, 4))),
        rays,
    )
    loss_part = loss_part[0, 0]
    grad_decode_out = grad_decode_out[:, :4]
    grad_far = lax.ppermute(grad_far, "strip", SWAP)
    grad_grid, beside, grad_deconv = deconv_bwd(grad_cells, grad_far, grid, edge, deconv)
    beside = lax.ppermute(beside, "strip", SWAP).astype(jnp.float32)
    grad_grid = grad_grid.at[:, :TC].add(jnp.where(place == 0, 0.0, beside))
    grad_grid = grad_grid.at[:, -TC:].add(jnp.where(place == 0, beside, 0.0))
    grad_stream = grad_grid.reshape(-1, D)
    grad_branch = grad_stream.astype(jnp.bfloat16)
    grad_hidden3, *panel_grads = mlp_bwd(panels, hidden3, grad_branch, up, act)
    grad_norm, grad_mod4, grad_mod5 = norm_three(grad_hidden3)
    grad_stream = grad_stream + grad_norm
    grad_branch2 = grad_stream.astype(jnp.bfloat16)
    grad_self = product_back(grad_branch2, square("out_self")).astype(jnp.bfloat16)
    panel_sums = PanelSums(panel_grads)
    grad_self = panel_sums.first(grad_self)
    early = attend_bwd(query2, kv_both, all_keys, (0, pairs - 1), 512, total_two, self_out, grad_self)
    early = (panel_sums.second(early[0]), *early[1:])
    grad_query2, grad_kv_own, grad_kv_far = attend_bwd(
        query2, kv_both, all_keys, (pairs - 1, pairs), 512, total_two, self_out, grad_self, early
    )
    grad_kv_far = lax.ppermute(grad_kv_far, "strip", SWAP)
    grad_kv = (grad_kv_own.astype(jnp.float32) + grad_kv_far.astype(jnp.float32)).astype(jnp.bfloat16)
    grad_hidden2 = project_back(grad_query2, grad_kv, tiled, TILES["qkv_self"], D)
    grad_norm, grad_mod2, grad_mod3 = norm_two(grad_hidden2)
    grad_stream = grad_stream + grad_norm
    grad_branch1 = grad_stream.astype(jnp.bfloat16)
    grad_cross = product_back(grad_branch1, square("out_cross")).astype(jnp.bfloat16)
    grad_query1, grad_image_kv = attend_bwd(
        query1, [image_kv], real_keys, (0, pairs), picture.shape[0], total_one, cross_out, grad_cross
    )
    grad_query1 = panel_sums.third(grad_query1)
    grad_norm, grad_mod0, grad_mod1 = norm_one(product_back(grad_query1, square("query_cross")))
    grad_stream = grad_stream + grad_norm
    grad_mods = jnp.stack([grad_mod0, grad_mod1, grad_mod2, grad_mod3, grad_mod4, grad_mod5])
    grad_modulate = lax.dynamic_update_slice_in_dim(
        jnp.zeros((6 * NCAM, D), jnp.bfloat16), grad_mods.astype(jnp.bfloat16), 6 * camera[0], 0
    )
    grad_triplane = lax.dynamic_update_slice_in_dim(
        jnp.zeros((3, strips, own_rows, D), jnp.bfloat16),
        grad_stream.astype(jnp.bfloat16).reshape(3, 1, own_rows, D),
        place,
        1,
    )
    grad_decode = jnp.concatenate([grad_decode_in.reshape(-1), grad_decode_out.reshape(-1)])
    grad_decode = jnp.pad(grad_decode, (0, END_GAP))
    total_tiles = tiled.shape[0]
    end = TILES["triplane"] + 3 * strips * own_rows // 8
    gap = TILES["qkv_self"] - TILES["gap"]
    arrays = [
        hidden1,
        grad_query1,
        picture,
        grad_image_kv,
        cross_out,
        grad_branch1,
        hidden2,
        grad_query2,
        grad_kv,
        self_out,
        grad_branch2,
    ]
    tall, low = (tokens, D), (picture.shape[0], DI)
    products = [
        (tall, (9, None), (10, None), TILES["out_self"], (1, 0)),
        (tall, (6, None), (7, None), TILES["qkv_self"], (3, 0)),
        (tall, (6, None), (8, 0), TILES["qkv_self"], (3, 1)),
        (tall, (6, None), (8, 1), TILES["qkv_self"], (3, 2)),
        (tall, (4, None), (5, None), TILES["out_cross"], (1, 0)),
        (low, (2, None), (3, 0), TILES["keyval_cross"], (2, 0)),
        (low, (2, None), (3, 1), TILES["keyval_cross"], (2, 1)),
        (tall, (0, None), (1, None), TILES["query_cross"], (1, 0)),
    ]
    copies = []
    for piece, first in (
        (grad_deconv, TILES["deconv"]),
        (grad_decode, TILES["decode"]),
        (grad_modulate, TILES["modulate"]),
        (grad_triplane, TILES["triplane"]),
        (jnp.zeros((gap, 8, WIDE), jnp.bfloat16), TILES["gap"]),
        (jnp.zeros((total_tiles - end, 8, WIDE), jnp.bfloat16), end),
    ):
        piece = piece.astype(jnp.bfloat16).reshape(-1, 8, WIDE)
        if piece.shape[0]:
            copies.append((len(arrays), first, piece.shape[0]))
            arrays.append(piece)
    row_grads = weight_grads(arrays, products, copies, total_tiles).reshape(-1, WIDE)
    if direct_links():
        summed, chunks, loss_sum = reduce_grads(row_grads, panel_sums.parts, loss_part)
        new_weights, new_first, new_second = adam(summed, weights, first_moment, second_moment)
    else:
        summed, chunks, loss_sum = reduce_grads_plainly(row_grads, panel_sums.parts, loss_part, weights.shape[0])
        new_weights, new_first, new_second = adam_plainly(summed, weights, first_moment, second_moment)
    new_blocks, block_grads, new_left, new_right, block_rms = shampoo(
        chunks, blocks, stat_left, stat_right, root_left, root_right
    )
    loss = loss_sum * factor
    return (
        loss,
        new_weights,
        new_first,
        new_second,
        new_blocks,
        block_grads,
        new_left,
        new_right,
        block_rms,
    )


def solution(mesh):
    placed = (
        P(("dp", "strip")),
        P("dp", None, None),
        P("dp", None, None),
        P("dp", None, None),
        P("dp", None, None),
        P("dp", None, None),
        P(("dp", "strip")),
        P(("dp", "strip")),
        P("dp", None, None),
        P("dp"),
        P("dp", None, None, "strip"),
        P("dp", "strip"),
        P("dp", None, None),
        P("dp", None),
    )
    return jax.shard_map(
        shards,
        mesh=mesh,
        in_specs=placed,
        out_specs=(
            P(),
            P(("dp", "strip")),
            P(("dp", "strip")),
            P(("dp", "strip")),
            P("dp", None, None),
            P("dp", None, None),
            P("dp", None, None),
            P("dp", None, None),
            P("dp"),
        ),
        check_vma=False,
    )
```

```python
import functools
import math

import jax
import jax.numpy as jnp
from jax import lax
from jax.experimental import pallas as pl
from jax.experimental.pallas import tpu as pltpu
from jax.sharding import PartitionSpec as P

D = 1024
HEAD_DIM = 64
HID = 4096
DI = 768
CH = 80
DEC_HID = 64
BLOCK = 128
PR = 8
TC = 32
S = 16
NCAM = 32
ADAM_STEP = 10


NORM_EPS = 1e-05
ADAM_RATE = 0.015
BETA_FIRST = 0.9
BETA_SECOND = 0.95
ADAM_EPS = 1e-08
WEIGHT_DECAY = 0.1
STAT_DECAY = 0.9
SHAMPOO_RATE = 0.01
RMS_EPS = 1e-06
HIGHEST_MODE = lax.Precision.HIGHEST
WIDE = 1024


def product(left, right):
    return jnp.dot(left, right, preferred_element_type=jnp.float32)


def product_back(left, right):
    return lax.dot_general(
        left, right, (((left.ndim - 1,), (1,)), ((), ())), preferred_element_type=jnp.float32
    )


def weight_grad(left, right):
    return lax.dot_general(
        left, right, (((0,), (0,)), ((), ())), preferred_element_type=jnp.float32
    )


def norm_mod(stream, scale, shift):
    centred = stream - jnp.mean(stream, -1, keepdims=True)
    spread = jnp.mean(centred * centred, -1, keepdims=True)
    return centred * lax.rsqrt(spread + NORM_EPS) * (1.0 + scale) + shift


def gelu_tanh(value):
    return jax.nn.gelu(value, approximate=True)


PAIR = 2 * HEAD_DIM
BRIEF = pl.CostEstimate(flops=1000000, transcendentals=0, bytes_accessed=100000)
LOG2E = math.log2(math.e)
EXP_SCALE = HEAD_DIM ** (-0.5) * LOG2E


def nt_dot(left, right):
    return lax.dot_general(left, right, (((1,), (1,)), ((), ())), preferred_element_type=jnp.float32)


def head_lanes(shape, head):
    return lax.broadcasted_iota(jnp.int32, shape, len(shape) - 1) // HEAD_DIM == head


def joined(refs, n):
    parts = [ref[n] for ref in refs]
    return parts[0] if len(parts) == 1 else jnp.concatenate(parts, 0)


def attend_fwd_kernel(real_keys, sources, q_ref, *refs):
    o_ref, lse_ref = refs[-2:]
    query, keys = q_ref[...], joined(refs[:sources], 0)
    values = joined(refs[:sources], 1).T
    outs = []
    for head in range(2):
        own = jnp.where(head_lanes(query.shape, head), query, 0)
        scores = nt_dot(keys, own)
        if real_keys < keys.shape[0]:
            at = lax.broadcasted_iota(jnp.int32, scores.shape, 0)
            scores = jnp.where(at < real_keys, scores, -3e38)
        top = jnp.max(scores, 0, keepdims=True)
        raised = jnp.exp2((scores - top) * EXP_SCALE)
        total = jnp.sum(raised, 0, keepdims=True)
        shares = (raised * (1.0 / total)).astype(jnp.bfloat16)
        outs.append(product(values[head * HEAD_DIM : (head + 1) * HEAD_DIM], shares))
        lse_ref[0, head : head + 1] = top * EXP_SCALE + jnp.log2(total)
    o_ref[...] = jnp.concatenate(outs, 0).T.astype(jnp.bfloat16)


def attend_fwd(query, sources, real_keys, span, earlier=()):
    count = query.shape[0]
    total_keys = sum(source.shape[1] for source in sources)
    low, high = span
    by_pair = pl.BlockSpec((count, PAIR), lambda j: (0, low + j))
    work = count * total_keys * (high - low) * PAIR
    return pl.pallas_call(
        functools.partial(attend_fwd_kernel, real_keys, len(sources)),
        grid=(high - low,),
        in_specs=[by_pair]
        + [pl.BlockSpec((2, source.shape[1], PAIR), lambda j: (0, 0, low + j)) for source in sources]
        + [pl.BlockSpec(memory_space=pl.ANY)] * len(earlier),
        out_specs=[by_pair, pl.BlockSpec((1, 8, count), lambda j: (low + j, 0, 0))],
        out_shape=[
            jax.ShapeDtypeStruct((count, D), jnp.bfloat16),
            jax.ShapeDtypeStruct((D // PAIR, 8, count), jnp.float32),
        ],
        input_output_aliases={1 + len(sources) + n: n for n in range(len(earlier))},
        compiler_params=pltpu.CompilerParams(vmem_limit_bytes=48 * 1024 * 1024),
        cost_estimate=BRIEF,
        name="attend_fwd",
    )(query, *sources, *earlier)


def attend_bwd_kernel(real_keys, chunk, sources, extra, q_ref, *refs):
    kv_refs = refs[:sources]
    lse_ref, o_ref, g_ref = refs[sources : sources + 3]
    dq_ref, *grad_refs = refs[sources + 3 + extra : sources + 4 + extra + sources]
    k_all, v_all, kt_ref, dk_sum, dv_sum = refs[sources + 4 + extra + sources :]
    k_all[...] = joined(kv_refs, 0)
    v_all[...] = joined(kv_refs, 1)
    kt_ref[...] = k_all[...].T
    query, grad = q_ref[...], g_ref[...]
    mixed = (grad.astype(jnp.float32) * o_ref[...].astype(jnp.float32)).T
    total_keys = k_all.shape[0]
    queries = [jnp.where(head_lanes(query.shape, head), query, 0) for head in range(2)]
    grads = [jnp.where(head_lanes(grad.shape, head), grad, 0) for head in range(2)]
    inner = [jnp.sum(mixed[head * HEAD_DIM : (head + 1) * HEAD_DIM], 0, keepdims=True) for head in range(2)]
    grad_query = [jnp.zeros((HEAD_DIM, query.shape[0]), jnp.float32) for head in range(2)]
    for at in range(0, total_keys, chunk):
        part = pl.ds(at, chunk)
        keys, values = k_all[part], v_all[part]
        for head in range(2):
            scores = nt_dot(keys, queries[head])
            shares = jnp.exp2(scores * EXP_SCALE - lse_ref[0, head : head + 1])
            if at + chunk > real_keys:
                row = at + lax.broadcasted_iota(jnp.int32, shares.shape, 0)
                shares = jnp.where(row < real_keys, shares, 0.0)
            grad_shares = nt_dot(values, grads[head])
            grad_scores = (shares * (grad_shares - inner[head])).astype(jnp.bfloat16)
            to_values = product(shares.astype(jnp.bfloat16), grads[head])
            to_keys = product(grad_scores, queries[head])
            if head == 0:
                dv_sum[part] = to_values
                dk_sum[part] = to_keys
            else:
                dv_sum[part] += to_values
                dk_sum[part] += to_keys
            grad_query[head] += product(
                kt_ref[head * HEAD_DIM : (head + 1) * HEAD_DIM, part], grad_scores
            )
    scale = HEAD_DIM ** (-0.5)
    dq_ref[...] = (jnp.concatenate(grad_query, 0) * scale).T.astype(jnp.bfloat16)
    start = 0
    for ref in grad_refs:
        part = pl.ds(start, ref.shape[1])
        ref[0] = (dk_sum[part] * scale).astype(jnp.bfloat16)
        ref[1] = dv_sum[part].astype(jnp.bfloat16)
        start += ref.shape[1]


def attend_bwd(query, sources, real_keys, span, chunk, totals, out, grad, earlier=()):
    count = query.shape[0]
    total_keys = sum(source.shape[1] for source in sources)
    low, high = span
    by_pair = pl.BlockSpec((count, PAIR), lambda j: (0, low + j))
    by_source = [pl.BlockSpec((2, source.shape[1], PAIR), lambda j: (0, 0, low + j)) for source in sources]
    first = 1 + len(sources) + 3
    work = count * total_keys * (high - low) * PAIR
    return pl.pallas_call(
        functools.partial(attend_bwd_kernel, real_keys, chunk, len(sources), len(earlier)),
        grid=(high - low,),
        in_specs=[by_pair]
        + by_source
        + [pl.BlockSpec((1, 8, count), lambda j: (low + j, 0, 0)), by_pair, by_pair]
        + [pl.BlockSpec(memory_space=pl.ANY)] * len(earlier),
        out_specs=[by_pair] + by_source,
        out_shape=[jax.ShapeDtypeStruct((count, D), jnp.bfloat16)]
        + [jax.ShapeDtypeStruct(source.shape, jnp.bfloat16) for source in sources],
        input_output_aliases={first + n: n for n in range(len(earlier))},
        scratch_shapes=[
            pltpu.VMEM((total_keys, PAIR), jnp.bfloat16),
            pltpu.VMEM((total_keys, PAIR), jnp.bfloat16),
            pltpu.VMEM((PAIR, total_keys), jnp.bfloat16),
            pltpu.VMEM((total_keys, PAIR), jnp.float32),
            pltpu.VMEM((total_keys, PAIR), jnp.float32),
        ],
        compiler_params=pltpu.CompilerParams(vmem_limit_bytes=48 * 1024 * 1024),
        cost_estimate=BRIEF,
        name="attend_bwd",
    )(query, *sources, totals, out, grad, *earlier)


GROUPS = 3


def render_kernel(samples_ref, near_ref, far_ref, wanted_ref, mask_ref, factor_ref, win_ref, wout_ref,
                  loss_ref, grad_ref, grad_far_ref, gin_ref, gout_ref,
                  table, inner_all, hidden_all, point_all, out_all, gout_all, sums):
    block = pl.program_id(0)
    half = near_ref.shape[1]
    cells = 2 * half
    group = table.shape[2]
    rays = samples_ref.shape[2]
    planes = near_ref.shape[0]

    @pl.when(block == 0)
    def _():
        loss_ref[...] = jnp.zeros_like(loss_ref)
        gin_ref[...] = jnp.zeros_like(gin_ref)
        gout_ref[...] = jnp.zeros_like(gout_ref)
        sums[...] = jnp.zeros_like(sums)
        table[...] = jnp.zeros_like(table)
        for plane in range(planes):
            turned = jnp.concatenate([near_ref[plane], far_ref[plane]], 0).T
            for g in range(GROUPS):
                width = min(group, cells - g * group)
                table[plane, g * CH : (g + 1) * CH, :width] = turned[:CH, g * group : g * group + width]

    step = 4
    width = step * rays
    win, wout = win_ref[...], wout_ref[...]

    def places_read(plane, s):
        rows = [samples_ref[plane, s + n : s + n + 1, :] for n in range(step)]
        at = jnp.concatenate(rows, 1)
        owner = at // group
        within = at - owner * group
        hot = lax.broadcasted_iota(jnp.int32, (group, width), 0) == within
        return owner, jnp.where(hot, 1.0, 0.0).astype(jnp.bfloat16)

    def tn_dot(left, right):
        return lax.dot_general(left, right, (((0,), (0,)), ((), ())), preferred_element_type=jnp.float32)

    for s in range(0, S, step):
        here = pl.ds(s * rays, width)
        point = jnp.zeros((CH, width), jnp.float32)
        for plane in range(planes):
            owner, hot = places_read(plane, s)
            found = product(table[plane], hot)
            value = found[:CH]
            for g in range(1, GROUPS):
                value = jnp.where(owner == g, found[g * CH : (g + 1) * CH], value)
            point = point + value
        point = point.astype(jnp.bfloat16)
        inner = tn_dot(win, point)
        hidden = (inner * jax.nn.sigmoid(inner)).astype(jnp.bfloat16)
        out_all[:, here] = tn_dot(wout, hidden)
        inner_all[:, here] = inner
        hidden_all[:, here] = hidden
        point_all[:, here] = point

    factor = factor_ref[0]
    mask = mask_ref[...]
    row = lax.broadcasted_iota(jnp.int32, (8, rays), 0)
    is_colour = (row >= 1) & (row <= 3)
    before = jnp.zeros((1, rays), jnp.float32)
    rgb = jnp.zeros((8, rays), jnp.float32)
    kept = []
    for s in range(S):
        out = out_all[:, s * rays : (s + 1) * rays]
        level = out[0:1]
        absorb = (4.0 / S) * (jnp.maximum(level, 0.0) + jnp.log1p(jnp.exp(-jnp.abs(level))))
        weight = jnp.exp(-before) * (1.0 - jnp.exp(-absorb))
        before = before + absorb
        colour = jax.nn.sigmoid(out)
        rgb = rgb + weight * colour
        kept.append((weight, jnp.exp(-before), colour))
    error = jnp.where(is_colour, rgb - wanted_ref[...], 0.0)
    loss_ref[...] += jnp.sum(mask * jnp.sum(error * error, 0, keepdims=True))
    pull = error * (2.0 * factor * mask)
    tail = jnp.zeros((1, rays), jnp.float32)
    for s in reversed(range(S)):
        weight, left_over, colour = kept[s]
        to_weight = jnp.sum(pull * colour, 0, keepdims=True)
        to_absorb = to_weight * left_over - tail
        tail = tail + to_weight * weight
        to_level = (4.0 / S) * to_absorb * colour[0:1]
        to_colour = weight * pull * colour * (1.0 - colour)
        gout_all[:, s * rays : (s + 1) * rays] = jnp.where(row == 0, to_level, to_colour).astype(jnp.bfloat16)

    for s in range(0, S, step):
        here = pl.ds(s * rays, width)
        pulled = gout_all[:, here]
        inner = inner_all[:, here]
        gate = jax.nn.sigmoid(inner)
        grad_inner = product(wout, pulled) * (gate * (1.0 + inner * (1.0 - gate)))
        grad_inner = grad_inner.astype(jnp.bfloat16)
        gout_ref[...] += nt_dot(hidden_all[:, here], pulled)
        gin_ref[...] += nt_dot(point_all[:, here], grad_inner)
        grad_point = product(win, grad_inner)
        coarse = grad_point.astype(jnp.bfloat16).astype(jnp.float32)
        fine = grad_point - coarse
        for plane in range(planes):
            owner, hot = places_read(plane, s)
            rows = [jnp.where(owner == g, coarse, 0.0) for g in range(GROUPS)]
            rows += [jnp.where(owner == g, fine, 0.0) for g in range(GROUPS)]
            stacked = jnp.concatenate(rows, 0).astype(jnp.bfloat16)
            added = nt_dot(stacked, hot)
            sums[plane] += added[: GROUPS * CH] + added[GROUPS * CH :]

    @pl.when(block == pl.num_programs(0) - 1)
    def _():
        for plane in range(planes):
            for g in range(GROUPS):
                for low, high, ref in ((0, half, grad_ref), (half, cells, grad_far_ref)):
                    start, stop = max(g * group, low), min((g + 1) * group, high)
                    if start < stop:
                        part = sums[plane, g * CH : (g + 1) * CH, start - g * group : stop - g * group]
                        ref[plane, :, start - low : stop - low] = part.astype(jnp.bfloat16)


def render(near, far, samples, wanted, mask, factor, decode_in, decode_out, rays):
    planes, half, _ = near.shape
    count = 2 * half
    all_rays = samples.shape[2]
    group = -(-count // (GROUPS * 128)) * 128
    points = S * rays
    whole = lambda *shape: pl.BlockSpec(shape, lambda n: (0,) * len(shape))
    return pl.pallas_call(
        render_kernel,
        grid=(all_rays // rays,),
        in_specs=[
            pl.BlockSpec((planes, S, rays), lambda n: (0, 0, n)),
            whole(*near.shape),
            whole(*far.shape),
            pl.BlockSpec((8, rays), lambda n: (0, n)),
            pl.BlockSpec((1, rays), lambda n: (0, n)),
            pl.BlockSpec(memory_space=pltpu.SMEM),
            whole(CH, DEC_HID),
            whole(DEC_HID, 8),
        ],
        out_specs=[whole(8, 128), whole(planes, CH, half), whole(planes, CH, half), whole(CH, DEC_HID), whole(DEC_HID, 8)],
        out_shape=[
            jax.ShapeDtypeStruct((8, 128), jnp.float32),
            jax.ShapeDtypeStruct((planes, CH, half), jnp.bfloat16),
            jax.ShapeDtypeStruct((planes, CH, half), jnp.bfloat16),
            jax.ShapeDtypeStruct((CH, DEC_HID), jnp.float32),
            jax.ShapeDtypeStruct((DEC_HID, 8), jnp.float32),
        ],
        scratch_shapes=[
            pltpu.VMEM((planes, GROUPS * CH, group), jnp.bfloat16),
            pltpu.VMEM((DEC_HID, points), jnp.float32),
            pltpu.VMEM((DEC_HID, points), jnp.bfloat16),
            pltpu.VMEM((CH, points), jnp.bfloat16),
            pltpu.VMEM((8, points), jnp.float32),
            pltpu.VMEM((8, points), jnp.bfloat16),
            pltpu.VMEM((planes, GROUPS * CH, group), jnp.float32),
        ],
        compiler_params=pltpu.CompilerParams(vmem_limit_bytes=48 * 1024 * 1024),
        name="render",
    )(samples, near, far, wanted, mask, factor, decode_in, decode_out)


def pick_kernel(pixel_ref, valid_ref, target_ref, mask_ref, wanted_ref, count_ref):
    pixels = valid_ref.shape[1]
    rays = pixel_ref.shape[1]
    hot = lax.broadcasted_iota(jnp.int32, (pixels, rays), 0) == pixel_ref[...]
    hot = jnp.where(hot, 1.0, 0.0).astype(jnp.bfloat16)
    rest = target_ref[...]
    rows = [valid_ref[...].astype(jnp.float32)]
    for _ in range(3):
        part = rest.astype(jnp.bfloat16).astype(jnp.float32)
        rows.append(part)
        rest = rest - part
    rows.append(jnp.zeros((6, pixels), jnp.float32))
    found = product(jnp.concatenate(rows, 0).astype(jnp.bfloat16), hot)
    mask = found[:1]
    mask_ref[...] = mask
    wanted_ref[...] = jnp.zeros_like(wanted_ref)
    wanted_ref[1:4] = found[1:4] + found[4:7] + found[7:10]
    count_ref[...] = jnp.broadcast_to(jnp.sum(mask, 1, keepdims=True), count_ref.shape)


def pick(pixel, valid, target):
    rays = pixel.shape[1]
    vmem = pl.BlockSpec(memory_space=pltpu.VMEM)
    return pl.pallas_call(
        pick_kernel,
        in_specs=[vmem] * 3,
        out_specs=[vmem] * 3,
        out_shape=[
            jax.ShapeDtypeStruct((1, rays), jnp.float32),
            jax.ShapeDtypeStruct((8, rays), jnp.float32),
            jax.ShapeDtypeStruct((8, 128), jnp.float32),
        ],
        compiler_params=pltpu.CompilerParams(vmem_limit_bytes=24 * 1024 * 1024),
        name="pick",
    )(pixel, valid, target)


MESH_ID = pl.DeviceIdType.MESH


def places():
    p = lax.axis_index("dp")
    c = lax.axis_index("strip")
    z = p // 4
    flip_x = p + 1 - 2 * (p % 2)
    flip_y = p + 2 - 4 * ((p // 2) % 2)
    both = flip_x + flip_y - p
    near = (1 - c) * flip_x + c * flip_y
    far = (1 - c) * flip_y + c * flip_x
    return p, c, z, near, far, both


def along_z(line, z, k):
    return ((z + k) % 4) * 4 + line % 4


def enter(peers):
    barrier = pltpu.get_barrier_semaphore()
    for peer in peers:
        pl.semaphore_signal(barrier, inc=1, device_id=peer, device_id_type=MESH_ID)
    pl.semaphore_wait(barrier, len(peers))


def flat_chunks(rows, n):
    part = rows // n
    return n, part, lambda p, c, j: (2 * p + c) * rows + j * part


def block_chunk(p, c, k):
    second = p // 8
    return ((1 - second) * ((2 * c + k) * 8 + p) + second * (4 * p + 2 * c + k)) * BLOCK


ORDER = [("near", 0), ("z", 1), ("far", 0), ("z", 2), ("z", 3), ("near", 1), ("near", 2), ("near", 3)]
ORDER += [("both", 0), ("far", 1), ("far", 2), ("far", 3), ("both", 1), ("both", 2), ("both", 3)]
ORDER += [("core", i) for i in range(16)]


def gather_kernel(layouts, stagger, *refs):
    count = len(layouts)
    fulls = refs[count + 1 : 2 * count + 1]
    line_full = refs[2 * count + 1]
    send, recv, local, z_send, line_recv, line_send = refs[2 * count + 2 : 2 * count + 8]
    held = refs[2 * count + 8 :]
    brought = [pltpu.make_async_copy(s, h, local.at[n]) for n, (s, h) in enumerate(zip(refs[: count + 1], held))]
    for copy in brought:
        copy.start()
    sources, line_source = held[:count], held[count]
    p, c, z, near, far, both = places()
    zs = [along_z(p, z, k) for k in range(4)]
    enter([(q, c) for q in zs[1:]] + [(near, c), (far, c), (p, 1 - c)])
    for copy in brought:
        copy.wait()
    jobs = [(a, j) for a, layout in enumerate(layouts) for j in range(layout[0])]
    me = (p, c)
    up, down = (p + 4, c), (p - 4, c)

    def target(owner, job):
        a, j = jobs[job]
        _, rows, place = layouts[a]
        return fulls[a].at[pl.ds(pl.multiple_of(place(*owner, j), 8), rows)]

    def source(owner, job):
        if owner is not me:
            return target(owner, job)
        a, j = jobs[job]
        rows = layouts[a][1]
        return sources[a].at[pl.ds(j * rows, rows)]

    def sending(owner, event, peer, job, sem=None):
        return pltpu.make_async_remote_copy(
            source(owner, job), target(owner, job), send.at[event, job] if sem is None else sem, recv.at[event, job],
            device_id=peer, device_id_type=MESH_ID,
        )

    def arrive(owner, event, job):
        t = target(owner, job)
        pltpu.make_async_remote_copy(
            t, t, send.at[event, job], recv.at[event, job], device_id=(p, 1 - c), device_id_type=MESH_ID
        ).wait_recv()

    def sending_up(distance, job):
        owner = me if distance == 1 else (zs[5 - distance], c)
        return sending(owner, 3 - distance, up, job, z_send.at[0, distance - 1, job])

    def sending_down(distance, job):
        owner = me if distance == 1 else (zs[distance - 1], c)
        return sending(owner, distance - 1, down, job, z_send.at[1, distance - 1, job])

    def line_up(distance):
        held_at = line_source if distance == 1 else line_full.at[5 - distance]
        return pltpu.make_async_remote_copy(
            held_at, line_full.at[4 - distance], line_send.at[0, distance - 1], line_recv.at[4 - distance],
            device_id=up, device_id_type=MESH_ID,
        )

    def line_down(distance):
        held_at = line_source if distance == 1 else line_full.at[distance - 1]
        return pltpu.make_async_remote_copy(
            held_at, line_full.at[distance], line_send.at[1, distance - 1], line_recv.at[distance],
            device_id=down, device_id_type=MESH_ID,
        )

    def each_way(distance, work):
        @pl.when(z + distance <= 3)
        def _():
            work(distance, True)

        @pl.when(z >= distance)
        def _():
            work(4 - distance, False)

    def pass_on(ups, downs, distance, *job):
        if distance > 3:
            return

        @pl.when((z < 3) & (z >= distance - 1))
        def _():
            ups(distance, *job)

        @pl.when((z > 0) & (z + distance - 1 <= 3))
        def _():
            downs(distance, *job)

    def begin(job):
        sending(me, 3, (near, c), job).start()

        @pl.when(z < 3)
        def _():
            sending_up(1, job).start()

        @pl.when(z > 0)
        def _():
            sending_down(1, job).start()

        sending(me, 7, (far, c), job).start()
        sending(me, 15, (p, 1 - c), job).start()
        pltpu.make_async_copy(source(me, job), target(me, job), local.at[job]).start()

    def take_z(k, above, job):
        owner = (zs[k], c)
        arrive(owner, k - 1, job)
        distance = k if above else 4 - k
        if distance < 3:

            @pl.when(z > 0 if above else z < 3)
            def _():
                (sending_down if above else sending_up)(distance + 1, job).start()

        sending(owner, 3 + k, (near, c), job).start()
        sending(owner, 7 + k, (far, c), job).start()
        sending(owner, 15 + k, (p, 1 - c), job).start()

    def take(kind, k, job):
        if kind == "near":
            owner = (along_z(near, z, k), c)
            arrive(owner, 3 + k, job)
            sending(owner, 11 + k, (far, c), job).start()
            sending(owner, 19 + k, (p, 1 - c), job).start()
        elif kind == "far":
            owner = (along_z(far, z, k), c)
            arrive(owner, 7 + k, job)
            sending(owner, 23 + k, (p, 1 - c), job).start()
        elif kind == "both":
            owner = (along_z(both, z, k), c)
            arrive(owner, 11 + k, job)
            sending(owner, 27 + k, (p, 1 - c), job).start()
        elif kind == "core":
            line = (p, far, near, both)[k // 4]
            arrive((along_z(line, z, k % 4), 1 - c), 15 + k, job)

    def line_arrive(k):
        spot = line_full.at[k]
        pltpu.make_async_remote_copy(
            spot, spot, line_send.at[0, 0], line_recv.at[k], device_id=(p, 1 - c), device_id_type=MESH_ID
        ).wait_recv()

    def line_take(k, above):
        line_arrive(k)
        distance = k if above else 4 - k
        if distance < 3:

            @pl.when(z > 0 if above else z < 3)
            def _():
                (line_down if above else line_up)(distance + 1).start()

    steps = [(2 * stagger + 2 + 3 * n, -2, n) for n in range(4)]
    for job in range(len(jobs)):
        begin_at = stagger * min(job, layouts[0][0] - 1)
        for i in range(-1, len(ORDER)):
            steps.append((begin_at + i + 1, i, job))
    own_line = pltpu.make_async_copy(line_source, line_full.at[0], line_recv.at[0])
    for _, i, job in sorted(steps):
        if i == -2:
            if job == 0:

                @pl.when(z < 3)
                def _():
                    line_up(1).start()

                @pl.when(z > 0)
                def _():
                    line_down(1).start()

                own_line.start()
            else:
                each_way(job, line_take)
        elif i < 0:
            begin(job)
        else:
            kind, k = ORDER[i]
            if kind == "z":
                each_way(k, lambda n, above: take_z(n, above, job))
            elif kind == "core" or k == 0:
                take(kind, k, job)
            else:
                each_way(k, lambda n, above: take(kind, n, job))
    own_line.wait()
    for distance in (1, 2, 3):
        pass_on(lambda d: line_up(d).wait_send(), lambda d: line_down(d).wait_send(), distance)
    for job in range(len(jobs)):
        for distance in (1, 2, 3):
            pass_on(lambda d, n: sending_up(d, n).wait_send(), lambda d, n: sending_down(d, n).wait_send(), distance, job)
        for k in range(4):
            owner = (zs[k], c) if k else me
            sending(owner, 3 + k, (near, c), job).wait_send()
            sending(owner, 7 + k, (far, c), job).wait_send()
            sending((along_z(near, z, k), c), 11 + k, (far, c), job).wait_send()
            sending(owner, 15 + k, (p, 1 - c), job).wait_send()
            for line, first in ((near, 19), (far, 23), (both, 27)):
                sending((along_z(line, z, k), c), first + k, (p, 1 - c), job).wait_send()
        pltpu.make_async_copy(source(me, job), target(me, job), local.at[job]).wait()


def gather_all(layouts, stagger, shards_in, line, name_id):
    copies = sum(l[0] for l in layouts)
    everywhere = pl.BlockSpec(memory_space=pl.ANY)
    shapes = [jax.ShapeDtypeStruct((32 * s.shape[0],) + s.shape[1:], s.dtype) for s in shards_in]
    shapes.append(jax.ShapeDtypeStruct((4,) + line.shape, line.dtype))
    return pl.pallas_call(
        functools.partial(gather_kernel, layouts, stagger),
        out_shape=shapes,
        in_specs=[everywhere] * len(shapes),
        out_specs=[everywhere] * len(shapes),
        scratch_shapes=[
            pltpu.SemaphoreType.DMA((31, copies)),
            pltpu.SemaphoreType.DMA((31, copies)),
            pltpu.SemaphoreType.DMA((copies,)),
            pltpu.SemaphoreType.DMA((2, 3, copies)),
            pltpu.SemaphoreType.DMA((4,)),
            pltpu.SemaphoreType.DMA((2, 3)),
        ]
        + [pltpu.VMEM(a.shape, a.dtype) for a in (*shards_in, line)],
        compiler_params=pltpu.CompilerParams(collective_id=name_id, has_side_effects=True),
        name="gather_all",
    )(*shards_in, line)


SUM_ORDER = [(3, 0), (3, 1), (3, 3), (3, 2), (2, 0), (2, 1), (2, 3), (2, 2)]
SUM_ORDER += [(1, 1), (1, 3), (1, 2), (1, 0), (0, 1), (0, 3), (0, 2), (0, 0)]
AHEAD = 3


def scatter_kernel(layouts, stagger, *refs):
    count = len(layouts)
    grads = refs[:count]
    line_grads = refs[count : count + 4]
    outs = refs[count + 4 : 2 * count + 4]
    line_out = refs[2 * count + 4]
    scratch = refs[2 * count + 5 :]
    line_parts, line_sums, line_got, line_sum, line_sems, line_load_sems = scratch[-6:]
    p, c, z, near, far, both = places()
    zs = [along_z(p, z, k) for k in range(4)]
    enter([(q, c) for q in zs[1:]] + [(near, c), (far, c), (p, 1 - c)])
    csend, crecv, bsend, brecv, load_sem, out_sem = scratch[:6]
    buffers = [scratch[6 + 6 * a : 12 + 6 * a] for a in range(count)]
    jobs = [(a, j) for a, layout in enumerate(layouts) for j in range(layout[0])]
    lines = (p, near, far, both)
    partner_lines = (p, far, near, both)

    def view(job, ref, slot):
        a, j = jobs[job]
        rows = layouts[a][1]
        return ref.at[slot, pl.ds(j * rows, rows)]

    def piece(owner, job):
        a, j = jobs[job]
        _, rows, place = layouts[a]
        at = place(*owner, j)
        return grads[a].at[pl.ds(at if isinstance(at, int) else pl.multiple_of(at, 8), rows)]

    def to_core(i, job):
        g, k = SUM_ORDER[i]
        owner = (along_z(partner_lines[g], z, k), 1 - c)
        rc = buffers[jobs[job][0]][0]
        return pltpu.make_async_remote_copy(
            piece(owner, job), view(job, rc, g * 4 + k), csend.at[i, job], crecv.at[i, job],
            device_id=(p, 1 - c), device_id_type=MESH_ID,
        )

    def load(i, job):
        g, k = SUM_ORDER[i]
        own = buffers[jobs[job][0]][4]
        return pltpu.make_async_copy(
            piece((along_z(lines[g], z, k), c), job), view(job, own, i % AHEAD), load_sem.at[i, job]
        )

    def onward(i, job):
        g, k = SUM_ORDER[i]
        rc, rb, ra, rz = buffers[jobs[job][0]][:4]
        if g == 3:
            target, event, peer = view(job, rb, 4 + k), 4 + k, (far, c)
        elif g == 2:
            target, event, peer = view(job, rb, k), k, (far, c)
        elif g == 1:
            target, event, peer = view(job, ra, k), 8 + k, (near, c)
        else:
            target, event, peer = view(job, rz, 3 - k), 12 + 3 - k, (zs[k], c)
        return pltpu.make_async_remote_copy(
            view(job, rc, g * 4 + k), target, bsend.at[event, job], brecv.at[event, job],
            device_id=peer, device_id_type=MESH_ID,
        )

    def landed(event, job):
        rc, rb, ra, rz = buffers[jobs[job][0]][:4]
        if event < 8:
            target = view(job, rb, event)
        elif event < 12:
            target = view(job, ra, event - 8)
        else:
            target = view(job, rz, event - 12)
        pltpu.make_async_remote_copy(
            target, target, bsend.at[event, job], brecv.at[event, job], device_id=(p, 1 - c), device_id_type=MESH_ID
        ).wait_recv()
        return target

    def add_up(parts, target):
        rows = target.shape[0]
        step = math.gcd(rows, 16)

        @pl.loop(0, rows // step)
        def _(n):
            at = pl.ds(pl.multiple_of(n * step, step), step)
            total = parts[0][at].astype(jnp.float32)
            for part in parts[1:]:
                total = total + part[at].astype(jnp.float32)
            target[at] = total.astype(target.dtype)

    def start(i, job):
        to_core(i, job).start()
        load(i, job).start()

    def final_copies(job):
        a, j = jobs[job]
        rows = layouts[a][1]
        return [pltpu.make_async_copy(view(job, buffers[a][5], 0), outs[a].at[pl.ds(j * rows, rows)], out_sem.at[job, 0])]

    line_loads = [
        [pltpu.make_async_copy(ref.at[k], line_parts.at[k, n], line_load_sems.at[k, n]) for n, ref in enumerate(line_grads)]
        for k in range(4)
    ]
    line_sends = {
        k: pltpu.make_async_remote_copy(
            line_sums.at[k], line_got.at[3 - k], line_sems.at[k], line_sems.at[7 - k],
            device_id=(zs[k], c), device_id_type=MESH_ID,
        )
        for k in (1, 3, 2)
    }

    def line_step(k):
        for load_part in line_loads[k]:
            load_part.wait()
        add_up([line_parts.at[k, n] for n in range(4)], line_sums.at[k])
        if k:
            line_sends[k].start()

    half = line_sum.shape[0]
    spot = line_out.at[pl.ds(pl.multiple_of(c * half, 8), half)]
    line_stores = [
        pltpu.make_async_copy(line_sum, spot, line_sems.at[7]),
        pltpu.make_async_remote_copy(
            line_sum, spot, line_sems.at[8], line_sems.at[9], device_id=(p, 1 - c), device_id_type=MESH_ID
        ),
    ]

    def line_finish():
        for k in (1, 2, 3):
            target = line_got.at[k - 1]
            pltpu.make_async_remote_copy(
                target, target, line_sems.at[k], line_sems.at[3 + k], device_id=(p, 1 - c), device_id_type=MESH_ID
            ).wait_recv()
        add_up([line_sums.at[0]] + [line_got.at[n] for n in range(3)], line_sum)
        for copy in line_stores:
            copy.start()

    def step(i, job):
        g, k = SUM_ORDER[i]
        rc, rb, ra, rz, own, done = buffers[jobs[job][0]]
        load(i, job).wait()
        to_core(i, job).wait_recv()
        here = view(job, rc, g * 4 + k)
        parts = [here, view(job, own, i % AHEAD)]
        if g == 1:
            parts.append(landed(4 + k, job))
        if g == 0:
            parts.append(landed(k, job))
            parts.append(landed(8 + k, job))
        if (g, k) == (0, 0):
            parts += [landed(12 + n, job) for n in range(3)]
            add_up(parts, view(job, done, 0))
            for copy in final_copies(job):
                copy.start()
        else:
            add_up(parts, here)
            onward(i, job).start()
        if i + AHEAD < 16:
            start(i + AHEAD, job)

    for k in (1, 3, 2, 0):
        for load_part in line_loads[k]:
            load_part.start()
    for job in range(len(jobs)):
        for n in range(AHEAD):
            start(n, job)
    steps = []
    for job in range(len(jobs)):
        begin = stagger * min(job, layouts[0][0] - 1)
        for i in range(16):
            steps.append((begin + i + 2 * (i // 4 - 1) * (i // 8), job, i))
    steps.append((max(steps)[0] - 6, 0, -1))
    for n, k in enumerate((1, 3, 2, 0)):
        steps.append((n, len(jobs), -2 - k))
    for _, job, i in sorted(steps):
        if i == -1:
            line_finish()
        elif i < 0:
            line_step(-2 - i)
        else:
            step(i, job)
    for job in range(len(jobs)):
        for i in range(16):
            to_core(i, job).wait_send()
            if i < 15:
                onward(i, job).wait_send()
        for copy in final_copies(job):
            copy.wait()
    for copy in line_sends.values():
        copy.wait_send()
    for copy in line_stores:
        copy.wait()


def scatter_sum(layouts, stagger, grads, lines, name_id):
    jobs = sum(l[0] for l in layouts)
    scratch = [
        pltpu.SemaphoreType.DMA((16, jobs)),
        pltpu.SemaphoreType.DMA((16, jobs)),
        pltpu.SemaphoreType.DMA((15, jobs)),
        pltpu.SemaphoreType.DMA((15, jobs)),
        pltpu.SemaphoreType.DMA((16, jobs)),
        pltpu.SemaphoreType.DMA((jobs, 3)),
    ]
    shapes = []
    for layout, grad in zip(layouts, grads):
        rows, width = layout[0] * layout[1], grad.shape[1]
        for slots in (16, 8, 4, 3, AHEAD):
            scratch.append(pltpu.VMEM((slots, rows, width), grad.dtype))
        scratch.append(pltpu.VMEM((1, rows, width), jnp.float32))
        shapes.append(jax.ShapeDtypeStruct((rows, width), jnp.float32))
    piece, kind = lines[-1].shape[1:], lines[-1].dtype
    scratch += [
        pltpu.VMEM((4, 4) + piece, kind),
        pltpu.VMEM((4,) + piece, kind),
        pltpu.VMEM((3,) + piece, kind),
        pltpu.VMEM(piece, kind),
        pltpu.SemaphoreType.DMA((10,)),
        pltpu.SemaphoreType.DMA((4, 4)),
    ]
    shapes.append(jax.ShapeDtypeStruct((2 * piece[0], piece[1]), kind))
    everywhere = pl.BlockSpec(memory_space=pl.ANY)
    return pl.pallas_call(
        functools.partial(scatter_kernel, layouts, stagger),
        out_shape=shapes,
        in_specs=[everywhere] * (len(grads) + len(lines)),
        out_specs=[everywhere] * len(shapes),
        scratch_shapes=scratch,
        compiler_params=pltpu.CompilerParams(
            collective_id=name_id, has_side_effects=True, vmem_limit_bytes=48 * 1024 * 1024
        ),
        name="scatter_sum",
    )(*grads, *lines)


GELU_A = math.sqrt(2.0 / math.pi)
GELU_B = 0.044715


def chunk_sources(first):
    p, c, z, _, _, _ = places()
    x, y = p % 2, (p // 2) % 2
    out = []
    for n in range(4):
        owner_z = (first + n) % 4
        k = (owner_z - z + 4) % 4
        for half in range(2):
            for other in range(2):
                core = (c + other) % 2
                for g in range(4):
                    dx = (1 - core) * (g % 2) + core * (g // 2)
                    dy = (1 - core) * (g // 2) + core * (g % 2)
                    owner = owner_z * 4 + ((y + dy) % 2) * 2 + (x + dx) % 2
                    out.append((other, g, k, half, block_chunk(owner, core, half) // BLOCK))
    return out


def panel_loads(refs, held, sems, first):
    if len(refs) == 1:
        for n in range(held.shape[0] // WIDE):
            at = pl.ds(n * WIDE, WIDE)
            pltpu.make_async_copy(refs[0].at[at], held.at[at], sems.at[n]).start()
        return
    for other, g, k, half, chunk in chunk_sources(first):
        source = refs[other * 4 + g].at[k, pl.ds(half * BLOCK, BLOCK)]
        target = held.at[pl.ds(pl.multiple_of(chunk * BLOCK, BLOCK), BLOCK)]
        pltpu.make_async_copy(source, target, sems.at[chunk // 8]).start()


def panel_ready(held, sems, n):
    at = pl.ds(pl.multiple_of(n * WIDE, WIDE), WIDE)
    pltpu.make_async_copy(held.at[at], held.at[at], sems.at[n]).wait()
    return held.at[at]


def mlp_fwd_kernel(count, *refs):
    sources = refs[:count]
    h_ref, s_ref, up_ref, act_ref, grid_ref, held, total, sems = refs[count:]
    step = pl.program_id(0)
    steps = pl.num_programs(0)

    @pl.when(step == 0)
    def _():
        panel_loads(sources, held, sems, 0)
        total[...] = s_ref[...]

    up = product(h_ref[...], panel_ready(held, sems, step)[...])
    up_ref[0] = up
    act = 0.5 * up * (1.0 + jnp.tanh(GELU_A * (up + GELU_B * up * up * up)))
    act = act.astype(jnp.bfloat16)
    act_ref[0] = act
    total[...] += product(act, panel_ready(held, sems, steps + step)[...])

    @pl.when(step == steps - 1)
    def _():
        grid_ref[...] = total[...].astype(jnp.bfloat16)


def mlp_fwd(panels, hidden, stream):
    rows = hidden.shape[0]
    steps = HID // WIDE
    whole = pl.BlockSpec((rows, WIDE), lambda n: (0, 0))
    part = pl.BlockSpec((1, rows, WIDE), lambda n: (n, 0, 0))
    return pl.pallas_call(
        functools.partial(mlp_fwd_kernel, len(panels)),
        grid=(steps,),
        in_specs=[pl.BlockSpec(memory_space=pl.ANY)] * len(panels) + [whole, whole],
        out_specs=[part, part, whole],
        out_shape=[
            jax.ShapeDtypeStruct((steps, rows, WIDE), jnp.float32),
            jax.ShapeDtypeStruct((steps, rows, WIDE), jnp.bfloat16),
            jax.ShapeDtypeStruct((rows, WIDE), jnp.bfloat16),
        ],
        scratch_shapes=[
            pltpu.VMEM((2 * HID, WIDE), jnp.bfloat16),
            pltpu.VMEM((rows, WIDE), jnp.float32),
            pltpu.SemaphoreType.DMA((2 * steps,)),
        ],
        compiler_params=pltpu.CompilerParams(vmem_limit_bytes=56 * 1024 * 1024),
        cost_estimate=BRIEF,
        name="mlp_fwd",
    )(*panels, hidden, stream)


def mlp_bwd_kernel(count, *refs):
    sources = refs[:count]
    outs = 2 if count > 1 else 1
    h_ref, g_ref, up_ref, act_ref = refs[count : count + 4]
    dh_ref = refs[count + 4]
    grads = refs[count + 5 : count + 5 + outs]
    held, staged, sems, out_sem = refs[count + 5 + outs :]
    step = pl.program_id(0)
    steps = pl.num_programs(0)

    @pl.when(step == 0)
    def _():
        panel_loads(sources, held, sems, 2)
        dh_ref[...] = jnp.zeros_like(dh_ref)

    def tn_dot(left, right):
        return lax.dot_general(left, right, (((0,), (0,)), ((), ())), preferred_element_type=jnp.float32)

    def drain(side):
        pltpu.make_async_copy(staged.at[side], staged.at[side], out_sem.at[side]).wait()

    def store(side):
        panel = side * steps + step
        source = staged.at[side]
        if count == 1:
            at = pl.ds(pl.multiple_of(panel * WIDE, WIDE), WIDE)
            pltpu.make_async_copy(source, grads[0].at[at], out_sem.at[side]).start()
            return
        p, c, z, _, _, _ = places()
        for n in range(8):
            if side == 0:
                owner, core, half = n, step // 2, step % 2
            else:
                row = step * 8 + n
                owner, core, half = 8 + row // 4, (n // 2) % 2, n % 2
            dx = (owner % 2 + p % 2) % 2
            dy = ((owner // 2) % 2 + (p // 2) % 2) % 2
            g = (1 - core) * (dx + 2 * dy) + core * (dy + 2 * dx)
            spot = g * 4 + (owner // 4 - z + 4) % 4
            at = pl.ds(pl.multiple_of(half * BLOCK, BLOCK), BLOCK)
            from_ref = source.at[pl.ds(n * BLOCK, BLOCK)]

            @pl.when((core + c) % 2 == 0)
            def _():
                pltpu.make_async_copy(from_ref, grads[0].at[spot, at], out_sem.at[side]).start()

            @pl.when((core + c) % 2 == 1)
            def _():
                pltpu.make_async_copy(from_ref, grads[1].at[spot, at], out_sem.at[side]).start()

    pulled = g_ref[...]

    @pl.when(step > 0)
    def _():
        drain(1)

    staged[1] = tn_dot(act_ref[0], pulled).astype(jnp.bfloat16)
    store(1)
    grad_act = nt_dot(pulled, panel_ready(held, sems, steps + step)[...])
    up = up_ref[0]
    square = up * up
    bend = jnp.tanh(GELU_A * up * (1.0 + GELU_B * square))
    slope = 0.5 * (1.0 + bend) + 0.5 * GELU_A * up * (1.0 - bend * bend) * (1.0 + 3.0 * GELU_B * square)
    grad_up = (grad_act * slope).astype(jnp.bfloat16)

    @pl.when(step > 0)
    def _():
        drain(0)

    staged[0] = tn_dot(h_ref[...], grad_up).astype(jnp.bfloat16)
    store(0)
    dh_ref[...] += nt_dot(grad_up, panel_ready(held, sems, step)[...])

    @pl.when(step == steps - 1)
    def _():
        drain(0)
        drain(1)


def mlp_bwd(panels, hidden, grad, up, act):
    rows = hidden.shape[0]
    steps = HID // WIDE
    whole = pl.BlockSpec((rows, WIDE), lambda n: (0, 0))
    part = pl.BlockSpec((1, rows, WIDE), lambda n: (n, 0, 0))
    if len(panels) == 1:
        shapes = [jax.ShapeDtypeStruct((2 * HID, WIDE), jnp.bfloat16)]
    else:
        shapes = [jax.ShapeDtypeStruct((16, 2 * BLOCK, WIDE), jnp.bfloat16)] * 2
    return pl.pallas_call(
        functools.partial(mlp_bwd_kernel, len(panels)),
        grid=(steps,),
        in_specs=[pl.BlockSpec(memory_space=pl.ANY)] * len(panels) + [whole, whole, part, part],
        out_specs=[whole] + [pl.BlockSpec(memory_space=pl.ANY)] * len(shapes),
        out_shape=[jax.ShapeDtypeStruct((rows, WIDE), jnp.float32)] + shapes,
        scratch_shapes=[
            pltpu.VMEM((2 * HID, WIDE), jnp.bfloat16),
            pltpu.VMEM((2, WIDE, WIDE), jnp.bfloat16),
            pltpu.SemaphoreType.DMA((2 * steps,)),
            pltpu.SemaphoreType.DMA((2,)),
        ],
        compiler_params=pltpu.CompilerParams(vmem_limit_bytes=58 * 1024 * 1024),
        cost_estimate=BRIEF,
        name="mlp_bwd",
    )(*panels, hidden, grad, up, act)


SLOT = 128
TAPS = 16


def spread_deconv_kernel(first, rows_ref, o_ref, raw, flat, turned, sem):
    load = pltpu.make_async_copy(rows_ref.at[pl.ds(first, raw.shape[0])], raw, sem)
    load.start()
    load.wait()
    whole = raw[...].reshape(TAPS * CH, WIDE).astype(jnp.float32)
    for n in range(WIDE // SLOT):
        flat[n] = whole[:, n * SLOT : (n + 1) * SLOT]
    lane = lax.broadcasted_iota(jnp.int32, (D // 4, SLOT), 1)

    def block(i, j):
        at = 10 * i + j
        return flat[at % 8, pl.ds(at // 8, D // 4, stride=5), :]

    for tap in range(TAPS):
        j, start = divmod(tap * CH, SLOT)
        for i in range(4):
            part = block(i, j)
            if start:
                part = pltpu.roll(part, SLOT - start, 1)
            if start + CH > SLOT:
                part = jnp.where(lane < SLOT - start, part, pltpu.roll(block(i, j + 1), SLOT - start, 1))
            turned[pl.ds(i, D // 4, stride=4), :] = jnp.where(lane < CH, part, 0.0)
        o_ref[:, tap * SLOT : (tap + 1) * SLOT] = turned[...].astype(jnp.bfloat16)


def spread_deconv(rows, first):
    return pl.pallas_call(
        functools.partial(spread_deconv_kernel, first),
        in_specs=[pl.BlockSpec(memory_space=pl.ANY)],
        out_specs=pl.BlockSpec(memory_space=pltpu.VMEM),
        out_shape=jax.ShapeDtypeStruct((D, TAPS * SLOT), jnp.bfloat16),
        scratch_shapes=[
            pltpu.VMEM((TAPS * CH // 8, 8, WIDE), jnp.bfloat16),
            pltpu.VMEM((WIDE // SLOT, TAPS * CH, SLOT), jnp.float32),
            pltpu.VMEM((D, SLOT), jnp.float32),
            pltpu.SemaphoreType.DMA,
        ],
        compiler_params=pltpu.CompilerParams(vmem_limit_bytes=32 * 1024 * 1024),
        name="spread_deconv",
    )(rows)


def with_edges(own, edge):
    place = lax.axis_index("strip")
    above = jnp.where(place == 0, jnp.zeros_like(edge), edge)
    below = jnp.where(place == 0, edge, jnp.zeros_like(edge))
    return jnp.concatenate([above, own, below], 0)


def moved(value, step):
    column = lax.broadcasted_iota(jnp.int32, value.shape, 0) % TC
    inside = (column + step >= 0) & (column + step < TC)
    return jnp.where(inside, pltpu.roll(value, (-step) % value.shape[0], 0), 0.0)


def deconv_fwd_kernel(grid_ref, edge_ref, w_ref, o_ref, taps, fine):
    padded = with_edges(grid_ref[0], edge_ref[0])
    rows = grid_ref.shape[1]
    taps[...] = product(padded, w_ref[...])

    def tap(kr, kc, r):
        slot = kr * 4 + kc
        return taps[pl.ds((r + 1) * TC, rows), slot * SLOT : (slot + 1) * SLOT]

    for i in range(2):
        for j in range(2):
            total = tap(i + 1, j + 1, 0) + tap(3 - 3 * i, j + 1, 2 * i - 1)
            side = tap(i + 1, 3 - 3 * j, 0) + tap(3 - 3 * i, 3 - 3 * j, 2 * i - 1)
            total = total + moved(side, 2 * j - 1)
            for a in range(rows // TC):
                fine[pl.ds((2 * a + i) * 2 * TC + j, TC, stride=2), :] = total[a * TC : (a + 1) * TC]
    o_ref[0] = fine[...].astype(jnp.bfloat16)


def deconv_fwd(grid, edge, weights):
    planes, rows, _ = grid.shape
    return pl.pallas_call(
        deconv_fwd_kernel,
        grid=(planes,),
        in_specs=[
            pl.BlockSpec((1, rows, D), lambda n: (n, 0, 0)),
            pl.BlockSpec((1, TC, D), lambda n: (n, 0, 0)),
            pl.BlockSpec(weights.shape, lambda n: (0, 0)),
        ],
        out_specs=pl.BlockSpec((1, 4 * rows, SLOT), lambda n: (n, 0, 0)),
        out_shape=jax.ShapeDtypeStruct((planes, 4 * rows, SLOT), jnp.bfloat16),
        scratch_shapes=[
            pltpu.VMEM((rows + 2 * TC, TAPS * SLOT), jnp.float32),
            pltpu.VMEM((4 * rows, SLOT), jnp.float32),
        ],
        compiler_params=pltpu.CompilerParams(vmem_limit_bytes=40 * 1024 * 1024),
        name="deconv_fwd",
    )(grid, edge, weights)


def deconv_bwd_kernel(own_ref, got_ref, grid_ref, edge_ref, w_ref, gx_ref, gedge_ref, gw_ref, fine, spread, tokens, sums, flat):
    plane = pl.program_id(0)
    rows = grid_ref.shape[1]
    high = rows + 2 * TC
    place = lax.axis_index("strip")
    total = own_ref[0].astype(jnp.float32) + got_ref[0].astype(jnp.float32)
    total = jnp.concatenate([total, jnp.zeros((SLOT - CH, total.shape[1]), jnp.float32)], 0)
    fine[...] = total.T
    here = pl.ds(plane * high, high)
    tokens[here] = with_edges(grid_ref[0], edge_ref[0])
    for i in range(2):
        for j in range(2):
            parts = [fine[pl.ds((2 * a + i) * 2 * TC + j, TC, stride=2), :] for a in range(rows // TC)]
            part = jnp.concatenate(parts, 0)
            for kr in (i + 1, 3 - 3 * i):
                for kc in (j + 1, 3 - 3 * j):
                    value = part if kc == j + 1 else moved(part, 1 - 2 * j)
                    start = TC if kr == i + 1 else (0 if i == 0 else 2 * TC)
                    pieces = [value]
                    if start:
                        pieces.insert(0, jnp.zeros((start, SLOT), jnp.float32))
                    if high - rows - start:
                        pieces.append(jnp.zeros((high - rows - start, SLOT), jnp.float32))
                    slot = kr * 4 + kc
                    spread[here, slot * SLOT : (slot + 1) * SLOT] = jnp.concatenate(pieces, 0).astype(jnp.bfloat16)
    back = nt_dot(spread[here], w_ref[...])
    gx_ref[0] = back[TC : TC + rows]
    gedge_ref[0] = jnp.where(place == 0, back[TC + rows :], back[:TC]).astype(jnp.bfloat16)

    @pl.when(plane == pl.num_programs(0) - 1)
    def _():
        wide = 512
        for n in range(TAPS * SLOT // wide):
            columns = slice(n * wide, (n + 1) * wide)
            part = lax.dot_general(
                tokens[...], spread[:, columns], (((0,), (0,)), ((), ())), preferred_element_type=jnp.float32
            )
            for m in range(wide // SLOT):
                sums[n * (wide // SLOT) + m] = part[:, m * SLOT : (m + 1) * SLOT]
        lane = lax.broadcasted_iota(jnp.int32, (D // 4, SLOT), 1)
        for i in range(4):
            for j in range(TAPS * CH // SLOT):
                block = None
                for tap in range(j * SLOT // CH, (j * SLOT + SLOT - 1) // CH + 1):
                    part = sums[tap, pl.ds(i, D // 4, stride=4), :]
                    shift = tap * CH - j * SLOT
                    if shift % SLOT:
                        part = pltpu.roll(part, shift % SLOT, 1)
                    block = part if block is None else jnp.where(lane < shift, block, part)
                at = 10 * i + j
                flat[at % 8, pl.ds(at // 8, D // 4, stride=5), :] = block
        whole = jnp.concatenate([flat[n] for n in range(WIDE // SLOT)], 1)
        gw_ref[...] = whole.astype(jnp.bfloat16).reshape(gw_ref.shape)


def deconv_bwd(own, got, grid, edge, weights):
    planes, rows, _ = grid.shape
    high = rows + 2 * TC
    by_plane = lambda *shape: pl.BlockSpec((1,) + shape, lambda n: (n, 0, 0))
    return pl.pallas_call(
        deconv_bwd_kernel,
        grid=(planes,),
        in_specs=[
            by_plane(*own.shape[1:]),
            by_plane(*got.shape[1:]),
            by_plane(rows, D),
            by_plane(TC, D),
            pl.BlockSpec(weights.shape, lambda n: (0, 0)),
        ],
        out_specs=[by_plane(rows, D), by_plane(TC, D), pl.BlockSpec((TAPS * CH // 8, 8, WIDE), lambda n: (0, 0, 0))],
        out_shape=[
            jax.ShapeDtypeStruct((planes, rows, D), jnp.float32),
            jax.ShapeDtypeStruct((planes, TC, D), jnp.bfloat16),
            jax.ShapeDtypeStruct((TAPS * CH // 8, 8, WIDE), jnp.bfloat16),
        ],
        scratch_shapes=[
            pltpu.VMEM((4 * rows, SLOT), jnp.float32),
            pltpu.VMEM((planes * high, TAPS * SLOT), jnp.bfloat16),
            pltpu.VMEM((planes * high, D), jnp.bfloat16),
            pltpu.VMEM((TAPS, D, SLOT), jnp.float32),
            pltpu.VMEM((WIDE // SLOT, TAPS * CH, SLOT), jnp.float32),
        ],
        compiler_params=pltpu.CompilerParams(vmem_limit_bytes=56 * 1024 * 1024),
        name="deconv_bwd",
    )(own, got, grid, edge, weights)


def panel_view(rows_ref, first, count, depth):
    region = rows_ref.at[pl.ds(first, depth // 8 * count)]
    return region.reshape(depth // 8, count, 8, WIDE)


def project_kernel(first, count, depth, lead, x_ref, rows_ref, *rest):
    outs, held, sems = rest[:-2], rest[-2], rest[-1]
    step = pl.program_id(0)
    panels = panel_view(rows_ref, first, count, depth)

    @pl.when(step == 0)
    def _():
        for n in range(count):
            pltpu.make_async_copy(panels.at[:, n], held.at[n], sems.at[n]).start()

    pltpu.make_async_copy(held.at[step], held.at[step], sems.at[step]).wait()
    result = product(x_ref[...], held[step].reshape(depth, WIDE)).astype(jnp.bfloat16)
    if lead:

        @pl.when(step == 0)
        def _():
            outs[0][...] = result

        @pl.when(step > 0)
        def _():
            outs[1][0] = result

    else:
        outs[0][0] = result


def project(x, rows, first, count, lead):
    tokens, depth = x.shape
    specs = [pl.BlockSpec((1, tokens, WIDE), lambda n: (jnp.maximum(n - lead, 0), 0, 0))]
    shapes = [jax.ShapeDtypeStruct((count - lead, tokens, WIDE), jnp.bfloat16)]
    if lead:
        specs.insert(0, pl.BlockSpec((tokens, WIDE), lambda n: (0, 0)))
        shapes.insert(0, jax.ShapeDtypeStruct((tokens, WIDE), jnp.bfloat16))
    return pl.pallas_call(
        functools.partial(project_kernel, first, count, depth, lead),
        grid=(count,),
        in_specs=[pl.BlockSpec((tokens, depth), lambda n: (0, 0)), pl.BlockSpec(memory_space=pl.ANY)],
        out_specs=specs,
        out_shape=shapes,
        scratch_shapes=[pltpu.VMEM((count, depth // 8, 8, WIDE), jnp.bfloat16), pltpu.SemaphoreType.DMA((count,))],
        compiler_params=pltpu.CompilerParams(vmem_limit_bytes=32 * 1024 * 1024),
        cost_estimate=BRIEF,
        name="project",
    )(x, rows)


def project_back_kernel(first, count, depth, lead_ref, g_ref, rows_ref, o_ref, held, sems):
    step = pl.program_id(0)
    panels = panel_view(rows_ref, first, count, depth)

    @pl.when(step == 0)
    def _():
        for n in range(count):
            pltpu.make_async_copy(panels.at[:, n], held.at[n], sems.at[n]).start()

    pltpu.make_async_copy(held.at[step], held.at[step], sems.at[step]).wait()
    grad = jnp.where(step == 0, lead_ref[...], g_ref[0])
    back = nt_dot(grad, held[step].reshape(depth, WIDE))

    @pl.when(step == 0)
    def _():
        o_ref[...] = back

    @pl.when(step > 0)
    def _():
        o_ref[...] += back


def project_back(lead, grads, rows, first, depth):
    others, tokens, _ = grads.shape
    count = others + 1
    return pl.pallas_call(
        functools.partial(project_back_kernel, first, count, depth),
        grid=(count,),
        in_specs=[
            pl.BlockSpec((tokens, WIDE), lambda n: (0, 0)),
            pl.BlockSpec((1, tokens, WIDE), lambda n: (jnp.maximum(n - 1, 0), 0, 0)),
            pl.BlockSpec(memory_space=pl.ANY),
        ],
        out_specs=pl.BlockSpec((tokens, depth), lambda n: (0, 0)),
        out_shape=jax.ShapeDtypeStruct((tokens, depth), jnp.float32),
        scratch_shapes=[pltpu.VMEM((count, depth // 8, 8, WIDE), jnp.bfloat16), pltpu.SemaphoreType.DMA((count,))],
        compiler_params=pltpu.CompilerParams(vmem_limit_bytes=32 * 1024 * 1024),
        cost_estimate=BRIEF,
        name="project_back",
    )(lead, grads, rows)


def weight_grads_kernel(products, copies, *refs):
    arrays = refs[: len(refs) - 9]
    out, left, right, staged, bounce, nothing, load_sem, store_sem, copy_sem = refs[len(refs) - 9 :]
    place = lax.axis_index("strip")
    step = pl.program_id(0)
    steps = len(products)

    def loads(n):
        side, (a, a_pick), (b, b_pick), _, _ = products[n]
        slot = n % 2
        source_a = arrays[a] if a_pick is None else arrays[a].at[a_pick]
        source_b = arrays[b] if b_pick is None else arrays[b].at[b_pick]
        rows, deep = side
        return [
            pltpu.make_async_copy(source_a, left.at[slot, pl.ds(0, rows), pl.ds(0, deep)], load_sem.at[slot, 0]),
            pltpu.make_async_copy(source_b, right.at[slot, pl.ds(0, rows)], load_sem.at[slot, 1]),
        ]

    def stores(n):
        (rows, deep), _, _, first, panels = products[n]
        slot = n % 2
        count, at = panels
        source = staged.at[slot, pl.ds(0, deep // 8)]
        target = panel_view(out, first, count, deep).at[:, at]
        return pltpu.make_async_copy(source, target, store_sem.at[slot])

    def bring(n):
        a, start, count, _, _ = copies[n]
        held = bounce.at[pl.ds(sum(c[2] for c in copies[:n] if c[0] is not None), count)]
        return pltpu.make_async_copy(arrays[a].at[pl.ds(start, count)], held, copy_sem.at[n, 0])

    def put(n):
        a, _, count, first, step = copies[n]
        if a is None:
            held = nothing.at[pl.ds(0, count)]
        else:
            held = bounce.at[pl.ds(sum(c[2] for c in copies[:n] if c[0] is not None), count)]
        return pltpu.make_async_copy(held, out.at[pl.ds(first + step * place, count)], copy_sem.at[n, 1])

    for n in range(steps):

        @pl.when(step == n)
        def _():
            if n == 0:
                for job in loads(0):
                    job.start()
                nothing[...] = jnp.zeros_like(nothing)
                for m in range(len(copies)):
                    if copies[m][0] is not None:
                        bring(m).start()
            if n == 1:
                for m in range(len(copies)):
                    if copies[m][0] is not None:
                        bring(m).wait()
                    put(m).start()
            if n + 1 < steps:
                for job in loads(n + 1):
                    job.start()
            for job in loads(n):
                job.wait()
            if n >= 2:
                stores(n - 2).wait()
            rows, deep = products[n][0]
            slot = n % 2
            total = lax.dot_general(
                left[slot, :rows, :deep], right[slot, :rows], (((0,), (0,)), ((), ())), preferred_element_type=jnp.float32
            )
            staged[slot, : deep // 8] = total.astype(jnp.bfloat16).reshape(deep // 8, 8, WIDE)
            stores(n).start()
            if n == steps - 1:
                if n > 0:
                    stores(n - 1).wait()
                stores(n).wait()
                for m in range(len(copies)):
                    put(m).wait()


def weight_grads(arrays, products, copies, tile_rows):
    rows = max(p[0][0] for p in products)
    deep = max(p[0][1] for p in products)
    everywhere = pl.BlockSpec(memory_space=pl.ANY)
    return pl.pallas_call(
        functools.partial(weight_grads_kernel, products, copies),
        grid=(len(products),),
        in_specs=[everywhere] * len(arrays),
        out_specs=everywhere,
        out_shape=jax.ShapeDtypeStruct((tile_rows, 8, WIDE), jnp.bfloat16),
        scratch_shapes=[
            pltpu.VMEM((2, rows, deep), jnp.bfloat16),
            pltpu.VMEM((2, rows, WIDE), jnp.bfloat16),
            pltpu.VMEM((2, deep // 8, 8, WIDE), jnp.bfloat16),
            pltpu.VMEM((sum(c[2] for c in copies if c[0] is not None), 8, WIDE), jnp.bfloat16),
            pltpu.VMEM((max(c[2] for c in copies if c[0] is None), 8, WIDE), jnp.bfloat16),
            pltpu.SemaphoreType.DMA((2, 2)),
            pltpu.SemaphoreType.DMA((2,)),
            pltpu.SemaphoreType.DMA((len(copies), 2)),
        ],
        compiler_params=pltpu.CompilerParams(vmem_limit_bytes=60 * 1024 * 1024),
        cost_estimate=BRIEF,
        name="weight_grads",
    )(*arrays)


TILE = 8 * WIDE
KV_AT = D * D
QKV_AT = KV_AT + DI * 2 * D + D * D
GAP_AT = QKV_AT + D * 3 * D + D * D + D * 16 * CH + CH * DEC_HID + DEC_HID * 4
QKV_GAP = -QKV_AT % (3 * TILE)
END_GAP = -GAP_AT % TILE
TILES = {}
_tile = 0
for _name, _rows in (
    ("query_cross", D),
    ("keyval_cross", 2 * DI),
    ("out_cross", D),
    ("gap", QKV_GAP // WIDE),
    ("qkv_self", 3 * D),
    ("out_self", D),
    ("deconv", 16 * CH),
    ("decode", 8),
    ("modulate", 6 * NCAM),
    ("triplane", 0),
):
    TILES[_name] = _tile
    _tile += _rows // 8


def direct_links():
    return lax.axis_size("dp") == 16 and lax.axis_size("strip") == 2


def regroup(rows, first, back):
    tile = first + lax.broadcasted_iota(jnp.int32, (rows.shape[0], 1), 0) // 8

    def turned(panels):
        shape = (-1, panels, 8, WIDE) if back else (-1, 8, panels, WIDE)
        return rows.reshape(shape).transpose(0, 2, 1, 3).reshape(rows.shape)

    in_kv = (tile >= TILES["keyval_cross"]) & (tile < TILES["out_cross"])
    in_qkv = (tile >= TILES["qkv_self"]) & (tile < TILES["out_self"])
    return jnp.where(in_kv, turned(2), jnp.where(in_qkv, turned(3), rows))


def tile_rows(length):
    return -(-length // (6 * TILE)) * 6


LANES = 128
TILE_LINES = TILE // LANES


def tile_place(tile):
    gap = QKV_GAP // LANES * jnp.where(tile >= TILES["gap"], 1, 0)
    return gap + END_GAP // LANES * jnp.where(tile >= TILES["modulate"], 1, 0)


def by_region(tile, work):
    in_kv = (tile >= TILES["keyval_cross"]) & (tile < TILES["out_cross"])
    in_qkv = (tile >= TILES["qkv_self"]) & (tile < TILES["out_self"])

    @pl.when(in_kv)
    def _():
        work(2)

    @pl.when(in_qkv)
    def _():
        work(3)

    @pl.when(jnp.logical_not(in_kv | in_qkv))
    def _():
        work(1)


def tile_lines(tile, first, panels):
    panel = lax.rem(tile, panels)
    return (tile - panel - first) * TILE_LINES + panel * 8


def prepare_kernel(own_ref, next_ref, blocks_ref, o_ref, chunks_ref, lines, tiles, sem):
    half = tiles.shape[0]
    core = lax.axis_index("strip")
    load = pltpu.make_async_copy(blocks_ref.at[pl.ds(core * half, half)], tiles, sem)
    load.start()
    place = lax.axis_index("dp") * 2 + core
    count = own_ref.shape[0]
    lines[:count] = own_ref[...]
    lines[count : count + next_ref.shape[0]] = next_ref[...]
    held = o_ref.shape[0] // 8
    first = place * held
    shift = place * (held * TILE_LINES - count)

    @pl.loop(0, held // 2)
    def _(n):
        def work(panels):
            rows = []
            for m in range(2):
                tile = first + 2 * n + m
                start = tile_lines(tile, first, panels) + shift - tile_place(tile)
                rows.append(jnp.concatenate([lines[pl.ds(start + j, 8, stride=8 * panels), :] for j in range(8)], 1))
            o_ref[pl.ds(pl.multiple_of(16 * n, 16), 16)] = jnp.concatenate(rows, 0).astype(jnp.bfloat16)

        by_region(first + 2 * n, work)

    load.wait()
    for n in range(half):
        at, column = n // 8 * BLOCK, n % 8 * BLOCK
        chunks_ref[at : at + BLOCK, column : column + BLOCK] = tiles[n].astype(jnp.bfloat16)


def prepare(weights, blocks):
    lines = weights.reshape(-1, LANES)
    count = lines.shape[0]
    held = tile_rows(weights.shape[0])
    reach = -(-32 * (held * TILE_LINES - count) // 8) * 8
    following = lax.ppermute(lines[:reach], AXES, [(n + 1, n) for n in range(31)])
    half = blocks.shape[0] // 2
    vmem = pl.BlockSpec(memory_space=pltpu.VMEM)
    return pl.pallas_call(
        prepare_kernel,
        in_specs=[vmem, vmem, pl.BlockSpec(memory_space=pl.ANY)],
        out_specs=[vmem, vmem],
        out_shape=[
            jax.ShapeDtypeStruct((held * 8, WIDE), jnp.bfloat16),
            jax.ShapeDtypeStruct((half // 8 * BLOCK, WIDE), jnp.bfloat16),
        ],
        scratch_shapes=[
            pltpu.VMEM((-(-(count + reach) // 8) * 8, LANES), jnp.float32),
            pltpu.VMEM((half, BLOCK, BLOCK), jnp.float32),
            pltpu.SemaphoreType.DMA,
        ],
        compiler_params=pltpu.CompilerParams(vmem_limit_bytes=16 * 1024 * 1024),
        name="prepare",
    )(lines, following, blocks)


def ungroup_kernel(rows_ref, o_ref):
    place = lax.axis_index("dp") * 2 + lax.axis_index("strip")
    held = rows_ref.shape[0] // 8
    first = place * held

    @pl.loop(0, held)
    def _(n):
        def work(panels):
            start = tile_lines(first + n, first, panels)
            at = pl.ds(pl.multiple_of(8 * n, 8), 8)
            for j in range(8):
                o_ref[pl.ds(start + j, 8, stride=8 * panels), :] = rows_ref[at, j * LANES : (j + 1) * LANES]

        by_region(first + n, work)


def ungroup(rows):
    vmem = pl.BlockSpec(memory_space=pltpu.VMEM)
    return pl.pallas_call(
        ungroup_kernel,
        in_specs=[vmem],
        out_specs=vmem,
        out_shape=jax.ShapeDtypeStruct((rows.size // LANES, LANES), jnp.float32),
        compiler_params=pltpu.CompilerParams(vmem_limit_bytes=16 * 1024 * 1024),
        name="ungroup",
    )(rows)


def adam_kernel(before_ref, sum_ref, w_ref, first_ref, second_ref, nw_ref, nfirst_ref, nsecond_ref, lines):
    place = lax.axis_index("dp") * 2 + lax.axis_index("strip")
    reach, summed, count = before_ref.shape[0], sum_ref.shape[0], w_ref.shape[0]
    lines[:reach] = before_ref[...]
    lines[reach : reach + summed] = sum_ref[...]
    shift = reach - place * (summed - count)
    gaps = (0, QKV_GAP // LANES, (QKV_GAP + END_GAP) // LANES)

    def update(at, rows):
        parts = [lines[pl.ds(shift + at + gap, rows), :] for gap in gaps]
        line = place * count + at + lax.broadcasted_iota(jnp.int32, (rows, LANES), 0)
        grad = jnp.where(line < QKV_AT // LANES, parts[0], jnp.where(line < GAP_AT // LANES, parts[1], parts[2]))
        here = pl.ds(at, rows)
        weights = w_ref[here]
        first = BETA_FIRST * first_ref[here] + (1.0 - BETA_FIRST) * grad
        second = BETA_SECOND * second_ref[here] + (1.0 - BETA_SECOND) * grad * grad
        nfirst_ref[here] = first
        nsecond_ref[here] = second
        fix_first = 1.0 - BETA_FIRST**ADAM_STEP
        fix_second = 1.0 - BETA_SECOND**ADAM_STEP
        step = first / fix_first / (jnp.sqrt(second / fix_second) + ADAM_EPS)
        nw_ref[here] = weights - ADAM_RATE * (step + WEIGHT_DECAY * weights)

    block = 32

    @pl.loop(0, count // block)
    def _(n):
        update(pl.multiple_of(block * n, block), block)

    if count % block:
        update(count - count % block, count % block)


def adam(rows, weights, first_moment, second_moment):
    length = weights.shape[0]
    count = length // LANES
    summed = ungroup(rows)
    reach = -(-32 * (summed.shape[0] - count) // 8) * 8
    before = lax.ppermute(summed[summed.shape[0] - reach :], AXES, [(n, n + 1) for n in range(31)])
    vmem = pl.BlockSpec(memory_space=pltpu.VMEM)
    gap = (QKV_GAP + END_GAP) // LANES
    results = pl.pallas_call(
        adam_kernel,
        in_specs=[vmem] * 5,
        out_specs=[vmem] * 3,
        out_shape=[jax.ShapeDtypeStruct((count, LANES), jnp.float32)] * 3,
        scratch_shapes=[pltpu.VMEM((-(-(reach + summed.shape[0] + gap) // 8) * 8, LANES), jnp.float32)],
        compiler_params=pltpu.CompilerParams(vmem_limit_bytes=32 * 1024 * 1024),
        name="adam",
    )(before, summed, *(a.reshape(count, LANES) for a in (weights, first_moment, second_moment)))
    return [result.reshape(length) for result in results]


def two_parts(value):
    coarse = value.astype(jnp.bfloat16)
    return coarse, (value - coarse.astype(jnp.float32)).astype(jnp.bfloat16)


def shampoo_kernel(tiles_ref, blocks_ref, sl_ref, sr_ref, rl_ref, rr_ref, nb_ref, g_ref, nl_ref, nr_ref, rms_ref):
    for n in range(8):
        grad = tiles_ref[:, n * BLOCK : (n + 1) * BLOCK]
        wide = grad.astype(jnp.float32)
        g_ref[n] = wide
        nl_ref[n] = STAT_DECAY * sl_ref[n] + (1.0 - STAT_DECAY) * nt_dot(grad, grad)
        square = lax.dot_general(grad, grad, (((0,), (0,)), ((), ())), preferred_element_type=jnp.float32)
        nr_ref[n] = STAT_DECAY * sr_ref[n] + (1.0 - STAT_DECAY) * square
        coarse, fine = two_parts(rr_ref[n])
        half = product(grad, jnp.concatenate([coarse, fine], 1))
        half_coarse, half_fine = two_parts(half[:, :BLOCK] + half[:, BLOCK:])
        coarse, fine = two_parts(rl_ref[n])
        cond = product(jnp.concatenate([coarse, fine], 1), jnp.concatenate([half_coarse, half_coarse], 0))
        cond = cond + product(coarse, half_fine)
        rms = jnp.sqrt(jnp.mean(cond * cond, axis=(0, 1), keepdims=True) + RMS_EPS)
        nb_ref[n] = blocks_ref[n] - SHAMPOO_RATE * cond / rms
        rms_ref[n : n + 1] = jnp.broadcast_to(rms, (1, LANES))


def shampoo(chunks, blocks, stat_left, stat_right, root_left, root_right):
    count = blocks.shape[0]
    eight = pl.BlockSpec((8, BLOCK, BLOCK), lambda n: (n, 0, 0))
    whole = jax.ShapeDtypeStruct(blocks.shape, jnp.float32)
    *results, rms = pl.pallas_call(
        shampoo_kernel,
        grid=(count // 8,),
        in_specs=[pl.BlockSpec((BLOCK, WIDE), lambda n: (n, 0))] + [eight] * 5,
        out_specs=[eight] * 4 + [pl.BlockSpec((8, LANES), lambda n: (n, 0))],
        out_shape=[whole] * 4 + [jax.ShapeDtypeStruct((count, LANES), jnp.float32)],
        compiler_params=pltpu.CompilerParams(vmem_limit_bytes=60 * 1024 * 1024),
        name="shampoo",
    )(chunks, blocks, stat_left, stat_right, root_left, root_right)
    return *results, rms[:, 0]


def chunks_of(tiles):
    return tiles.reshape(-1, 8, BLOCK, BLOCK).transpose(0, 2, 1, 3).reshape(-1, WIDE)


def tiles_of(chunks):
    return chunks.reshape(-1, BLOCK, 8, BLOCK).transpose(0, 2, 1, 3).reshape(-1, BLOCK, BLOCK)


def panels_of(chunks):
    half = chunks.shape[0] // 2
    first = chunks[:half].reshape(D // BLOCK, HID // WIDE, BLOCK, WIDE).transpose(1, 0, 2, 3)
    return jnp.concatenate([first.reshape(half, WIDE), chunks[half:]])


def chunks_of_panels(panels):
    half = panels.shape[0] // 2
    first = panels[:half].reshape(HID // WIDE, D // BLOCK, BLOCK, WIDE).transpose(1, 0, 2, 3)
    return jnp.concatenate([first.reshape(half, WIDE), panels[half:]])


META = (1, 8, lambda p, c, j: (2 * p + c) * 8)
SWAP = ((0, 1), (1, 0))
AXES = ("dp", "strip")


def pairs_to(target):
    return [(2 * p + c, sum(v * w for v, w in zip(target(p, c), (2, 1)))) for p in range(16) for c in range(2)]


NEAR = pairs_to(lambda p, c: (p ^ (1 + c), c))
FAR = pairs_to(lambda p, c: (p ^ (2 - c), c))
CORE = pairs_to(lambda p, c: (p, 1 - c))


def gather_weights(weights, blocks, part):
    if direct_links():
        own, tiles = prepare(weights, blocks)
        rows, parts, line = gather_all([flat_chunks(own.shape[0], 3), META], 4, [own, part], tiles, 0)
        near = lax.ppermute(line, AXES, NEAR)
        return rows, [line, near], jnp.sum(parts[::8, 0])
    flat = lax.all_gather(weights.astype(jnp.bfloat16), AXES, axis=0, tiled=True)
    tiles = lax.all_gather(blocks.astype(jnp.bfloat16), "dp", axis=0, tiled=True)
    gaps = [jnp.zeros((QKV_GAP,), flat.dtype), jnp.zeros((END_GAP,), flat.dtype)]
    rows = jnp.concatenate([flat[:QKV_AT], gaps[0], flat[QKV_AT:GAP_AT], gaps[1], flat[GAP_AT:]])
    rows = jnp.pad(rows, (0, -rows.shape[0] % (6 * TILE))).reshape(-1, WIDE)
    return regroup(rows, 0, False), [panels_of(chunks_of(tiles))], lax.psum(part[0, 0], AXES)


class Panels:
    def __init__(self, parts):
        self.parts = parts
        self.staged = len(parts) > 1

    def first(self, before):
        if not self.staged:
            return before
        line, near = self.parts
        near, before = lax.optimization_barrier((near, before))
        self.parts = [line, near, lax.ppermute(line, AXES, FAR)]
        return before

    def second(self, before):
        if not self.staged:
            return before
        line, near, far = self.parts
        far, before = lax.optimization_barrier((far, before))
        self.parts = [line, near, far, lax.ppermute(near, AXES, FAR)]
        return before

    def third(self, after, beside):
        if not self.staged:
            return self.parts, beside
        line, near, far, both = self.parts
        both, after, beside = lax.optimization_barrier((both, after, beside))
        others = [lax.ppermute(group, AXES, CORE) for group in (line, near, far, both)]
        return [line, near, far, both] + others, beside


class PanelSums:
    def __init__(self, grads):
        self.parts = grads
        self.staged = len(grads) > 1
        if self.staged:
            self.mine = grads[0]
            self.got = lax.ppermute(grads[1], AXES, CORE)

    def added(self, at, *parts):
        total = self.mine[at].astype(jnp.float32) + self.got[at].astype(jnp.float32)
        for part in parts:
            total = total + part.astype(jnp.float32)
        return total.astype(jnp.bfloat16)

    def first(self, before):
        if not self.staged:
            return before
        away, before = lax.optimization_barrier((self.added(slice(8, 16)), before))
        self.away = lax.ppermute(away, AXES, FAR)
        return before

    def second(self, before):
        if not self.staged:
            return before
        self.away, before = lax.optimization_barrier((self.away, before))
        near, before = lax.optimization_barrier((self.added(slice(4, 8), self.away[4:]), before))
        self.last = lax.ppermute(near, AXES, NEAR)
        return before

    def third(self, before):
        if not self.staged:
            return before
        self.last, before = lax.optimization_barrier((self.last, before))
        self.parts = [self.mine, self.got, self.away, self.last]
        return before


def reduce_grads(rows, panels, part):
    everyone = (1, 8, lambda p, c, j: 0)
    summed, parts, tiles = scatter_sum([flat_chunks(rows.shape[0] // 32, 3), everyone], 6, [rows, part], panels, 1)
    return summed, tiles, parts[0, 0]


def reduce_grads_plainly(rows, panels, part, length):
    flat = regroup(rows, 0, True).astype(jnp.float32).reshape(-1)
    flat = jnp.concatenate(
        [flat[:QKV_AT], flat[QKV_AT + QKV_GAP : GAP_AT + QKV_GAP], flat[GAP_AT + QKV_GAP + END_GAP :]]
    )
    devices = lax.axis_size("dp") * lax.axis_size("strip")
    flat = jnp.pad(flat, (0, max(0, devices * length - flat.shape[0])))[: devices * length]
    tiles = tiles_of(chunks_of_panels(panels[0])).astype(jnp.float32)
    flat_sum = lax.psum_scatter(flat, AXES, scatter_dimension=0, tiled=True)
    tile_sum = lax.psum_scatter(tiles, AXES, scatter_dimension=0, tiled=True)
    tile_sum = lax.all_gather(tile_sum.astype(jnp.bfloat16), "strip", axis=0, tiled=True)
    return flat_sum, chunks_of(tile_sum), lax.psum(part[0, 0], AXES)


def adam_plainly(grad, weights, first_moment, second_moment):
    new_first = BETA_FIRST * first_moment + (1.0 - BETA_FIRST) * grad
    new_second = BETA_SECOND * second_moment + (1.0 - BETA_SECOND) * grad * grad
    fix_first = 1.0 - BETA_FIRST**ADAM_STEP
    fix_second = 1.0 - BETA_SECOND**ADAM_STEP
    moved = new_first / fix_first / (jnp.sqrt(new_second / fix_second) + ADAM_EPS)
    return weights - ADAM_RATE * (moved + WEIGHT_DECAY * weights), new_first, new_second


def shards(
    weights,
    blocks,
    stat_left,
    stat_right,
    root_left,
    root_right,
    first_moment,
    second_moment,
    image,
    camera,
    samples,
    ray_pixel,
    target,
    valid,
):
    strips = lax.axis_size("strip")
    place = lax.axis_index("strip")
    mask, wanted, own_count = pick(ray_pixel, valid, target[0])
    rows, panels, count = gather_weights(weights, blocks, own_count)
    tiled = rows.reshape(-1, 8, WIDE)

    def square(name):
        return rows[TILES[name] * 8 : TILES[name] * 8 + D]

    def plain(name, count):
        return rows[TILES[name] * 8 : TILES[name] * 8 + count]

    deconv = spread_deconv(tiled, TILES["deconv"])
    decode = plain("decode", 8).reshape(-1)
    decode_in = decode[: CH * DEC_HID].reshape(CH, DEC_HID)
    decode_out = decode[CH * DEC_HID : CH * DEC_HID + DEC_HID * 4].reshape(DEC_HID, 4)
    picture = image[0]
    real_keys = picture.shape[0]
    picture = jnp.pad(picture, ((0, -real_keys % 16), (0, 0)))
    mods = lax.dynamic_slice_in_dim(plain("modulate", 6 * NCAM), 6 * camera[0], 6).astype(jnp.float32)
    own_rows = PR * TC
    stream0 = jnp.concatenate(
        [
            lax.dynamic_slice_in_dim(rows, TILES["triplane"] * 8 + (strips * plane + place) * own_rows, own_rows)
            for plane in range(3)
        ]
    ).astype(jnp.float32)
    hidden1, norm_one = jax.vjp(norm_mod, stream0, mods[0], mods[1])
    hidden1 = hidden1.astype(jnp.bfloat16)
    query1 = product(hidden1, square("query_cross")).astype(jnp.bfloat16)
    (image_kv,) = project(picture, tiled, TILES["keyval_cross"], 2, 0)
    pairs = D // PAIR
    tokens = query1.shape[0]
    cross_out, total_one = attend_fwd(query1, [image_kv], real_keys, (0, pairs))
    stream1 = stream0 + product(cross_out, square("out_cross"))
    hidden2, norm_two = jax.vjp(norm_mod, stream1, mods[2], mods[3])
    hidden2 = hidden2.astype(jnp.bfloat16)
    panels = Panels(panels)
    hidden2 = panels.first(hidden2)
    query2, kv_own = project(hidden2, tiled, TILES["qkv_self"], 3, 1)
    kv_both = [kv_own, lax.ppermute(kv_own, "strip", SWAP)]
    all_keys = 2 * kv_own.shape[1]
    early = attend_fwd(query2, kv_both, all_keys, (0, pairs // 2))
    early = (panels.second(early[0]), early[1])
    self_out, total_two = attend_fwd(query2, kv_both, all_keys, (pairs // 2, pairs), early)
    panels, deconv = panels.third(self_out, deconv)
    stream2 = stream1 + product(self_out, square("out_self"))
    hidden3, norm_three = jax.vjp(norm_mod, stream2, mods[4], mods[5])
    hidden3 = hidden3.astype(jnp.bfloat16)
    up, act, grid = mlp_fwd(panels, hidden3, stream2)
    grid = grid.reshape(3, own_rows, D)
    edge = lax.ppermute(jnp.where(place == 0, grid[:, -TC:], grid[:, :TC]), "strip", SWAP)
    cells = deconv_fwd(grid, edge, deconv)
    cells_far = lax.ppermute(cells, "strip", SWAP)
    rays = ray_pixel.shape[1]
    factor = 1.0 / jnp.maximum(count, 1.0)
    loss_part, grad_cells, grad_far, grad_decode_in, grad_decode_out = render(
        cells,
        cells_far,
        (samples[0] + place * cells.shape[1]) % (2 * cells.shape[1]),
        wanted,
        mask,
        factor.reshape(1),
        decode_in,
        jnp.pad(decode_out, ((0, 0), (0, 4))),
        rays,
    )
    grad_decode_out = grad_decode_out[:, :4]
    grad_far = lax.ppermute(grad_far, "strip", SWAP)
    grad_grid, beside, grad_deconv = deconv_bwd(grad_cells, grad_far, grid, edge, deconv)
    beside = lax.ppermute(beside, "strip", SWAP).astype(jnp.float32)
    grad_grid = grad_grid.at[:, :TC].add(jnp.where(place == 0, 0.0, beside))
    grad_grid = grad_grid.at[:, -TC:].add(jnp.where(place == 0, beside, 0.0))
    grad_stream = grad_grid.reshape(-1, D)
    grad_branch = grad_stream.astype(jnp.bfloat16)
    grad_hidden3, *panel_grads = mlp_bwd(panels, hidden3, grad_branch, up, act)
    grad_norm, grad_mod4, grad_mod5 = norm_three(grad_hidden3)
    grad_stream = grad_stream + grad_norm
    grad_branch2 = grad_stream.astype(jnp.bfloat16)
    grad_self = product_back(grad_branch2, square("out_self")).astype(jnp.bfloat16)
    panel_sums = PanelSums(panel_grads)
    grad_self = panel_sums.first(grad_self)
    early = attend_bwd(query2, kv_both, all_keys, (0, pairs - 1), 512, total_two, self_out, grad_self)
    early = (panel_sums.second(early[0]), *early[1:])
    grad_query2, grad_kv_own, grad_kv_far = attend_bwd(
        query2, kv_both, all_keys, (pairs - 1, pairs), 512, total_two, self_out, grad_self, early
    )
    grad_kv_far = lax.ppermute(grad_kv_far, "strip", SWAP)
    grad_kv = (grad_kv_own.astype(jnp.float32) + grad_kv_far.astype(jnp.float32)).astype(jnp.bfloat16)
    grad_hidden2 = project_back(grad_query2, grad_kv, tiled, TILES["qkv_self"], D)
    grad_norm, grad_mod2, grad_mod3 = norm_two(grad_hidden2)
    grad_stream = grad_stream + grad_norm
    grad_branch1 = grad_stream.astype(jnp.bfloat16)
    grad_cross = product_back(grad_branch1, square("out_cross")).astype(jnp.bfloat16)
    grad_query1, grad_image_kv = attend_bwd(
        query1, [image_kv], real_keys, (0, pairs), picture.shape[0], total_one, cross_out, grad_cross
    )
    grad_query1 = panel_sums.third(grad_query1)
    grad_norm, grad_mod0, grad_mod1 = norm_one(product_back(grad_query1, square("query_cross")))
    grad_stream = grad_stream + grad_norm
    grad_mods = jnp.stack([grad_mod0, grad_mod1, grad_mod2, grad_mod3, grad_mod4, grad_mod5])
    grad_modulate = lax.dynamic_update_slice_in_dim(
        jnp.zeros((6 * NCAM, D), jnp.bfloat16), grad_mods.astype(jnp.bfloat16), 6 * camera[0], 0
    )
    grad_decode = jnp.concatenate([grad_decode_in.reshape(-1), grad_decode_out.reshape(-1)])
    grad_decode = jnp.pad(grad_decode, (0, END_GAP))
    total_tiles = tiled.shape[0]
    end = TILES["triplane"] + 3 * strips * own_rows // 8
    gap = TILES["qkv_self"] - TILES["gap"]
    arrays = [
        hidden1,
        grad_query1,
        picture,
        grad_image_kv,
        cross_out,
        grad_branch1,
        hidden2,
        grad_query2,
        grad_kv,
        self_out,
        grad_branch2,
    ]
    tall, low = (tokens, D), (picture.shape[0], DI)
    products = [
        (tall, (9, None), (10, None), TILES["out_self"], (1, 0)),
        (tall, (6, None), (7, None), TILES["qkv_self"], (3, 0)),
        (tall, (6, None), (8, 0), TILES["qkv_self"], (3, 1)),
        (tall, (6, None), (8, 1), TILES["qkv_self"], (3, 2)),
        (tall, (4, None), (5, None), TILES["out_cross"], (1, 0)),
        (low, (2, None), (3, 0), TILES["keyval_cross"], (2, 0)),
        (low, (2, None), (3, 1), TILES["keyval_cross"], (2, 1)),
        (tall, (0, None), (1, None), TILES["query_cross"], (1, 0)),
    ]
    grad_tokens = grad_stream.astype(jnp.bfloat16)
    copies = []
    for piece, first in (
        (grad_deconv, TILES["deconv"]),
        (grad_decode, TILES["decode"]),
        (grad_modulate, TILES["modulate"]),
        (grad_tokens, None),
    ):
        piece = piece.astype(jnp.bfloat16).reshape(-1, 8, WIDE)
        if first is None:
            part = own_rows // 8
            for plane in range(3):
                first = TILES["triplane"] + 2 * plane * part
                copies.append((len(arrays), plane * part, part, first, part))
                copies.append((None, 0, part, first + part, -part))
        else:
            copies.append((len(arrays), 0, piece.shape[0], first, 0))
        arrays.append(piece)
    for first, count in ((TILES["gap"], gap), (end, total_tiles - end)):
        part = own_rows // 8
        for start in range(0, count, part):
            copies.append((None, 0, min(part, count - start), first + start, 0))
    row_grads = weight_grads(arrays, products, copies, total_tiles).reshape(-1, WIDE)
    if direct_links():
        summed, chunks, loss_sum = reduce_grads(row_grads, panel_sums.parts, loss_part)
        new_weights, new_first, new_second = adam(summed, weights, first_moment, second_moment)
    else:
        summed, chunks, loss_sum = reduce_grads_plainly(row_grads, panel_sums.parts, loss_part, weights.shape[0])
        new_weights, new_first, new_second = adam_plainly(summed, weights, first_moment, second_moment)
    new_blocks, block_grads, new_left, new_right, block_rms = shampoo(
        chunks, blocks, stat_left, stat_right, root_left, root_right
    )
    loss = loss_sum * factor
    return (
        loss,
        new_weights,
        new_first,
        new_second,
        new_blocks,
        block_grads,
        new_left,
        new_right,
        block_rms,
    )


def solution(mesh):
    placed = (
        P(("dp", "strip")),
        P("dp", None, None),
        P("dp", None, None),
        P("dp", None, None),
        P("dp", None, None),
        P("dp", None, None),
        P(("dp", "strip")),
        P(("dp", "strip")),
        P("dp", None, None),
        P("dp"),
        P("dp", None, None, "strip"),
        P("dp", "strip"),
        P("dp", None, None),
        P("dp", None),
    )
    return jax.shard_map(
        shards,
        mesh=mesh,
        in_specs=placed,
        out_specs=(
            P(),
            P(("dp", "strip")),
            P(("dp", "strip")),
            P(("dp", "strip")),
            P("dp", None, None),
            P("dp", None, None),
            P("dp", None, None),
            P("dp", None, None),
            P("dp"),
        ),
        check_vma=False,
    )
```

```python
import functools
import math

import jax
import jax.numpy as jnp
from jax import lax
from jax.experimental import pallas as pl
from jax.experimental.pallas import tpu as pltpu
from jax.sharding import PartitionSpec as P

D = 1024
HEAD_DIM = 64
HID = 4096
DI = 768
CH = 80
DEC_HID = 64
BLOCK = 128
PR = 8
TC = 32
S = 16
NCAM = 32
ADAM_STEP = 10


NORM_EPS = 1e-05
ADAM_RATE = 0.015
BETA_FIRST = 0.9
BETA_SECOND = 0.95
ADAM_EPS = 1e-08
WEIGHT_DECAY = 0.1
STAT_DECAY = 0.9
SHAMPOO_RATE = 0.01
RMS_EPS = 1e-06
HIGHEST_MODE = lax.Precision.HIGHEST
WIDE = 1024


def product(left, right):
    return jnp.dot(left, right, preferred_element_type=jnp.float32)


def product_back(left, right):
    return lax.dot_general(
        left, right, (((left.ndim - 1,), (1,)), ((), ())), preferred_element_type=jnp.float32
    )


def weight_grad(left, right):
    return lax.dot_general(
        left, right, (((0,), (0,)), ((), ())), preferred_element_type=jnp.float32
    )


def norm_mod(stream, scale, shift):
    centred = stream - jnp.mean(stream, -1, keepdims=True)
    spread = jnp.mean(centred * centred, -1, keepdims=True)
    return centred * lax.rsqrt(spread + NORM_EPS) * (1.0 + scale) + shift


def gelu_tanh(value):
    return jax.nn.gelu(value, approximate=True)


PAIR = 2 * HEAD_DIM
BRIEF = pl.CostEstimate(flops=1000000, transcendentals=0, bytes_accessed=100000)
LOG2E = math.log2(math.e)
EXP_SCALE = HEAD_DIM ** (-0.5) * LOG2E


def nt_dot(left, right):
    return lax.dot_general(left, right, (((1,), (1,)), ((), ())), preferred_element_type=jnp.float32)


def head_lanes(shape, head):
    return lax.broadcasted_iota(jnp.int32, shape, len(shape) - 1) // HEAD_DIM == head


def joined(refs, n):
    parts = [ref[n] for ref in refs]
    return parts[0] if len(parts) == 1 else jnp.concatenate(parts, 0)


def attend_fwd_kernel(real_keys, sources, q_ref, *refs):
    o_ref, lse_ref = refs[-2:]
    query, keys = q_ref[...], joined(refs[:sources], 0)
    values = joined(refs[:sources], 1).T
    outs = []
    heads = [jnp.where(head_lanes(query.shape, head), query, 0) for head in range(2)]
    all_scores = [nt_dot(keys, own) for own in heads]
    for head, scores in enumerate(all_scores):
        if real_keys < keys.shape[0]:
            at = lax.broadcasted_iota(jnp.int32, scores.shape, 0)
            scores = jnp.where(at < real_keys, scores, -3e38)
        top = jnp.max(scores, 0, keepdims=True)
        raised = jnp.exp2((scores - top) * EXP_SCALE)
        total = jnp.sum(raised, 0, keepdims=True)
        shares = (raised * (1.0 / total)).astype(jnp.bfloat16)
        outs.append(product(values[head * HEAD_DIM : (head + 1) * HEAD_DIM], shares))
        lse_ref[0, head : head + 1] = top * EXP_SCALE + jnp.log2(total)
    o_ref[...] = jnp.concatenate(outs, 0).T.astype(jnp.bfloat16)


def attend_fwd(query, sources, real_keys, span, earlier=()):
    count = query.shape[0]
    total_keys = sum(source.shape[1] for source in sources)
    low, high = span
    by_pair = pl.BlockSpec((count, PAIR), lambda j: (0, low + j))
    work = count * total_keys * (high - low) * PAIR
    return pl.pallas_call(
        functools.partial(attend_fwd_kernel, real_keys, len(sources)),
        grid=(high - low,),
        in_specs=[by_pair]
        + [pl.BlockSpec((2, source.shape[1], PAIR), lambda j: (0, 0, low + j)) for source in sources]
        + [pl.BlockSpec(memory_space=pl.ANY)] * len(earlier),
        out_specs=[by_pair, pl.BlockSpec((1, 8, count), lambda j: (low + j, 0, 0))],
        out_shape=[
            jax.ShapeDtypeStruct((count, D), jnp.bfloat16),
            jax.ShapeDtypeStruct((D // PAIR, 8, count), jnp.float32),
        ],
        input_output_aliases={1 + len(sources) + n: n for n in range(len(earlier))},
        compiler_params=pltpu.CompilerParams(vmem_limit_bytes=48 * 1024 * 1024),
        cost_estimate=BRIEF,
        name="attend_fwd",
    )(query, *sources, *earlier)


def attend_bwd_kernel(real_keys, chunk, sources, extra, q_ref, *refs):
    kv_refs = refs[:sources]
    lse_ref, o_ref, g_ref = refs[sources : sources + 3]
    dq_ref, *grad_refs = refs[sources + 3 + extra : sources + 4 + extra + sources]
    k_all, v_all, kt_ref, dk_sum, dv_sum = refs[sources + 4 + extra + sources :]
    k_all[...] = joined(kv_refs, 0)
    v_all[...] = joined(kv_refs, 1)
    kt_ref[...] = k_all[...].T
    query, grad = q_ref[...], g_ref[...]
    mixed = (grad.astype(jnp.float32) * o_ref[...].astype(jnp.float32)).T
    total_keys = k_all.shape[0]
    queries = [jnp.where(head_lanes(query.shape, head), query, 0) for head in range(2)]
    grads = [jnp.where(head_lanes(grad.shape, head), grad, 0) for head in range(2)]
    inner = [jnp.sum(mixed[head * HEAD_DIM : (head + 1) * HEAD_DIM], 0, keepdims=True) for head in range(2)]
    grad_query = [jnp.zeros((HEAD_DIM, query.shape[0]), jnp.float32) for head in range(2)]
    def opened(at):
        part = pl.ds(at, chunk)
        keys, values = k_all[part], v_all[part]
        return [(nt_dot(keys, queries[head]), nt_dot(values, grads[head])) for head in range(2)]

    ahead = opened(0)
    for at in range(0, total_keys, chunk):
        part = pl.ds(at, chunk)
        now = ahead
        if at + chunk < total_keys:
            ahead = opened(at + chunk)
        for head, (scores, grad_shares) in enumerate(now):
            shares = jnp.exp2(scores * EXP_SCALE - lse_ref[0, head : head + 1])
            if at + chunk > real_keys:
                row = at + lax.broadcasted_iota(jnp.int32, shares.shape, 0)
                shares = jnp.where(row < real_keys, shares, 0.0)
            grad_scores = (shares * (grad_shares - inner[head])).astype(jnp.bfloat16)
            to_values = product(shares.astype(jnp.bfloat16), grads[head])
            to_keys = product(grad_scores, queries[head])
            if head == 0:
                dv_sum[part] = to_values
                dk_sum[part] = to_keys
            else:
                dv_sum[part] += to_values
                dk_sum[part] += to_keys
            grad_query[head] += product(
                kt_ref[head * HEAD_DIM : (head + 1) * HEAD_DIM, part], grad_scores
            )
    scale = HEAD_DIM ** (-0.5)
    dq_ref[...] = (jnp.concatenate(grad_query, 0) * scale).T.astype(jnp.bfloat16)
    start = 0
    for ref in grad_refs:
        part = pl.ds(start, ref.shape[1])
        ref[0] = (dk_sum[part] * scale).astype(jnp.bfloat16)
        ref[1] = dv_sum[part].astype(jnp.bfloat16)
        start += ref.shape[1]


def attend_bwd(query, sources, real_keys, span, chunk, totals, out, grad, earlier=()):
    count = query.shape[0]
    total_keys = sum(source.shape[1] for source in sources)
    low, high = span
    by_pair = pl.BlockSpec((count, PAIR), lambda j: (0, low + j))
    by_source = [pl.BlockSpec((2, source.shape[1], PAIR), lambda j: (0, 0, low + j)) for source in sources]
    first = 1 + len(sources) + 3
    work = count * total_keys * (high - low) * PAIR
    return pl.pallas_call(
        functools.partial(attend_bwd_kernel, real_keys, chunk, len(sources), len(earlier)),
        grid=(high - low,),
        in_specs=[by_pair]
        + by_source
        + [pl.BlockSpec((1, 8, count), lambda j: (low + j, 0, 0)), by_pair, by_pair]
        + [pl.BlockSpec(memory_space=pl.ANY)] * len(earlier),
        out_specs=[by_pair] + by_source,
        out_shape=[jax.ShapeDtypeStruct((count, D), jnp.bfloat16)]
        + [jax.ShapeDtypeStruct(source.shape, jnp.bfloat16) for source in sources],
        input_output_aliases={first + n: n for n in range(len(earlier))},
        scratch_shapes=[
            pltpu.VMEM((total_keys, PAIR), jnp.bfloat16),
            pltpu.VMEM((total_keys, PAIR), jnp.bfloat16),
            pltpu.VMEM((PAIR, total_keys), jnp.bfloat16),
            pltpu.VMEM((total_keys, PAIR), jnp.float32),
            pltpu.VMEM((total_keys, PAIR), jnp.float32),
        ],
        compiler_params=pltpu.CompilerParams(vmem_limit_bytes=48 * 1024 * 1024),
        cost_estimate=BRIEF,
        name="attend_bwd",
    )(query, *sources, totals, out, grad, *earlier)


GROUPS = 3


def render_kernel(samples_ref, near_ref, far_ref, wanted_ref, mask_ref, factor_ref, win_ref, wout_ref,
                  loss_ref, grad_ref, grad_far_ref, gin_ref, gout_ref,
                  table, inner_all, hidden_all, point_all, out_all, gout_all, sums):
    block = pl.program_id(0)
    half = near_ref.shape[1]
    cells = 2 * half
    group = table.shape[2]
    rays = samples_ref.shape[2]
    planes = near_ref.shape[0]

    @pl.when(block == 0)
    def _():
        loss_ref[...] = jnp.zeros_like(loss_ref)
        gin_ref[...] = jnp.zeros_like(gin_ref)
        gout_ref[...] = jnp.zeros_like(gout_ref)
        sums[...] = jnp.zeros_like(sums)
        table[...] = jnp.zeros_like(table)
        for plane in range(planes):
            turned = jnp.concatenate([near_ref[plane], far_ref[plane]], 0).T
            for g in range(GROUPS):
                width = min(group, cells - g * group)
                table[plane, g * CH : (g + 1) * CH, :width] = turned[:CH, g * group : g * group + width]

    step = 4
    width = step * rays
    win, wout = win_ref[...], wout_ref[...]

    def places_read(plane, s):
        rows = [samples_ref[plane, s + n : s + n + 1, :] for n in range(step)]
        at = jnp.concatenate(rows, 1)
        owner = at // group
        within = at - owner * group
        hot = lax.broadcasted_iota(jnp.int32, (group, width), 0) == within
        return owner, jnp.where(hot, 1.0, 0.0).astype(jnp.bfloat16)

    def tn_dot(left, right):
        return lax.dot_general(left, right, (((0,), (0,)), ((), ())), preferred_element_type=jnp.float32)

    for s in range(0, S, step):
        here = pl.ds(s * rays, width)
        point = jnp.zeros((CH, width), jnp.float32)
        for plane in range(planes):
            owner, hot = places_read(plane, s)
            found = product(table[plane], hot)
            value = found[:CH]
            for g in range(1, GROUPS):
                value = jnp.where(owner == g, found[g * CH : (g + 1) * CH], value)
            point = point + value
        point = point.astype(jnp.bfloat16)
        inner = tn_dot(win, point)
        hidden = (inner * jax.nn.sigmoid(inner)).astype(jnp.bfloat16)
        out_all[:, here] = tn_dot(wout, hidden)
        inner_all[:, here] = inner
        hidden_all[:, here] = hidden
        point_all[:, here] = point

    factor = factor_ref[0]
    mask = mask_ref[...]
    row = lax.broadcasted_iota(jnp.int32, (8, rays), 0)
    is_colour = (row >= 1) & (row <= 3)
    before = jnp.zeros((1, rays), jnp.float32)
    rgb = jnp.zeros((8, rays), jnp.float32)
    kept = []
    for s in range(S):
        out = out_all[:, s * rays : (s + 1) * rays]
        level = out[0:1]
        absorb = (4.0 / S) * (jnp.maximum(level, 0.0) + jnp.log1p(jnp.exp(-jnp.abs(level))))
        weight = jnp.exp(-before) * (1.0 - jnp.exp(-absorb))
        before = before + absorb
        colour = jax.nn.sigmoid(out)
        rgb = rgb + weight * colour
        kept.append((weight, jnp.exp(-before), colour))
    error = jnp.where(is_colour, rgb - wanted_ref[...], 0.0)
    loss_ref[...] += jnp.sum(mask * jnp.sum(error * error, 0, keepdims=True))
    pull = error * (2.0 * factor * mask)
    tail = jnp.zeros((1, rays), jnp.float32)
    for s in reversed(range(S)):
        weight, left_over, colour = kept[s]
        to_weight = jnp.sum(pull * colour, 0, keepdims=True)
        to_absorb = to_weight * left_over - tail
        tail = tail + to_weight * weight
        to_level = (4.0 / S) * to_absorb * colour[0:1]
        to_colour = weight * pull * colour * (1.0 - colour)
        gout_all[:, s * rays : (s + 1) * rays] = jnp.where(row == 0, to_level, to_colour).astype(jnp.bfloat16)

    for s in range(0, S, step):
        here = pl.ds(s * rays, width)
        pulled = gout_all[:, here]
        inner = inner_all[:, here]
        gate = jax.nn.sigmoid(inner)
        grad_inner = product(wout, pulled) * (gate * (1.0 + inner * (1.0 - gate)))
        grad_inner = grad_inner.astype(jnp.bfloat16)
        gout_ref[...] += nt_dot(hidden_all[:, here], pulled)
        gin_ref[...] += nt_dot(point_all[:, here], grad_inner)
        grad_point = product(win, grad_inner)
        coarse = grad_point.astype(jnp.bfloat16).astype(jnp.float32)
        fine = grad_point - coarse
        for plane in range(planes):
            owner, hot = places_read(plane, s)
            rows = [jnp.where(owner == g, coarse, 0.0) for g in range(GROUPS)]
            rows += [jnp.where(owner == g, fine, 0.0) for g in range(GROUPS)]
            stacked = jnp.concatenate(rows, 0).astype(jnp.bfloat16)
            added = nt_dot(stacked, hot)
            sums[plane] += added[: GROUPS * CH] + added[GROUPS * CH :]

    @pl.when(block == pl.num_programs(0) - 1)
    def _():
        for plane in range(planes):
            for g in range(GROUPS):
                for low, high, ref in ((0, half, grad_ref), (half, cells, grad_far_ref)):
                    start, stop = max(g * group, low), min((g + 1) * group, high)
                    if start < stop:
                        part = sums[plane, g * CH : (g + 1) * CH, start - g * group : stop - g * group]
                        ref[plane, :, start - low : stop - low] = part.astype(jnp.bfloat16)


def render(near, far, samples, wanted, mask, factor, decode_in, decode_out, rays):
    planes, half, _ = near.shape
    count = 2 * half
    all_rays = samples.shape[2]
    group = -(-count // (GROUPS * 128)) * 128
    points = S * rays
    whole = lambda *shape: pl.BlockSpec(shape, lambda n: (0,) * len(shape))
    return pl.pallas_call(
        render_kernel,
        grid=(all_rays // rays,),
        in_specs=[
            pl.BlockSpec((planes, S, rays), lambda n: (0, 0, n)),
            whole(*near.shape),
            whole(*far.shape),
            pl.BlockSpec((8, rays), lambda n: (0, n)),
            pl.BlockSpec((1, rays), lambda n: (0, n)),
            pl.BlockSpec(memory_space=pltpu.SMEM),
            whole(CH, DEC_HID),
            whole(DEC_HID, 8),
        ],
        out_specs=[whole(8, 128), whole(planes, CH, half), whole(planes, CH, half), whole(CH, DEC_HID), whole(DEC_HID, 8)],
        out_shape=[
            jax.ShapeDtypeStruct((8, 128), jnp.float32),
            jax.ShapeDtypeStruct((planes, CH, half), jnp.bfloat16),
            jax.ShapeDtypeStruct((planes, CH, half), jnp.bfloat16),
            jax.ShapeDtypeStruct((CH, DEC_HID), jnp.float32),
            jax.ShapeDtypeStruct((DEC_HID, 8), jnp.float32),
        ],
        scratch_shapes=[
            pltpu.VMEM((planes, GROUPS * CH, group), jnp.bfloat16),
            pltpu.VMEM((DEC_HID, points), jnp.float32),
            pltpu.VMEM((DEC_HID, points), jnp.bfloat16),
            pltpu.VMEM((CH, points), jnp.bfloat16),
            pltpu.VMEM((8, points), jnp.float32),
            pltpu.VMEM((8, points), jnp.bfloat16),
            pltpu.VMEM((planes, GROUPS * CH, group), jnp.float32),
        ],
        compiler_params=pltpu.CompilerParams(vmem_limit_bytes=48 * 1024 * 1024),
        name="render",
    )(samples, near, far, wanted, mask, factor, decode_in, decode_out)


def pick_kernel(pixel_ref, valid_ref, target_ref, mask_ref, wanted_ref, count_ref):
    pixels = valid_ref.shape[1]
    rays = pixel_ref.shape[1]
    hot = lax.broadcasted_iota(jnp.int32, (pixels, rays), 0) == pixel_ref[...]
    hot = jnp.where(hot, 1.0, 0.0).astype(jnp.bfloat16)
    rest = target_ref[...]
    rows = [valid_ref[...].astype(jnp.float32)]
    for _ in range(3):
        part = rest.astype(jnp.bfloat16).astype(jnp.float32)
        rows.append(part)
        rest = rest - part
    rows.append(jnp.zeros((6, pixels), jnp.float32))
    found = product(jnp.concatenate(rows, 0).astype(jnp.bfloat16), hot)
    mask = found[:1]
    mask_ref[...] = mask
    wanted_ref[...] = jnp.zeros_like(wanted_ref)
    wanted_ref[1:4] = found[1:4] + found[4:7] + found[7:10]
    count_ref[...] = jnp.broadcast_to(jnp.sum(mask, 1, keepdims=True), count_ref.shape)


def pick(pixel, valid, target):
    rays = pixel.shape[1]
    vmem = pl.BlockSpec(memory_space=pltpu.VMEM)
    return pl.pallas_call(
        pick_kernel,
        in_specs=[vmem] * 3,
        out_specs=[vmem] * 3,
        out_shape=[
            jax.ShapeDtypeStruct((1, rays), jnp.float32),
            jax.ShapeDtypeStruct((8, rays), jnp.float32),
            jax.ShapeDtypeStruct((8, 128), jnp.float32),
        ],
        compiler_params=pltpu.CompilerParams(vmem_limit_bytes=24 * 1024 * 1024),
        name="pick",
    )(pixel, valid, target)


MESH_ID = pl.DeviceIdType.MESH


def places():
    p = lax.axis_index("dp")
    c = lax.axis_index("strip")
    z = p // 4
    flip_x = p + 1 - 2 * (p % 2)
    flip_y = p + 2 - 4 * ((p // 2) % 2)
    both = flip_x + flip_y - p
    near = (1 - c) * flip_x + c * flip_y
    far = (1 - c) * flip_y + c * flip_x
    return p, c, z, near, far, both


def along_z(line, z, k):
    return ((z + k) % 4) * 4 + line % 4


def enter(peers):
    barrier = pltpu.get_barrier_semaphore()
    for peer in peers:
        pl.semaphore_signal(barrier, inc=1, device_id=peer, device_id_type=MESH_ID)
    pl.semaphore_wait(barrier, len(peers))


def flat_chunks(rows, n):
    part = rows // n
    return n, part, lambda p, c, j: (2 * p + c) * rows + j * part


def block_chunk(p, c, k):
    second = p // 8
    return ((1 - second) * ((2 * c + k) * 8 + p) + second * (4 * p + 2 * c + k)) * BLOCK


ORDER = [("near", 0), ("z", 1), ("far", 0), ("z", 2), ("z", 3), ("near", 1), ("near", 2), ("near", 3)]
ORDER += [("both", 0), ("far", 1), ("far", 2), ("far", 3), ("both", 1), ("both", 2), ("both", 3)]
ORDER += [("core", i) for i in range(16)]


def gather_kernel(layouts, stagger, *refs):
    count = len(layouts)
    fulls = refs[count + 1 : 2 * count + 1]
    line_full = refs[2 * count + 1]
    send, recv, local, z_send, line_recv, line_send = refs[2 * count + 2 : 2 * count + 8]
    held = refs[2 * count + 8 :]
    brought = [pltpu.make_async_copy(s, h, local.at[n]) for n, (s, h) in enumerate(zip(refs[: count + 1], held))]
    for copy in brought:
        copy.start()
    sources, line_source = held[:count], held[count]
    p, c, z, near, far, both = places()
    zs = [along_z(p, z, k) for k in range(4)]
    enter([(q, c) for q in zs[1:]] + [(near, c), (far, c), (p, 1 - c)])
    for copy in brought:
        copy.wait()
    jobs = [(a, j) for a, layout in enumerate(layouts) for j in range(layout[0])]
    me = (p, c)
    up, down = (p + 4, c), (p - 4, c)

    def target(owner, job):
        a, j = jobs[job]
        _, rows, place = layouts[a]
        return fulls[a].at[pl.ds(pl.multiple_of(place(*owner, j), 8), rows)]

    def source(owner, job):
        if owner is not me:
            return target(owner, job)
        a, j = jobs[job]
        rows = layouts[a][1]
        return sources[a].at[pl.ds(j * rows, rows)]

    def sending(owner, event, peer, job, sem=None):
        return pltpu.make_async_remote_copy(
            source(owner, job), target(owner, job), send.at[event, job] if sem is None else sem, recv.at[event, job],
            device_id=peer, device_id_type=MESH_ID,
        )

    def arrive(owner, event, job):
        t = target(owner, job)
        pltpu.make_async_remote_copy(
            t, t, send.at[event, job], recv.at[event, job], device_id=(p, 1 - c), device_id_type=MESH_ID
        ).wait_recv()

    def sending_up(distance, job):
        owner = me if distance == 1 else (zs[5 - distance], c)
        return sending(owner, 3 - distance, up, job, z_send.at[0, distance - 1, job])

    def sending_down(distance, job):
        owner = me if distance == 1 else (zs[distance - 1], c)
        return sending(owner, distance - 1, down, job, z_send.at[1, distance - 1, job])

    def line_up(distance):
        held_at = line_source if distance == 1 else line_full.at[5 - distance]
        return pltpu.make_async_remote_copy(
            held_at, line_full.at[4 - distance], line_send.at[0, distance - 1], line_recv.at[4 - distance],
            device_id=up, device_id_type=MESH_ID,
        )

    def line_down(distance):
        held_at = line_source if distance == 1 else line_full.at[distance - 1]
        return pltpu.make_async_remote_copy(
            held_at, line_full.at[distance], line_send.at[1, distance - 1], line_recv.at[distance],
            device_id=down, device_id_type=MESH_ID,
        )

    def each_way(distance, work):
        @pl.when(z + distance <= 3)
        def _():
            work(distance, True)

        @pl.when(z >= distance)
        def _():
            work(4 - distance, False)

    def pass_on(ups, downs, distance, *job):
        if distance > 3:
            return

        @pl.when((z < 3) & (z >= distance - 1))
        def _():
            ups(distance, *job)

        @pl.when((z > 0) & (z + distance - 1 <= 3))
        def _():
            downs(distance, *job)

    def begin(job):
        sending(me, 3, (near, c), job).start()

        @pl.when(z < 3)
        def _():
            sending_up(1, job).start()

        @pl.when(z > 0)
        def _():
            sending_down(1, job).start()

        sending(me, 7, (far, c), job).start()
        sending(me, 15, (p, 1 - c), job).start()
        pltpu.make_async_copy(source(me, job), target(me, job), local.at[job]).start()

    def take_z(k, above, job):
        owner = (zs[k], c)
        arrive(owner, k - 1, job)
        distance = k if above else 4 - k
        if distance < 3:

            @pl.when(z > 0 if above else z < 3)
            def _():
                (sending_down if above else sending_up)(distance + 1, job).start()

        sending(owner, 3 + k, (near, c), job).start()
        sending(owner, 7 + k, (far, c), job).start()
        sending(owner, 15 + k, (p, 1 - c), job).start()

    def take(kind, k, job):
        if kind == "near":
            owner = (along_z(near, z, k), c)
            arrive(owner, 3 + k, job)
            sending(owner, 11 + k, (far, c), job).start()
            sending(owner, 19 + k, (p, 1 - c), job).start()
        elif kind == "far":
            owner = (along_z(far, z, k), c)
            arrive(owner, 7 + k, job)
            sending(owner, 23 + k, (p, 1 - c), job).start()
        elif kind == "both":
            owner = (along_z(both, z, k), c)
            arrive(owner, 11 + k, job)
            sending(owner, 27 + k, (p, 1 - c), job).start()
        elif kind == "core":
            line = (p, far, near, both)[k // 4]
            arrive((along_z(line, z, k % 4), 1 - c), 15 + k, job)

    def line_arrive(k):
        spot = line_full.at[k]
        pltpu.make_async_remote_copy(
            spot, spot, line_send.at[0, 0], line_recv.at[k], device_id=(p, 1 - c), device_id_type=MESH_ID
        ).wait_recv()

    def line_take(k, above):
        line_arrive(k)
        distance = k if above else 4 - k
        if distance < 3:

            @pl.when(z > 0 if above else z < 3)
            def _():
                (line_down if above else line_up)(distance + 1).start()

    steps = [(2 * stagger + 2 + 3 * n, -2, n) for n in range(4)]
    for job in range(len(jobs)):
        begin_at = stagger * min(job, layouts[0][0] - 1)
        for i in range(-1, len(ORDER)):
            steps.append((begin_at + i + 1, i, job))
    own_line = pltpu.make_async_copy(line_source, line_full.at[0], line_recv.at[0])
    for _, i, job in sorted(steps):
        if i == -2:
            if job == 0:

                @pl.when(z < 3)
                def _():
                    line_up(1).start()

                @pl.when(z > 0)
                def _():
                    line_down(1).start()

                own_line.start()
            else:
                each_way(job, line_take)
        elif i < 0:
            begin(job)
        else:
            kind, k = ORDER[i]
            if kind == "z":
                each_way(k, lambda n, above: take_z(n, above, job))
            elif kind == "core" or k == 0:
                take(kind, k, job)
            else:
                each_way(k, lambda n, above: take(kind, n, job))
    own_line.wait()
    for distance in (1, 2, 3):
        pass_on(lambda d: line_up(d).wait_send(), lambda d: line_down(d).wait_send(), distance)
    for job in range(len(jobs)):
        for distance in (1, 2, 3):
            pass_on(lambda d, n: sending_up(d, n).wait_send(), lambda d, n: sending_down(d, n).wait_send(), distance, job)
        for k in range(4):
            owner = (zs[k], c) if k else me
            sending(owner, 3 + k, (near, c), job).wait_send()
            sending(owner, 7 + k, (far, c), job).wait_send()
            sending((along_z(near, z, k), c), 11 + k, (far, c), job).wait_send()
            sending(owner, 15 + k, (p, 1 - c), job).wait_send()
            for line, first in ((near, 19), (far, 23), (both, 27)):
                sending((along_z(line, z, k), c), first + k, (p, 1 - c), job).wait_send()
        pltpu.make_async_copy(source(me, job), target(me, job), local.at[job]).wait()


def gather_all(layouts, stagger, shards_in, line, name_id):
    copies = sum(l[0] for l in layouts)
    everywhere = pl.BlockSpec(memory_space=pl.ANY)
    shapes = [jax.ShapeDtypeStruct((32 * s.shape[0],) + s.shape[1:], s.dtype) for s in shards_in]
    shapes.append(jax.ShapeDtypeStruct((4,) + line.shape, line.dtype))
    return pl.pallas_call(
        functools.partial(gather_kernel, layouts, stagger),
        out_shape=shapes,
        in_specs=[everywhere] * len(shapes),
        out_specs=[everywhere] * len(shapes),
        scratch_shapes=[
            pltpu.SemaphoreType.DMA((31, copies)),
            pltpu.SemaphoreType.DMA((31, copies)),
            pltpu.SemaphoreType.DMA((copies,)),
            pltpu.SemaphoreType.DMA((2, 3, copies)),
            pltpu.SemaphoreType.DMA((4,)),
            pltpu.SemaphoreType.DMA((2, 3)),
        ]
        + [pltpu.VMEM(a.shape, a.dtype) for a in (*shards_in, line)],
        compiler_params=pltpu.CompilerParams(collective_id=name_id, has_side_effects=True),
        name="gather_all",
    )(*shards_in, line)


SUM_ORDER = [(3, 0), (3, 1), (3, 3), (3, 2), (2, 0), (2, 1), (2, 3), (2, 2)]
SUM_ORDER += [(1, 1), (1, 3), (1, 2), (1, 0), (0, 1), (0, 3), (0, 2), (0, 0)]
AHEAD = 3


def scatter_kernel(layouts, stagger, *refs):
    count = len(layouts)
    grads = refs[:count]
    line_grads = refs[count : count + 4]
    outs = refs[count + 4 : 2 * count + 4]
    line_out = refs[2 * count + 4]
    scratch = refs[2 * count + 5 :]
    line_parts, line_sums, line_got, line_sum, line_sems, line_load_sems = scratch[-6:]
    p, c, z, near, far, both = places()
    zs = [along_z(p, z, k) for k in range(4)]
    enter([(q, c) for q in zs[1:]] + [(near, c), (far, c), (p, 1 - c)])
    csend, crecv, bsend, brecv, load_sem, out_sem = scratch[:6]
    buffers = [scratch[6 + 6 * a : 12 + 6 * a] for a in range(count)]
    jobs = [(a, j) for a, layout in enumerate(layouts) for j in range(layout[0])]
    lines = (p, near, far, both)
    partner_lines = (p, far, near, both)

    def view(job, ref, slot):
        a, j = jobs[job]
        rows = layouts[a][1]
        return ref.at[slot, pl.ds(j * rows, rows)]

    def piece(owner, job):
        a, j = jobs[job]
        _, rows, place = layouts[a]
        at = place(*owner, j)
        return grads[a].at[pl.ds(at if isinstance(at, int) else pl.multiple_of(at, 8), rows)]

    def to_core(i, job):
        g, k = SUM_ORDER[i]
        owner = (along_z(partner_lines[g], z, k), 1 - c)
        rc = buffers[jobs[job][0]][0]
        return pltpu.make_async_remote_copy(
            piece(owner, job), view(job, rc, g * 4 + k), csend.at[i, job], crecv.at[i, job],
            device_id=(p, 1 - c), device_id_type=MESH_ID,
        )

    def load(i, job):
        g, k = SUM_ORDER[i]
        own = buffers[jobs[job][0]][4]
        return pltpu.make_async_copy(
            piece((along_z(lines[g], z, k), c), job), view(job, own, i % AHEAD), load_sem.at[i, job]
        )

    def onward(i, job):
        g, k = SUM_ORDER[i]
        rc, rb, ra, rz = buffers[jobs[job][0]][:4]
        if g == 3:
            target, event, peer = view(job, rb, 4 + k), 4 + k, (far, c)
        elif g == 2:
            target, event, peer = view(job, rb, k), k, (far, c)
        elif g == 1:
            target, event, peer = view(job, ra, k), 8 + k, (near, c)
        else:
            target, event, peer = view(job, rz, 3 - k), 12 + 3 - k, (zs[k], c)
        return pltpu.make_async_remote_copy(
            view(job, rc, g * 4 + k), target, bsend.at[event, job], brecv.at[event, job],
            device_id=peer, device_id_type=MESH_ID,
        )

    def landed(event, job):
        rc, rb, ra, rz = buffers[jobs[job][0]][:4]
        if event < 8:
            target = view(job, rb, event)
        elif event < 12:
            target = view(job, ra, event - 8)
        else:
            target = view(job, rz, event - 12)
        pltpu.make_async_remote_copy(
            target, target, bsend.at[event, job], brecv.at[event, job], device_id=(p, 1 - c), device_id_type=MESH_ID
        ).wait_recv()
        return target

    def add_up(parts, target):
        rows = target.shape[0]
        step = math.gcd(rows, 16)

        @pl.loop(0, rows // step)
        def _(n):
            at = pl.ds(pl.multiple_of(n * step, step), step)
            total = parts[0][at].astype(jnp.float32)
            for part in parts[1:]:
                total = total + part[at].astype(jnp.float32)
            target[at] = total.astype(target.dtype)

    def start(i, job):
        to_core(i, job).start()
        load(i, job).start()

    def final_copies(job):
        a, j = jobs[job]
        rows = layouts[a][1]
        return [pltpu.make_async_copy(view(job, buffers[a][5], 0), outs[a].at[pl.ds(j * rows, rows)], out_sem.at[job, 0])]

    line_loads = [
        [pltpu.make_async_copy(ref.at[k], line_parts.at[k, n], line_load_sems.at[k, n]) for n, ref in enumerate(line_grads)]
        for k in range(4)
    ]
    line_sends = {
        k: pltpu.make_async_remote_copy(
            line_sums.at[k], line_got.at[3 - k], line_sems.at[k], line_sems.at[7 - k],
            device_id=(zs[k], c), device_id_type=MESH_ID,
        )
        for k in (1, 3, 2)
    }

    def line_step(k):
        for load_part in line_loads[k]:
            load_part.wait()
        add_up([line_parts.at[k, n] for n in range(4)], line_sums.at[k])
        if k:
            line_sends[k].start()

    half = line_sum.shape[0]
    spot = line_out.at[pl.ds(pl.multiple_of(c * half, 8), half)]
    line_stores = [
        pltpu.make_async_copy(line_sum, spot, line_sems.at[7]),
        pltpu.make_async_remote_copy(
            line_sum, spot, line_sems.at[8], line_sems.at[9], device_id=(p, 1 - c), device_id_type=MESH_ID
        ),
    ]

    def line_finish():
        for k in (1, 2, 3):
            target = line_got.at[k - 1]
            pltpu.make_async_remote_copy(
                target, target, line_sems.at[k], line_sems.at[3 + k], device_id=(p, 1 - c), device_id_type=MESH_ID
            ).wait_recv()
        add_up([line_sums.at[0]] + [line_got.at[n] for n in range(3)], line_sum)
        for copy in line_stores:
            copy.start()

    def step(i, job):
        g, k = SUM_ORDER[i]
        rc, rb, ra, rz, own, done = buffers[jobs[job][0]]
        load(i, job).wait()
        to_core(i, job).wait_recv()
        here = view(job, rc, g * 4 + k)
        parts = [here, view(job, own, i % AHEAD)]
        if g == 1:
            parts.append(landed(4 + k, job))
        if g == 0:
            parts.append(landed(k, job))
            parts.append(landed(8 + k, job))
        if (g, k) == (0, 0):
            parts += [landed(12 + n, job) for n in range(3)]
            add_up(parts, view(job, done, 0))
            for copy in final_copies(job):
                copy.start()
        else:
            add_up(parts, here)
            onward(i, job).start()
        if i + AHEAD < 16:
            start(i + AHEAD, job)

    for k in (1, 3, 2, 0):
        for load_part in line_loads[k]:
            load_part.start()
    for job in range(len(jobs)):
        for n in range(AHEAD):
            start(n, job)
    steps = []
    for job in range(len(jobs)):
        begin = stagger * min(job, layouts[0][0] - 1)
        for i in range(16):
            steps.append((begin + i + 2 * (i // 4 - 1) * (i // 8), job, i))
    steps.append((max(steps)[0] - 6, 0, -1))
    for n, k in enumerate((1, 3, 2, 0)):
        steps.append((n, len(jobs), -2 - k))
    for _, job, i in sorted(steps):
        if i == -1:
            line_finish()
        elif i < 0:
            line_step(-2 - i)
        else:
            step(i, job)
    for job in range(len(jobs)):
        for i in range(16):
            to_core(i, job).wait_send()
            if i < 15:
                onward(i, job).wait_send()
        for copy in final_copies(job):
            copy.wait()
    for copy in line_sends.values():
        copy.wait_send()
    for copy in line_stores:
        copy.wait()


def scatter_sum(layouts, stagger, grads, lines, name_id):
    jobs = sum(l[0] for l in layouts)
    scratch = [
        pltpu.SemaphoreType.DMA((16, jobs)),
        pltpu.SemaphoreType.DMA((16, jobs)),
        pltpu.SemaphoreType.DMA((15, jobs)),
        pltpu.SemaphoreType.DMA((15, jobs)),
        pltpu.SemaphoreType.DMA((16, jobs)),
        pltpu.SemaphoreType.DMA((jobs, 3)),
    ]
    shapes = []
    for layout, grad in zip(layouts, grads):
        rows, width = layout[0] * layout[1], grad.shape[1]
        for slots in (16, 8, 4, 3, AHEAD):
            scratch.append(pltpu.VMEM((slots, rows, width), grad.dtype))
        scratch.append(pltpu.VMEM((1, rows, width), jnp.float32))
        shapes.append(jax.ShapeDtypeStruct((rows, width), jnp.float32))
    piece, kind = lines[-1].shape[1:], lines[-1].dtype
    scratch += [
        pltpu.VMEM((4, 4) + piece, kind),
        pltpu.VMEM((4,) + piece, kind),
        pltpu.VMEM((3,) + piece, kind),
        pltpu.VMEM(piece, kind),
        pltpu.SemaphoreType.DMA((10,)),
        pltpu.SemaphoreType.DMA((4, 4)),
    ]
    shapes.append(jax.ShapeDtypeStruct((2 * piece[0], piece[1]), kind))
    everywhere = pl.BlockSpec(memory_space=pl.ANY)
    return pl.pallas_call(
        functools.partial(scatter_kernel, layouts, stagger),
        out_shape=shapes,
        in_specs=[everywhere] * (len(grads) + len(lines)),
        out_specs=[everywhere] * len(shapes),
        scratch_shapes=scratch,
        compiler_params=pltpu.CompilerParams(
            collective_id=name_id, has_side_effects=True, vmem_limit_bytes=48 * 1024 * 1024
        ),
        name="scatter_sum",
    )(*grads, *lines)


GELU_A = math.sqrt(2.0 / math.pi)
GELU_B = 0.044715


def chunk_sources(first):
    p, c, z, _, _, _ = places()
    x, y = p % 2, (p // 2) % 2
    out = []
    for n in range(4):
        owner_z = (first + n) % 4
        k = (owner_z - z + 4) % 4
        for half in range(2):
            for other in range(2):
                core = (c + other) % 2
                for g in range(4):
                    dx = (1 - core) * (g % 2) + core * (g // 2)
                    dy = (1 - core) * (g // 2) + core * (g % 2)
                    owner = owner_z * 4 + ((y + dy) % 2) * 2 + (x + dx) % 2
                    out.append((other, g, k, half, block_chunk(owner, core, half) // BLOCK))
    return out


def panel_loads(refs, held, sems, first):
    if len(refs) == 1:
        for n in range(held.shape[0] // WIDE):
            at = pl.ds(n * WIDE, WIDE)
            pltpu.make_async_copy(refs[0].at[at], held.at[at], sems.at[n]).start()
        return
    for other, g, k, half, chunk in chunk_sources(first):
        source = refs[other * 4 + g].at[k, pl.ds(half * BLOCK, BLOCK)]
        target = held.at[pl.ds(pl.multiple_of(chunk * BLOCK, BLOCK), BLOCK)]
        pltpu.make_async_copy(source, target, sems.at[chunk // 8]).start()


def panel_ready(held, sems, n):
    at = pl.ds(pl.multiple_of(n * WIDE, WIDE), WIDE)
    pltpu.make_async_copy(held.at[at], held.at[at], sems.at[n]).wait()
    return held.at[at]


def mlp_fwd_kernel(count, *refs):
    sources = refs[:count]
    h_ref, s_ref, up_ref, act_ref, grid_ref, held, total, sems = refs[count:]
    step = pl.program_id(0)
    steps = pl.num_programs(0)

    @pl.when(step == 0)
    def _():
        panel_loads(sources, held, sems, 0)
        total[...] = s_ref[...]

    up = product(h_ref[...], panel_ready(held, sems, step)[...])
    up_ref[0] = up
    act = 0.5 * up * (1.0 + jnp.tanh(GELU_A * (up + GELU_B * up * up * up)))
    act = act.astype(jnp.bfloat16)
    act_ref[0] = act
    total[...] += product(act, panel_ready(held, sems, steps + step)[...])

    @pl.when(step == steps - 1)
    def _():
        grid_ref[...] = total[...].astype(jnp.bfloat16)


def mlp_fwd(panels, hidden, stream):
    rows = hidden.shape[0]
    steps = HID // WIDE
    whole = pl.BlockSpec((rows, WIDE), lambda n: (0, 0))
    part = pl.BlockSpec((1, rows, WIDE), lambda n: (n, 0, 0))
    return pl.pallas_call(
        functools.partial(mlp_fwd_kernel, len(panels)),
        grid=(steps,),
        in_specs=[pl.BlockSpec(memory_space=pl.ANY)] * len(panels) + [whole, whole],
        out_specs=[part, part, whole],
        out_shape=[
            jax.ShapeDtypeStruct((steps, rows, WIDE), jnp.float32),
            jax.ShapeDtypeStruct((steps, rows, WIDE), jnp.bfloat16),
            jax.ShapeDtypeStruct((rows, WIDE), jnp.bfloat16),
        ],
        scratch_shapes=[
            pltpu.VMEM((2 * HID, WIDE), jnp.bfloat16),
            pltpu.VMEM((rows, WIDE), jnp.float32),
            pltpu.SemaphoreType.DMA((2 * steps,)),
        ],
        compiler_params=pltpu.CompilerParams(vmem_limit_bytes=56 * 1024 * 1024),
        cost_estimate=BRIEF,
        name="mlp_fwd",
    )(*panels, hidden, stream)


def mlp_bwd_kernel(count, *refs):
    sources = refs[:count]
    outs = 2 if count > 1 else 1
    h_ref, g_ref, up_ref, act_ref = refs[count : count + 4]
    dh_ref = refs[count + 4]
    grads = refs[count + 5 : count + 5 + outs]
    held, staged, sems, out_sem = refs[count + 5 + outs :]
    step = pl.program_id(0)
    steps = pl.num_programs(0)

    @pl.when(step == 0)
    def _():
        panel_loads(sources, held, sems, 2)
        dh_ref[...] = jnp.zeros_like(dh_ref)

    def tn_dot(left, right):
        return lax.dot_general(left, right, (((0,), (0,)), ((), ())), preferred_element_type=jnp.float32)

    def drain(side):
        pltpu.make_async_copy(staged.at[side], staged.at[side], out_sem.at[side]).wait()

    def store(side):
        panel = side * steps + step
        source = staged.at[side]
        if count == 1:
            at = pl.ds(pl.multiple_of(panel * WIDE, WIDE), WIDE)
            pltpu.make_async_copy(source, grads[0].at[at], out_sem.at[side]).start()
            return
        p, c, z, _, _, _ = places()
        for n in range(8):
            if side == 0:
                owner, core, half = n, step // 2, step % 2
            else:
                row = step * 8 + n
                owner, core, half = 8 + row // 4, (n // 2) % 2, n % 2
            dx = (owner % 2 + p % 2) % 2
            dy = ((owner // 2) % 2 + (p // 2) % 2) % 2
            g = (1 - core) * (dx + 2 * dy) + core * (dy + 2 * dx)
            spot = g * 4 + (owner // 4 - z + 4) % 4
            at = pl.ds(pl.multiple_of(half * BLOCK, BLOCK), BLOCK)
            from_ref = source.at[pl.ds(n * BLOCK, BLOCK)]

            @pl.when((core + c) % 2 == 0)
            def _():
                pltpu.make_async_copy(from_ref, grads[0].at[spot, at], out_sem.at[side]).start()

            @pl.when((core + c) % 2 == 1)
            def _():
                pltpu.make_async_copy(from_ref, grads[1].at[spot, at], out_sem.at[side]).start()

    pulled = g_ref[...]

    @pl.when(step > 0)
    def _():
        drain(1)

    staged[1] = tn_dot(act_ref[0], pulled).astype(jnp.bfloat16)
    store(1)
    grad_act = nt_dot(pulled, panel_ready(held, sems, steps + step)[...])
    up = up_ref[0]
    square = up * up
    bend = jnp.tanh(GELU_A * up * (1.0 + GELU_B * square))
    slope = 0.5 * (1.0 + bend) + 0.5 * GELU_A * up * (1.0 - bend * bend) * (1.0 + 3.0 * GELU_B * square)
    grad_up = (grad_act * slope).astype(jnp.bfloat16)

    @pl.when(step > 0)
    def _():
        drain(0)

    staged[0] = tn_dot(h_ref[...], grad_up).astype(jnp.bfloat16)
    store(0)
    dh_ref[...] += nt_dot(grad_up, panel_ready(held, sems, step)[...])

    @pl.when(step == steps - 1)
    def _():
        drain(0)
        drain(1)


def mlp_bwd(panels, hidden, grad, up, act):
    rows = hidden.shape[0]
    steps = HID // WIDE
    whole = pl.BlockSpec((rows, WIDE), lambda n: (0, 0))
    part = pl.BlockSpec((1, rows, WIDE), lambda n: (n, 0, 0))
    if len(panels) == 1:
        shapes = [jax.ShapeDtypeStruct((2 * HID, WIDE), jnp.bfloat16)]
    else:
        shapes = [jax.ShapeDtypeStruct((16, 2 * BLOCK, WIDE), jnp.bfloat16)] * 2
    return pl.pallas_call(
        functools.partial(mlp_bwd_kernel, len(panels)),
        grid=(steps,),
        in_specs=[pl.BlockSpec(memory_space=pl.ANY)] * len(panels) + [whole, whole, part, part],
        out_specs=[whole] + [pl.BlockSpec(memory_space=pl.ANY)] * len(shapes),
        out_shape=[jax.ShapeDtypeStruct((rows, WIDE), jnp.float32)] + shapes,
        scratch_shapes=[
            pltpu.VMEM((2 * HID, WIDE), jnp.bfloat16),
            pltpu.VMEM((2, WIDE, WIDE), jnp.bfloat16),
            pltpu.SemaphoreType.DMA((2 * steps,)),
            pltpu.SemaphoreType.DMA((2,)),
        ],
        compiler_params=pltpu.CompilerParams(vmem_limit_bytes=58 * 1024 * 1024),
        cost_estimate=BRIEF,
        name="mlp_bwd",
    )(*panels, hidden, grad, up, act)


SLOT = 128
TAPS = 16


def spread_deconv_kernel(first, rows_ref, o_ref, raw, flat, turned, sem):
    load = pltpu.make_async_copy(rows_ref.at[pl.ds(first, raw.shape[0])], raw, sem)
    load.start()
    load.wait()
    whole = raw[...].reshape(TAPS * CH, WIDE).astype(jnp.float32)
    for n in range(WIDE // SLOT):
        flat[n] = whole[:, n * SLOT : (n + 1) * SLOT]
    lane = lax.broadcasted_iota(jnp.int32, (D // 4, SLOT), 1)

    def block(i, j):
        at = 10 * i + j
        return flat[at % 8, pl.ds(at // 8, D // 4, stride=5), :]

    for tap in range(TAPS):
        j, start = divmod(tap * CH, SLOT)
        for i in range(4):
            part = block(i, j)
            if start:
                part = pltpu.roll(part, SLOT - start, 1)
            if start + CH > SLOT:
                part = jnp.where(lane < SLOT - start, part, pltpu.roll(block(i, j + 1), SLOT - start, 1))
            turned[pl.ds(i, D // 4, stride=4), :] = jnp.where(lane < CH, part, 0.0)
        o_ref[:, tap * SLOT : (tap + 1) * SLOT] = turned[...].astype(jnp.bfloat16)


def spread_deconv(rows, first):
    return pl.pallas_call(
        functools.partial(spread_deconv_kernel, first),
        in_specs=[pl.BlockSpec(memory_space=pl.ANY)],
        out_specs=pl.BlockSpec(memory_space=pltpu.VMEM),
        out_shape=jax.ShapeDtypeStruct((D, TAPS * SLOT), jnp.bfloat16),
        scratch_shapes=[
            pltpu.VMEM((TAPS * CH // 8, 8, WIDE), jnp.bfloat16),
            pltpu.VMEM((WIDE // SLOT, TAPS * CH, SLOT), jnp.float32),
            pltpu.VMEM((D, SLOT), jnp.float32),
            pltpu.SemaphoreType.DMA,
        ],
        compiler_params=pltpu.CompilerParams(vmem_limit_bytes=32 * 1024 * 1024),
        name="spread_deconv",
    )(rows)


def with_edges(own, edge):
    place = lax.axis_index("strip")
    above = jnp.where(place == 0, jnp.zeros_like(edge), edge)
    below = jnp.where(place == 0, edge, jnp.zeros_like(edge))
    return jnp.concatenate([above, own, below], 0)


def moved(value, step):
    column = lax.broadcasted_iota(jnp.int32, value.shape, 0) % TC
    inside = (column + step >= 0) & (column + step < TC)
    return jnp.where(inside, pltpu.roll(value, (-step) % value.shape[0], 0), 0.0)


def deconv_fwd_kernel(grid_ref, edge_ref, w_ref, o_ref, taps, fine):
    padded = with_edges(grid_ref[0], edge_ref[0])
    rows = grid_ref.shape[1]
    taps[...] = product(padded, w_ref[...])

    def tap(kr, kc, r):
        slot = kr * 4 + kc
        return taps[pl.ds((r + 1) * TC, rows), slot * SLOT : (slot + 1) * SLOT]

    for i in range(2):
        for j in range(2):
            total = tap(i + 1, j + 1, 0) + tap(3 - 3 * i, j + 1, 2 * i - 1)
            side = tap(i + 1, 3 - 3 * j, 0) + tap(3 - 3 * i, 3 - 3 * j, 2 * i - 1)
            total = total + moved(side, 2 * j - 1)
            for a in range(rows // TC):
                fine[pl.ds((2 * a + i) * 2 * TC + j, TC, stride=2), :] = total[a * TC : (a + 1) * TC]
    o_ref[0] = fine[...].astype(jnp.bfloat16)


def deconv_fwd(grid, edge, weights):
    planes, rows, _ = grid.shape
    return pl.pallas_call(
        deconv_fwd_kernel,
        grid=(planes,),
        in_specs=[
            pl.BlockSpec((1, rows, D), lambda n: (n, 0, 0)),
            pl.BlockSpec((1, TC, D), lambda n: (n, 0, 0)),
            pl.BlockSpec(weights.shape, lambda n: (0, 0)),
        ],
        out_specs=pl.BlockSpec((1, 4 * rows, SLOT), lambda n: (n, 0, 0)),
        out_shape=jax.ShapeDtypeStruct((planes, 4 * rows, SLOT), jnp.bfloat16),
        scratch_shapes=[
            pltpu.VMEM((rows + 2 * TC, TAPS * SLOT), jnp.float32),
            pltpu.VMEM((4 * rows, SLOT), jnp.float32),
        ],
        compiler_params=pltpu.CompilerParams(vmem_limit_bytes=40 * 1024 * 1024),
        name="deconv_fwd",
    )(grid, edge, weights)


def deconv_bwd_kernel(own_ref, got_ref, grid_ref, edge_ref, w_ref, gx_ref, gedge_ref, gw_ref, fine, spread, tokens, sums, flat):
    plane = pl.program_id(0)
    rows = grid_ref.shape[1]
    high = rows + 2 * TC
    place = lax.axis_index("strip")
    total = own_ref[0].astype(jnp.float32) + got_ref[0].astype(jnp.float32)
    total = jnp.concatenate([total, jnp.zeros((SLOT - CH, total.shape[1]), jnp.float32)], 0)
    fine[...] = total.T
    here = pl.ds(plane * high, high)
    tokens[here] = with_edges(grid_ref[0], edge_ref[0])
    for i in range(2):
        for j in range(2):
            parts = [fine[pl.ds((2 * a + i) * 2 * TC + j, TC, stride=2), :] for a in range(rows // TC)]
            part = jnp.concatenate(parts, 0)
            for kr in (i + 1, 3 - 3 * i):
                for kc in (j + 1, 3 - 3 * j):
                    value = part if kc == j + 1 else moved(part, 1 - 2 * j)
                    start = TC if kr == i + 1 else (0 if i == 0 else 2 * TC)
                    pieces = [value]
                    if start:
                        pieces.insert(0, jnp.zeros((start, SLOT), jnp.float32))
                    if high - rows - start:
                        pieces.append(jnp.zeros((high - rows - start, SLOT), jnp.float32))
                    slot = kr * 4 + kc
                    spread[here, slot * SLOT : (slot + 1) * SLOT] = jnp.concatenate(pieces, 0).astype(jnp.bfloat16)
    back = nt_dot(spread[here], w_ref[...])
    gx_ref[0] = back[TC : TC + rows]
    gedge_ref[0] = jnp.where(place == 0, back[TC + rows :], back[:TC]).astype(jnp.bfloat16)

    @pl.when(plane == pl.num_programs(0) - 1)
    def _():
        wide = 512
        for n in range(TAPS * SLOT // wide):
            columns = slice(n * wide, (n + 1) * wide)
            part = lax.dot_general(
                tokens[...], spread[:, columns], (((0,), (0,)), ((), ())), preferred_element_type=jnp.float32
            )
            for m in range(wide // SLOT):
                sums[n * (wide // SLOT) + m] = part[:, m * SLOT : (m + 1) * SLOT]
        lane = lax.broadcasted_iota(jnp.int32, (D // 4, SLOT), 1)
        for i in range(4):
            for j in range(TAPS * CH // SLOT):
                block = None
                for tap in range(j * SLOT // CH, (j * SLOT + SLOT - 1) // CH + 1):
                    part = sums[tap, pl.ds(i, D // 4, stride=4), :]
                    shift = tap * CH - j * SLOT
                    if shift % SLOT:
                        part = pltpu.roll(part, shift % SLOT, 1)
                    block = part if block is None else jnp.where(lane < shift, block, part)
                at = 10 * i + j
                flat[at % 8, pl.ds(at // 8, D // 4, stride=5), :] = block
        whole = jnp.concatenate([flat[n] for n in range(WIDE // SLOT)], 1)
        gw_ref[...] = whole.astype(jnp.bfloat16).reshape(gw_ref.shape)


def deconv_bwd(own, got, grid, edge, weights):
    planes, rows, _ = grid.shape
    high = rows + 2 * TC
    by_plane = lambda *shape: pl.BlockSpec((1,) + shape, lambda n: (n, 0, 0))
    return pl.pallas_call(
        deconv_bwd_kernel,
        grid=(planes,),
        in_specs=[
            by_plane(*own.shape[1:]),
            by_plane(*got.shape[1:]),
            by_plane(rows, D),
            by_plane(TC, D),
            pl.BlockSpec(weights.shape, lambda n: (0, 0)),
        ],
        out_specs=[by_plane(rows, D), by_plane(TC, D), pl.BlockSpec((TAPS * CH // 8, 8, WIDE), lambda n: (0, 0, 0))],
        out_shape=[
            jax.ShapeDtypeStruct((planes, rows, D), jnp.float32),
            jax.ShapeDtypeStruct((planes, TC, D), jnp.bfloat16),
            jax.ShapeDtypeStruct((TAPS * CH // 8, 8, WIDE), jnp.bfloat16),
        ],
        scratch_shapes=[
            pltpu.VMEM((4 * rows, SLOT), jnp.float32),
            pltpu.VMEM((planes * high, TAPS * SLOT), jnp.bfloat16),
            pltpu.VMEM((planes * high, D), jnp.bfloat16),
            pltpu.VMEM((TAPS, D, SLOT), jnp.float32),
            pltpu.VMEM((WIDE // SLOT, TAPS * CH, SLOT), jnp.float32),
        ],
        compiler_params=pltpu.CompilerParams(vmem_limit_bytes=56 * 1024 * 1024),
        name="deconv_bwd",
    )(own, got, grid, edge, weights)


def panel_view(rows_ref, first, count, depth):
    region = rows_ref.at[pl.ds(first, depth // 8 * count)]
    return region.reshape(depth // 8, count, 8, WIDE)


def project_kernel(first, count, depth, lead, x_ref, rows_ref, *rest):
    outs, held, sems = rest[:-2], rest[-2], rest[-1]
    step = pl.program_id(0)
    panels = panel_view(rows_ref, first, count, depth)

    @pl.when(step == 0)
    def _():
        for n in range(count):
            pltpu.make_async_copy(panels.at[:, n], held.at[n], sems.at[n]).start()

    pltpu.make_async_copy(held.at[step], held.at[step], sems.at[step]).wait()
    result = product(x_ref[...], held[step].reshape(depth, WIDE)).astype(jnp.bfloat16)
    if lead:

        @pl.when(step == 0)
        def _():
            outs[0][...] = result

        @pl.when(step > 0)
        def _():
            outs[1][0] = result

    else:
        outs[0][0] = result


def project(x, rows, first, count, lead):
    tokens, depth = x.shape
    specs = [pl.BlockSpec((1, tokens, WIDE), lambda n: (jnp.maximum(n - lead, 0), 0, 0))]
    shapes = [jax.ShapeDtypeStruct((count - lead, tokens, WIDE), jnp.bfloat16)]
    if lead:
        specs.insert(0, pl.BlockSpec((tokens, WIDE), lambda n: (0, 0)))
        shapes.insert(0, jax.ShapeDtypeStruct((tokens, WIDE), jnp.bfloat16))
    return pl.pallas_call(
        functools.partial(project_kernel, first, count, depth, lead),
        grid=(count,),
        in_specs=[pl.BlockSpec((tokens, depth), lambda n: (0, 0)), pl.BlockSpec(memory_space=pl.ANY)],
        out_specs=specs,
        out_shape=shapes,
        scratch_shapes=[pltpu.VMEM((count, depth // 8, 8, WIDE), jnp.bfloat16), pltpu.SemaphoreType.DMA((count,))],
        compiler_params=pltpu.CompilerParams(vmem_limit_bytes=32 * 1024 * 1024),
        cost_estimate=BRIEF,
        name="project",
    )(x, rows)


def project_back_kernel(first, count, depth, lead_ref, own_ref, far_ref, rows_ref, o_ref, sum_ref, held, sems):
    step = pl.program_id(0)
    panels = panel_view(rows_ref, first, count, depth)

    @pl.when(step == 0)
    def _():
        for n in range(count):
            pltpu.make_async_copy(panels.at[:, n], held.at[n], sems.at[n]).start()

    pltpu.make_async_copy(held.at[step], held.at[step], sems.at[step]).wait()
    both = (own_ref[0].astype(jnp.float32) + far_ref[0].astype(jnp.float32)).astype(jnp.bfloat16)
    sum_ref[0] = both
    grad = jnp.where(step == 0, lead_ref[...], both)
    back = nt_dot(grad, held[step].reshape(depth, WIDE))

    @pl.when(step == 0)
    def _():
        o_ref[...] = back

    @pl.when(step > 0)
    def _():
        o_ref[...] += back


def project_back(lead, own, far, rows, first, depth):
    others, tokens, _ = own.shape
    count = others + 1
    panel = pl.BlockSpec((1, tokens, WIDE), lambda n: (jnp.maximum(n - 1, 0), 0, 0))
    return pl.pallas_call(
        functools.partial(project_back_kernel, first, count, depth),
        grid=(count,),
        in_specs=[
            pl.BlockSpec((tokens, WIDE), lambda n: (0, 0)),
            panel,
            panel,
            pl.BlockSpec(memory_space=pl.ANY),
        ],
        out_specs=[pl.BlockSpec((tokens, depth), lambda n: (0, 0)), panel],
        out_shape=[
            jax.ShapeDtypeStruct((tokens, depth), jnp.float32),
            jax.ShapeDtypeStruct((others, tokens, WIDE), jnp.bfloat16),
        ],
        scratch_shapes=[pltpu.VMEM((count, depth // 8, 8, WIDE), jnp.bfloat16), pltpu.SemaphoreType.DMA((count,))],
        compiler_params=pltpu.CompilerParams(vmem_limit_bytes=44 * 1024 * 1024),
        cost_estimate=BRIEF,
        name="project_back",
    )(lead, own, far, rows)


def weight_grads_kernel(products, copies, *refs):
    arrays = refs[: len(refs) - 9]
    out, left, right, staged, bounce, nothing, load_sem, store_sem, copy_sem = refs[len(refs) - 9 :]
    place = lax.axis_index("strip")
    step = pl.program_id(0)
    steps = len(products)

    def loads(n):
        side, (a, a_pick), (b, b_pick), _, _ = products[n]
        slot = n % 2
        source_a = arrays[a] if a_pick is None else arrays[a].at[a_pick]
        source_b = arrays[b] if b_pick is None else arrays[b].at[b_pick]
        rows, deep = side
        return [
            pltpu.make_async_copy(source_a, left.at[slot, pl.ds(0, rows), pl.ds(0, deep)], load_sem.at[slot, 0]),
            pltpu.make_async_copy(source_b, right.at[slot, pl.ds(0, rows)], load_sem.at[slot, 1]),
        ]

    def stores(n):
        (rows, deep), _, _, first, panels = products[n]
        slot = n % 2
        count, at = panels
        source = staged.at[slot, pl.ds(0, deep // 8)]
        target = panel_view(out, first, count, deep).at[:, at]
        return pltpu.make_async_copy(source, target, store_sem.at[slot])

    def bring(n):
        a, start, count, _, _ = copies[n]
        held = bounce.at[pl.ds(sum(c[2] for c in copies[:n] if c[0] is not None), count)]
        return pltpu.make_async_copy(arrays[a].at[pl.ds(start, count)], held, copy_sem.at[n, 0])

    def put(n):
        a, _, count, first, step = copies[n]
        if a is None:
            held = nothing.at[pl.ds(0, count)]
        else:
            held = bounce.at[pl.ds(sum(c[2] for c in copies[:n] if c[0] is not None), count)]
        return pltpu.make_async_copy(held, out.at[pl.ds(first + step * place, count)], copy_sem.at[n, 1])

    for n in range(steps):

        @pl.when(step == n)
        def _():
            if n == 0:
                for job in loads(0):
                    job.start()
                nothing[...] = jnp.zeros_like(nothing)
                for m in range(len(copies)):
                    if copies[m][0] is not None:
                        bring(m).start()
            if n == 1:
                for m in range(len(copies)):
                    if copies[m][0] is not None:
                        bring(m).wait()
                    put(m).start()
            if n + 1 < steps:
                for job in loads(n + 1):
                    job.start()
            for job in loads(n):
                job.wait()
            if n >= 2:
                stores(n - 2).wait()
            rows, deep = products[n][0]
            slot = n % 2
            total = lax.dot_general(
                left[slot, :rows, :deep], right[slot, :rows], (((0,), (0,)), ((), ())), preferred_element_type=jnp.float32
            )
            staged[slot, : deep // 8] = total.astype(jnp.bfloat16).reshape(deep // 8, 8, WIDE)
            stores(n).start()
            if n == steps - 1:
                if n > 0:
                    stores(n - 1).wait()
                stores(n).wait()
                for m in range(len(copies)):
                    put(m).wait()


def weight_grads(arrays, products, copies, tile_rows):
    rows = max(p[0][0] for p in products)
    deep = max(p[0][1] for p in products)
    everywhere = pl.BlockSpec(memory_space=pl.ANY)
    return pl.pallas_call(
        functools.partial(weight_grads_kernel, products, copies),
        grid=(len(products),),
        in_specs=[everywhere] * len(arrays),
        out_specs=everywhere,
        out_shape=jax.ShapeDtypeStruct((tile_rows, 8, WIDE), jnp.bfloat16),
        scratch_shapes=[
            pltpu.VMEM((2, rows, deep), jnp.bfloat16),
            pltpu.VMEM((2, rows, WIDE), jnp.bfloat16),
            pltpu.VMEM((2, deep // 8, 8, WIDE), jnp.bfloat16),
            pltpu.VMEM((sum(c[2] for c in copies if c[0] is not None), 8, WIDE), jnp.bfloat16),
            pltpu.VMEM((max(c[2] for c in copies if c[0] is None), 8, WIDE), jnp.bfloat16),
            pltpu.SemaphoreType.DMA((2, 2)),
            pltpu.SemaphoreType.DMA((2,)),
            pltpu.SemaphoreType.DMA((len(copies), 2)),
        ],
        compiler_params=pltpu.CompilerParams(vmem_limit_bytes=60 * 1024 * 1024),
        cost_estimate=BRIEF,
        name="weight_grads",
    )(*arrays)


TILE = 8 * WIDE
KV_AT = D * D
QKV_AT = KV_AT + DI * 2 * D + D * D
GAP_AT = QKV_AT + D * 3 * D + D * D + D * 16 * CH + CH * DEC_HID + DEC_HID * 4
QKV_GAP = -QKV_AT % (3 * TILE)
END_GAP = -GAP_AT % TILE
TILES = {}
_tile = 0
for _name, _rows in (
    ("query_cross", D),
    ("keyval_cross", 2 * DI),
    ("out_cross", D),
    ("gap", QKV_GAP // WIDE),
    ("qkv_self", 3 * D),
    ("out_self", D),
    ("deconv", 16 * CH),
    ("decode", 8),
    ("modulate", 6 * NCAM),
    ("triplane", 0),
):
    TILES[_name] = _tile
    _tile += _rows // 8


def direct_links():
    return lax.axis_size("dp") == 16 and lax.axis_size("strip") == 2


def regroup(rows, first, back):
    tile = first + lax.broadcasted_iota(jnp.int32, (rows.shape[0], 1), 0) // 8

    def turned(panels):
        shape = (-1, panels, 8, WIDE) if back else (-1, 8, panels, WIDE)
        return rows.reshape(shape).transpose(0, 2, 1, 3).reshape(rows.shape)

    in_kv = (tile >= TILES["keyval_cross"]) & (tile < TILES["out_cross"])
    in_qkv = (tile >= TILES["qkv_self"]) & (tile < TILES["out_self"])
    return jnp.where(in_kv, turned(2), jnp.where(in_qkv, turned(3), rows))


def tile_rows(length):
    return -(-length // (6 * TILE)) * 6


LANES = 128
TILE_LINES = TILE // LANES


def tile_place(tile):
    gap = QKV_GAP // LANES * jnp.where(tile >= TILES["gap"], 1, 0)
    return gap + END_GAP // LANES * jnp.where(tile >= TILES["modulate"], 1, 0)


def by_region(tile, work):
    in_kv = (tile >= TILES["keyval_cross"]) & (tile < TILES["out_cross"])
    in_qkv = (tile >= TILES["qkv_self"]) & (tile < TILES["out_self"])

    @pl.when(in_kv)
    def _():
        work(2)

    @pl.when(in_qkv)
    def _():
        work(3)

    @pl.when(jnp.logical_not(in_kv | in_qkv))
    def _():
        work(1)


def tile_lines(tile, first, panels):
    panel = lax.rem(tile, panels)
    return (tile - panel - first) * TILE_LINES + panel * 8


def prepare_kernel(own_ref, next_ref, blocks_ref, o_ref, chunks_ref, lines, tiles, sem):
    half = tiles.shape[0]
    core = lax.axis_index("strip")
    load = pltpu.make_async_copy(blocks_ref.at[pl.ds(core * half, half)], tiles, sem)
    load.start()
    place = lax.axis_index("dp") * 2 + core
    count = own_ref.shape[0]
    lines[:count] = own_ref[...]
    lines[count : count + next_ref.shape[0]] = next_ref[...]
    held = o_ref.shape[0] // 8
    first = place * held
    shift = place * (held * TILE_LINES - count)

    @pl.loop(0, held // 2)
    def _(n):
        def work(panels):
            rows = []
            for m in range(2):
                tile = first + 2 * n + m
                start = tile_lines(tile, first, panels) + shift - tile_place(tile)
                rows.append(jnp.concatenate([lines[pl.ds(start + j, 8, stride=8 * panels), :] for j in range(8)], 1))
            o_ref[pl.ds(pl.multiple_of(16 * n, 16), 16)] = jnp.concatenate(rows, 0).astype(jnp.bfloat16)

        by_region(first + 2 * n, work)

    load.wait()
    for n in range(half):
        at, column = n // 8 * BLOCK, n % 8 * BLOCK
        chunks_ref[at : at + BLOCK, column : column + BLOCK] = tiles[n].astype(jnp.bfloat16)


def prepare(weights, blocks):
    lines = weights.reshape(-1, LANES)
    count = lines.shape[0]
    held = tile_rows(weights.shape[0])
    reach = -(-32 * (held * TILE_LINES - count) // 8) * 8
    following = lax.ppermute(lines[:reach], AXES, [(n + 1, n) for n in range(31)])
    half = blocks.shape[0] // 2
    vmem = pl.BlockSpec(memory_space=pltpu.VMEM)
    return pl.pallas_call(
        prepare_kernel,
        in_specs=[vmem, vmem, pl.BlockSpec(memory_space=pl.ANY)],
        out_specs=[vmem, vmem],
        out_shape=[
            jax.ShapeDtypeStruct((held * 8, WIDE), jnp.bfloat16),
            jax.ShapeDtypeStruct((half // 8 * BLOCK, WIDE), jnp.bfloat16),
        ],
        scratch_shapes=[
            pltpu.VMEM((-(-(count + reach) // 8) * 8, LANES), jnp.float32),
            pltpu.VMEM((half, BLOCK, BLOCK), jnp.float32),
            pltpu.SemaphoreType.DMA,
        ],
        compiler_params=pltpu.CompilerParams(vmem_limit_bytes=16 * 1024 * 1024),
        name="prepare",
    )(lines, following, blocks)


def ungroup_kernel(rows_ref, o_ref):
    place = lax.axis_index("dp") * 2 + lax.axis_index("strip")
    held = rows_ref.shape[0] // 8
    first = place * held

    @pl.loop(0, held)
    def _(n):
        def work(panels):
            start = tile_lines(first + n, first, panels)
            at = pl.ds(pl.multiple_of(8 * n, 8), 8)
            for j in range(8):
                o_ref[pl.ds(start + j, 8, stride=8 * panels), :] = rows_ref[at, j * LANES : (j + 1) * LANES]

        by_region(first + n, work)


def ungroup(rows):
    vmem = pl.BlockSpec(memory_space=pltpu.VMEM)
    return pl.pallas_call(
        ungroup_kernel,
        in_specs=[vmem],
        out_specs=vmem,
        out_shape=jax.ShapeDtypeStruct((rows.size // LANES, LANES), jnp.float32),
        compiler_params=pltpu.CompilerParams(vmem_limit_bytes=16 * 1024 * 1024),
        name="ungroup",
    )(rows)


def adam_kernel(before_ref, sum_ref, w_ref, first_ref, second_ref, nw_ref, nfirst_ref, nsecond_ref, lines):
    place = lax.axis_index("dp") * 2 + lax.axis_index("strip")
    reach, summed, count = before_ref.shape[0], sum_ref.shape[0], w_ref.shape[0]
    lines[:reach] = before_ref[...]
    lines[reach : reach + summed] = sum_ref[...]
    shift = reach - place * (summed - count)
    gaps = (0, QKV_GAP // LANES, (QKV_GAP + END_GAP) // LANES)

    def update(at, rows):
        parts = [lines[pl.ds(shift + at + gap, rows), :] for gap in gaps]
        line = place * count + at + lax.broadcasted_iota(jnp.int32, (rows, LANES), 0)
        grad = jnp.where(line < QKV_AT // LANES, parts[0], jnp.where(line < GAP_AT // LANES, parts[1], parts[2]))
        here = pl.ds(at, rows)
        weights = w_ref[here]
        first = BETA_FIRST * first_ref[here] + (1.0 - BETA_FIRST) * grad
        second = BETA_SECOND * second_ref[here] + (1.0 - BETA_SECOND) * grad * grad
        nfirst_ref[here] = first
        nsecond_ref[here] = second
        fix_first = 1.0 - BETA_FIRST**ADAM_STEP
        fix_second = 1.0 - BETA_SECOND**ADAM_STEP
        step = first / fix_first / (jnp.sqrt(second / fix_second) + ADAM_EPS)
        nw_ref[here] = weights - ADAM_RATE * (step + WEIGHT_DECAY * weights)

    block = 32

    @pl.loop(0, count // block)
    def _(n):
        update(pl.multiple_of(block * n, block), block)

    if count % block:
        update(count - count % block, count % block)


def adam(rows, weights, first_moment, second_moment):
    length = weights.shape[0]
    count = length // LANES
    summed = ungroup(rows)
    reach = -(-32 * (summed.shape[0] - count) // 8) * 8
    before = lax.ppermute(summed[summed.shape[0] - reach :], AXES, [(n, n + 1) for n in range(31)])
    vmem = pl.BlockSpec(memory_space=pltpu.VMEM)
    gap = (QKV_GAP + END_GAP) // LANES
    results = pl.pallas_call(
        adam_kernel,
        in_specs=[vmem] * 5,
        out_specs=[vmem] * 3,
        out_shape=[jax.ShapeDtypeStruct((count, LANES), jnp.float32)] * 3,
        scratch_shapes=[pltpu.VMEM((-(-(reach + summed.shape[0] + gap) // 8) * 8, LANES), jnp.float32)],
        compiler_params=pltpu.CompilerParams(vmem_limit_bytes=32 * 1024 * 1024),
        name="adam",
    )(before, summed, *(a.reshape(count, LANES) for a in (weights, first_moment, second_moment)))
    return [result.reshape(length) for result in results]


def two_parts(value):
    coarse = value.astype(jnp.bfloat16)
    return coarse, (value - coarse.astype(jnp.float32)).astype(jnp.bfloat16)


def shampoo_kernel(tiles_ref, blocks_ref, sl_ref, sr_ref, rl_ref, rr_ref, nb_ref, g_ref, nl_ref, nr_ref, rms_ref):
    count = blocks_ref.shape[0]
    grads = [tiles_ref[:, n * BLOCK : (n + 1) * BLOCK] for n in range(count)]
    halves = []
    for n, grad in enumerate(grads):
        coarse, fine = two_parts(rr_ref[n])
        half = product(grad, jnp.concatenate([coarse, fine], 1))
        halves.append(half[:, :BLOCK] + half[:, BLOCK:])
    for n, grad in enumerate(grads):
        g_ref[n] = grad.astype(jnp.float32)
        nl_ref[n] = STAT_DECAY * sl_ref[n] + (1.0 - STAT_DECAY) * nt_dot(grad, grad)
        square = lax.dot_general(grad, grad, (((0,), (0,)), ((), ())), preferred_element_type=jnp.float32)
        nr_ref[n] = STAT_DECAY * sr_ref[n] + (1.0 - STAT_DECAY) * square
    conds = []
    for n, half in enumerate(halves):
        half_coarse, half_fine = two_parts(half)
        coarse, fine = two_parts(rl_ref[n])
        cond = product(jnp.concatenate([coarse, fine], 1), jnp.concatenate([half_coarse, half_coarse], 0))
        conds.append(cond + product(coarse, half_fine))
    for n, cond in enumerate(conds):
        rms = jnp.sqrt(jnp.mean(cond * cond, axis=(0, 1), keepdims=True) + RMS_EPS)
        nb_ref[n] = blocks_ref[n] - (SHAMPOO_RATE / rms) * cond
        rms_ref[n : n + 1] = jnp.broadcast_to(rms, (1, LANES))


def shampoo(chunks, blocks, stat_left, stat_right, root_left, root_right):
    count = blocks.shape[0]
    eight = pl.BlockSpec((8, BLOCK, BLOCK), lambda n: (n, 0, 0))
    whole = jax.ShapeDtypeStruct(blocks.shape, jnp.float32)
    *results, rms = pl.pallas_call(
        shampoo_kernel,
        grid=(count // 8,),
        in_specs=[pl.BlockSpec((BLOCK, WIDE), lambda n: (n, 0))] + [eight] * 5,
        out_specs=[eight] * 4 + [pl.BlockSpec((8, LANES), lambda n: (n, 0))],
        out_shape=[whole] * 4 + [jax.ShapeDtypeStruct((count, LANES), jnp.float32)],
        compiler_params=pltpu.CompilerParams(vmem_limit_bytes=60 * 1024 * 1024),
        name="shampoo",
    )(chunks, blocks, stat_left, stat_right, root_left, root_right)
    return *results, rms[:, 0]


def chunks_of(tiles):
    return tiles.reshape(-1, 8, BLOCK, BLOCK).transpose(0, 2, 1, 3).reshape(-1, WIDE)


def tiles_of(chunks):
    return chunks.reshape(-1, BLOCK, 8, BLOCK).transpose(0, 2, 1, 3).reshape(-1, BLOCK, BLOCK)


def panels_of(chunks):
    half = chunks.shape[0] // 2
    first = chunks[:half].reshape(D // BLOCK, HID // WIDE, BLOCK, WIDE).transpose(1, 0, 2, 3)
    return jnp.concatenate([first.reshape(half, WIDE), chunks[half:]])


def chunks_of_panels(panels):
    half = panels.shape[0] // 2
    first = panels[:half].reshape(HID // WIDE, D // BLOCK, BLOCK, WIDE).transpose(1, 0, 2, 3)
    return jnp.concatenate([first.reshape(half, WIDE), panels[half:]])


META = (1, 8, lambda p, c, j: (2 * p + c) * 8)
SWAP = ((0, 1), (1, 0))
AXES = ("dp", "strip")


def pairs_to(target):
    return [(2 * p + c, sum(v * w for v, w in zip(target(p, c), (2, 1)))) for p in range(16) for c in range(2)]


NEAR = pairs_to(lambda p, c: (p ^ (1 + c), c))
FAR = pairs_to(lambda p, c: (p ^ (2 - c), c))
CORE = pairs_to(lambda p, c: (p, 1 - c))


def gather_weights(weights, blocks, part):
    if direct_links():
        own, tiles = prepare(weights, blocks)
        rows, parts, line = gather_all([flat_chunks(own.shape[0], 3), META], 4, [own, part], tiles, 0)
        near = lax.ppermute(line, AXES, NEAR)
        return rows, [line, near], jnp.sum(parts[::8, 0])
    flat = lax.all_gather(weights.astype(jnp.bfloat16), AXES, axis=0, tiled=True)
    tiles = lax.all_gather(blocks.astype(jnp.bfloat16), "dp", axis=0, tiled=True)
    gaps = [jnp.zeros((QKV_GAP,), flat.dtype), jnp.zeros((END_GAP,), flat.dtype)]
    rows = jnp.concatenate([flat[:QKV_AT], gaps[0], flat[QKV_AT:GAP_AT], gaps[1], flat[GAP_AT:]])
    rows = jnp.pad(rows, (0, -rows.shape[0] % (6 * TILE))).reshape(-1, WIDE)
    return regroup(rows, 0, False), [panels_of(chunks_of(tiles))], lax.psum(part[0, 0], AXES)


class Panels:
    def __init__(self, parts):
        self.parts = parts
        self.staged = len(parts) > 1

    def first(self, before):
        if not self.staged:
            return before
        line, near = self.parts
        near, before = lax.optimization_barrier((near, before))
        self.parts = [line, near, lax.ppermute(line, AXES, FAR)]
        return before

    def second(self, before):
        if not self.staged:
            return before
        line, near, far = self.parts
        far, before = lax.optimization_barrier((far, before))
        self.parts = [line, near, far, lax.ppermute(near, AXES, FAR)]
        return before

    def third(self, after, beside):
        if not self.staged:
            return self.parts, beside
        line, near, far, both = self.parts
        both, after, beside = lax.optimization_barrier((both, after, beside))
        others = [lax.ppermute(group, AXES, CORE) for group in (line, near, far, both)]
        return [line, near, far, both] + others, beside


class PanelSums:
    def __init__(self, grads):
        self.parts = grads
        self.staged = len(grads) > 1
        if self.staged:
            self.mine = grads[0]
            self.got = lax.ppermute(grads[1], AXES, CORE)

    def added(self, at, *parts):
        total = self.mine[at].astype(jnp.float32) + self.got[at].astype(jnp.float32)
        for part in parts:
            total = total + part.astype(jnp.float32)
        return total.astype(jnp.bfloat16)

    def first(self, before):
        if not self.staged:
            return before
        away, before = lax.optimization_barrier((self.added(slice(8, 16)), before))
        self.away = lax.ppermute(away, AXES, FAR)
        return before

    def second(self, before):
        if not self.staged:
            return before
        self.away, before = lax.optimization_barrier((self.away, before))
        near, before = lax.optimization_barrier((self.added(slice(4, 8), self.away[4:]), before))
        self.last = lax.ppermute(near, AXES, NEAR)
        return before

    def third(self, before):
        if not self.staged:
            return before
        self.last, before = lax.optimization_barrier((self.last, before))
        self.parts = [self.mine, self.got, self.away, self.last]
        return before


def reduce_grads(rows, panels, part):
    everyone = (1, 8, lambda p, c, j: 0)
    summed, parts, tiles = scatter_sum([flat_chunks(rows.shape[0] // 32, 3), everyone], 6, [rows, part], panels, 1)
    return summed, tiles, parts[0, 0]


def reduce_grads_plainly(rows, panels, part, length):
    flat = regroup(rows, 0, True).astype(jnp.float32).reshape(-1)
    flat = jnp.concatenate(
        [flat[:QKV_AT], flat[QKV_AT + QKV_GAP : GAP_AT + QKV_GAP], flat[GAP_AT + QKV_GAP + END_GAP :]]
    )
    devices = lax.axis_size("dp") * lax.axis_size("strip")
    flat = jnp.pad(flat, (0, max(0, devices * length - flat.shape[0])))[: devices * length]
    tiles = tiles_of(chunks_of_panels(panels[0])).astype(jnp.float32)
    flat_sum = lax.psum_scatter(flat, AXES, scatter_dimension=0, tiled=True)
    tile_sum = lax.psum_scatter(tiles, AXES, scatter_dimension=0, tiled=True)
    tile_sum = lax.all_gather(tile_sum.astype(jnp.bfloat16), "strip", axis=0, tiled=True)
    return flat_sum, chunks_of(tile_sum), lax.psum(part[0, 0], AXES)


def adam_plainly(grad, weights, first_moment, second_moment):
    new_first = BETA_FIRST * first_moment + (1.0 - BETA_FIRST) * grad
    new_second = BETA_SECOND * second_moment + (1.0 - BETA_SECOND) * grad * grad
    fix_first = 1.0 - BETA_FIRST**ADAM_STEP
    fix_second = 1.0 - BETA_SECOND**ADAM_STEP
    moved = new_first / fix_first / (jnp.sqrt(new_second / fix_second) + ADAM_EPS)
    return weights - ADAM_RATE * (moved + WEIGHT_DECAY * weights), new_first, new_second


def shards(
    weights,
    blocks,
    stat_left,
    stat_right,
    root_left,
    root_right,
    first_moment,
    second_moment,
    image,
    camera,
    samples,
    ray_pixel,
    target,
    valid,
):
    strips = lax.axis_size("strip")
    place = lax.axis_index("strip")
    mask, wanted, own_count = pick(ray_pixel, valid, target[0])
    rows, panels, count = gather_weights(weights, blocks, own_count)
    tiled = rows.reshape(-1, 8, WIDE)

    def square(name):
        return rows[TILES[name] * 8 : TILES[name] * 8 + D]

    def plain(name, count):
        return rows[TILES[name] * 8 : TILES[name] * 8 + count]

    deconv = spread_deconv(tiled, TILES["deconv"])
    decode = plain("decode", 8).reshape(-1)
    decode_in = decode[: CH * DEC_HID].reshape(CH, DEC_HID)
    decode_out = decode[CH * DEC_HID : CH * DEC_HID + DEC_HID * 4].reshape(DEC_HID, 4)
    picture = image[0]
    real_keys = picture.shape[0]
    picture = jnp.pad(picture, ((0, -real_keys % 16), (0, 0)))
    mods = lax.dynamic_slice_in_dim(plain("modulate", 6 * NCAM), 6 * camera[0], 6).astype(jnp.float32)
    own_rows = PR * TC
    stream0 = jnp.concatenate(
        [
            lax.dynamic_slice_in_dim(rows, TILES["triplane"] * 8 + (strips * plane + place) * own_rows, own_rows)
            for plane in range(3)
        ]
    ).astype(jnp.float32)
    hidden1, norm_one = jax.vjp(norm_mod, stream0, mods[0], mods[1])
    hidden1 = hidden1.astype(jnp.bfloat16)
    query1 = product(hidden1, square("query_cross")).astype(jnp.bfloat16)
    (image_kv,) = project(picture, tiled, TILES["keyval_cross"], 2, 0)
    pairs = D // PAIR
    tokens = query1.shape[0]
    cross_out, total_one = attend_fwd(query1, [image_kv], real_keys, (0, pairs))
    stream1 = stream0 + product(cross_out, square("out_cross"))
    hidden2, norm_two = jax.vjp(norm_mod, stream1, mods[2], mods[3])
    hidden2 = hidden2.astype(jnp.bfloat16)
    panels = Panels(panels)
    hidden2 = panels.first(hidden2)
    query2, kv_own = project(hidden2, tiled, TILES["qkv_self"], 3, 1)
    kv_both = [kv_own, lax.ppermute(kv_own, "strip", SWAP)]
    all_keys = 2 * kv_own.shape[1]
    early = attend_fwd(query2, kv_both, all_keys, (0, pairs // 2))
    early = (panels.second(early[0]), early[1])
    self_out, total_two = attend_fwd(query2, kv_both, all_keys, (pairs // 2, pairs), early)
    panels, deconv = panels.third(self_out, deconv)
    stream2 = stream1 + product(self_out, square("out_self"))
    hidden3, norm_three = jax.vjp(norm_mod, stream2, mods[4], mods[5])
    hidden3 = hidden3.astype(jnp.bfloat16)
    up, act, grid = mlp_fwd(panels, hidden3, stream2)
    grid = grid.reshape(3, own_rows, D)
    edge = lax.ppermute(jnp.where(place == 0, grid[:, -TC:], grid[:, :TC]), "strip", SWAP)
    cells = deconv_fwd(grid, edge, deconv)
    cells_far = lax.ppermute(cells, "strip", SWAP)
    rays = ray_pixel.shape[1]
    factor = 1.0 / jnp.maximum(count, 1.0)
    loss_part, grad_cells, grad_far, grad_decode_in, grad_decode_out = render(
        cells,
        cells_far,
        (samples[0] + place * cells.shape[1]) % (2 * cells.shape[1]),
        wanted,
        mask,
        factor.reshape(1),
        decode_in,
        jnp.pad(decode_out, ((0, 0), (0, 4))),
        rays,
    )
    grad_decode_out = grad_decode_out[:, :4]
    grad_far = lax.ppermute(grad_far, "strip", SWAP)
    grad_grid, beside, grad_deconv = deconv_bwd(grad_cells, grad_far, grid, edge, deconv)
    beside = lax.ppermute(beside, "strip", SWAP).astype(jnp.float32)
    rest = own_rows - TC
    above = jnp.pad(jnp.where(place == 0, 0.0, beside), ((0, 0), (0, rest), (0, 0)))
    below = jnp.pad(jnp.where(place == 0, beside, 0.0), ((0, 0), (rest, 0), (0, 0)))
    grad_grid = grad_grid + above + below
    grad_stream = grad_grid.reshape(-1, D)
    grad_branch = grad_stream.astype(jnp.bfloat16)
    grad_hidden3, *panel_grads = mlp_bwd(panels, hidden3, grad_branch, up, act)
    grad_norm, grad_mod4, grad_mod5 = norm_three(grad_hidden3)
    grad_stream = grad_stream + grad_norm
    grad_branch2 = grad_stream.astype(jnp.bfloat16)
    grad_self = product_back(grad_branch2, square("out_self")).astype(jnp.bfloat16)
    panel_sums = PanelSums(panel_grads)
    grad_self = panel_sums.first(grad_self)
    early = attend_bwd(query2, kv_both, all_keys, (0, pairs - 1), 512, total_two, self_out, grad_self)
    early = (panel_sums.second(early[0]), *early[1:])
    grad_query2, grad_kv_own, grad_kv_far = attend_bwd(
        query2, kv_both, all_keys, (pairs - 1, pairs), 512, total_two, self_out, grad_self, early
    )
    grad_kv_far = lax.ppermute(grad_kv_far, "strip", SWAP)
    grad_hidden2, grad_kv = project_back(grad_query2, grad_kv_own, grad_kv_far, tiled, TILES["qkv_self"], D)
    grad_norm, grad_mod2, grad_mod3 = norm_two(grad_hidden2)
    grad_stream = grad_stream + grad_norm
    grad_branch1 = grad_stream.astype(jnp.bfloat16)
    grad_cross = product_back(grad_branch1, square("out_cross")).astype(jnp.bfloat16)
    grad_query1, grad_image_kv = attend_bwd(
        query1, [image_kv], real_keys, (0, pairs), picture.shape[0], total_one, cross_out, grad_cross
    )
    grad_query1 = panel_sums.third(grad_query1)
    grad_norm, grad_mod0, grad_mod1 = norm_one(product_back(grad_query1, square("query_cross")))
    grad_stream = grad_stream + grad_norm
    grad_mods = jnp.stack([grad_mod0, grad_mod1, grad_mod2, grad_mod3, grad_mod4, grad_mod5])
    grad_modulate = lax.dynamic_update_slice_in_dim(
        jnp.zeros((6 * NCAM, D), jnp.bfloat16), grad_mods.astype(jnp.bfloat16), 6 * camera[0], 0
    )
    grad_decode = jnp.concatenate([grad_decode_in.reshape(-1), grad_decode_out.reshape(-1)])
    grad_decode = jnp.pad(grad_decode, (0, END_GAP))
    total_tiles = tiled.shape[0]
    end = TILES["triplane"] + 3 * strips * own_rows // 8
    gap = TILES["qkv_self"] - TILES["gap"]
    arrays = [
        hidden1,
        grad_query1,
        picture,
        grad_image_kv,
        cross_out,
        grad_branch1,
        hidden2,
        grad_query2,
        grad_kv,
        self_out,
        grad_branch2,
    ]
    tall, low = (tokens, D), (picture.shape[0], DI)
    products = [
        (tall, (9, None), (10, None), TILES["out_self"], (1, 0)),
        (tall, (6, None), (7, None), TILES["qkv_self"], (3, 0)),
        (tall, (6, None), (8, 0), TILES["qkv_self"], (3, 1)),
        (tall, (6, None), (8, 1), TILES["qkv_self"], (3, 2)),
        (tall, (4, None), (5, None), TILES["out_cross"], (1, 0)),
        (low, (2, None), (3, 0), TILES["keyval_cross"], (2, 0)),
        (low, (2, None), (3, 1), TILES["keyval_cross"], (2, 1)),
        (tall, (0, None), (1, None), TILES["query_cross"], (1, 0)),
    ]
    grad_tokens = grad_stream.astype(jnp.bfloat16)
    copies = []
    for piece, first in (
        (grad_deconv, TILES["deconv"]),
        (grad_decode, TILES["decode"]),
        (grad_modulate, TILES["modulate"]),
        (grad_tokens, None),
    ):
        piece = piece.astype(jnp.bfloat16).reshape(-1, 8, WIDE)
        if first is None:
            part = own_rows // 8
            for plane in range(3):
                first = TILES["triplane"] + 2 * plane * part
                copies.append((len(arrays), plane * part, part, first, part))
                copies.append((None, 0, part, first + part, -part))
        else:
            copies.append((len(arrays), 0, piece.shape[0], first, 0))
        arrays.append(piece)
    for first, count in ((TILES["gap"], gap), (end, total_tiles - end)):
        part = own_rows // 8
        for start in range(0, count, part):
            copies.append((None, 0, min(part, count - start), first + start, 0))
    row_grads = weight_grads(arrays, products, copies, total_tiles).reshape(-1, WIDE)
    if direct_links():
        summed, chunks, loss_sum = reduce_grads(row_grads, panel_sums.parts, loss_part)
        new_weights, new_first, new_second = adam(summed, weights, first_moment, second_moment)
    else:
        summed, chunks, loss_sum = reduce_grads_plainly(row_grads, panel_sums.parts, loss_part, weights.shape[0])
        new_weights, new_first, new_second = adam_plainly(summed, weights, first_moment, second_moment)
    new_blocks, block_grads, new_left, new_right, block_rms = shampoo(
        chunks, blocks, stat_left, stat_right, root_left, root_right
    )
    loss = loss_sum * factor
    return (
        loss,
        new_weights,
        new_first,
        new_second,
        new_blocks,
        block_grads,
        new_left,
        new_right,
        block_rms,
    )


def solution(mesh):
    placed = (
        P(("dp", "strip")),
        P("dp", None, None),
        P("dp", None, None),
        P("dp", None, None),
        P("dp", None, None),
        P("dp", None, None),
        P(("dp", "strip")),
        P(("dp", "strip")),
        P("dp", None, None),
        P("dp"),
        P("dp", None, None, "strip"),
        P("dp", "strip"),
        P("dp", None, None),
        P("dp", None),
    )
    return jax.shard_map(
        shards,
        mesh=mesh,
        in_specs=placed,
        out_specs=(
            P(),
            P(("dp", "strip")),
            P(("dp", "strip")),
            P(("dp", "strip")),
            P("dp", None, None),
            P("dp", None, None),
            P("dp", None, None),
            P("dp", None, None),
            P("dp"),
        ),
        check_vma=False,
    )
```

```python
import functools
import math

import jax
import jax.numpy as jnp
from jax import lax
from jax.experimental import pallas as pl
from jax.experimental.pallas import tpu as pltpu
from jax.sharding import PartitionSpec as P

D = 1024
HEAD_DIM = 64
HID = 4096
DI = 768
CH = 80
DEC_HID = 64
BLOCK = 128
PR = 8
TC = 32
S = 16
NCAM = 32
ADAM_STEP = 10


NORM_EPS = 1e-05
ADAM_RATE = 0.015
BETA_FIRST = 0.9
BETA_SECOND = 0.95
ADAM_EPS = 1e-08
WEIGHT_DECAY = 0.1
STAT_DECAY = 0.9
SHAMPOO_RATE = 0.01
RMS_EPS = 1e-06
HIGHEST_MODE = lax.Precision.HIGHEST
WIDE = 1024


def product(left, right):
    return jnp.dot(left, right, preferred_element_type=jnp.float32)


def product_back(left, right):
    return lax.dot_general(
        left, right, (((left.ndim - 1,), (1,)), ((), ())), preferred_element_type=jnp.float32
    )


def weight_grad(left, right):
    return lax.dot_general(
        left, right, (((0,), (0,)), ((), ())), preferred_element_type=jnp.float32
    )


def norm_mod(stream, scale, shift):
    centred = stream - jnp.mean(stream, -1, keepdims=True)
    spread = jnp.mean(centred * centred, -1, keepdims=True)
    return centred * lax.rsqrt(spread + NORM_EPS) * (1.0 + scale) + shift


def gelu_tanh(value):
    return jax.nn.gelu(value, approximate=True)


PAIR = 2 * HEAD_DIM
BRIEF = pl.CostEstimate(flops=1000000, transcendentals=0, bytes_accessed=100000)
LOG2E = math.log2(math.e)
EXP_SCALE = HEAD_DIM ** (-0.5) * LOG2E


def nt_dot(left, right):
    return lax.dot_general(left, right, (((1,), (1,)), ((), ())), preferred_element_type=jnp.float32)


def head_lanes(shape, head):
    return lax.broadcasted_iota(jnp.int32, shape, len(shape) - 1) // HEAD_DIM == head


def joined(refs, n):
    parts = [ref[n] for ref in refs]
    return parts[0] if len(parts) == 1 else jnp.concatenate(parts, 0)


def attend_fwd_kernel(real_keys, sources, q_ref, *refs):
    o_ref, lse_ref = refs[-2:]
    query, keys = q_ref[...], joined(refs[:sources], 0)
    values = joined(refs[:sources], 1).T
    outs = []
    heads = [jnp.where(head_lanes(query.shape, head), query, 0) for head in range(2)]
    all_scores = [nt_dot(keys, own) for own in heads]
    for head, scores in enumerate(all_scores):
        if real_keys < keys.shape[0]:
            at = lax.broadcasted_iota(jnp.int32, scores.shape, 0)
            scores = jnp.where(at < real_keys, scores, -3e38)
        top = jnp.max(scores, 0, keepdims=True)
        raised = jnp.exp2((scores - top) * EXP_SCALE)
        total = jnp.sum(raised, 0, keepdims=True)
        shares = (raised * (1.0 / total)).astype(jnp.bfloat16)
        outs.append(product(values[head * HEAD_DIM : (head + 1) * HEAD_DIM], shares))
        lse_ref[0, head : head + 1] = top * EXP_SCALE + jnp.log2(total)
    o_ref[...] = jnp.concatenate(outs, 0).T.astype(jnp.bfloat16)


def attend_fwd(query, sources, real_keys, span, earlier=()):
    count = query.shape[0]
    total_keys = sum(source.shape[1] for source in sources)
    low, high = span
    by_pair = pl.BlockSpec((count, PAIR), lambda j: (0, low + j))
    work = count * total_keys * (high - low) * PAIR
    return pl.pallas_call(
        functools.partial(attend_fwd_kernel, real_keys, len(sources)),
        grid=(high - low,),
        in_specs=[by_pair]
        + [pl.BlockSpec((2, source.shape[1], PAIR), lambda j: (0, 0, low + j)) for source in sources]
        + [pl.BlockSpec(memory_space=pl.ANY)] * len(earlier),
        out_specs=[by_pair, pl.BlockSpec((1, 8, count), lambda j: (low + j, 0, 0))],
        out_shape=[
            jax.ShapeDtypeStruct((count, D), jnp.bfloat16),
            jax.ShapeDtypeStruct((D // PAIR, 8, count), jnp.float32),
        ],
        input_output_aliases={1 + len(sources) + n: n for n in range(len(earlier))},
        compiler_params=pltpu.CompilerParams(vmem_limit_bytes=48 * 1024 * 1024),
        cost_estimate=BRIEF,
        name="attend_fwd",
    )(query, *sources, *earlier)


def attend_bwd_kernel(real_keys, chunk, sources, extra, q_ref, *refs):
    kv_refs = refs[:sources]
    lse_ref, o_ref, g_ref = refs[sources : sources + 3]
    dq_ref, *grad_refs = refs[sources + 3 + extra : sources + 4 + extra + sources]
    k_all, v_all, kt_ref, dk_sum, dv_sum = refs[sources + 4 + extra + sources :]
    k_all[...] = joined(kv_refs, 0)
    v_all[...] = joined(kv_refs, 1)
    kt_ref[...] = k_all[...].T
    query, grad = q_ref[...], g_ref[...]
    mixed = (grad.astype(jnp.float32) * o_ref[...].astype(jnp.float32)).T
    total_keys = k_all.shape[0]
    queries = [jnp.where(head_lanes(query.shape, head), query, 0) for head in range(2)]
    grads = [jnp.where(head_lanes(grad.shape, head), grad, 0) for head in range(2)]
    inner = [jnp.sum(mixed[head * HEAD_DIM : (head + 1) * HEAD_DIM], 0, keepdims=True) for head in range(2)]
    grad_query = [jnp.zeros((HEAD_DIM, query.shape[0]), jnp.float32) for head in range(2)]
    def opened(at):
        part = pl.ds(at, chunk)
        keys, values = k_all[part], v_all[part]
        return [(nt_dot(keys, queries[head]), nt_dot(values, grads[head])) for head in range(2)]

    ahead = opened(0)
    for at in range(0, total_keys, chunk):
        part = pl.ds(at, chunk)
        now = ahead
        if at + chunk < total_keys:
            ahead = opened(at + chunk)
        for head, (scores, grad_shares) in enumerate(now):
            shares = jnp.exp2(scores * EXP_SCALE - lse_ref[0, head : head + 1])
            if at + chunk > real_keys:
                row = at + lax.broadcasted_iota(jnp.int32, shares.shape, 0)
                shares = jnp.where(row < real_keys, shares, 0.0)
            grad_scores = (shares * (grad_shares - inner[head])).astype(jnp.bfloat16)
            to_values = product(shares.astype(jnp.bfloat16), grads[head])
            to_keys = product(grad_scores, queries[head])
            if head == 0:
                dv_sum[part] = to_values
                dk_sum[part] = to_keys
            else:
                dv_sum[part] += to_values
                dk_sum[part] += to_keys
            grad_query[head] += product(
                kt_ref[head * HEAD_DIM : (head + 1) * HEAD_DIM, part], grad_scores
            )
    scale = HEAD_DIM ** (-0.5)
    dq_ref[...] = (jnp.concatenate(grad_query, 0) * scale).T.astype(jnp.bfloat16)
    start = 0
    for ref in grad_refs:
        part = pl.ds(start, ref.shape[1])
        ref[0] = (dk_sum[part] * scale).astype(jnp.bfloat16)
        ref[1] = dv_sum[part].astype(jnp.bfloat16)
        start += ref.shape[1]


def attend_bwd(query, sources, real_keys, span, chunk, totals, out, grad, earlier=()):
    count = query.shape[0]
    total_keys = sum(source.shape[1] for source in sources)
    low, high = span
    by_pair = pl.BlockSpec((count, PAIR), lambda j: (0, low + j))
    by_source = [pl.BlockSpec((2, source.shape[1], PAIR), lambda j: (0, 0, low + j)) for source in sources]
    first = 1 + len(sources) + 3
    work = count * total_keys * (high - low) * PAIR
    return pl.pallas_call(
        functools.partial(attend_bwd_kernel, real_keys, chunk, len(sources), len(earlier)),
        grid=(high - low,),
        in_specs=[by_pair]
        + by_source
        + [pl.BlockSpec((1, 8, count), lambda j: (low + j, 0, 0)), by_pair, by_pair]
        + [pl.BlockSpec(memory_space=pl.ANY)] * len(earlier),
        out_specs=[by_pair] + by_source,
        out_shape=[jax.ShapeDtypeStruct((count, D), jnp.bfloat16)]
        + [jax.ShapeDtypeStruct(source.shape, jnp.bfloat16) for source in sources],
        input_output_aliases={first + n: n for n in range(len(earlier))},
        scratch_shapes=[
            pltpu.VMEM((total_keys, PAIR), jnp.bfloat16),
            pltpu.VMEM((total_keys, PAIR), jnp.bfloat16),
            pltpu.VMEM((PAIR, total_keys), jnp.bfloat16),
            pltpu.VMEM((total_keys, PAIR), jnp.float32),
            pltpu.VMEM((total_keys, PAIR), jnp.float32),
        ],
        compiler_params=pltpu.CompilerParams(vmem_limit_bytes=48 * 1024 * 1024),
        cost_estimate=BRIEF,
        name="attend_bwd",
    )(query, *sources, totals, out, grad, *earlier)


GROUPS = 3


def render_kernel(samples_ref, near_ref, far_ref, wanted_ref, mask_ref, factor_ref, win_ref, wout_ref,
                  loss_ref, grad_ref, grad_far_ref, gin_ref, gout_ref,
                  table, inner_all, hidden_all, point_all, out_all, gout_all, sums):
    block = pl.program_id(0)
    half = near_ref.shape[1]
    cells = 2 * half
    group = table.shape[2]
    rays = samples_ref.shape[2]
    planes = near_ref.shape[0]

    @pl.when(block == 0)
    def _():
        loss_ref[...] = jnp.zeros_like(loss_ref)
        gin_ref[...] = jnp.zeros_like(gin_ref)
        gout_ref[...] = jnp.zeros_like(gout_ref)
        sums[...] = jnp.zeros_like(sums)
        table[...] = jnp.zeros_like(table)
        for plane in range(planes):
            turned = jnp.concatenate([near_ref[plane], far_ref[plane]], 0).T
            for g in range(GROUPS):
                width = min(group, cells - g * group)
                table[plane, g * CH : (g + 1) * CH, :width] = turned[:CH, g * group : g * group + width]

    step = 8
    width = step * rays
    win, wout = win_ref[...], wout_ref[...]

    def places_read(plane, s):
        rows = [samples_ref[plane, s + n : s + n + 1, :] for n in range(step)]
        at = jnp.concatenate(rows, 1)
        owner = at // group
        within = at - owner * group
        hot = lax.broadcasted_iota(jnp.int32, (group, width), 0) == within
        return owner, jnp.where(hot, 1.0, 0.0).astype(jnp.bfloat16)

    def tn_dot(left, right):
        return lax.dot_general(left, right, (((0,), (0,)), ((), ())), preferred_element_type=jnp.float32)

    for s in range(0, S, step):
        here = pl.ds(s * rays, width)
        point = jnp.zeros((CH, width), jnp.float32)
        for plane in range(planes):
            owner, hot = places_read(plane, s)
            found = product(table[plane], hot)
            value = found[:CH]
            for g in range(1, GROUPS):
                value = jnp.where(owner == g, found[g * CH : (g + 1) * CH], value)
            point = point + value
        point = point.astype(jnp.bfloat16)
        inner = tn_dot(win, point)
        hidden = (inner * jax.nn.sigmoid(inner)).astype(jnp.bfloat16)
        out_all[:, here] = tn_dot(wout, hidden)
        inner_all[:, here] = inner
        hidden_all[:, here] = hidden
        point_all[:, here] = point

    factor = factor_ref[0]
    mask = mask_ref[...]
    row = lax.broadcasted_iota(jnp.int32, (8, rays), 0)
    is_colour = (row >= 1) & (row <= 3)
    before = jnp.zeros((1, rays), jnp.float32)
    rgb = jnp.zeros((8, rays), jnp.float32)
    kept = []
    for s in range(S):
        out = out_all[:, s * rays : (s + 1) * rays]
        level = out[0:1]
        absorb = (4.0 / S) * (jnp.maximum(level, 0.0) + jnp.log1p(jnp.exp(-jnp.abs(level))))
        weight = jnp.exp(-before) * (1.0 - jnp.exp(-absorb))
        before = before + absorb
        colour = jax.nn.sigmoid(out)
        rgb = rgb + weight * colour
        kept.append((weight, jnp.exp(-before), colour))
    error = jnp.where(is_colour, rgb - wanted_ref[...], 0.0)
    loss_ref[...] += jnp.sum(mask * jnp.sum(error * error, 0, keepdims=True))
    pull = error * (2.0 * factor * mask)
    tail = jnp.zeros((1, rays), jnp.float32)
    for s in reversed(range(S)):
        weight, left_over, colour = kept[s]
        to_weight = jnp.sum(pull * colour, 0, keepdims=True)
        to_absorb = to_weight * left_over - tail
        tail = tail + to_weight * weight
        to_level = (4.0 / S) * to_absorb * colour[0:1]
        to_colour = weight * pull * colour * (1.0 - colour)
        gout_all[:, s * rays : (s + 1) * rays] = jnp.where(row == 0, to_level, to_colour).astype(jnp.bfloat16)

    for s in range(0, S, step):
        here = pl.ds(s * rays, width)
        pulled = gout_all[:, here]
        inner = inner_all[:, here]
        gate = jax.nn.sigmoid(inner)
        grad_inner = product(wout, pulled) * (gate * (1.0 + inner * (1.0 - gate)))
        grad_inner = grad_inner.astype(jnp.bfloat16)
        gout_ref[...] += nt_dot(hidden_all[:, here], pulled)
        gin_ref[...] += nt_dot(point_all[:, here], grad_inner)
        grad_point = product(win, grad_inner)
        coarse = grad_point.astype(jnp.bfloat16).astype(jnp.float32)
        fine = grad_point - coarse
        for plane in range(planes):
            owner, hot = places_read(plane, s)
            rows = [jnp.where(owner == g, coarse, 0.0) for g in range(GROUPS)]
            rows += [jnp.where(owner == g, fine, 0.0) for g in range(GROUPS)]
            stacked = jnp.concatenate(rows, 0).astype(jnp.bfloat16)
            added = nt_dot(stacked, hot)
            sums[plane] += added[: GROUPS * CH] + added[GROUPS * CH :]

    @pl.when(block == pl.num_programs(0) - 1)
    def _():
        for plane in range(planes):
            for g in range(GROUPS):
                for low, high, ref in ((0, half, grad_ref), (half, cells, grad_far_ref)):
                    start, stop = max(g * group, low), min((g + 1) * group, high)
                    if start < stop:
                        part = sums[plane, g * CH : (g + 1) * CH, start - g * group : stop - g * group]
                        ref[plane, :, start - low : stop - low] = part.astype(jnp.bfloat16)


def render(near, far, samples, wanted, mask, factor, decode_in, decode_out, rays):
    planes, half, _ = near.shape
    count = 2 * half
    all_rays = samples.shape[2]
    group = -(-count // (GROUPS * 128)) * 128
    points = S * rays
    whole = lambda *shape: pl.BlockSpec(shape, lambda n: (0,) * len(shape))
    return pl.pallas_call(
        render_kernel,
        grid=(all_rays // rays,),
        in_specs=[
            pl.BlockSpec((planes, S, rays), lambda n: (0, 0, n)),
            whole(*near.shape),
            whole(*far.shape),
            pl.BlockSpec((8, rays), lambda n: (0, n)),
            pl.BlockSpec((1, rays), lambda n: (0, n)),
            pl.BlockSpec(memory_space=pltpu.SMEM),
            whole(CH, DEC_HID),
            whole(DEC_HID, 8),
        ],
        out_specs=[whole(8, 128), whole(planes, CH, half), whole(planes, CH, half), whole(CH, DEC_HID), whole(DEC_HID, 8)],
        out_shape=[
            jax.ShapeDtypeStruct((8, 128), jnp.float32),
            jax.ShapeDtypeStruct((planes, CH, half), jnp.bfloat16),
            jax.ShapeDtypeStruct((planes, CH, half), jnp.bfloat16),
            jax.ShapeDtypeStruct((CH, DEC_HID), jnp.float32),
            jax.ShapeDtypeStruct((DEC_HID, 8), jnp.float32),
        ],
        scratch_shapes=[
            pltpu.VMEM((planes, GROUPS * CH, group), jnp.bfloat16),
            pltpu.VMEM((DEC_HID, points), jnp.float32),
            pltpu.VMEM((DEC_HID, points), jnp.bfloat16),
            pltpu.VMEM((CH, points), jnp.bfloat16),
            pltpu.VMEM((8, points), jnp.float32),
            pltpu.VMEM((8, points), jnp.bfloat16),
            pltpu.VMEM((planes, GROUPS * CH, group), jnp.float32),
        ],
        compiler_params=pltpu.CompilerParams(vmem_limit_bytes=48 * 1024 * 1024),
        name="render",
    )(samples, near, far, wanted, mask, factor, decode_in, decode_out)


def pick_kernel(pixel_ref, valid_ref, target_ref, mask_ref, wanted_ref, count_ref):
    pixels = valid_ref.shape[1]
    rays = pixel_ref.shape[1]
    hot = lax.broadcasted_iota(jnp.int32, (pixels, rays), 0) == pixel_ref[...]
    hot = jnp.where(hot, 1.0, 0.0).astype(jnp.bfloat16)
    rest = target_ref[...]
    rows = [valid_ref[...].astype(jnp.float32)]
    for _ in range(3):
        part = rest.astype(jnp.bfloat16).astype(jnp.float32)
        rows.append(part)
        rest = rest - part
    rows.append(jnp.zeros((6, pixels), jnp.float32))
    found = product(jnp.concatenate(rows, 0).astype(jnp.bfloat16), hot)
    mask = found[:1]
    mask_ref[...] = mask
    wanted_ref[...] = jnp.zeros_like(wanted_ref)
    wanted_ref[1:4] = found[1:4] + found[4:7] + found[7:10]
    count_ref[...] = jnp.broadcast_to(jnp.sum(mask, 1, keepdims=True), count_ref.shape)


def pick(pixel, valid, target):
    rays = pixel.shape[1]
    vmem = pl.BlockSpec(memory_space=pltpu.VMEM)
    return pl.pallas_call(
        pick_kernel,
        in_specs=[vmem] * 3,
        out_specs=[vmem] * 3,
        out_shape=[
            jax.ShapeDtypeStruct((1, rays), jnp.float32),
            jax.ShapeDtypeStruct((8, rays), jnp.float32),
            jax.ShapeDtypeStruct((8, 128), jnp.float32),
        ],
        compiler_params=pltpu.CompilerParams(vmem_limit_bytes=24 * 1024 * 1024),
        name="pick",
    )(pixel, valid, target)


MESH_ID = pl.DeviceIdType.MESH


def places():
    p = lax.axis_index("dp")
    c = lax.axis_index("strip")
    z = p // 4
    flip_x = p + 1 - 2 * (p % 2)
    flip_y = p + 2 - 4 * ((p // 2) % 2)
    both = flip_x + flip_y - p
    near = (1 - c) * flip_x + c * flip_y
    far = (1 - c) * flip_y + c * flip_x
    return p, c, z, near, far, both


def along_z(line, z, k):
    return ((z + k) % 4) * 4 + line % 4


def enter(peers):
    barrier = pltpu.get_barrier_semaphore()
    for peer in peers:
        pl.semaphore_signal(barrier, inc=1, device_id=peer, device_id_type=MESH_ID)
    pl.semaphore_wait(barrier, len(peers))


def flat_chunks(rows, n):
    part = rows // n
    return n, part, lambda p, c, j: (2 * p + c) * rows + j * part


def block_chunk(p, c, k):
    second = p // 8
    return ((1 - second) * ((2 * c + k) * 8 + p) + second * (4 * p + 2 * c + k)) * BLOCK


ORDER = [("near", 0), ("z", 1), ("far", 0), ("z", 2), ("z", 3), ("near", 1), ("near", 2), ("near", 3)]
ORDER += [("both", 0), ("far", 1), ("far", 2), ("far", 3), ("both", 1), ("both", 2), ("both", 3)]
ORDER += [("core", i) for i in range(16)]


def gather_kernel(layouts, stagger, *refs):
    count = len(layouts)
    fulls = refs[count + 1 : 2 * count + 1]
    line_full = refs[2 * count + 1]
    send, recv, local, z_send, line_recv, line_send = refs[2 * count + 2 : 2 * count + 8]
    held = refs[2 * count + 8 :]
    brought = [pltpu.make_async_copy(s, h, local.at[n]) for n, (s, h) in enumerate(zip(refs[: count + 1], held))]
    for copy in brought:
        copy.start()
    sources, line_source = held[:count], held[count]
    p, c, z, near, far, both = places()
    zs = [along_z(p, z, k) for k in range(4)]
    enter([(q, c) for q in zs[1:]] + [(near, c), (far, c), (p, 1 - c)])
    for copy in brought:
        copy.wait()
    jobs = [(a, j) for a, layout in enumerate(layouts) for j in range(layout[0])]
    me = (p, c)
    up, down = (p + 4, c), (p - 4, c)

    def target(owner, job):
        a, j = jobs[job]
        _, rows, place = layouts[a]
        return fulls[a].at[pl.ds(pl.multiple_of(place(*owner, j), 8), rows)]

    def source(owner, job):
        if owner is not me:
            return target(owner, job)
        a, j = jobs[job]
        rows = layouts[a][1]
        return sources[a].at[pl.ds(j * rows, rows)]

    def sending(owner, event, peer, job, sem=None):
        return pltpu.make_async_remote_copy(
            source(owner, job), target(owner, job), send.at[event, job] if sem is None else sem, recv.at[event, job],
            device_id=peer, device_id_type=MESH_ID,
        )

    def arrive(owner, event, job):
        t = target(owner, job)
        pltpu.make_async_remote_copy(
            t, t, send.at[event, job], recv.at[event, job], device_id=(p, 1 - c), device_id_type=MESH_ID
        ).wait_recv()

    def sending_up(distance, job):
        owner = me if distance == 1 else (zs[5 - distance], c)
        return sending(owner, 3 - distance, up, job, z_send.at[0, distance - 1, job])

    def sending_down(distance, job):
        owner = me if distance == 1 else (zs[distance - 1], c)
        return sending(owner, distance - 1, down, job, z_send.at[1, distance - 1, job])

    def line_up(distance):
        held_at = line_source if distance == 1 else line_full.at[5 - distance]
        return pltpu.make_async_remote_copy(
            held_at, line_full.at[4 - distance], line_send.at[0, distance - 1], line_recv.at[4 - distance],
            device_id=up, device_id_type=MESH_ID,
        )

    def line_down(distance):
        held_at = line_source if distance == 1 else line_full.at[distance - 1]
        return pltpu.make_async_remote_copy(
            held_at, line_full.at[distance], line_send.at[1, distance - 1], line_recv.at[distance],
            device_id=down, device_id_type=MESH_ID,
        )

    def each_way(distance, work):
        @pl.when(z + distance <= 3)
        def _():
            work(distance, True)

        @pl.when(z >= distance)
        def _():
            work(4 - distance, False)

    def pass_on(ups, downs, distance, *job):
        if distance > 3:
            return

        @pl.when((z < 3) & (z >= distance - 1))
        def _():
            ups(distance, *job)

        @pl.when((z > 0) & (z + distance - 1 <= 3))
        def _():
            downs(distance, *job)

    def begin(job):
        sending(me, 3, (near, c), job).start()

        @pl.when(z < 3)
        def _():
            sending_up(1, job).start()

        @pl.when(z > 0)
        def _():
            sending_down(1, job).start()

        sending(me, 7, (far, c), job).start()
        sending(me, 15, (p, 1 - c), job).start()
        pltpu.make_async_copy(source(me, job), target(me, job), local.at[job]).start()

    def take_z(k, above, job):
        owner = (zs[k], c)
        arrive(owner, k - 1, job)
        distance = k if above else 4 - k
        if distance < 3:

            @pl.when(z > 0 if above else z < 3)
            def _():
                (sending_down if above else sending_up)(distance + 1, job).start()

        sending(owner, 3 + k, (near, c), job).start()
        sending(owner, 7 + k, (far, c), job).start()
        sending(owner, 15 + k, (p, 1 - c), job).start()

    def take(kind, k, job):
        if kind == "near":
            owner = (along_z(near, z, k), c)
            arrive(owner, 3 + k, job)
            sending(owner, 11 + k, (far, c), job).start()
            sending(owner, 19 + k, (p, 1 - c), job).start()
        elif kind == "far":
            owner = (along_z(far, z, k), c)
            arrive(owner, 7 + k, job)
            sending(owner, 23 + k, (p, 1 - c), job).start()
        elif kind == "both":
            owner = (along_z(both, z, k), c)
            arrive(owner, 11 + k, job)
            sending(owner, 27 + k, (p, 1 - c), job).start()
        elif kind == "core":
            line = (p, far, near, both)[k // 4]
            arrive((along_z(line, z, k % 4), 1 - c), 15 + k, job)

    def line_arrive(k):
        spot = line_full.at[k]
        pltpu.make_async_remote_copy(
            spot, spot, line_send.at[0, 0], line_recv.at[k], device_id=(p, 1 - c), device_id_type=MESH_ID
        ).wait_recv()

    def line_take(k, above):
        line_arrive(k)
        distance = k if above else 4 - k
        if distance < 3:

            @pl.when(z > 0 if above else z < 3)
            def _():
                (line_down if above else line_up)(distance + 1).start()

    steps = [(2 * stagger + 2 + 3 * n, -2, n) for n in range(4)]
    for job in range(len(jobs)):
        begin_at = stagger * min(job, layouts[0][0] - 1)
        for i in range(-1, len(ORDER)):
            steps.append((begin_at + i + 1, i, job))
    own_line = pltpu.make_async_copy(line_source, line_full.at[0], line_recv.at[0])
    for _, i, job in sorted(steps):
        if i == -2:
            if job == 0:

                @pl.when(z < 3)
                def _():
                    line_up(1).start()

                @pl.when(z > 0)
                def _():
                    line_down(1).start()

                own_line.start()
            else:
                each_way(job, line_take)
        elif i < 0:
            begin(job)
        else:
            kind, k = ORDER[i]
            if kind == "z":
                each_way(k, lambda n, above: take_z(n, above, job))
            elif kind == "core" or k == 0:
                take(kind, k, job)
            else:
                each_way(k, lambda n, above: take(kind, n, job))
    own_line.wait()
    for distance in (1, 2, 3):
        pass_on(lambda d: line_up(d).wait_send(), lambda d: line_down(d).wait_send(), distance)
    for job in range(len(jobs)):
        for distance in (1, 2, 3):
            pass_on(lambda d, n: sending_up(d, n).wait_send(), lambda d, n: sending_down(d, n).wait_send(), distance, job)
        for k in range(4):
            owner = (zs[k], c) if k else me
            sending(owner, 3 + k, (near, c), job).wait_send()
            sending(owner, 7 + k, (far, c), job).wait_send()
            sending((along_z(near, z, k), c), 11 + k, (far, c), job).wait_send()
            sending(owner, 15 + k, (p, 1 - c), job).wait_send()
            for line, first in ((near, 19), (far, 23), (both, 27)):
                sending((along_z(line, z, k), c), first + k, (p, 1 - c), job).wait_send()
        pltpu.make_async_copy(source(me, job), target(me, job), local.at[job]).wait()


def gather_all(layouts, stagger, shards_in, line, name_id):
    copies = sum(l[0] for l in layouts)
    everywhere = pl.BlockSpec(memory_space=pl.ANY)
    shapes = [jax.ShapeDtypeStruct((32 * s.shape[0],) + s.shape[1:], s.dtype) for s in shards_in]
    shapes.append(jax.ShapeDtypeStruct((4,) + line.shape, line.dtype))
    return pl.pallas_call(
        functools.partial(gather_kernel, layouts, stagger),
        out_shape=shapes,
        in_specs=[everywhere] * len(shapes),
        out_specs=[everywhere] * len(shapes),
        scratch_shapes=[
            pltpu.SemaphoreType.DMA((31, copies)),
            pltpu.SemaphoreType.DMA((31, copies)),
            pltpu.SemaphoreType.DMA((copies,)),
            pltpu.SemaphoreType.DMA((2, 3, copies)),
            pltpu.SemaphoreType.DMA((4,)),
            pltpu.SemaphoreType.DMA((2, 3)),
        ]
        + [pltpu.VMEM(a.shape, a.dtype) for a in (*shards_in, line)],
        compiler_params=pltpu.CompilerParams(collective_id=name_id, has_side_effects=True),
        name="gather_all",
    )(*shards_in, line)


SUM_ORDER = [(3, 0), (3, 1), (3, 3), (3, 2), (2, 0), (2, 1), (2, 3), (2, 2)]
SUM_ORDER += [(1, 1), (1, 3), (1, 2), (1, 0), (0, 1), (0, 3), (0, 2), (0, 0)]
AHEAD = 3


def scatter_kernel(layouts, stagger, *refs):
    count = len(layouts)
    grads = refs[:count]
    line_grads = refs[count : count + 4]
    outs = refs[count + 4 : 2 * count + 4]
    line_out = refs[2 * count + 4]
    scratch = refs[2 * count + 5 :]
    line_parts, line_sums, line_got, line_sum, line_sems, line_load_sems, line_send, line_recv = scratch[-8:]
    p, c, z, near, far, both = places()
    up, down = (p + 4, c), (p - 4, c)
    zs = [along_z(p, z, k) for k in range(4)]
    enter([(q, c) for q in zs[1:]] + [(near, c), (far, c), (p, 1 - c)])
    csend, crecv, bsend, brecv, load_sem, out_sem = scratch[:6]
    buffers = [scratch[6 + 6 * a : 12 + 6 * a] for a in range(count)]
    jobs = [(a, j) for a, layout in enumerate(layouts) for j in range(layout[0])]
    lines = (p, near, far, both)
    partner_lines = (p, far, near, both)

    def view(job, ref, slot):
        a, j = jobs[job]
        rows = layouts[a][1]
        return ref.at[slot, pl.ds(j * rows, rows)]

    def piece(owner, job):
        a, j = jobs[job]
        _, rows, place = layouts[a]
        at = place(*owner, j)
        return grads[a].at[pl.ds(at if isinstance(at, int) else pl.multiple_of(at, 8), rows)]

    def to_core(i, job):
        g, k = SUM_ORDER[i]
        owner = (along_z(partner_lines[g], z, k), 1 - c)
        rc = buffers[jobs[job][0]][0]
        return pltpu.make_async_remote_copy(
            piece(owner, job), view(job, rc, g * 4 + k), csend.at[i, job], crecv.at[i, job],
            device_id=(p, 1 - c), device_id_type=MESH_ID,
        )

    def load(i, job):
        g, k = SUM_ORDER[i]
        own = buffers[jobs[job][0]][4]
        return pltpu.make_async_copy(
            piece((along_z(lines[g], z, k), c), job), view(job, own, i % AHEAD), load_sem.at[i, job]
        )

    def onward(i, job):
        g, k = SUM_ORDER[i]
        rc, rb, ra, rz = buffers[jobs[job][0]][:4]
        if g == 3:
            target, event, peer = view(job, rb, 4 + k), 4 + k, (far, c)
        elif g == 2:
            target, event, peer = view(job, rb, k), k, (far, c)
        elif g == 1:
            target, event, peer = view(job, ra, k), 8 + k, (near, c)
        else:
            target, event, peer = view(job, rz, 3 - k), 12 + 3 - k, (zs[k], c)
        return pltpu.make_async_remote_copy(
            view(job, rc, g * 4 + k), target, bsend.at[event, job], brecv.at[event, job],
            device_id=peer, device_id_type=MESH_ID,
        )

    def landed(event, job):
        rc, rb, ra, rz = buffers[jobs[job][0]][:4]
        if event < 8:
            target = view(job, rb, event)
        elif event < 12:
            target = view(job, ra, event - 8)
        else:
            target = view(job, rz, event - 12)
        pltpu.make_async_remote_copy(
            target, target, bsend.at[event, job], brecv.at[event, job], device_id=(p, 1 - c), device_id_type=MESH_ID
        ).wait_recv()
        return target

    def add_up(parts, target):
        rows = target.shape[0]
        step = math.gcd(rows, 16)

        @pl.loop(0, rows // step)
        def _(n):
            at = pl.ds(pl.multiple_of(n * step, step), step)
            total = parts[0][at].astype(jnp.float32)
            for part in parts[1:]:
                total = total + part[at].astype(jnp.float32)
            target[at] = total.astype(target.dtype)

    def flow(sums, got, sends, recvs, upwards, distance):
        side = 0 if upwards else 1
        return pltpu.make_async_remote_copy(
            sums(distance if upwards else 4 - distance), got(3 * side + distance - 1),
            sends(side, distance - 1), recvs(side, distance - 1),
            device_id=up if upwards else down, device_id_type=MESH_ID,
        )

    def flow_landed(got, sends, recvs, upwards, left):
        side = 0 if upwards else 1
        spot = got(3 * side + left)
        pltpu.make_async_remote_copy(
            spot, spot, sends(side, left), recvs(side, left), device_id=(p, 1 - c), device_id_type=MESH_ID
        ).wait_recv()
        return spot

    def flow_step(sums, got, sends, recvs, distance):
        for upwards in (True, False):

            @pl.when(z + distance <= 3 if upwards else z >= distance)
            def _():
                if distance < 3:

                    @pl.when(z > 0 if upwards else z < 3)
                    def _():
                        here = sums(distance if upwards else 4 - distance)
                        add_up([here, flow_landed(got, sends, recvs, upwards, distance)], here)

                flow(sums, got, sends, recvs, upwards, distance).start()

    def flow_finish(parts, got, sends, recvs, target):
        @pl.when(z == 0)
        def _():
            add_up(parts + [flow_landed(got, sends, recvs, False, 0)], target)

        @pl.when(z == 3)
        def _():
            add_up(parts + [flow_landed(got, sends, recvs, True, 0)], target)

        @pl.when((z > 0) & (z < 3))
        def _():
            both_ways = [flow_landed(got, sends, recvs, way, 0) for way in (True, False)]
            add_up(parts + both_ways, target)

    def flow_sent(sums, got, sends, recvs):
        for distance in (1, 2, 3):
            for upwards in (True, False):

                @pl.when(z + distance <= 3 if upwards else z >= distance)
                def _():
                    flow(sums, got, sends, recvs, upwards, distance).wait_send()

    line_flow = (
        lambda k: line_sums.at[k],
        lambda slot: line_got.at[slot],
        lambda side, n: line_send.at[side, n],
        lambda side, n: line_recv.at[side, n],
    )

    def start(i, job):
        to_core(i, job).start()
        load(i, job).start()

    def final_copies(job):
        a, j = jobs[job]
        rows = layouts[a][1]
        return [pltpu.make_async_copy(view(job, buffers[a][5], 0), outs[a].at[pl.ds(j * rows, rows)], out_sem.at[job, 0])]

    line_loads = [
        [pltpu.make_async_copy(ref.at[k], line_parts.at[k, n], line_load_sems.at[k, n]) for n, ref in enumerate(line_grads)]
        for k in range(4)
    ]
    def line_step(k):
        for load_part in line_loads[k]:
            load_part.wait()
        add_up([line_parts.at[k, n] for n in range(4)], line_sums.at[k])

    half = line_sum.shape[0]
    spot = line_out.at[pl.ds(pl.multiple_of(c * half, 8), half)]
    line_stores = [
        pltpu.make_async_copy(line_sum, spot, line_sems.at[7]),
        pltpu.make_async_remote_copy(
            line_sum, spot, line_sems.at[8], line_sems.at[9], device_id=(p, 1 - c), device_id_type=MESH_ID
        ),
    ]

    def line_finish():
        flow_finish([line_sums.at[0]], *line_flow[1:], line_sum)
        for copy in line_stores:
            copy.start()

    def step(i, job):
        g, k = SUM_ORDER[i]
        rc, rb, ra, rz, own, done = buffers[jobs[job][0]]
        load(i, job).wait()
        to_core(i, job).wait_recv()
        here = view(job, rc, g * 4 + k)
        parts = [here, view(job, own, i % AHEAD)]
        if g == 1:
            parts.append(landed(4 + k, job))
        if g == 0:
            parts.append(landed(k, job))
            parts.append(landed(8 + k, job))
        if (g, k) == (0, 0):
            parts += [landed(12 + n, job) for n in range(3)]
            add_up(parts, view(job, done, 0))
            for copy in final_copies(job):
                copy.start()
        else:
            add_up(parts, here)
            onward(i, job).start()
        if i + AHEAD < 16:
            start(i + AHEAD, job)

    for k in (1, 3, 2, 0):
        for load_part in line_loads[k]:
            load_part.start()
    for job in range(len(jobs)):
        for n in range(AHEAD):
            start(n, job)
    steps = []
    for job in range(len(jobs)):
        begin = stagger * min(job, layouts[0][0] - 1)
        for i in range(16):
            steps.append((begin + i + 2 * (i // 4 - 1) * (i // 8), job, i))
    steps.append((max(steps)[0] - 6, 0, -1))
    for n, k in enumerate((1, 3, 2, 0)):
        steps.append((n, len(jobs), -2 - k))
    for n, distance in enumerate((3, 2, 1)):
        steps.append((4 + 3 * n, len(jobs), -5 - distance))
    for _, job, i in sorted(steps):
        if i == -1:
            line_finish()
        elif i < -5:
            flow_step(*line_flow, -5 - i)
        elif i < 0:
            line_step(-2 - i)
        else:
            step(i, job)
    for job in range(len(jobs)):
        for i in range(16):
            to_core(i, job).wait_send()
            if i < 15:
                onward(i, job).wait_send()
        for copy in final_copies(job):
            copy.wait()
    flow_sent(*line_flow)
    for copy in line_stores:
        copy.wait()


def scatter_sum(layouts, stagger, grads, lines, name_id):
    jobs = sum(l[0] for l in layouts)
    scratch = [
        pltpu.SemaphoreType.DMA((16, jobs)),
        pltpu.SemaphoreType.DMA((16, jobs)),
        pltpu.SemaphoreType.DMA((15, jobs)),
        pltpu.SemaphoreType.DMA((15, jobs)),
        pltpu.SemaphoreType.DMA((16, jobs)),
        pltpu.SemaphoreType.DMA((jobs, 3)),
    ]
    shapes = []
    for layout, grad in zip(layouts, grads):
        rows, width = layout[0] * layout[1], grad.shape[1]
        for slots in (16, 8, 4, 3, AHEAD):
            scratch.append(pltpu.VMEM((slots, rows, width), grad.dtype))
        scratch.append(pltpu.VMEM((1, rows, width), jnp.float32))
        shapes.append(jax.ShapeDtypeStruct((rows, width), jnp.float32))
    piece, kind = lines[-1].shape[1:], lines[-1].dtype
    scratch += [
        pltpu.VMEM((4, 4) + piece, kind),
        pltpu.VMEM((4,) + piece, kind),
        pltpu.VMEM((6,) + piece, kind),
        pltpu.VMEM(piece, kind),
        pltpu.SemaphoreType.DMA((10,)),
        pltpu.SemaphoreType.DMA((4, 4)),
        pltpu.SemaphoreType.DMA((2, 3)),
        pltpu.SemaphoreType.DMA((2, 3)),
    ]
    shapes.append(jax.ShapeDtypeStruct((2 * piece[0], piece[1]), kind))
    everywhere = pl.BlockSpec(memory_space=pl.ANY)
    return pl.pallas_call(
        functools.partial(scatter_kernel, layouts, stagger),
        out_shape=shapes,
        in_specs=[everywhere] * (len(grads) + len(lines)),
        out_specs=[everywhere] * len(shapes),
        scratch_shapes=scratch,
        compiler_params=pltpu.CompilerParams(
            collective_id=name_id, has_side_effects=True, vmem_limit_bytes=48 * 1024 * 1024
        ),
        name="scatter_sum",
    )(*grads, *lines)


GELU_A = math.sqrt(2.0 / math.pi)
GELU_B = 0.044715


def chunk_sources(first):
    p, c, z, _, _, _ = places()
    x, y = p % 2, (p // 2) % 2
    out = []
    for n in range(4):
        owner_z = (first + n) % 4
        k = (owner_z - z + 4) % 4
        for half in range(2):
            for other in range(2):
                core = (c + other) % 2
                for g in range(4):
                    dx = (1 - core) * (g % 2) + core * (g // 2)
                    dy = (1 - core) * (g // 2) + core * (g % 2)
                    owner = owner_z * 4 + ((y + dy) % 2) * 2 + (x + dx) % 2
                    out.append((other, g, k, half, block_chunk(owner, core, half) // BLOCK))
    return out


def panel_loads(refs, held, sems, first):
    if len(refs) == 1:
        for n in range(held.shape[0] // WIDE):
            at = pl.ds(n * WIDE, WIDE)
            pltpu.make_async_copy(refs[0].at[at], held.at[at], sems.at[n]).start()
        return
    for other, g, k, half, chunk in chunk_sources(first):
        source = refs[other * 4 + g].at[k, pl.ds(half * BLOCK, BLOCK)]
        target = held.at[pl.ds(pl.multiple_of(chunk * BLOCK, BLOCK), BLOCK)]
        pltpu.make_async_copy(source, target, sems.at[chunk // 8]).start()


def panel_ready(held, sems, n):
    at = pl.ds(pl.multiple_of(n * WIDE, WIDE), WIDE)
    pltpu.make_async_copy(held.at[at], held.at[at], sems.at[n]).wait()
    return held.at[at]


def mlp_fwd_kernel(count, *refs):
    sources = refs[:count]
    h_ref, s_ref, up_ref, act_ref, grid_ref, held, total, sems = refs[count:]
    step = pl.program_id(0)
    steps = pl.num_programs(0)

    @pl.when(step == 0)
    def _():
        panel_loads(sources, held, sems, 0)
        total[...] = s_ref[...]

    up = product(h_ref[...], panel_ready(held, sems, step)[...])
    up_ref[0] = up
    act = 0.5 * up * (1.0 + jnp.tanh(GELU_A * (up + GELU_B * up * up * up)))
    act = act.astype(jnp.bfloat16)
    act_ref[0] = act
    total[...] += product(act, panel_ready(held, sems, steps + step)[...])

    @pl.when(step == steps - 1)
    def _():
        grid_ref[...] = total[...].astype(jnp.bfloat16)


def mlp_fwd(panels, hidden, stream):
    rows = hidden.shape[0]
    steps = HID // WIDE
    whole = pl.BlockSpec((rows, WIDE), lambda n: (0, 0))
    part = pl.BlockSpec((1, rows, WIDE), lambda n: (n, 0, 0))
    return pl.pallas_call(
        functools.partial(mlp_fwd_kernel, len(panels)),
        grid=(steps,),
        in_specs=[pl.BlockSpec(memory_space=pl.ANY)] * len(panels) + [whole, whole],
        out_specs=[part, part, whole],
        out_shape=[
            jax.ShapeDtypeStruct((steps, rows, WIDE), jnp.float32),
            jax.ShapeDtypeStruct((steps, rows, WIDE), jnp.bfloat16),
            jax.ShapeDtypeStruct((rows, WIDE), jnp.bfloat16),
        ],
        scratch_shapes=[
            pltpu.VMEM((2 * HID, WIDE), jnp.bfloat16),
            pltpu.VMEM((rows, WIDE), jnp.float32),
            pltpu.SemaphoreType.DMA((2 * steps,)),
        ],
        compiler_params=pltpu.CompilerParams(vmem_limit_bytes=56 * 1024 * 1024),
        cost_estimate=BRIEF,
        name="mlp_fwd",
    )(*panels, hidden, stream)


def mlp_bwd_kernel(count, *refs):
    sources = refs[:count]
    outs = 2 if count > 1 else 1
    h_ref, g_ref, up_ref, act_ref = refs[count : count + 4]
    dh_ref = refs[count + 4]
    grads = refs[count + 5 : count + 5 + outs]
    held, staged, sems, out_sem = refs[count + 5 + outs :]
    step = pl.program_id(0)
    steps = pl.num_programs(0)

    @pl.when(step == 0)
    def _():
        panel_loads(sources, held, sems, 2)
        dh_ref[...] = jnp.zeros_like(dh_ref)

    def tn_dot(left, right):
        return lax.dot_general(left, right, (((0,), (0,)), ((), ())), preferred_element_type=jnp.float32)

    def drain(side):
        pltpu.make_async_copy(staged.at[side], staged.at[side], out_sem.at[side]).wait()

    def store(side):
        panel = side * steps + step
        source = staged.at[side]
        if count == 1:
            at = pl.ds(pl.multiple_of(panel * WIDE, WIDE), WIDE)
            pltpu.make_async_copy(source, grads[0].at[at], out_sem.at[side]).start()
            return
        p, c, z, _, _, _ = places()
        for n in range(8):
            if side == 0:
                owner, core, half = n, step // 2, step % 2
            else:
                row = step * 8 + n
                owner, core, half = 8 + row // 4, (n // 2) % 2, n % 2
            dx = (owner % 2 + p % 2) % 2
            dy = ((owner // 2) % 2 + (p // 2) % 2) % 2
            g = (1 - core) * (dx + 2 * dy) + core * (dy + 2 * dx)
            spot = g * 4 + (owner // 4 - z + 4) % 4
            at = pl.ds(pl.multiple_of(half * BLOCK, BLOCK), BLOCK)
            from_ref = source.at[pl.ds(n * BLOCK, BLOCK)]

            @pl.when((core + c) % 2 == 0)
            def _():
                pltpu.make_async_copy(from_ref, grads[0].at[spot, at], out_sem.at[side]).start()

            @pl.when((core + c) % 2 == 1)
            def _():
                pltpu.make_async_copy(from_ref, grads[1].at[spot, at], out_sem.at[side]).start()

    pulled = g_ref[...]

    @pl.when(step > 0)
    def _():
        drain(1)

    staged[1] = tn_dot(act_ref[0], pulled).astype(jnp.bfloat16)
    store(1)
    grad_act = nt_dot(pulled, panel_ready(held, sems, steps + step)[...])
    up = up_ref[0]
    square = up * up
    bend = jnp.tanh(GELU_A * up * (1.0 + GELU_B * square))
    slope = 0.5 * (1.0 + bend) + 0.5 * GELU_A * up * (1.0 - bend * bend) * (1.0 + 3.0 * GELU_B * square)
    grad_up = (grad_act * slope).astype(jnp.bfloat16)

    @pl.when(step > 0)
    def _():
        drain(0)

    staged[0] = tn_dot(h_ref[...], grad_up).astype(jnp.bfloat16)
    store(0)
    dh_ref[...] += nt_dot(grad_up, panel_ready(held, sems, step)[...])

    @pl.when(step == steps - 1)
    def _():
        drain(0)
        drain(1)


def mlp_bwd(panels, hidden, grad, up, act):
    rows = hidden.shape[0]
    steps = HID // WIDE
    whole = pl.BlockSpec((rows, WIDE), lambda n: (0, 0))
    part = pl.BlockSpec((1, rows, WIDE), lambda n: (n, 0, 0))
    if len(panels) == 1:
        shapes = [jax.ShapeDtypeStruct((2 * HID, WIDE), jnp.bfloat16)]
    else:
        shapes = [jax.ShapeDtypeStruct((16, 2 * BLOCK, WIDE), jnp.bfloat16)] * 2
    return pl.pallas_call(
        functools.partial(mlp_bwd_kernel, len(panels)),
        grid=(steps,),
        in_specs=[pl.BlockSpec(memory_space=pl.ANY)] * len(panels) + [whole, whole, part, part],
        out_specs=[whole] + [pl.BlockSpec(memory_space=pl.ANY)] * len(shapes),
        out_shape=[jax.ShapeDtypeStruct((rows, WIDE), jnp.float32)] + shapes,
        scratch_shapes=[
            pltpu.VMEM((2 * HID, WIDE), jnp.bfloat16),
            pltpu.VMEM((2, WIDE, WIDE), jnp.bfloat16),
            pltpu.SemaphoreType.DMA((2 * steps,)),
            pltpu.SemaphoreType.DMA((2,)),
        ],
        compiler_params=pltpu.CompilerParams(vmem_limit_bytes=58 * 1024 * 1024),
        cost_estimate=BRIEF,
        name="mlp_bwd",
    )(*panels, hidden, grad, up, act)


SLOT = 128
TAPS = 16


def spread_deconv_kernel(first, rows_ref, o_ref, raw, flat, turned, sem):
    load = pltpu.make_async_copy(rows_ref.at[pl.ds(first, raw.shape[0])], raw, sem)
    load.start()
    load.wait()
    whole = raw[...].reshape(TAPS * CH, WIDE).astype(jnp.float32)
    for n in range(WIDE // SLOT):
        flat[n] = whole[:, n * SLOT : (n + 1) * SLOT]
    lane = lax.broadcasted_iota(jnp.int32, (D // 4, SLOT), 1)

    def block(i, j):
        at = 10 * i + j
        return flat[at % 8, pl.ds(at // 8, D // 4, stride=5), :]

    for tap in range(TAPS):
        j, start = divmod(tap * CH, SLOT)
        for i in range(4):
            part = block(i, j)
            if start:
                part = pltpu.roll(part, SLOT - start, 1)
            if start + CH > SLOT:
                part = jnp.where(lane < SLOT - start, part, pltpu.roll(block(i, j + 1), SLOT - start, 1))
            turned[pl.ds(i, D // 4, stride=4), :] = jnp.where(lane < CH, part, 0.0)
        o_ref[:, tap * SLOT : (tap + 1) * SLOT] = turned[...].astype(jnp.bfloat16)


def spread_deconv(rows, first):
    return pl.pallas_call(
        functools.partial(spread_deconv_kernel, first),
        in_specs=[pl.BlockSpec(memory_space=pl.ANY)],
        out_specs=pl.BlockSpec(memory_space=pltpu.VMEM),
        out_shape=jax.ShapeDtypeStruct((D, TAPS * SLOT), jnp.bfloat16),
        scratch_shapes=[
            pltpu.VMEM((TAPS * CH // 8, 8, WIDE), jnp.bfloat16),
            pltpu.VMEM((WIDE // SLOT, TAPS * CH, SLOT), jnp.float32),
            pltpu.VMEM((D, SLOT), jnp.float32),
            pltpu.SemaphoreType.DMA,
        ],
        compiler_params=pltpu.CompilerParams(vmem_limit_bytes=32 * 1024 * 1024),
        name="spread_deconv",
    )(rows)


def with_edges(own, edge):
    place = lax.axis_index("strip")
    above = jnp.where(place == 0, jnp.zeros_like(edge), edge)
    below = jnp.where(place == 0, edge, jnp.zeros_like(edge))
    return jnp.concatenate([above, own, below], 0)


def moved(value, step):
    column = lax.broadcasted_iota(jnp.int32, value.shape, 0) % TC
    inside = (column + step >= 0) & (column + step < TC)
    return jnp.where(inside, pltpu.roll(value, (-step) % value.shape[0], 0), 0.0)


def deconv_fwd_kernel(grid_ref, edge_ref, w_ref, o_ref, taps, fine):
    padded = with_edges(grid_ref[0], edge_ref[0])
    rows = grid_ref.shape[1]
    taps[...] = product(padded, w_ref[...])

    def tap(kr, kc, r):
        slot = kr * 4 + kc
        return taps[pl.ds((r + 1) * TC, rows), slot * SLOT : (slot + 1) * SLOT]

    for i in range(2):
        for j in range(2):
            total = tap(i + 1, j + 1, 0) + tap(3 - 3 * i, j + 1, 2 * i - 1)
            side = tap(i + 1, 3 - 3 * j, 0) + tap(3 - 3 * i, 3 - 3 * j, 2 * i - 1)
            total = total + moved(side, 2 * j - 1)
            for a in range(rows // TC):
                fine[pl.ds((2 * a + i) * 2 * TC + j, TC, stride=2), :] = total[a * TC : (a + 1) * TC]
    o_ref[0] = fine[...].astype(jnp.bfloat16)


def deconv_fwd(grid, edge, weights):
    planes, rows, _ = grid.shape
    return pl.pallas_call(
        deconv_fwd_kernel,
        grid=(planes,),
        in_specs=[
            pl.BlockSpec((1, rows, D), lambda n: (n, 0, 0)),
            pl.BlockSpec((1, TC, D), lambda n: (n, 0, 0)),
            pl.BlockSpec(weights.shape, lambda n: (0, 0)),
        ],
        out_specs=pl.BlockSpec((1, 4 * rows, SLOT), lambda n: (n, 0, 0)),
        out_shape=jax.ShapeDtypeStruct((planes, 4 * rows, SLOT), jnp.bfloat16),
        scratch_shapes=[
            pltpu.VMEM((rows + 2 * TC, TAPS * SLOT), jnp.float32),
            pltpu.VMEM((4 * rows, SLOT), jnp.float32),
        ],
        compiler_params=pltpu.CompilerParams(vmem_limit_bytes=40 * 1024 * 1024),
        name="deconv_fwd",
    )(grid, edge, weights)


def deconv_bwd_kernel(own_ref, got_ref, grid_ref, edge_ref, w_ref, gx_ref, gedge_ref, gw_ref, fine, spread, tokens, sums, flat):
    plane = pl.program_id(0)
    rows = grid_ref.shape[1]
    high = rows + 2 * TC
    place = lax.axis_index("strip")
    total = own_ref[0].astype(jnp.float32) + got_ref[0].astype(jnp.float32)
    total = jnp.concatenate([total, jnp.zeros((SLOT - CH, total.shape[1]), jnp.float32)], 0)
    fine[...] = total.T
    here = pl.ds(plane * high, high)
    tokens[here] = with_edges(grid_ref[0], edge_ref[0])
    for i in range(2):
        for j in range(2):
            parts = [fine[pl.ds((2 * a + i) * 2 * TC + j, TC, stride=2), :] for a in range(rows // TC)]
            part = jnp.concatenate(parts, 0)
            for kr in (i + 1, 3 - 3 * i):
                for kc in (j + 1, 3 - 3 * j):
                    value = part if kc == j + 1 else moved(part, 1 - 2 * j)
                    start = TC if kr == i + 1 else (0 if i == 0 else 2 * TC)
                    pieces = [value]
                    if start:
                        pieces.insert(0, jnp.zeros((start, SLOT), jnp.float32))
                    if high - rows - start:
                        pieces.append(jnp.zeros((high - rows - start, SLOT), jnp.float32))
                    slot = kr * 4 + kc
                    spread[here, slot * SLOT : (slot + 1) * SLOT] = jnp.concatenate(pieces, 0).astype(jnp.bfloat16)
    back = nt_dot(spread[here], w_ref[...])
    gx_ref[0] = back[TC : TC + rows]
    gedge_ref[0] = jnp.where(place == 0, back[TC + rows :], back[:TC]).astype(jnp.bfloat16)

    @pl.when(plane == pl.num_programs(0) - 1)
    def _():
        wide = 512
        for n in range(TAPS * SLOT // wide):
            columns = slice(n * wide, (n + 1) * wide)
            part = lax.dot_general(
                tokens[...], spread[:, columns], (((0,), (0,)), ((), ())), preferred_element_type=jnp.float32
            )
            for m in range(wide // SLOT):
                sums[n * (wide // SLOT) + m] = part[:, m * SLOT : (m + 1) * SLOT]
        lane = lax.broadcasted_iota(jnp.int32, (D // 4, SLOT), 1)
        for i in range(4):
            for j in range(TAPS * CH // SLOT):
                block = None
                for tap in range(j * SLOT // CH, (j * SLOT + SLOT - 1) // CH + 1):
                    part = sums[tap, pl.ds(i, D // 4, stride=4), :]
                    shift = tap * CH - j * SLOT
                    if shift % SLOT:
                        part = pltpu.roll(part, shift % SLOT, 1)
                    block = part if block is None else jnp.where(lane < shift, block, part)
                at = 10 * i + j
                flat[at % 8, pl.ds(at // 8, D // 4, stride=5), :] = block
        whole = jnp.concatenate([flat[n] for n in range(WIDE // SLOT)], 1)
        gw_ref[...] = whole.astype(jnp.bfloat16).reshape(gw_ref.shape)


def deconv_bwd(own, got, grid, edge, weights):
    planes, rows, _ = grid.shape
    high = rows + 2 * TC
    by_plane = lambda *shape: pl.BlockSpec((1,) + shape, lambda n: (n, 0, 0))
    return pl.pallas_call(
        deconv_bwd_kernel,
        grid=(planes,),
        in_specs=[
            by_plane(*own.shape[1:]),
            by_plane(*got.shape[1:]),
            by_plane(rows, D),
            by_plane(TC, D),
            pl.BlockSpec(weights.shape, lambda n: (0, 0)),
        ],
        out_specs=[by_plane(rows, D), by_plane(TC, D), pl.BlockSpec((TAPS * CH // 8, 8, WIDE), lambda n: (0, 0, 0))],
        out_shape=[
            jax.ShapeDtypeStruct((planes, rows, D), jnp.float32),
            jax.ShapeDtypeStruct((planes, TC, D), jnp.bfloat16),
            jax.ShapeDtypeStruct((TAPS * CH // 8, 8, WIDE), jnp.bfloat16),
        ],
        scratch_shapes=[
            pltpu.VMEM((4 * rows, SLOT), jnp.float32),
            pltpu.VMEM((planes * high, TAPS * SLOT), jnp.bfloat16),
            pltpu.VMEM((planes * high, D), jnp.bfloat16),
            pltpu.VMEM((TAPS, D, SLOT), jnp.float32),
            pltpu.VMEM((WIDE // SLOT, TAPS * CH, SLOT), jnp.float32),
        ],
        compiler_params=pltpu.CompilerParams(vmem_limit_bytes=56 * 1024 * 1024),
        name="deconv_bwd",
    )(own, got, grid, edge, weights)


def panel_view(rows_ref, first, count, depth):
    region = rows_ref.at[pl.ds(first, depth // 8 * count)]
    return region.reshape(depth // 8, count, 8, WIDE)


def project_kernel(first, count, depth, lead, x_ref, rows_ref, *rest):
    outs, held, sems = rest[:-2], rest[-2], rest[-1]
    step = pl.program_id(0)
    panels = panel_view(rows_ref, first, count, depth)

    @pl.when(step == 0)
    def _():
        for n in range(count):
            pltpu.make_async_copy(panels.at[:, n], held.at[n], sems.at[n]).start()

    pltpu.make_async_copy(held.at[step], held.at[step], sems.at[step]).wait()
    result = product(x_ref[...], held[step].reshape(depth, WIDE)).astype(jnp.bfloat16)
    if lead:

        @pl.when(step == 0)
        def _():
            outs[0][...] = result

        @pl.when(step > 0)
        def _():
            outs[1][0] = result

    else:
        outs[0][0] = result


def project(x, rows, first, count, lead):
    tokens, depth = x.shape
    specs = [pl.BlockSpec((1, tokens, WIDE), lambda n: (jnp.maximum(n - lead, 0), 0, 0))]
    shapes = [jax.ShapeDtypeStruct((count - lead, tokens, WIDE), jnp.bfloat16)]
    if lead:
        specs.insert(0, pl.BlockSpec((tokens, WIDE), lambda n: (0, 0)))
        shapes.insert(0, jax.ShapeDtypeStruct((tokens, WIDE), jnp.bfloat16))
    return pl.pallas_call(
        functools.partial(project_kernel, first, count, depth, lead),
        grid=(count,),
        in_specs=[pl.BlockSpec((tokens, depth), lambda n: (0, 0)), pl.BlockSpec(memory_space=pl.ANY)],
        out_specs=specs,
        out_shape=shapes,
        scratch_shapes=[pltpu.VMEM((count, depth // 8, 8, WIDE), jnp.bfloat16), pltpu.SemaphoreType.DMA((count,))],
        compiler_params=pltpu.CompilerParams(vmem_limit_bytes=32 * 1024 * 1024),
        cost_estimate=BRIEF,
        name="project",
    )(x, rows)


def project_back_kernel(first, count, depth, lead_ref, own_ref, far_ref, rows_ref, o_ref, sum_ref, held, sems):
    step = pl.program_id(0)
    panels = panel_view(rows_ref, first, count, depth)

    @pl.when(step == 0)
    def _():
        for n in range(count):
            pltpu.make_async_copy(panels.at[:, n], held.at[n], sems.at[n]).start()

    pltpu.make_async_copy(held.at[step], held.at[step], sems.at[step]).wait()
    both = (own_ref[0].astype(jnp.float32) + far_ref[0].astype(jnp.float32)).astype(jnp.bfloat16)
    sum_ref[0] = both
    grad = jnp.where(step == 0, lead_ref[...], both)
    back = nt_dot(grad, held[step].reshape(depth, WIDE))

    @pl.when(step == 0)
    def _():
        o_ref[...] = back

    @pl.when(step > 0)
    def _():
        o_ref[...] += back


def project_back(lead, own, far, rows, first, depth):
    others, tokens, _ = own.shape
    count = others + 1
    panel = pl.BlockSpec((1, tokens, WIDE), lambda n: (jnp.maximum(n - 1, 0), 0, 0))
    return pl.pallas_call(
        functools.partial(project_back_kernel, first, count, depth),
        grid=(count,),
        in_specs=[
            pl.BlockSpec((tokens, WIDE), lambda n: (0, 0)),
            panel,
            panel,
            pl.BlockSpec(memory_space=pl.ANY),
        ],
        out_specs=[pl.BlockSpec((tokens, depth), lambda n: (0, 0)), panel],
        out_shape=[
            jax.ShapeDtypeStruct((tokens, depth), jnp.float32),
            jax.ShapeDtypeStruct((others, tokens, WIDE), jnp.bfloat16),
        ],
        scratch_shapes=[pltpu.VMEM((count, depth // 8, 8, WIDE), jnp.bfloat16), pltpu.SemaphoreType.DMA((count,))],
        compiler_params=pltpu.CompilerParams(vmem_limit_bytes=44 * 1024 * 1024),
        cost_estimate=BRIEF,
        name="project_back",
    )(lead, own, far, rows)


def weight_grads_kernel(products, copies, *refs):
    arrays = refs[: len(refs) - 9]
    out, left, right, staged, bounce, nothing, load_sem, store_sem, copy_sem = refs[len(refs) - 9 :]
    place = lax.axis_index("strip")
    step = pl.program_id(0)
    steps = len(products)

    def loads(n):
        side, (a, a_pick), (b, b_pick), _, _ = products[n]
        slot = n % 2
        source_a = arrays[a] if a_pick is None else arrays[a].at[a_pick]
        source_b = arrays[b] if b_pick is None else arrays[b].at[b_pick]
        rows, deep = side
        return [
            pltpu.make_async_copy(source_a, left.at[slot, pl.ds(0, rows), pl.ds(0, deep)], load_sem.at[slot, 0]),
            pltpu.make_async_copy(source_b, right.at[slot, pl.ds(0, rows)], load_sem.at[slot, 1]),
        ]

    def stores(n):
        (rows, deep), _, _, first, panels = products[n]
        slot = n % 2
        count, at = panels
        source = staged.at[slot, pl.ds(0, deep // 8)]
        target = panel_view(out, first, count, deep).at[:, at]
        return pltpu.make_async_copy(source, target, store_sem.at[slot])

    def bring(n):
        a, start, count, _, _ = copies[n]
        held = bounce.at[pl.ds(sum(c[2] for c in copies[:n] if c[0] is not None), count)]
        return pltpu.make_async_copy(arrays[a].at[pl.ds(start, count)], held, copy_sem.at[n, 0])

    def put(n):
        a, _, count, first, step = copies[n]
        if a is None:
            held = nothing.at[pl.ds(0, count)]
        else:
            held = bounce.at[pl.ds(sum(c[2] for c in copies[:n] if c[0] is not None), count)]
        return pltpu.make_async_copy(held, out.at[pl.ds(first + step * place, count)], copy_sem.at[n, 1])

    for n in range(steps):

        @pl.when(step == n)
        def _():
            if n == 0:
                for job in loads(0):
                    job.start()
                nothing[...] = jnp.zeros_like(nothing)
                for m in range(len(copies)):
                    if copies[m][0] is not None:
                        bring(m).start()
            if n == 1:
                for m in range(len(copies)):
                    if copies[m][0] is not None:
                        bring(m).wait()
                    put(m).start()
            if n + 1 < steps:
                for job in loads(n + 1):
                    job.start()
            for job in loads(n):
                job.wait()
            if n >= 2:
                stores(n - 2).wait()
            rows, deep = products[n][0]
            slot = n % 2
            total = lax.dot_general(
                left[slot, :rows, :deep], right[slot, :rows], (((0,), (0,)), ((), ())), preferred_element_type=jnp.float32
            )
            staged[slot, : deep // 8] = total.astype(jnp.bfloat16).reshape(deep // 8, 8, WIDE)
            stores(n).start()
            if n == steps - 1:
                if n > 0:
                    stores(n - 1).wait()
                stores(n).wait()
                for m in range(len(copies)):
                    put(m).wait()


def weight_grads(arrays, products, copies, tile_rows):
    rows = max(p[0][0] for p in products)
    deep = max(p[0][1] for p in products)
    everywhere = pl.BlockSpec(memory_space=pl.ANY)
    return pl.pallas_call(
        functools.partial(weight_grads_kernel, products, copies),
        grid=(len(products),),
        in_specs=[everywhere] * len(arrays),
        out_specs=everywhere,
        out_shape=jax.ShapeDtypeStruct((tile_rows, 8, WIDE), jnp.bfloat16),
        scratch_shapes=[
            pltpu.VMEM((2, rows, deep), jnp.bfloat16),
            pltpu.VMEM((2, rows, WIDE), jnp.bfloat16),
            pltpu.VMEM((2, deep // 8, 8, WIDE), jnp.bfloat16),
            pltpu.VMEM((sum(c[2] for c in copies if c[0] is not None), 8, WIDE), jnp.bfloat16),
            pltpu.VMEM((max(c[2] for c in copies if c[0] is None), 8, WIDE), jnp.bfloat16),
            pltpu.SemaphoreType.DMA((2, 2)),
            pltpu.SemaphoreType.DMA((2,)),
            pltpu.SemaphoreType.DMA((len(copies), 2)),
        ],
        compiler_params=pltpu.CompilerParams(vmem_limit_bytes=60 * 1024 * 1024),
        cost_estimate=BRIEF,
        name="weight_grads",
    )(*arrays)


TILE = 8 * WIDE
KV_AT = D * D
QKV_AT = KV_AT + DI * 2 * D + D * D
GAP_AT = QKV_AT + D * 3 * D + D * D + D * 16 * CH + CH * DEC_HID + DEC_HID * 4
QKV_GAP = -QKV_AT % (3 * TILE)
END_GAP = -GAP_AT % TILE
TILES = {}
_tile = 0
for _name, _rows in (
    ("query_cross", D),
    ("keyval_cross", 2 * DI),
    ("out_cross", D),
    ("gap", QKV_GAP // WIDE),
    ("qkv_self", 3 * D),
    ("out_self", D),
    ("deconv", 16 * CH),
    ("decode", 8),
    ("modulate", 6 * NCAM),
    ("triplane", 0),
):
    TILES[_name] = _tile
    _tile += _rows // 8


def direct_links():
    return lax.axis_size("dp") == 16 and lax.axis_size("strip") == 2


def regroup(rows, first, back):
    tile = first + lax.broadcasted_iota(jnp.int32, (rows.shape[0], 1), 0) // 8

    def turned(panels):
        shape = (-1, panels, 8, WIDE) if back else (-1, 8, panels, WIDE)
        return rows.reshape(shape).transpose(0, 2, 1, 3).reshape(rows.shape)

    in_kv = (tile >= TILES["keyval_cross"]) & (tile < TILES["out_cross"])
    in_qkv = (tile >= TILES["qkv_self"]) & (tile < TILES["out_self"])
    return jnp.where(in_kv, turned(2), jnp.where(in_qkv, turned(3), rows))


def tile_rows(length):
    return -(-length // (6 * TILE)) * 6


LANES = 128
TILE_LINES = TILE // LANES


def tile_place(tile):
    gap = QKV_GAP // LANES * jnp.where(tile >= TILES["gap"], 1, 0)
    return gap + END_GAP // LANES * jnp.where(tile >= TILES["modulate"], 1, 0)


def by_region(tile, work):
    in_kv = (tile >= TILES["keyval_cross"]) & (tile < TILES["out_cross"])
    in_qkv = (tile >= TILES["qkv_self"]) & (tile < TILES["out_self"])

    @pl.when(in_kv)
    def _():
        work(2)

    @pl.when(in_qkv)
    def _():
        work(3)

    @pl.when(jnp.logical_not(in_kv | in_qkv))
    def _():
        work(1)


def tile_lines(tile, first, panels):
    panel = lax.rem(tile, panels)
    return (tile - panel - first) * TILE_LINES + panel * 8


def prepare_kernel(own_ref, next_ref, blocks_ref, o_ref, chunks_ref, lines, tiles, sem):
    half = tiles.shape[0]
    core = lax.axis_index("strip")
    load = pltpu.make_async_copy(blocks_ref.at[pl.ds(core * half, half)], tiles, sem)
    load.start()
    place = lax.axis_index("dp") * 2 + core
    count = own_ref.shape[0]
    lines[:count] = own_ref[...]
    lines[count : count + next_ref.shape[0]] = next_ref[...]
    held = o_ref.shape[0] // 8
    first = place * held
    shift = place * (held * TILE_LINES - count)

    @pl.loop(0, held // 2)
    def _(n):
        def work(panels):
            rows = []
            for m in range(2):
                tile = first + 2 * n + m
                start = tile_lines(tile, first, panels) + shift - tile_place(tile)
                rows.append(jnp.concatenate([lines[pl.ds(start + j, 8, stride=8 * panels), :] for j in range(8)], 1))
            o_ref[pl.ds(pl.multiple_of(16 * n, 16), 16)] = jnp.concatenate(rows, 0).astype(jnp.bfloat16)

        by_region(first + 2 * n, work)

    load.wait()
    for n in range(half):
        at, column = n // 8 * BLOCK, n % 8 * BLOCK
        chunks_ref[at : at + BLOCK, column : column + BLOCK] = tiles[n].astype(jnp.bfloat16)


def prepare(weights, blocks):
    lines = weights.reshape(-1, LANES)
    count = lines.shape[0]
    held = tile_rows(weights.shape[0])
    reach = -(-32 * (held * TILE_LINES - count) // 8) * 8
    following = lax.ppermute(lines[:reach], AXES, [(n + 1, n) for n in range(31)])
    half = blocks.shape[0] // 2
    vmem = pl.BlockSpec(memory_space=pltpu.VMEM)
    return pl.pallas_call(
        prepare_kernel,
        in_specs=[vmem, vmem, pl.BlockSpec(memory_space=pl.ANY)],
        out_specs=[vmem, vmem],
        out_shape=[
            jax.ShapeDtypeStruct((held * 8, WIDE), jnp.bfloat16),
            jax.ShapeDtypeStruct((half // 8 * BLOCK, WIDE), jnp.bfloat16),
        ],
        scratch_shapes=[
            pltpu.VMEM((-(-(count + reach) // 8) * 8, LANES), jnp.float32),
            pltpu.VMEM((half, BLOCK, BLOCK), jnp.float32),
            pltpu.SemaphoreType.DMA,
        ],
        compiler_params=pltpu.CompilerParams(vmem_limit_bytes=16 * 1024 * 1024),
        name="prepare",
    )(lines, following, blocks)


def ungroup_kernel(rows_ref, o_ref):
    place = lax.axis_index("dp") * 2 + lax.axis_index("strip")
    held = rows_ref.shape[0] // 8
    first = place * held

    @pl.loop(0, held)
    def _(n):
        def work(panels):
            start = tile_lines(first + n, first, panels)
            at = pl.ds(pl.multiple_of(8 * n, 8), 8)
            for j in range(8):
                o_ref[pl.ds(start + j, 8, stride=8 * panels), :] = rows_ref[at, j * LANES : (j + 1) * LANES]

        by_region(first + n, work)


def ungroup(rows):
    vmem = pl.BlockSpec(memory_space=pltpu.VMEM)
    return pl.pallas_call(
        ungroup_kernel,
        in_specs=[vmem],
        out_specs=vmem,
        out_shape=jax.ShapeDtypeStruct((rows.size // LANES, LANES), jnp.float32),
        compiler_params=pltpu.CompilerParams(vmem_limit_bytes=16 * 1024 * 1024),
        name="ungroup",
    )(rows)


def adam_kernel(before_ref, sum_ref, w_ref, first_ref, second_ref, nw_ref, nfirst_ref, nsecond_ref, lines):
    place = lax.axis_index("dp") * 2 + lax.axis_index("strip")
    reach, summed, count = before_ref.shape[0], sum_ref.shape[0], w_ref.shape[0]
    lines[:reach] = before_ref[...]
    lines[reach : reach + summed] = sum_ref[...]
    shift = reach - place * (summed - count)
    gaps = (0, QKV_GAP // LANES, (QKV_GAP + END_GAP) // LANES)

    def update(at, rows):
        parts = [lines[pl.ds(shift + at + gap, rows), :] for gap in gaps]
        line = place * count + at + lax.broadcasted_iota(jnp.int32, (rows, LANES), 0)
        grad = jnp.where(line < QKV_AT // LANES, parts[0], jnp.where(line < GAP_AT // LANES, parts[1], parts[2]))
        here = pl.ds(at, rows)
        weights = w_ref[here]
        first = BETA_FIRST * first_ref[here] + (1.0 - BETA_FIRST) * grad
        second = BETA_SECOND * second_ref[here] + (1.0 - BETA_SECOND) * grad * grad
        nfirst_ref[here] = first
        nsecond_ref[here] = second
        fix_first = 1.0 - BETA_FIRST**ADAM_STEP
        fix_second = 1.0 - BETA_SECOND**ADAM_STEP
        step = first / fix_first / (jnp.sqrt(second / fix_second) + ADAM_EPS)
        nw_ref[here] = weights - ADAM_RATE * (step + WEIGHT_DECAY * weights)

    block = 32

    @pl.loop(0, count // block)
    def _(n):
        update(pl.multiple_of(block * n, block), block)

    if count % block:
        update(count - count % block, count % block)


def adam(rows, weights, first_moment, second_moment):
    length = weights.shape[0]
    count = length // LANES
    summed = ungroup(rows)
    reach = -(-32 * (summed.shape[0] - count) // 8) * 8
    before = lax.ppermute(summed[summed.shape[0] - reach :], AXES, [(n, n + 1) for n in range(31)])
    vmem = pl.BlockSpec(memory_space=pltpu.VMEM)
    gap = (QKV_GAP + END_GAP) // LANES
    results = pl.pallas_call(
        adam_kernel,
        in_specs=[vmem] * 5,
        out_specs=[vmem] * 3,
        out_shape=[jax.ShapeDtypeStruct((count, LANES), jnp.float32)] * 3,
        scratch_shapes=[pltpu.VMEM((-(-(reach + summed.shape[0] + gap) // 8) * 8, LANES), jnp.float32)],
        compiler_params=pltpu.CompilerParams(vmem_limit_bytes=32 * 1024 * 1024),
        name="adam",
    )(before, summed, *(a.reshape(count, LANES) for a in (weights, first_moment, second_moment)))
    return [result.reshape(length) for result in results]


def two_parts(value):
    coarse = value.astype(jnp.bfloat16)
    return coarse, (value - coarse.astype(jnp.float32)).astype(jnp.bfloat16)


def shampoo_kernel(tiles_ref, blocks_ref, sl_ref, sr_ref, rl_ref, rr_ref, nb_ref, g_ref, nl_ref, nr_ref, rms_ref):
    count = blocks_ref.shape[0]
    grads = [tiles_ref[:, n * BLOCK : (n + 1) * BLOCK] for n in range(count)]
    halves = []
    for n, grad in enumerate(grads):
        coarse, fine = two_parts(rr_ref[n])
        half = product(grad, jnp.concatenate([coarse, fine], 1))
        halves.append(half[:, :BLOCK] + half[:, BLOCK:])
    for n, grad in enumerate(grads):
        g_ref[n] = grad.astype(jnp.float32)
        nl_ref[n] = STAT_DECAY * sl_ref[n] + (1.0 - STAT_DECAY) * nt_dot(grad, grad)
        square = lax.dot_general(grad, grad, (((0,), (0,)), ((), ())), preferred_element_type=jnp.float32)
        nr_ref[n] = STAT_DECAY * sr_ref[n] + (1.0 - STAT_DECAY) * square
    conds = []
    for n, half in enumerate(halves):
        half_coarse, half_fine = two_parts(half)
        coarse, fine = two_parts(rl_ref[n])
        cond = product(jnp.concatenate([coarse, fine], 1), jnp.concatenate([half_coarse, half_coarse], 0))
        conds.append(cond + product(coarse, half_fine))
    for n, cond in enumerate(conds):
        rms = jnp.sqrt(jnp.mean(cond * cond, axis=(0, 1), keepdims=True) + RMS_EPS)
        nb_ref[n] = blocks_ref[n] - (SHAMPOO_RATE / rms) * cond
        rms_ref[n : n + 1] = jnp.broadcast_to(rms, (1, LANES))


def shampoo(chunks, blocks, stat_left, stat_right, root_left, root_right):
    count = blocks.shape[0]
    eight = pl.BlockSpec((8, BLOCK, BLOCK), lambda n: (n, 0, 0))
    whole = jax.ShapeDtypeStruct(blocks.shape, jnp.float32)
    *results, rms = pl.pallas_call(
        shampoo_kernel,
        grid=(count // 8,),
        in_specs=[pl.BlockSpec((BLOCK, WIDE), lambda n: (n, 0))] + [eight] * 5,
        out_specs=[eight] * 4 + [pl.BlockSpec((8, LANES), lambda n: (n, 0))],
        out_shape=[whole] * 4 + [jax.ShapeDtypeStruct((count, LANES), jnp.float32)],
        compiler_params=pltpu.CompilerParams(vmem_limit_bytes=60 * 1024 * 1024),
        name="shampoo",
    )(chunks, blocks, stat_left, stat_right, root_left, root_right)
    return *results, rms[:, 0]


def chunks_of(tiles):
    return tiles.reshape(-1, 8, BLOCK, BLOCK).transpose(0, 2, 1, 3).reshape(-1, WIDE)


def tiles_of(chunks):
    return chunks.reshape(-1, BLOCK, 8, BLOCK).transpose(0, 2, 1, 3).reshape(-1, BLOCK, BLOCK)


def panels_of(chunks):
    half = chunks.shape[0] // 2
    first = chunks[:half].reshape(D // BLOCK, HID // WIDE, BLOCK, WIDE).transpose(1, 0, 2, 3)
    return jnp.concatenate([first.reshape(half, WIDE), chunks[half:]])


def chunks_of_panels(panels):
    half = panels.shape[0] // 2
    first = panels[:half].reshape(HID // WIDE, D // BLOCK, BLOCK, WIDE).transpose(1, 0, 2, 3)
    return jnp.concatenate([first.reshape(half, WIDE), panels[half:]])


META = (1, 8, lambda p, c, j: (2 * p + c) * 8)
SWAP = ((0, 1), (1, 0))
AXES = ("dp", "strip")


def pairs_to(target):
    return [(2 * p + c, sum(v * w for v, w in zip(target(p, c), (2, 1)))) for p in range(16) for c in range(2)]


NEAR = pairs_to(lambda p, c: (p ^ (1 + c), c))
FAR = pairs_to(lambda p, c: (p ^ (2 - c), c))
CORE = pairs_to(lambda p, c: (p, 1 - c))


def gather_weights(weights, blocks, part):
    if direct_links():
        own, tiles = prepare(weights, blocks)
        rows, parts, line = gather_all([flat_chunks(own.shape[0], 3), META], 4, [own, part], tiles, 0)
        near = lax.ppermute(line, AXES, NEAR)
        return rows, [line, near], jnp.sum(parts[::8, 0])
    flat = lax.all_gather(weights.astype(jnp.bfloat16), AXES, axis=0, tiled=True)
    tiles = lax.all_gather(blocks.astype(jnp.bfloat16), "dp", axis=0, tiled=True)
    gaps = [jnp.zeros((QKV_GAP,), flat.dtype), jnp.zeros((END_GAP,), flat.dtype)]
    rows = jnp.concatenate([flat[:QKV_AT], gaps[0], flat[QKV_AT:GAP_AT], gaps[1], flat[GAP_AT:]])
    rows = jnp.pad(rows, (0, -rows.shape[0] % (6 * TILE))).reshape(-1, WIDE)
    return regroup(rows, 0, False), [panels_of(chunks_of(tiles))], lax.psum(part[0, 0], AXES)


class Panels:
    def __init__(self, parts):
        self.parts = parts
        self.staged = len(parts) > 1

    def first(self, before):
        if not self.staged:
            return before
        line, near = self.parts
        near, before = lax.optimization_barrier((near, before))
        self.parts = [line, near, lax.ppermute(line, AXES, FAR)]
        return before

    def second(self, before):
        if not self.staged:
            return before
        line, near, far = self.parts
        far, before = lax.optimization_barrier((far, before))
        self.parts = [line, near, far, lax.ppermute(near, AXES, FAR)]
        return before

    def third(self, after, beside):
        if not self.staged:
            return self.parts, beside
        line, near, far, both = self.parts
        both, after, beside = lax.optimization_barrier((both, after, beside))
        others = [lax.ppermute(group, AXES, CORE) for group in (line, near, far, both)]
        return [line, near, far, both] + others, beside


class PanelSums:
    def __init__(self, grads):
        self.parts = grads
        self.staged = len(grads) > 1
        if self.staged:
            self.mine = grads[0]
            self.got = lax.ppermute(grads[1], AXES, CORE)

    def added(self, at, *parts):
        total = self.mine[at].astype(jnp.float32) + self.got[at].astype(jnp.float32)
        for part in parts:
            total = total + part.astype(jnp.float32)
        return total.astype(jnp.bfloat16)

    def first(self, before):
        if not self.staged:
            return before
        away, before = lax.optimization_barrier((self.added(slice(8, 16)), before))
        self.away = lax.ppermute(away, AXES, FAR)
        return before

    def second(self, before):
        if not self.staged:
            return before
        self.away, before = lax.optimization_barrier((self.away, before))
        near, before = lax.optimization_barrier((self.added(slice(4, 8), self.away[4:]), before))
        self.last = lax.ppermute(near, AXES, NEAR)
        return before

    def third(self, before):
        if not self.staged:
            return before
        self.last, before = lax.optimization_barrier((self.last, before))
        self.parts = [self.mine, self.got, self.away, self.last]
        return before


def reduce_grads(rows, panels, part):
    everyone = (1, 8, lambda p, c, j: 0)
    summed, parts, tiles = scatter_sum([flat_chunks(rows.shape[0] // 32, 3), everyone], 6, [rows, part], panels, 1)
    return summed, tiles, parts[0, 0]


def reduce_grads_plainly(rows, panels, part, length):
    flat = regroup(rows, 0, True).astype(jnp.float32).reshape(-1)
    flat = jnp.concatenate(
        [flat[:QKV_AT], flat[QKV_AT + QKV_GAP : GAP_AT + QKV_GAP], flat[GAP_AT + QKV_GAP + END_GAP :]]
    )
    devices = lax.axis_size("dp") * lax.axis_size("strip")
    flat = jnp.pad(flat, (0, max(0, devices * length - flat.shape[0])))[: devices * length]
    tiles = tiles_of(chunks_of_panels(panels[0])).astype(jnp.float32)
    flat_sum = lax.psum_scatter(flat, AXES, scatter_dimension=0, tiled=True)
    tile_sum = lax.psum_scatter(tiles, AXES, scatter_dimension=0, tiled=True)
    tile_sum = lax.all_gather(tile_sum.astype(jnp.bfloat16), "strip", axis=0, tiled=True)
    return flat_sum, chunks_of(tile_sum), lax.psum(part[0, 0], AXES)


def adam_plainly(grad, weights, first_moment, second_moment):
    new_first = BETA_FIRST * first_moment + (1.0 - BETA_FIRST) * grad
    new_second = BETA_SECOND * second_moment + (1.0 - BETA_SECOND) * grad * grad
    fix_first = 1.0 - BETA_FIRST**ADAM_STEP
    fix_second = 1.0 - BETA_SECOND**ADAM_STEP
    moved = new_first / fix_first / (jnp.sqrt(new_second / fix_second) + ADAM_EPS)
    return weights - ADAM_RATE * (moved + WEIGHT_DECAY * weights), new_first, new_second


def shards(
    weights,
    blocks,
    stat_left,
    stat_right,
    root_left,
    root_right,
    first_moment,
    second_moment,
    image,
    camera,
    samples,
    ray_pixel,
    target,
    valid,
):
    strips = lax.axis_size("strip")
    place = lax.axis_index("strip")
    mask, wanted, own_count = pick(ray_pixel, valid, target[0])
    rows, panels, count = gather_weights(weights, blocks, own_count)
    tiled = rows.reshape(-1, 8, WIDE)

    def square(name):
        return rows[TILES[name] * 8 : TILES[name] * 8 + D]

    def plain(name, count):
        return rows[TILES[name] * 8 : TILES[name] * 8 + count]

    deconv = spread_deconv(tiled, TILES["deconv"])
    decode = plain("decode", 8).reshape(-1)
    decode_in = decode[: CH * DEC_HID].reshape(CH, DEC_HID)
    decode_out = decode[CH * DEC_HID : CH * DEC_HID + DEC_HID * 4].reshape(DEC_HID, 4)
    picture = image[0]
    real_keys = picture.shape[0]
    picture = jnp.pad(picture, ((0, -real_keys % 16), (0, 0)))
    mods = lax.dynamic_slice_in_dim(plain("modulate", 6 * NCAM), 6 * camera[0], 6).astype(jnp.float32)
    own_rows = PR * TC
    stream0 = jnp.concatenate(
        [
            lax.dynamic_slice_in_dim(rows, TILES["triplane"] * 8 + (strips * plane + place) * own_rows, own_rows)
            for plane in range(3)
        ]
    ).astype(jnp.float32)
    hidden1, norm_one = jax.vjp(norm_mod, stream0, mods[0], mods[1])
    hidden1 = hidden1.astype(jnp.bfloat16)
    query1 = product(hidden1, square("query_cross")).astype(jnp.bfloat16)
    (image_kv,) = project(picture, tiled, TILES["keyval_cross"], 2, 0)
    pairs = D // PAIR
    tokens = query1.shape[0]
    cross_out, total_one = attend_fwd(query1, [image_kv], real_keys, (0, pairs))
    stream1 = stream0 + product(cross_out, square("out_cross"))
    hidden2, norm_two = jax.vjp(norm_mod, stream1, mods[2], mods[3])
    hidden2 = hidden2.astype(jnp.bfloat16)
    panels = Panels(panels)
    hidden2 = panels.first(hidden2)
    query2, kv_own = project(hidden2, tiled, TILES["qkv_self"], 3, 1)
    kv_both = [kv_own, lax.ppermute(kv_own, "strip", SWAP)]
    all_keys = 2 * kv_own.shape[1]
    early = attend_fwd(query2, kv_both, all_keys, (0, pairs // 2))
    early = (panels.second(early[0]), early[1])
    self_out, total_two = attend_fwd(query2, kv_both, all_keys, (pairs // 2, pairs), early)
    panels, deconv = panels.third(self_out, deconv)
    stream2 = stream1 + product(self_out, square("out_self"))
    hidden3, norm_three = jax.vjp(norm_mod, stream2, mods[4], mods[5])
    hidden3 = hidden3.astype(jnp.bfloat16)
    up, act, grid = mlp_fwd(panels, hidden3, stream2)
    grid = grid.reshape(3, own_rows, D)
    edge = lax.ppermute(jnp.where(place == 0, grid[:, -TC:], grid[:, :TC]), "strip", SWAP)
    cells = deconv_fwd(grid, edge, deconv)
    cells_far = lax.ppermute(cells, "strip", SWAP)
    rays = ray_pixel.shape[1]
    factor = 1.0 / jnp.maximum(count, 1.0)
    loss_part, grad_cells, grad_far, grad_decode_in, grad_decode_out = render(
        cells,
        cells_far,
        (samples[0] + place * cells.shape[1]) % (2 * cells.shape[1]),
        wanted,
        mask,
        factor.reshape(1),
        decode_in,
        jnp.pad(decode_out, ((0, 0), (0, 4))),
        rays,
    )
    grad_decode_out = grad_decode_out[:, :4]
    grad_far = lax.ppermute(grad_far, "strip", SWAP)
    grad_grid, beside, grad_deconv = deconv_bwd(grad_cells, grad_far, grid, edge, deconv)
    beside = lax.ppermute(beside, "strip", SWAP).astype(jnp.float32)
    rest = own_rows - TC
    above = jnp.pad(jnp.where(place == 0, 0.0, beside), ((0, 0), (0, rest), (0, 0)))
    below = jnp.pad(jnp.where(place == 0, beside, 0.0), ((0, 0), (rest, 0), (0, 0)))
    grad_grid = grad_grid + above + below
    grad_stream = grad_grid.reshape(-1, D)
    grad_branch = grad_stream.astype(jnp.bfloat16)
    grad_hidden3, *panel_grads = mlp_bwd(panels, hidden3, grad_branch, up, act)
    grad_norm, grad_mod4, grad_mod5 = norm_three(grad_hidden3)
    grad_stream = grad_stream + grad_norm
    grad_branch2 = grad_stream.astype(jnp.bfloat16)
    grad_self = product_back(grad_branch2, square("out_self")).astype(jnp.bfloat16)
    panel_sums = PanelSums(panel_grads)
    grad_self = panel_sums.first(grad_self)
    early = attend_bwd(query2, kv_both, all_keys, (0, pairs - 1), 512, total_two, self_out, grad_self)
    early = (panel_sums.second(early[0]), *early[1:])
    grad_query2, grad_kv_own, grad_kv_far = attend_bwd(
        query2, kv_both, all_keys, (pairs - 1, pairs), 512, total_two, self_out, grad_self, early
    )
    grad_kv_far = lax.ppermute(grad_kv_far, "strip", SWAP)
    grad_hidden2, grad_kv = project_back(grad_query2, grad_kv_own, grad_kv_far, tiled, TILES["qkv_self"], D)
    grad_norm, grad_mod2, grad_mod3 = norm_two(grad_hidden2)
    grad_stream = grad_stream + grad_norm
    grad_branch1 = grad_stream.astype(jnp.bfloat16)
    grad_cross = product_back(grad_branch1, square("out_cross")).astype(jnp.bfloat16)
    grad_query1, grad_image_kv = attend_bwd(
        query1, [image_kv], real_keys, (0, pairs), picture.shape[0], total_one, cross_out, grad_cross
    )
    grad_query1 = panel_sums.third(grad_query1)
    grad_norm, grad_mod0, grad_mod1 = norm_one(product_back(grad_query1, square("query_cross")))
    grad_stream = grad_stream + grad_norm
    grad_mods = jnp.stack([grad_mod0, grad_mod1, grad_mod2, grad_mod3, grad_mod4, grad_mod5])
    grad_modulate = lax.dynamic_update_slice_in_dim(
        jnp.zeros((6 * NCAM, D), jnp.bfloat16), grad_mods.astype(jnp.bfloat16), 6 * camera[0], 0
    )
    grad_decode = jnp.concatenate([grad_decode_in.reshape(-1), grad_decode_out.reshape(-1)])
    grad_decode = jnp.pad(grad_decode, (0, END_GAP))
    total_tiles = tiled.shape[0]
    end = TILES["triplane"] + 3 * strips * own_rows // 8
    gap = TILES["qkv_self"] - TILES["gap"]
    arrays = [
        hidden1,
        grad_query1,
        picture,
        grad_image_kv,
        cross_out,
        grad_branch1,
        hidden2,
        grad_query2,
        grad_kv,
        self_out,
        grad_branch2,
    ]
    tall, low = (tokens, D), (picture.shape[0], DI)
    products = [
        (tall, (9, None), (10, None), TILES["out_self"], (1, 0)),
        (tall, (6, None), (7, None), TILES["qkv_self"], (3, 0)),
        (tall, (6, None), (8, 0), TILES["qkv_self"], (3, 1)),
        (tall, (6, None), (8, 1), TILES["qkv_self"], (3, 2)),
        (tall, (4, None), (5, None), TILES["out_cross"], (1, 0)),
        (low, (2, None), (3, 0), TILES["keyval_cross"], (2, 0)),
        (low, (2, None), (3, 1), TILES["keyval_cross"], (2, 1)),
        (tall, (0, None), (1, None), TILES["query_cross"], (1, 0)),
    ]
    grad_tokens = grad_stream.astype(jnp.bfloat16)
    copies = []
    for piece, first in (
        (grad_deconv, TILES["deconv"]),
        (grad_decode, TILES["decode"]),
        (grad_modulate, TILES["modulate"]),
        (grad_tokens, None),
    ):
        piece = piece.astype(jnp.bfloat16).reshape(-1, 8, WIDE)
        if first is None:
            part = own_rows // 8
            for plane in range(3):
                first = TILES["triplane"] + 2 * plane * part
                copies.append((len(arrays), plane * part, part, first, part))
                copies.append((None, 0, part, first + part, -part))
        else:
            copies.append((len(arrays), 0, piece.shape[0], first, 0))
        arrays.append(piece)
    for first, count in ((TILES["gap"], gap), (end, total_tiles - end)):
        part = own_rows // 8
        for start in range(0, count, part):
            copies.append((None, 0, min(part, count - start), first + start, 0))
    row_grads = weight_grads(arrays, products, copies, total_tiles).reshape(-1, WIDE)
    if direct_links():
        summed, chunks, loss_sum = reduce_grads(row_grads, panel_sums.parts, loss_part)
        new_weights, new_first, new_second = adam(summed, weights, first_moment, second_moment)
    else:
        summed, chunks, loss_sum = reduce_grads_plainly(row_grads, panel_sums.parts, loss_part, weights.shape[0])
        new_weights, new_first, new_second = adam_plainly(summed, weights, first_moment, second_moment)
    new_blocks, block_grads, new_left, new_right, block_rms = shampoo(
        chunks, blocks, stat_left, stat_right, root_left, root_right
    )
    loss = loss_sum * factor
    return (
        loss,
        new_weights,
        new_first,
        new_second,
        new_blocks,
        block_grads,
        new_left,
        new_right,
        block_rms,
    )


def solution(mesh):
    placed = (
        P(("dp", "strip")),
        P("dp", None, None),
        P("dp", None, None),
        P("dp", None, None),
        P("dp", None, None),
        P("dp", None, None),
        P(("dp", "strip")),
        P(("dp", "strip")),
        P("dp", None, None),
        P("dp"),
        P("dp", None, None, "strip"),
        P("dp", "strip"),
        P("dp", None, None),
        P("dp", None),
    )
    return jax.shard_map(
        shards,
        mesh=mesh,
        in_specs=placed,
        out_specs=(
            P(),
            P(("dp", "strip")),
            P(("dp", "strip")),
            P(("dp", "strip")),
            P("dp", None, None),
            P("dp", None, None),
            P("dp", None, None),
            P("dp", None, None),
            P("dp"),
        ),
        check_vma=False,
    )
```
